32 devices in a mesh: ctx: 16 (over z, y, x), wt: 2 (over core).
Axes of the slice: x: 2, y: 2, z: 4, core: 2. Of those that a mesh axis runs over, the one named last changes fastest.
Arguments:
- tokens: bfloat16 [8192, 2048], P('ctx'), may hold values from -6 to 6
- cotangent: bfloat16 [8192, 2048], P('ctx'), may hold values from -6 to 6
- mix_norm_gain: bfloat16 [2048], P('ctx'), may hold values from 0.5 to 1.5
- ssm_gate_proj: bfloat16 [2048, 3072], P('ctx', 'wt'), may hold values from -0.125 to 0.125
- ssm_input_proj: bfloat16 [2048, 3072], P('ctx', 'wt'), may hold values from -0.125 to 0.125
- ssm_bc_proj: bfloat16 [2048, 512], P('ctx'), may hold values from -0.125 to 0.125
- ssm_step_proj: bfloat16 [2048, 48], P('ctx', 'wt'), may hold values from -0.125 to 0.125
- conv_in_weight: bfloat16 [3072, 4], P('wt'), may hold values from -3 to 3
- conv_in_bias: bfloat16 [3072], P('wt'), may hold values from -3 to 3
- conv_bc_weight: bfloat16 [512, 4], P('ctx'), may hold values from -3 to 3
- conv_bc_bias: bfloat16 [512], P('ctx'), may hold values from -3 to 3
- step_bias: bfloat16 [48], P('wt'), may hold values from -12 to -5
- decay_log: bfloat16 [48], P('wt'), may hold values from 0 to 1.3984375
- skip_gain: bfloat16 [48], P('wt'), may hold values from 0.5 to 1.5
- ssm_out_proj: bfloat16 [3072, 2048], P('wt', 'ctx'), may hold values from -0.109375 to 0.109375
- query_proj: bfloat16 [2048, 1024], P('ctx', 'wt'), may hold values from -0.125 to 0.125
- key_proj: bfloat16 [2048, 256], P('ctx', 'wt'), may hold values from -0.125 to 0.125
- value_proj: bfloat16 [2048, 256], P('ctx', 'wt'), may hold values from -0.125 to 0.125
- attn_out_proj: bfloat16 [1024, 2048], P('wt', 'ctx'), may hold values from -3 to 3
- ffn_norm_gain: bfloat16 [2048], P('ctx'), may hold values from 0.5 to 1.5
- ffn_gate_proj: bfloat16 [2048, 4096], P('ctx', 'wt'), may hold values from -0.125 to 0.125
- ffn_up_proj: bfloat16 [2048, 4096], P('ctx', 'wt'), may hold values from -0.125 to 0.125
- ffn_down_proj: bfloat16 [4096, 2048], P('wt', 'ctx'), may hold values from -0.09375 to 0.09375
- extra_blocks: int32 [4], replicated, may hold values from 1 to 7, 12 in all
- seq_order: int32 [4], replicated, may hold values from 0 to 3, each once
- pad_rows: int32 [4], replicated, may hold values from 0 to 255
Outputs:
- layer_out: bfloat16 [8192, 2048], P('ctx')
- tokens_grad: bfloat16 [8192, 2048], P('ctx')
- mix_norm_gain_grad: float32 [2048], P('ctx')
- ssm_gate_proj_grad: float32 [2048, 3072], P('ctx', 'wt')
- ssm_input_proj_grad: float32 [2048, 3072], P('ctx', 'wt')
- ssm_bc_proj_grad: float32 [2048, 512], P('ctx')
- ssm_step_proj_grad: float32 [2048, 48], P('ctx', 'wt')
- conv_in_weight_grad: float32 [3072, 4], P('wt')
- conv_in_bias_grad: float32 [3072], P('wt')
- conv_bc_weight_grad: float32 [512, 4], P('ctx')
- conv_bc_bias_grad: float32 [512], P('ctx')
- step_bias_grad: float32 [48], P('wt')
- decay_log_grad: float32 [48], P('wt')
- skip_gain_grad: float32 [48], P('wt')
- ssm_out_proj_grad: float32 [3072, 2048], P('wt', 'ctx')
- query_proj_grad: float32 [2048, 1024], P('ctx', 'wt')
- key_proj_grad: float32 [2048, 256], P('ctx', 'wt')
- value_proj_grad: float32 [2048, 256], P('ctx', 'wt')
- attn_out_proj_grad: float32 [1024, 2048], P('wt', 'ctx')
- ffn_norm_gain_grad: float32 [2048], P('ctx')
- ffn_gate_proj_grad: float32 [2048, 4096], P('ctx', 'wt')
- ffn_up_proj_grad: float32 [2048, 4096], P('ctx', 'wt')
- ffn_down_proj_grad: float32 [4096, 2048], P('wt', 'ctx')
The draws below stay inside these ranges and needn't reach their ends.
Inputs may be any that keep to these rules, and one draw needn't show every extreme that they name: Sequence s occupies extra_blocks[s] + 1 blocks of 512 rows; the entries sum to 12, and one of them is 7. `seq_order`: A permutation of the sequences.
All inputs are finite; a program needn't handle non-finite values.
Results may differ from the reference program's by a relative error of at most 0.015.
Values may be sent and summed in bfloat16 or wider, within the bound.
No kernel may reach another device: no remote copies, remote signals or barrier semaphores. Data moves between devices by JAX's collectives and lax.ppermute only.
A program may use at most 448 MiB of HBM per device.

```python
import math
from functools import partial
import jax
import jax.numpy as jnp
import numpy as np
from jax import lax

D = 2048
DI = 3072
HM = 48
P_SIZE = 64
NS = 256
HQ = 8
HK = 2
HD = 128
FF = 4096
KW = 4
TOK_DEV = 512
MAXB = 8
NSEQ = 4
TOKENS = 8192
N_CTX = 16


def with_ends(array, key, smallest, high):
    place = [jax.random.randint(jax.random.fold_in(key, axis), (), 0, length) for axis, length in enumerate(array.shape)]
    main_axis = array.shape.index(max(array.shape))
    beside = place[:main_axis] + [(place[main_axis] + 1) % array.shape[main_axis]] + place[main_axis + 1:]
    return array.at[tuple(place)].set(smallest).at[tuple(beside)].set(high)


def raised(array, key, source, target, blocks, factor):
    def block_of(position):
        return (jnp.arange(array.shape[position]) // (array.shape[position] // blocks)).reshape((-1,) + (1,) * (array.ndim - 1 - position))

    near = jax.random.permutation(key, blocks)[block_of(target)]
    far = (block_of(target) + blocks // 2) % blocks
    return jnp.where((block_of(source) == near) | (block_of(source) == far), factor * array, array)


def steps_of(rng, extent, shards, low, largest):
    def one(dim, shards_of):
        draws = jax.random.uniform(jax.random.fold_in(jax.random.fold_in(rng, 6), dim), (shards_of,), jnp.float32, low / len(shards), largest / len(shards))
        return jnp.repeat(jnp.exp(draws), extent[dim] // shards_of).reshape((-1,) + (1,) * (len(extent) - dim - 1))

    gain = one(*shards[0])
    for cut in shards[1:]:
        gain = gain * one(*cut)
    return gain


def split_up(amount, total, bound, skew):
    loads = [(1 << 20) // math.isqrt(grade ** skew) + 1 for grade in range(2, amount + 1)]
    surplus, holding = total - bound - (amount - 1), [1] * (amount - 1)
    while surplus > 0:
        candidates = [i for i in range(amount - 1) if holding[i] < bound]
        mass, remaining = sum([loads[i] for i in candidates]), surplus
        for i in candidates:
            more = min(bound - holding[i], max(1, remaining * loads[i] // mass), surplus)
            holding[i] = holding[i] + more
            surplus = surplus - more
    return np.array([bound] + holding)


def uneven_parts(own_key, amount, total, limit, skew):
    if amount == 2:
        one = jax.random.randint(own_key, (), max(1, total - limit), min(limit, total - 1) + 1)
        return jnp.stack([one, total - one])
    lengths = jnp.asarray(split_up(amount, total, limit, skew), jnp.int32)
    pairs = (amount - 1) // 2
    source_of, receiver = lengths[1:1 + 2 * pairs:2], lengths[2:2 + 2 * pairs:2]
    margin = jnp.minimum(source_of - 1, limit - receiver)
    shifted = jax.random.randint(jax.random.fold_in(own_key, 1), (pairs,), 0, 1 << 20) % (margin + 1)
    lengths = lengths.at[1:1 + 2 * pairs:2].set(source_of - shifted).at[2:2 + 2 * pairs:2].set(receiver + shifted)
    return lengths[jax.random.permutation(jax.random.fold_in(own_key, 2), amount)]


def scatter_about(key, shape, scale, reach, cuts=(), held_as=jnp.bfloat16):
    result = scale * jax.random.normal(key, shape, jnp.float32)
    if cuts:
        result = result * steps_of(key, shape, cuts, -0.22, 0.18)
    return jnp.clip(result, -reach, reach).astype(held_as)


def noise_with(rng, shape, spread, reach, shards, heavy, kind=jnp.bfloat16):
    drawn = spread * jax.random.normal(rng, shape, jnp.float32)
    if shards:
        drawn = drawn * steps_of(rng, shape, shards, -0.22, 0.18)
    return jnp.clip(raised(drawn, jax.random.fold_in(rng, 3), *heavy), -reach, reach).astype(kind)


def setup_inputs(seed: int = 0) -> dict:
    arg_keys = jax.random.split(jax.random.key(seed), 27)
    tokens = noise_with(arg_keys[0], (TOKENS, D), 1.0, 6.0, ((0, 16),), (0, 1, 16, 2.0))
    cotangent = noise_with(arg_keys[1], (TOKENS, D), 1.0, 6.0, ((0, 16),), (0, 1, 16, 2.0))
    mix_norm_gain = jnp.clip(1.0 + 0.1 * jax.random.normal(arg_keys[2], (D,), jnp.float32), 0.5, 1.5).astype(jnp.bfloat16)
    ssm_gate_proj = scatter_about(arg_keys[3], (D, DI), D ** -0.5, 0.125, ((0, 16), (1, 2)))
    ssm_input_proj = scatter_about(arg_keys[4], (D, DI), D ** -0.5, 0.125, ((0, 16), (1, 2)))
    ssm_bc_proj = scatter_about(arg_keys[5], (D, 2 * NS), D ** -0.5, 0.125, ((0, 16),))
    ssm_step_proj = scatter_about(arg_keys[6], (D, HM), D ** -0.5, 0.125, ((0, 16), (1, 2)))
    conv_in_weight = scatter_about(arg_keys[7], (DI, KW), KW ** -0.5, 3.0, ((0, 2),))
    conv_in_bias = scatter_about(arg_keys[8], (DI,), 0.5, 3.0, ((0, 2),))
    conv_bc_weight = scatter_about(arg_keys[9], (2 * NS, KW), KW ** -0.5, 3.0, ((0, 16),))
    conv_bc_bias = scatter_about(arg_keys[10], (2 * NS,), 0.5, 3.0, ((0, 16),))
    step_bias = jnp.clip(-12.0 + 7.0 * jax.random.uniform(arg_keys[11], (HM,), jnp.float32) ** steps_of(arg_keys[11], (HM,), ((0, 2),), -0.2, 0.2), -12.0, -5.0).astype(jnp.bfloat16)
    decay_log = jnp.clip(1.3984375 * jax.random.uniform(arg_keys[12], (HM,), jnp.float32) ** steps_of(arg_keys[12], (HM,), ((0, 2),), -0.2, 0.2), 0.0, 1.3984375).astype(jnp.bfloat16)
    skip_gain = jnp.clip(0.5 + 1.0 * jax.random.uniform(arg_keys[13], (HM,), jnp.float32) ** steps_of(arg_keys[13], (HM,), ((0, 2),), -0.2, 0.2), 0.5, 1.5).astype(jnp.bfloat16)
    ssm_out_proj = scatter_about(arg_keys[14], (DI, D), DI ** -0.5, 0.109375, ((0, 2), (1, 16)))
    query_proj = scatter_about(arg_keys[15], (D, HQ * HD), D ** -0.5, 0.125, ((0, 16), (1, 2)))
    key_proj = scatter_about(arg_keys[16], (D, HK * HD), D ** -0.5, 0.125, ((0, 16), (1, 2)))
    value_proj = scatter_about(arg_keys[17], (D, HK * HD), D ** -0.5, 0.125, ((0, 16), (1, 2)))
    attn_out_proj = scatter_about(arg_keys[18], (HQ * HD, D), 4 ** -0.5, 3.0, ((0, 2), (1, 16)))
    ffn_norm_gain = jnp.clip(1.0 + 0.1 * jax.random.normal(arg_keys[19], (D,), jnp.float32), 0.5, 1.5).astype(jnp.bfloat16)
    ffn_gate_proj = scatter_about(arg_keys[20], (D, FF), D ** -0.5, 0.125, ((0, 16), (1, 2)))
    ffn_up_proj = scatter_about(arg_keys[21], (D, FF), D ** -0.5, 0.125, ((0, 16), (1, 2)))
    ffn_down_proj = scatter_about(arg_keys[22], (FF, D), FF ** -0.5, 0.09375, ((0, 2), (1, 16)))
    extra_blocks = uneven_parts(arg_keys[23], NSEQ, N_CTX - NSEQ, MAXB - 1, 1).astype(jnp.int32)
    seq_order = jax.random.permutation(arg_keys[24], NSEQ).astype(jnp.int32)
    pad_rows = with_ends(jax.random.randint(arg_keys[25], (NSEQ,), 0, TOK_DEV // 2), jax.random.fold_in(arg_keys[25], 1), 0, (TOK_DEV // 2) - 1).astype(jnp.int32)
    return dict(tokens=tokens, cotangent=cotangent, mix_norm_gain=mix_norm_gain, ssm_gate_proj=ssm_gate_proj, ssm_input_proj=ssm_input_proj, ssm_bc_proj=ssm_bc_proj, ssm_step_proj=ssm_step_proj, conv_in_weight=conv_in_weight, conv_in_bias=conv_in_bias, conv_bc_weight=conv_bc_weight, conv_bc_bias=conv_bc_bias, step_bias=step_bias, decay_log=decay_log, skip_gain=skip_gain, ssm_out_proj=ssm_out_proj, query_proj=query_proj, key_proj=key_proj, value_proj=value_proj, attn_out_proj=attn_out_proj, ffn_norm_gain=ffn_norm_gain, ffn_gate_proj=ffn_gate_proj, ffn_up_proj=ffn_up_proj, ffn_down_proj=ffn_down_proj, extra_blocks=extra_blocks, seq_order=seq_order, pad_rows=pad_rows)


@jax.custom_vjp
def low(v):
    return lax.optimization_barrier(v.astype(jnp.bfloat16)).astype(jnp.float32)

@jax.custom_vjp
def low_back(v):
    return v

def low_keep(v):
    return (low(v), None)

def low_pass(kept, grad):
    return (grad,)

def back_keep(v):
    return (v, None)

def back_low(kept, grad):
    return (low(grad),)
low.defvjp(low_keep, low_pass)
low_back.defvjp(back_keep, back_low)
epsilon = 1e-05
rope_base = 100000000000.0
highest = lax.Precision.HIGHEST
masked_score = -1e+30

def exact_dot(left_side, right_side):
    return jnp.dot(left_side, right_side, precision=highest)

def rms_scale(values, gain_vec):
    return values * lax.rsqrt(lax.optimization_barrier(jnp.mean(values * values, axis=-1, keepdims=True)) + epsilon) * gain_vec

def rotary_tables(positions):
    exponents = jnp.arange(HD // 2, dtype=jnp.float32) * (2.0 / HD)
    frequency = jnp.power(jnp.float32(rope_base), -exponents)
    angles = positions.astype(jnp.float32)[:, None] * frequency[None, :]
    return (jnp.cos(angles), jnp.sin(angles))

def rotate(values, cos_table, sin_table):
    half_dim = values.shape[-1] // 2
    first_half = values[..., :half_dim]
    second_half = values[..., half_dim:]
    cos_table = cos_table[:, None, :]
    sin_table = sin_table[:, None, :]
    return jnp.concatenate([first_half * cos_table - second_half * sin_table, second_half * cos_table + first_half * sin_table], axis=-1)

def window_mask(within, pad_here, block_rows):
    key_index = jnp.arange(MAXB * block_rows, dtype=jnp.int32)
    key_block = key_index // block_rows
    key_row = key_index - key_block * block_rows
    distance = MAXB - 1 - key_block
    query_row = jnp.arange(block_rows, dtype=jnp.int32)
    key_ok = jnp.where(distance == 0, key_row < block_rows - pad_here, distance <= within)
    return key_ok[None, :] & ((distance[None, :] > 0) | (key_row[None, :] <= query_row[:, None]))

def conv_silu(extended, weight, offset):
    kernel_width = weight.shape[1]
    length = extended.shape[0] - kernel_width + 1
    summed = offset[None, :] + extended[:length] * weight[None, :, 0]
    for shift_index in range(1, kernel_width):
        summed = summed + extended[shift_index:shift_index + length] * weight[None, :, shift_index]
    return jax.nn.silu(summed)

def mamba_inner(ext_in, ext_bc, step_raw, conv_in_weight, conv_in_bias, conv_bc_weight, conv_bc_bias, step_bias, decay_log, skip_gain):
    conv_acts = conv_silu(ext_in, conv_in_weight, conv_in_bias)
    bc_acts = conv_silu(ext_bc, conv_bc_weight, conv_bc_bias)
    state_dim = bc_acts.shape[1] // 2
    b_part = bc_acts[:, :state_dim]
    c_part = bc_acts[:, state_dim:]
    length = conv_acts.shape[0]
    head_count = step_raw.shape[1]
    gram_matrix = jnp.dot(c_part, b_part.T, precision=highest)
    lower_tri = jnp.arange(length)[:, None] >= jnp.arange(length)[None, :]

    def one_head(pieces):
        acts_head, raw_head, bias_head, log_head, skip_head = pieces
        step_size = jax.nn.softplus(raw_head + bias_head)
        cumulative = jnp.cumsum(-jnp.exp(log_head) * step_size)
        log_gaps = jnp.where(lower_tri, cumulative[:, None] - cumulative[None, :], 0.0)
        weights = jnp.where(lower_tri, jnp.exp(log_gaps), 0.0) * gram_matrix * step_size[None, :]
        intra_out = jnp.dot(weights, acts_head, precision=highest) + skip_head * acts_head
        tail_weight = jnp.exp(cumulative[-1] - cumulative) * step_size
        states = jnp.dot((b_part * tail_weight[:, None]).T, acts_head, precision=highest)
        return (intra_out, states, jnp.exp(cumulative[-1]), jnp.exp(cumulative))
    head_acts = conv_acts.reshape(length, head_count, -1).transpose(1, 0, 2)
    intra_out, states, decays, growth = lax.map(jax.checkpoint(one_head), (head_acts, step_raw.T, step_bias, decay_log, skip_gain))
    return (intra_out.transpose(1, 0, 2).reshape(length, -1), states, decays, growth, c_part)

def mamba_finish(intra_out, growth, c_part, state_in, gate_pre):
    length = intra_out.shape[0]
    carried = jnp.einsum('ln,hnp->lhp', c_part, state_in, precision=highest) * growth.T[:, :, None]
    return (intra_out + carried.reshape(length, -1)) * jax.nn.silu(gate_pre)

def attend_block(query_block, key_window, value_window, allowed):
    scores = jnp.einsum('qkgd,skd->kgqs', query_block, key_window, precision=highest) * HD ** (-0.5)
    scores = low_back(scores)
    scores = jnp.where(allowed[None, None], scores, masked_score)
    probs = low(jax.nn.softmax(scores, axis=-1))
    return jnp.einsum('kgqs,skd->qkgd', probs, value_window, precision=highest)

def block_layout(extra_blocks, seq_order, pad_rows):
    counts = extra_blocks[seq_order] + 1
    slot_ends = jnp.cumsum(counts).astype(jnp.int32)
    starts = slot_ends - counts
    blocks = jnp.arange(N_CTX, dtype=jnp.int32)
    inside = (starts[None, :] <= blocks[:, None]) & (blocks[:, None] < slot_ends[None, :])
    within = lax.optimization_barrier(jnp.sum(jnp.where(inside, blocks[:, None] - starts[None, :], 0), axis=1)).astype(jnp.int32)
    last_block = inside & (slot_ends[None, :] - 1 == blocks[:, None])
    pad_here = lax.optimization_barrier(jnp.sum(jnp.where(last_block, pad_rows[seq_order][None, :], 0), axis=1)).astype(jnp.int32)
    return (within, pad_here)

def hybrid_layer(layout, tokens, mix_norm_gain, ssm_gate_proj, ssm_input_proj, ssm_bc_proj, ssm_step_proj, conv_in_weight, conv_in_bias, conv_bc_weight, conv_bc_bias, step_bias, decay_log, skip_gain, ssm_out_proj, query_proj, key_proj, value_proj, attn_out_proj, ffn_norm_gain, ffn_gate_proj, ffn_up_proj, ffn_down_proj):
    within, pad_here = layout
    block_rows = TOK_DEV
    total_rows = tokens.shape[0]
    row_ids = jnp.arange(block_rows, dtype=jnp.int32)
    valid_rows = (row_ids[None, :] < block_rows - pad_here[:, None]).astype(jnp.float32).reshape(-1)
    positions = (within[:, None] * block_rows + row_ids[None, :]).reshape(-1)
    keep_state = (within > 0).astype(jnp.float32)
    normed = low(rms_scale(tokens, mix_norm_gain))
    gate_pre = low_back(exact_dot(normed, ssm_gate_proj))
    input_pre = low_back(exact_dot(normed, ssm_input_proj))
    bc_pre = low_back(exact_dot(normed, ssm_bc_proj))
    step_raw = low_back(exact_dot(normed, ssm_step_proj))
    rim_rows = KW - 1

    def with_rim(stream):
        blocked = stream.reshape(N_CTX, block_rows, -1)
        earlier = jnp.concatenate([jnp.zeros_like(blocked[:1, :rim_rows]), blocked[:-1, block_rows - rim_rows:]], axis=0)
        return jnp.concatenate([earlier * keep_state[:, None, None], blocked], axis=1)

    def block_step(carried, pieces):
        ext_in, ext_bc, raw_block, gate_block, keep_block = pieces
        intra_out, states, decays, growth, c_part = mamba_inner(ext_in, ext_bc, raw_block, conv_in_weight, conv_in_bias, conv_bc_weight, conv_bc_bias, step_bias, decay_log, skip_gain)
        state_in = carried * keep_block
        gated = mamba_finish(intra_out, growth, c_part, state_in, gate_block)
        return (decays[:, None, None] * state_in + states, gated)
    start_state = jnp.zeros((HM, NS, P_SIZE), jnp.float32)
    final_state, gated = lax.scan(jax.checkpoint(block_step), start_state, (with_rim(input_pre), with_rim(bc_pre), step_raw.reshape(N_CTX, block_rows, HM), gate_pre.reshape(N_CTX, block_rows, DI), keep_state))
    ssm_out = low(gated.reshape(total_rows, DI))
    cos_table, sin_table = rotary_tables(positions)
    query_all = low(rotate(low_back(exact_dot(normed, query_proj)).reshape(total_rows, HQ, HD), cos_table, sin_table))
    key_all = low(rotate(low_back(exact_dot(normed, key_proj)).reshape(total_rows, HK, HD), cos_table, sin_table))
    value_all = low(low_back(exact_dot(normed, value_proj))).reshape(total_rows, HK, HD)
    leading = jnp.zeros(((MAXB - 1) * block_rows, HK, HD), jnp.float32)
    key_padded = jnp.concatenate([leading, key_all], axis=0)
    value_padded = jnp.concatenate([leading, value_all], axis=0)

    def one_block(pieces):
        query_block, block_index, within_block, pad_block = pieces
        row_start = (block_index * block_rows).astype(jnp.int32)
        key_window = lax.dynamic_slice_in_dim(key_padded, row_start, MAXB * block_rows, 0)
        value_window = lax.dynamic_slice_in_dim(value_padded, row_start, MAXB * block_rows, 0)
        allowed = window_mask(within_block, pad_block, block_rows)
        return attend_block(query_block, key_window, value_window, allowed)
    attended = lax.map(jax.checkpoint(one_block), (query_all.reshape(N_CTX, block_rows, HK, HQ // HK, HD), jnp.arange(N_CTX, dtype=jnp.int32), within, pad_here))
    attn_low = low(low_back(attended.reshape(total_rows, HQ * HD)))
    mixed_sum = low_back(exact_dot(ssm_out, ssm_out_proj) + exact_dot(attn_low, attn_out_proj))
    hidden = tokens + mixed_sum
    normed_two = low(rms_scale(hidden, ffn_norm_gain))
    gate_all = low_back(exact_dot(normed_two, ffn_gate_proj))
    up_all = low_back(exact_dot(normed_two, ffn_up_proj))
    ffn_act = low(jax.nn.silu(gate_all) * up_all)
    ffn_out = low_back(exact_dot(ffn_act, ffn_down_proj))
    return (hidden + ffn_out) * valid_rows[:, None]

def reference(tokens, cotangent, mix_norm_gain, ssm_gate_proj, ssm_input_proj, ssm_bc_proj, ssm_step_proj, conv_in_weight, conv_in_bias, conv_bc_weight, conv_bc_bias, step_bias, decay_log, skip_gain, ssm_out_proj, query_proj, key_proj, value_proj, attn_out_proj, ffn_norm_gain, ffn_gate_proj, ffn_up_proj, ffn_down_proj, extra_blocks, seq_order, pad_rows):
    layout = block_layout(extra_blocks, seq_order, pad_rows)
    floats = tuple((array_in.astype(jnp.float32) for array_in in (tokens, mix_norm_gain, ssm_gate_proj, ssm_input_proj, ssm_bc_proj, ssm_step_proj, conv_in_weight, conv_in_bias, conv_bc_weight, conv_bc_bias, step_bias, decay_log, skip_gain, ssm_out_proj, query_proj, key_proj, value_proj, attn_out_proj, ffn_norm_gain, ffn_gate_proj, ffn_up_proj, ffn_down_proj)))
    layer_out, layer_back = jax.vjp(partial(hybrid_layer, layout), *floats)
    gradients = layer_back(cotangent.astype(jnp.float32))
    return (layer_out.astype(jnp.bfloat16), gradients[0].astype(jnp.bfloat16), gradients[1], gradients[2], gradients[3], gradients[4], gradients[5], gradients[6], gradients[7], gradients[8], gradients[9], gradients[10], gradients[11], gradients[12], gradients[13], gradients[14], gradients[15], gradients[16], gradients[17], gradients[18], gradients[19], gradients[20], gradients[21])
```

```python
import jax
import jax.numpy as jnp
from jax import lax
from jax.experimental import pallas as pl
from jax.experimental.pallas import tpu as pltpu
from jax.sharding import PartitionSpec as P

HD = 128
KW = 4
MAXB = 8


epsilon = 1e-05
rope_base = 100000000000.0
highest = lax.Precision.HIGHEST
masked_score = -1e30


def shifted(value, axis, steps):
    count = lax.axis_size(axis)
    leading, last = (max(0, -steps), min(count, count - steps))
    return lax.ppermute(value, axis, [(source, source + steps) for source in range(leading, last)])


def hop(value, code):
    if code == 0:
        return value
    count = lax.axis_size("ctx")
    return lax.ppermute(value, "ctx", [(source, source ^ code) for source in range(count)])


def swap(value):
    return lax.ppermute(value, "wt", [(0, 1), (1, 0)])


def pair_sum(value):
    rounded = lax.reduce_precision(value, 8, 7)
    return rounded + swap(rounded.astype(jnp.bfloat16)).astype(jnp.float32)


def slot_devices(count):
    high = count // 4
    return [4 * (slot % high) + slot // high for slot in range(count)]


def gathered(piece, axis, first):
    high = lax.axis_size("ctx") // 4
    second = 3 - first
    quarter = jnp.concatenate([piece] + [hop(piece, 4 * k) for k in range(1, high)], axis=axis)
    parts = {0: quarter, first: hop(quarter, first)}
    parts[second] = hop(quarter, second)
    parts[3] = hop(parts[first], second)
    return jnp.concatenate([parts[k] for k in range(4)], axis=axis)


def reduced(parts, axis, first):
    high = lax.axis_size("ctx") // 4
    second = 3 - first
    low = [part.astype(jnp.bfloat16) for part in parts]
    near = parts[0] + hop(low[first], first).astype(jnp.float32)
    far = parts[second] + hop(low[3], first).astype(jnp.float32)
    quarter = near + hop(far.astype(jnp.bfloat16), second).astype(jnp.float32)
    blocks = jnp.split(quarter, high, axis=axis)
    total = blocks[0]
    for k in range(1, high):
        total = total + hop(blocks[k].astype(jnp.bfloat16), 4 * k).astype(jnp.float32)
    return total


def summed(value):
    bit = 1
    while bit < lax.axis_size("ctx"):
        value = value + hop(value, bit)
        bit *= 2
    return value


def reordered(value, order):
    blocks = order.shape[0]
    rows, width = value.shape[0], value.shape[1] // blocks
    if width % 128:
        return jnp.take(value.reshape(rows, blocks, width), order, axis=1).reshape(rows, -1)

    def body(order_ref, in_ref, out_ref):
        out_ref[...] = in_ref[...]

    return pl.pallas_call(
        body,
        out_shape=jax.ShapeDtypeStruct(value.shape, value.dtype),
        grid_spec=pltpu.PrefetchScalarGridSpec(
            num_scalar_prefetch=1,
            grid=(blocks,),
            in_specs=[pl.BlockSpec((rows, width), lambda s, order_ref: (0, order_ref[s]))],
            out_specs=pl.BlockSpec((rows, width), lambda s, order_ref: (0, s)),
        ),
        name="reordered",
    )(order, value)


def carried_states(states, decays, reverse):
    me = lax.axis_index("ctx")
    place = me % 4
    width = states.shape[1] // 4
    low = states.astype(jnp.bfloat16)

    def quarter(value, index):
        return lax.dynamic_slice_in_dim(value, index * width, width, 1)

    got = [hop(quarter(low, place ^ k), k) for k in range(4)]
    got_decay = [hop(quarter(decays, place ^ k), k) for k in range(4)]

    def in_order(pieces):
        odd = place % 2 == 1
        pieces = [jnp.where(odd, pieces[k ^ 1], pieces[k]) for k in range(4)]
        upper = place >= 2
        return [jnp.where(upper, pieces[k ^ 2], pieces[k]) for k in range(4)]

    blocks = [piece.astype(jnp.float32) for piece in in_order(got)]
    rates = in_order(got_decay)
    if reverse:
        blocks, rates = (blocks[::-1], rates[::-1])
    total, rate = (blocks[0], rates[0])
    for block, block_rate in zip(blocks[1:], rates[1:]):
        total, rate = (block + block_rate * total, block_rate * rate)
    step = -4 if reverse else 4
    total_low = total.astype(jnp.bfloat16)
    near, near_rate = (shifted(total_low, "ctx", step), shifted(rate, "ctx", step))
    far = shifted(total_low, "ctx", 2 * step)
    state = near.astype(jnp.float32) + near_rate * far.astype(jnp.float32)
    reached = []
    for block, block_rate in zip(blocks, rates):
        reached.append(state.astype(jnp.bfloat16))
        state = block + block_rate * state
    if reverse:
        reached = reached[::-1]
    mine = in_order(reached)
    back = in_order([hop(mine[k], k) for k in range(4)])
    return jnp.concatenate(back, axis=1)


def plain_product(left_side, right_side):
    return jnp.dot(left_side, right_side, preferred_element_type=jnp.float32)


def product_by_rows(left_side, right_side):
    return lax.dot_general(
        left_side, right_side, (((1,), (1,)), ((), ())), preferred_element_type=jnp.float32
    )


def product_of_cols(left_side, right_side):
    return lax.dot_general(
        left_side, right_side, (((0,), (0,)), ((), ())), preferred_element_type=jnp.float32
    )


def rms_scale(values, gain_vec):
    return (
        values * lax.rsqrt(jnp.mean(values * values, axis=-1, keepdims=True) + epsilon) * gain_vec
    )


def rotary_tables(positions):
    exponents = jnp.arange(HD // 2, dtype=jnp.float32) * (2.0 / HD)
    frequency = jnp.power(jnp.float32(rope_base), -exponents)
    angles = positions.astype(jnp.float32)[:, None] * frequency[None, :]
    return (jnp.cos(angles), jnp.sin(angles))


def rotate(values, cos_table, sin_table):
    half_dim = values.shape[-1] // 2
    first_half = values[..., :half_dim]
    second_half = values[..., half_dim:]
    cos_table = cos_table[:, None, :]
    sin_table = sin_table[:, None, :]
    return jnp.concatenate(
        [
            first_half * cos_table - second_half * sin_table,
            second_half * cos_table + first_half * sin_table,
        ],
        axis=-1,
    )


def window_mask(within, pad_here, block_rows):
    key_index = jnp.arange(MAXB * block_rows, dtype=jnp.int32)
    key_block = key_index // block_rows
    key_row = key_index - key_block * block_rows
    distance = MAXB - 1 - key_block
    query_row = jnp.arange(block_rows, dtype=jnp.int32)
    key_ok = jnp.where(distance == 0, key_row < block_rows - pad_here, distance <= within)
    return key_ok[None, :] & ((distance[None, :] > 0) | (key_row[None, :] <= query_row[:, None]))


def conv_silu(extended, weight, offset):
    kernel_width = weight.shape[1]
    length = extended.shape[0] - kernel_width + 1
    summed = offset[None, :] + extended[:length] * weight[None, :, 0]
    for shift_index in range(1, kernel_width):
        summed = (
            summed + extended[shift_index : shift_index + length] * weight[None, :, shift_index]
        )
    return jax.nn.silu(summed)


def mamba_inner(
    ext_in,
    ext_bc,
    step_raw,
    conv_in_weight,
    conv_in_bias,
    conv_bc_weight,
    conv_bc_bias,
    step_bias,
    decay_log,
    skip_gain,
):
    conv_acts = conv_silu(ext_in, conv_in_weight, conv_in_bias)
    bc_acts = conv_silu(ext_bc, conv_bc_weight, conv_bc_bias)
    state_dim = bc_acts.shape[1] // 2
    b_part = bc_acts[:, :state_dim]
    c_part = bc_acts[:, state_dim:]
    length = conv_acts.shape[0]
    head_count = step_raw.shape[1]
    gram_matrix = jnp.dot(c_part, b_part.T, precision=highest)
    lower_tri = jnp.arange(length)[:, None] >= jnp.arange(length)[None, :]

    def one_head(pieces):
        acts_head, raw_head, bias_head, log_head, skip_head = pieces
        step_size = jax.nn.softplus(raw_head + bias_head)
        cumulative = jnp.cumsum(-jnp.exp(log_head) * step_size)
        log_gaps = jnp.where(lower_tri, cumulative[:, None] - cumulative[None, :], 0.0)
        weights = jnp.where(lower_tri, jnp.exp(log_gaps), 0.0) * gram_matrix * step_size[None, :]
        intra_out = jnp.dot(weights, acts_head, precision=highest) + skip_head * acts_head
        tail_weight = jnp.exp(cumulative[-1] - cumulative) * step_size
        states = jnp.dot((b_part * tail_weight[:, None]).T, acts_head, precision=highest)
        return (intra_out, states, jnp.exp(cumulative[-1]), jnp.exp(cumulative))

    head_acts = conv_acts.reshape(length, head_count, -1).transpose(1, 0, 2)
    intra_out, states, decays, growth = lax.map(
        jax.checkpoint(one_head), (head_acts, step_raw.T, step_bias, decay_log, skip_gain)
    )
    return (intra_out.transpose(1, 0, 2).reshape(length, -1), states, decays, growth, c_part)


def mamba_finish(intra_out, growth, c_part, state_in, gate_pre):
    length = intra_out.shape[0]
    carried = jnp.einsum("ln,hnp->lhp", c_part, state_in, precision=highest) * growth.T[:, :, None]
    return (intra_out + carried.reshape(length, -1)) * jax.nn.silu(gate_pre)


def chain_combine(earlier, later):
    return (earlier[0] * later[0], later[0][:, None, None] * earlier[1] + later[1])


def per_device(
    tokens,
    cotangent,
    mix_norm_gain,
    ssm_gate_proj,
    ssm_input_proj,
    ssm_bc_proj,
    ssm_step_proj,
    conv_in_weight,
    conv_in_bias,
    conv_bc_weight,
    conv_bc_bias,
    step_bias,
    decay_log,
    skip_gain,
    ssm_out_proj,
    query_proj,
    key_proj,
    value_proj,
    attn_out_proj,
    ffn_norm_gain,
    ffn_gate_proj,
    ffn_up_proj,
    ffn_down_proj,
    extra_blocks,
    seq_order,
    pad_rows,
):
    block_rows = tokens.shape[0]
    block_index = lax.axis_index("ctx")
    seq_count = seq_order.shape[0]
    slot_ids = jnp.arange(seq_count, dtype=jnp.int32)
    chosen = (seq_order[:, None] == slot_ids[None, :]).astype(jnp.int32)
    counts = jnp.sum(chosen * extra_blocks[None, :], axis=1) + 1
    slot_pads = jnp.sum(chosen * pad_rows[None, :], axis=1)
    slot_ends = jnp.cumsum(counts)
    starts = slot_ends - counts
    inside = (starts <= block_index) & (block_index < slot_ends)
    within = jnp.sum(jnp.where(inside, block_index - starts, 0))
    pad_here = jnp.sum(jnp.where(inside & (slot_ends - 1 == block_index), slot_pads, 0))
    row_ids = jnp.arange(block_rows, dtype=jnp.int32)
    valid_rows = (row_ids < block_rows - pad_here).astype(jnp.float32)
    positions = within * block_rows + row_ids
    keep_state = (within > 0).astype(jnp.float32)
    devices = lax.axis_size("ctx")
    codes = jnp.asarray(slot_devices(devices), jnp.int32)
    from_whole = jnp.bitwise_xor(codes, block_index)
    to_whole = jnp.argsort(from_whole).astype(jnp.int32)
    rows_here = mix_norm_gain.shape[0]
    misc_here = jnp.concatenate(
        [
            ssm_step_proj,
            mix_norm_gain[:, None],
            ffn_norm_gain[:, None],
            conv_bc_weight.reshape(rows_here, 1),
            jnp.pad(conv_bc_bias, (0, rows_here - conv_bc_bias.shape[0]))[:, None],
        ],
        axis=1,
    )
    steps = ssm_step_proj.shape[1]
    misc_here = jnp.pad(misc_here, ((0, 0), (0, 128 - misc_here.shape[1])))
    inner, shared = (ssm_input_proj.shape[1], ssm_bc_proj.shape[1])
    heads_wide, pair_wide = (query_proj.shape[1], key_proj.shape[1])
    first_weights = gathered(
        jnp.concatenate([ssm_input_proj, ssm_bc_proj, misc_here], axis=1), 0, 1
    )
    second_weights = gathered(
        jnp.concatenate([query_proj, key_proj, value_proj, ssm_gate_proj], axis=1), 0, 2
    )
    out_weights = gathered(jnp.concatenate([ssm_out_proj, attn_out_proj], axis=0), 1, 1)
    ffn_gate_weight = gathered(ffn_gate_proj, 0, 2)
    ffn_up_weight = gathered(ffn_up_proj, 0, 1)
    ffn_down_weight = gathered(ffn_down_proj, 1, 2)
    misc = first_weights[:, inner + shared :]
    mix_gain, gain_two = (misc[:, steps], misc[:, steps + 1])

    def whole_order(column):
        return jnp.take(column.reshape(devices, rows_here), to_whole, axis=0)

    conv_bc_full = whole_order(misc[:, steps + 2]).reshape(shared, KW)
    conv_bc_offset = whole_order(misc[:, steps + 3])[:, : conv_bc_bias.shape[0]].reshape(shared)
    tokens = reordered(tokens, from_whole)
    cotangent = reordered(cotangent, from_whole)
    inputs = tokens.astype(jnp.float32)
    normed_one, norm_one_back = jax.vjp(rms_scale, inputs, mix_gain.astype(jnp.float32))
    normed_low = normed_one.astype(jnp.bfloat16)
    first_pre = plain_product(normed_low, first_weights)
    second_pre = plain_product(normed_low, second_weights)
    input_pre = first_pre[:, :inner]
    bc_pre = first_pre[:, inner : inner + shared]
    step_raw = first_pre[:, inner + shared : inner + shared + steps]
    query_pre = second_pre[:, :heads_wide]
    key_pre = second_pre[:, heads_wide : heads_wide + pair_wide]
    value_pre = second_pre[:, heads_wide + pair_wide : heads_wide + 2 * pair_wide]
    gate_pre = second_pre[:, heads_wide + 2 * pair_wide :]
    rim_rows = KW - 1
    rim_in, rim_bc = shifted(
        (input_pre[block_rows - rim_rows :], bc_pre[block_rows - rim_rows :]), "ctx", 1
    )
    ext_in = jnp.concatenate([rim_in * keep_state, input_pre], axis=0)
    ext_bc = jnp.concatenate([rim_bc * keep_state, bc_pre], axis=0)
    inner_out, inner_back = jax.vjp(
        mamba_inner,
        ext_in,
        ext_bc,
        step_raw,
        conv_in_weight.astype(jnp.float32),
        conv_in_bias.astype(jnp.float32),
        conv_bc_full.astype(jnp.float32),
        conv_bc_offset.astype(jnp.float32),
        step_bias.astype(jnp.float32),
        decay_log.astype(jnp.float32),
        skip_gain.astype(jnp.float32),
    )
    intra_out, local_states, decays, growth, c_part = inner_out
    head_count, state_dim, head_dim = local_states.shape

    def as_matrix(states):
        return states.transpose(1, 0, 2).reshape(state_dim, -1)

    def as_heads(matrix):
        return matrix.astype(jnp.float32).reshape(state_dim, head_count, head_dim).transpose(1, 0, 2)

    decay_row = jnp.repeat(keep_state * decays, head_dim)[None, :]
    state_in = keep_state * as_heads(carried_states(as_matrix(local_states), decay_row, False))
    ssm_gated, finish_back = jax.vjp(mamba_finish, intra_out, growth, c_part, state_in, gate_pre)
    ssm_low = ssm_gated.astype(jnp.bfloat16)
    cos_table, sin_table = rotary_tables(positions)
    query_rot = rotate(
        query_pre.reshape(block_rows, -1, HD), cos_table, sin_table
    ).astype(jnp.bfloat16)
    key_rot = rotate(
        key_pre.reshape(block_rows, -1, HD), cos_table, sin_table
    ).astype(jnp.bfloat16)
    value_low = value_pre.astype(jnp.bfloat16)
    key_heads = key_rot.shape[1]
    own_pair = jnp.concatenate([key_rot.reshape(block_rows, -1), value_low], axis=1)
    earlier_pairs = [shifted(own_pair, "ctx", distance) for distance in range(MAXB - 1, 0, -1)]
    window_pairs = jnp.concatenate(earlier_pairs + [own_pair], axis=0)
    key_window = window_pairs[:, : key_heads * HD].reshape(-1, key_heads, HD)
    value_window = window_pairs[:, key_heads * HD :].reshape(-1, key_heads, HD)
    query_groups = query_rot.reshape(block_rows, key_heads, -1, HD)
    allowed = window_mask(within, pad_here, block_rows)
    score_scale = HD ** (-0.5)
    scores = (
        jnp.einsum("qkgd,skd->kgqs", query_groups, key_window, preferred_element_type=jnp.float32)
        * score_scale
    )
    scores = jnp.where(allowed[None, None], scores, masked_score)
    row_top = jnp.max(scores, axis=-1, keepdims=True)
    exp_scores = jnp.exp(scores - row_top)
    totals = jnp.sum(exp_scores, axis=-1, keepdims=True)
    log_total = row_top + jnp.log(totals)
    probs_low = (exp_scores / totals).astype(jnp.bfloat16)
    attended = jnp.einsum(
        "kgqs,skd->qkgd", probs_low, value_window, preferred_element_type=jnp.float32
    )
    attn_low = attended.reshape(block_rows, -1).astype(jnp.bfloat16)
    mixed_low = jnp.concatenate([ssm_low, attn_low], axis=1)
    mixed_sum = pair_sum(plain_product(mixed_low, out_weights))
    hidden = inputs + mixed_sum
    normed_two, norm_two_back = jax.vjp(rms_scale, hidden, gain_two.astype(jnp.float32))
    normed_two_low = normed_two.astype(jnp.bfloat16)
    ffn_gate = plain_product(normed_two_low, ffn_gate_weight)
    ffn_up = plain_product(normed_two_low, ffn_up_weight)
    ffn_act = (jax.nn.silu(ffn_gate) * ffn_up).astype(jnp.bfloat16)
    ffn_part = plain_product(ffn_act, ffn_down_weight)
    ffn_sum = pair_sum(ffn_part)
    layer_out = ((hidden + ffn_sum) * valid_rows[:, None]).astype(jnp.bfloat16)
    cot_low = (cotangent.astype(jnp.float32) * valid_rows[:, None]).astype(jnp.bfloat16)
    grad_out = cot_low.astype(jnp.float32)
    def in_quarters(value):
        return jnp.split(value, 4, axis=1)

    def rows_grad(left_side, right_side, first):
        return reduced([product_of_cols(part, right_side) for part in in_quarters(left_side)], 0, first)

    def cols_grad(left_side, right_side, first):
        return reduced([product_of_cols(left_side, part) for part in in_quarters(right_side)], 1, first)

    ffn_down_grad = cols_grad(ffn_act, cot_low, 1)
    act_grad = product_by_rows(cot_low, ffn_down_weight)
    gate_sigmoid = jax.nn.sigmoid(ffn_gate)
    ffn_gate_low = (
        act_grad * ffn_up * gate_sigmoid * (1.0 + ffn_gate * (1.0 - gate_sigmoid))
    ).astype(jnp.bfloat16)
    ffn_up_low = (act_grad * jax.nn.silu(ffn_gate)).astype(jnp.bfloat16)
    ffn_gate_grad = rows_grad(normed_two_low, ffn_gate_low, 2)
    ffn_up_grad = rows_grad(normed_two_low, ffn_up_low, 1)
    norm_two_part = product_by_rows(ffn_gate_low, ffn_gate_weight) + product_by_rows(
        ffn_up_low, ffn_up_weight
    )
    norm_two_grad = pair_sum(norm_two_part)
    hidden_norm_grad, gain_two_grad = norm_two_back(norm_two_grad)
    hidden_grad = grad_out + hidden_norm_grad
    hidden_low = hidden_grad.astype(jnp.bfloat16)
    out_grad = cols_grad(mixed_low, hidden_low, 2)
    mixed_grad = product_by_rows(hidden_low, out_weights)
    attn_grad_low = (
        mixed_grad[:, inner:]
        .astype(jnp.bfloat16)
        .reshape(block_rows, key_heads, -1, HD)
    )
    scores_again = (
        jnp.einsum("qkgd,skd->kgqs", query_groups, key_window, preferred_element_type=jnp.float32)
        * score_scale
    )
    probs = jnp.where(allowed[None, None], jnp.exp(scores_again - log_total), 0.0)
    probs_back_low = probs.astype(jnp.bfloat16)
    prob_grad = jnp.einsum(
        "qkgd,skd->kgqs", attn_grad_low, value_window, preferred_element_type=jnp.float32
    )
    row_dots = jnp.sum(probs * prob_grad, axis=-1, keepdims=True)
    score_grad_low = (probs * (prob_grad - row_dots)).astype(jnp.bfloat16)
    query_grad = (
        jnp.einsum("kgqs,skd->qkgd", score_grad_low, key_window, preferred_element_type=jnp.float32)
        * score_scale
    )
    key_grad = (
        jnp.einsum(
            "kgqs,qkgd->skd", score_grad_low, query_groups, preferred_element_type=jnp.float32
        )
        * score_scale
    )
    value_grad = jnp.einsum(
        "kgqs,qkgd->skd", probs_back_low, attn_grad_low, preferred_element_type=jnp.float32
    )
    pair_grad = jnp.concatenate(
        [key_grad.reshape(-1, key_heads * HD), value_grad.reshape(-1, key_heads * HD)], axis=1
    )
    own_pair_grad = pair_grad[(MAXB - 1) * block_rows :]
    for distance in range(1, MAXB):
        pair_piece = pair_grad[(MAXB - 1 - distance) * block_rows : (MAXB - distance) * block_rows]
        own_pair_grad = own_pair_grad + shifted(
            pair_piece.astype(jnp.bfloat16), "ctx", -distance
        ).astype(pair_piece.dtype)
    key_grad_low = (
        rotate(
            own_pair_grad[:, : key_heads * HD].reshape(block_rows, key_heads, HD),
            cos_table,
            -sin_table,
        )
        .reshape(block_rows, -1)
        .astype(jnp.bfloat16)
    )
    value_grad_low = own_pair_grad[:, key_heads * HD :].astype(jnp.bfloat16)
    query_grad_low = (
        rotate(query_grad.reshape(block_rows, -1, HD), cos_table, -sin_table)
        .reshape(block_rows, -1)
        .astype(jnp.bfloat16)
    )
    ssm_grad = mixed_grad[:, :inner]
    intra_grad, growth_grad, c_grad, state_in_grad, gate_pre_grad = finish_back(ssm_grad)
    later_grad = as_heads(carried_states(as_matrix(keep_state * state_in_grad), decay_row, True))
    decays_grad = jnp.sum(state_in * later_grad, axis=(1, 2))
    inner_grads = inner_back((intra_grad, later_grad, decays_grad, growth_grad, c_grad))
    ext_in_grad = inner_grads[0]
    ext_bc_grad = inner_grads[1]
    back_in, back_bc = shifted(
        (keep_state * ext_in_grad[:rim_rows], keep_state * ext_bc_grad[:rim_rows]), "ctx", -1
    )
    input_pre_grad = ext_in_grad[rim_rows:] + jnp.pad(back_in, ((block_rows - rim_rows, 0), (0, 0)))
    bc_pre_part = ext_bc_grad[rim_rows:] + jnp.pad(back_bc, ((block_rows - rim_rows, 0), (0, 0)))
    input_grad_low = input_pre_grad.astype(jnp.bfloat16)
    ssm_gate_low = gate_pre_grad.astype(jnp.bfloat16)
    step_grad_low = inner_grads[2].astype(jnp.bfloat16)
    no_misc = jnp.zeros((block_rows, 128 - steps), jnp.bfloat16)
    first_grads = jnp.concatenate(
        [input_grad_low, bc_pre_part.astype(jnp.bfloat16), step_grad_low, no_misc], axis=1
    )
    second_grads = jnp.concatenate(
        [query_grad_low, key_grad_low, value_grad_low, ssm_gate_low], axis=1
    )
    norm_one_grad = pair_sum(
        product_by_rows(first_grads, first_weights) + product_by_rows(second_grads, second_weights)
    )
    bc_grad_low = pair_sum(bc_pre_part).astype(jnp.bfloat16)
    conv_bc_grads = jnp.concatenate([inner_grads[5].reshape(-1), inner_grads[6]])
    conv_bc_grads = conv_bc_grads + swap(conv_bc_grads)
    inputs_norm_grad, gain_one_grad = norm_one_back(norm_one_grad)
    tokens_grad = (hidden_grad + inputs_norm_grad).astype(jnp.bfloat16)
    first_grads = jnp.concatenate([input_grad_low, bc_grad_low, step_grad_low, no_misc], axis=1)
    first_grad = rows_grad(normed_low, first_grads, 1)
    second_grad = rows_grad(normed_low, second_grads, 2)
    small = [
        inner_grads[3].reshape(-1),
        inner_grads[4],
        inner_grads[7],
        inner_grads[8],
        inner_grads[9],
        conv_bc_grads,
        whole_order(gain_one_grad).reshape(-1),
        whole_order(gain_two_grad).reshape(-1),
    ]
    packed = jnp.concatenate(small)
    filled = -packed.shape[0] % 1024
    packed = summed(jnp.pad(packed, (0, filled)).reshape(-1, 128)).reshape(-1)
    sums, at = ([], 0)
    for part in small:
        sums.append(packed[at : at + part.shape[0]])
        at += part.shape[0]

    def own(vector, count):
        return lax.dynamic_slice_in_dim(vector, block_index * count, count, 0)

    conv_bc_sums = sums[5]
    conv_rows = conv_bc_weight.shape[0]
    return (
        reordered(layer_out, to_whole),
        reordered(tokens_grad, to_whole),
        own(sums[6], rows_here),
        second_grad[:, heads_wide + 2 * pair_wide :],
        first_grad[:, :inner],
        first_grad[:, inner : inner + shared],
        first_grad[:, inner + shared : inner + shared + steps],
        sums[0].reshape(inner, KW),
        sums[1],
        own(conv_bc_sums[: shared * KW], conv_rows * KW).reshape(conv_rows, KW),
        own(conv_bc_sums[shared * KW :], conv_rows),
        sums[2],
        sums[3],
        sums[4],
        out_grad[:inner],
        second_grad[:, :heads_wide],
        second_grad[:, heads_wide : heads_wide + pair_wide],
        second_grad[:, heads_wide + pair_wide : heads_wide + 2 * pair_wide],
        out_grad[inner:],
        own(sums[7], rows_here),
        ffn_gate_grad,
        ffn_up_grad,
        ffn_down_grad,
    )


def solution(mesh):
    return jax.shard_map(
        per_device,
        mesh=mesh,
        in_specs=(
            P("ctx", None),
            P("ctx", None),
            P("ctx"),
            P("ctx", "wt"),
            P("ctx", "wt"),
            P("ctx", None),
            P("ctx", "wt"),
            P("wt", None),
            P("wt"),
            P("ctx", None),
            P("ctx"),
            P("wt"),
            P("wt"),
            P("wt"),
            P("wt", "ctx"),
            P("ctx", "wt"),
            P("ctx", "wt"),
            P("ctx", "wt"),
            P("wt", "ctx"),
            P("ctx"),
            P("ctx", "wt"),
            P("ctx", "wt"),
            P("wt", "ctx"),
            P(),
            P(),
            P(),
        ),
        out_specs=(
            P("ctx", None),
            P("ctx", None),
            P("ctx"),
            P("ctx", "wt"),
            P("ctx", "wt"),
            P("ctx", None),
            P("ctx", "wt"),
            P("wt", None),
            P("wt"),
            P("ctx", None),
            P("ctx"),
            P("wt"),
            P("wt"),
            P("wt"),
            P("wt", "ctx"),
            P("ctx", "wt"),
            P("ctx", "wt"),
            P("ctx", "wt"),
            P("wt", "ctx"),
            P("ctx"),
            P("ctx", "wt"),
            P("ctx", "wt"),
            P("wt", "ctx"),
        ),
        check_vma=False,
    )
```

```python
import jax
import jax.numpy as jnp
from jax import lax
from jax.experimental import pallas as pl
from jax.experimental.pallas import tpu as pltpu
from jax.sharding import PartitionSpec as P

HD = 128
KW = 4
MAXB = 8
SCAN_ROWS = 128


epsilon = 1e-05
rope_base = 100000000000.0
highest = lax.Precision.HIGHEST
masked_score = -1e30


def shifted(value, axis, steps):
    count = lax.axis_size(axis)
    leading, last = (max(0, -steps), min(count, count - steps))
    return lax.ppermute(value, axis, [(source, source + steps) for source in range(leading, last)])


def hop(value, code):
    if code == 0:
        return value
    count = lax.axis_size("ctx")
    return lax.ppermute(value, "ctx", [(source, source ^ code) for source in range(count)])


def swap(value):
    return lax.ppermute(value, "wt", [(0, 1), (1, 0)])


def pair_sum(value):
    rounded = lax.reduce_precision(value, 8, 7)
    return rounded + swap(rounded.astype(jnp.bfloat16)).astype(jnp.float32)


def slot_devices(count):
    high = count // 4
    return [4 * (slot % high) + slot // high for slot in range(count)]


def gathered(piece, axis, first):
    high = lax.axis_size("ctx") // 4
    second = 3 - first
    quarter = jnp.concatenate([piece] + [hop(piece, 4 * k) for k in range(1, high)], axis=axis)
    parts = {0: quarter, first: hop(quarter, first)}
    parts[second] = hop(quarter, second)
    parts[3] = hop(parts[first], second)
    return jnp.concatenate([parts[k] for k in range(4)], axis=axis)


def reduced(parts, axis, first):
    high = lax.axis_size("ctx") // 4
    second = 3 - first
    low = [part.astype(jnp.bfloat16) for part in parts]
    near = parts[0] + hop(low[first], first).astype(jnp.float32)
    far = parts[second] + hop(low[3], first).astype(jnp.float32)
    quarter = near + hop(far.astype(jnp.bfloat16), second).astype(jnp.float32)
    blocks = jnp.split(quarter, high, axis=axis)
    total = blocks[0]
    for k in range(1, high):
        total = total + hop(blocks[k].astype(jnp.bfloat16), 4 * k).astype(jnp.float32)
    return total


def summed(value):
    bit = 1
    while bit < lax.axis_size("ctx"):
        value = value + hop(value, bit)
        bit *= 2
    return value


def reordered(value, order):
    blocks = order.shape[0]
    rows, width = value.shape[0], value.shape[1] // blocks
    if width % 128:
        return jnp.take(value.reshape(rows, blocks, width), order, axis=1).reshape(rows, -1)

    def body(order_ref, in_ref, out_ref):
        out_ref[...] = in_ref[...]

    return pl.pallas_call(
        body,
        out_shape=jax.ShapeDtypeStruct(value.shape, value.dtype),
        grid_spec=pltpu.PrefetchScalarGridSpec(
            num_scalar_prefetch=1,
            grid=(blocks,),
            in_specs=[pl.BlockSpec((rows, width), lambda s, order_ref: (0, order_ref[s]))],
            out_specs=pl.BlockSpec((rows, width), lambda s, order_ref: (0, s)),
        ),
        name="reordered",
    )(order, value)


def carried_states(states, decays, reverse):
    me = lax.axis_index("ctx")
    place = me % 4
    width = states.shape[1] // 4
    low = states.astype(jnp.bfloat16)

    def quarter(value, index):
        return lax.dynamic_slice_in_dim(value, index * width, width, 1)

    got = [hop(quarter(low, place ^ k), k) for k in range(4)]
    got_decay = [hop(quarter(decays, place ^ k), k) for k in range(4)]

    def in_order(pieces):
        odd = place % 2 == 1
        pieces = [jnp.where(odd, pieces[k ^ 1], pieces[k]) for k in range(4)]
        upper = place >= 2
        return [jnp.where(upper, pieces[k ^ 2], pieces[k]) for k in range(4)]

    blocks = [piece.astype(jnp.float32) for piece in in_order(got)]
    rates = in_order(got_decay)
    if reverse:
        blocks, rates = (blocks[::-1], rates[::-1])
    total, rate = (blocks[0], rates[0])
    for block, block_rate in zip(blocks[1:], rates[1:]):
        total, rate = (block + block_rate * total, block_rate * rate)
    step = -4 if reverse else 4
    total_low = total.astype(jnp.bfloat16)
    near, near_rate = (shifted(total_low, "ctx", step), shifted(rate, "ctx", step))
    far = shifted(total_low, "ctx", 2 * step)
    state = near.astype(jnp.float32) + near_rate * far.astype(jnp.float32)
    reached = []
    for block, block_rate in zip(blocks, rates):
        reached.append(state.astype(jnp.bfloat16))
        state = block + block_rate * state
    if reverse:
        reached = reached[::-1]
    mine = in_order(reached)
    back = in_order([hop(mine[k], k) for k in range(4)])
    return jnp.concatenate(back, axis=1)


def plain_product(left_side, right_side):
    return jnp.dot(left_side, right_side, preferred_element_type=jnp.float32)


def product_by_rows(left_side, right_side):
    return lax.dot_general(
        left_side, right_side, (((1,), (1,)), ((), ())), preferred_element_type=jnp.float32
    )


def product_of_cols(left_side, right_side):
    return lax.dot_general(
        left_side, right_side, (((0,), (0,)), ((), ())), preferred_element_type=jnp.float32
    )


def rms_scale(values, gain_vec):
    return (
        values * lax.rsqrt(jnp.mean(values * values, axis=-1, keepdims=True) + epsilon) * gain_vec
    )


def rotary_tables(positions):
    exponents = jnp.arange(HD // 2, dtype=jnp.float32) * (2.0 / HD)
    frequency = jnp.power(jnp.float32(rope_base), -exponents)
    angles = positions.astype(jnp.float32)[:, None] * frequency[None, :]
    return (jnp.cos(angles), jnp.sin(angles))


def rotate(values, cos_table, sin_table):
    half_dim = values.shape[-1] // 2
    first_half = values[..., :half_dim]
    second_half = values[..., half_dim:]
    cos_table = cos_table[:, None, :]
    sin_table = sin_table[:, None, :]
    return jnp.concatenate(
        [
            first_half * cos_table - second_half * sin_table,
            second_half * cos_table + first_half * sin_table,
        ],
        axis=-1,
    )


def window_mask(within, pad_here, block_rows):
    key_index = jnp.arange(MAXB * block_rows, dtype=jnp.int32)
    key_block = key_index // block_rows
    key_row = key_index - key_block * block_rows
    distance = MAXB - 1 - key_block
    query_row = jnp.arange(block_rows, dtype=jnp.int32)
    key_ok = jnp.where(distance == 0, key_row < block_rows - pad_here, distance <= within)
    return key_ok[None, :] & ((distance[None, :] > 0) | (key_row[None, :] <= query_row[:, None]))


def convolved(rim, block, taps):
    length = block.shape[0]
    extended = jnp.concatenate([rim, block], axis=0)
    first = rim.shape[0] - (KW - 1)
    summed = taps[KW : KW + 1]
    for j in range(KW):
        summed = summed + extended[first + j : first + j + length] * taps[j : j + 1]
    return (extended, summed)


def convolved_back(extended, pre_grad, taps):
    length = pre_grad.shape[0]
    rim_rows = extended.shape[0] - length
    first = rim_rows - (KW - 1)
    zeros = jnp.zeros((8, pre_grad.shape[1]), jnp.float32)
    padded = jnp.concatenate([zeros, pre_grad, zeros], axis=0)
    total = jnp.zeros_like(extended)
    rows = []
    for j in range(KW):
        start = 8 - rim_rows + KW - 1 - j
        total = total + padded[start : start + rim_rows + length] * taps[j : j + 1]
        rows.append(
            jnp.sum(pre_grad * extended[first + j : first + j + length], axis=0, keepdims=True)
        )
    rows.append(jnp.sum(pre_grad, axis=0, keepdims=True))
    return (total, rows)


def silu_slope(value, sigmoid):
    return sigmoid * (1.0 + value * (1.0 - sigmoid))


def low_dot(left_side, right_side, left_axis, right_axis):
    return lax.dot_general(
        left_side.astype(jnp.bfloat16),
        right_side.astype(jnp.bfloat16),
        (((left_axis,), (right_axis,)), ((), ())),
        preferred_element_type=jnp.float32,
    )


def lower_gram(c_low, b_low):
    length = c_low.shape[0]
    gram = low_dot(c_low, b_low, 1, 1)
    rows = lax.broadcasted_iota(jnp.int32, (length, length), 0)
    cols = lax.broadcasted_iota(jnp.int32, (length, length), 1)
    return jnp.where(rows >= cols, gram, 0.0)


def scan_blocks(inner, shared, length, wide):
    return [
        pl.BlockSpec((length, wide), lambda i: (0, i)),
        pl.BlockSpec((8, wide), lambda i: (0, i)),
        pl.BlockSpec((8, wide), lambda i: (0, i)),
        pl.BlockSpec((length, shared), lambda i: (0, inner // shared)),
        pl.BlockSpec((8, shared), lambda i: (0, inner // shared)),
        pl.BlockSpec((8, shared), lambda i: (0, 0)),
        pl.BlockSpec((1, length, 2), lambda i: (i, 0, 0)),
        pl.BlockSpec((1, length, 2), lambda i: (i, 0, 0)),
        pl.BlockSpec((1, 2, length), lambda i: (i, 0, 0)),
    ]


def scan_forward(first_pre, rims, taps, bc_taps, step_cols, sum_cols, sum_rows, inner, shared):
    length = first_pre.shape[0]
    pairs = step_cols.shape[0]
    wide = inner // pairs
    size = wide // 2
    state_dim = shared // 2
    part = min(SCAN_ROWS, length)

    def body(
        in_ref, rim_ref, tap_ref, bc_ref, bc_rim_ref, bc_tap_ref, step_ref, col_ref, row_ref,
        out_ref, state_ref, bc_low_ref, gram_ref,
    ):
        @pl.when(pl.program_id(0) == 0)
        def _():
            _, pre = convolved(bc_rim_ref[...], bc_ref[...], bc_tap_ref[...])
            acts = (pre * jax.nn.sigmoid(pre)).astype(jnp.bfloat16)
            bc_low_ref[...] = acts
            gram_ref[...] = lower_gram(acts[:, state_dim:], acts[:, :state_dim])

        taps_here = tap_ref[...]
        _, pre = convolved(rim_ref[...], in_ref[...], taps_here)
        acts = pre * jax.nn.sigmoid(pre)
        outs, tails = ([], [])
        for head in range(2):
            lanes = slice(head * size, (head + 1) * size)
            step = step_ref[0][:, head : head + 1]
            col = col_ref[0][:, head : head + 1]
            row = row_ref[0][head : head + 1, :]
            stepped = acts[:, lanes] * step
            stepped_low = stepped.astype(jnp.bfloat16)
            for at in range(0, length, part):
                end = at + part
                decay = jnp.exp(jnp.minimum(col[at:end] - row[:, :end], 0.0))
                weights = (decay * gram_ref[at:end, :end]).astype(jnp.bfloat16)
                out_ref[at:end, lanes] = low_dot(weights, stepped_low[:end], 1, 0) + (
                    taps_here[KW + 1 : KW + 2, lanes] * acts[at:end, lanes]
                )
            tails.append(stepped * jnp.exp(col[length - 1 : length] - col))
        tail = jnp.concatenate(tails, axis=1)
        state_ref[...] = low_dot(bc_low_ref[:, :state_dim], tail, 0, 0).astype(jnp.bfloat16)

    return pl.pallas_call(
        body,
        grid=(pairs,),
        out_shape=(
            jax.ShapeDtypeStruct((length, inner), jnp.float32),
            jax.ShapeDtypeStruct((state_dim, inner), jnp.bfloat16),
            jax.ShapeDtypeStruct((length, shared), jnp.bfloat16),
        ),
        in_specs=scan_blocks(inner, shared, length, wide),
        out_specs=(
            pl.BlockSpec((length, wide), lambda i: (0, i)),
            pl.BlockSpec((state_dim, wide), lambda i: (0, i)),
            pl.BlockSpec((length, shared), lambda i: (0, 0)),
        ),
        scratch_shapes=[pltpu.VMEM((length, length), jnp.float32)],
        compiler_params=pltpu.CompilerParams(vmem_limit_bytes=48 << 20),
        name="scan_forward",
    )(first_pre, rims, taps, first_pre, rims, bc_taps, step_cols, sum_cols, sum_rows)


def scan_gated(intra, state_in, bc_low, sum_cols, second_pre, gate_at):
    length, inner = intra.shape
    pairs = sum_cols.shape[0]
    wide = inner // pairs
    size = wide // 2
    state_dim = bc_low.shape[1] // 2

    def body(intra_ref, state_ref, c_ref, col_ref, gate_ref, out_ref, act_ref):
        carried = low_dot(c_ref[...], state_ref[...], 1, 0)
        gate = gate_ref[...]
        silu = gate * jax.nn.sigmoid(gate)
        for head in range(2):
            lanes = slice(head * size, (head + 1) * size)
            growth = jnp.exp(col_ref[0][:, head : head + 1])
            whole = intra_ref[:, lanes] + carried[:, lanes] * growth
            out_ref[:, lanes] = whole
            act_ref[:, lanes] = (whole * silu[:, lanes]).astype(jnp.bfloat16)

    block = pl.BlockSpec((length, wide), lambda i: (0, i))
    return pl.pallas_call(
        body,
        grid=(pairs,),
        out_shape=(
            jax.ShapeDtypeStruct((length, inner), jnp.float32),
            jax.ShapeDtypeStruct((length, inner), jnp.bfloat16),
        ),
        in_specs=[
            block,
            pl.BlockSpec((state_dim, wide), lambda i: (0, i)),
            pl.BlockSpec((length, state_dim), lambda i: (0, 1)),
            pl.BlockSpec((1, length, 2), lambda i: (i, 0, 0)),
            pl.BlockSpec((length, wide), lambda i: (0, gate_at // wide + i)),
        ],
        out_specs=(block, block),
        compiler_params=pltpu.CompilerParams(vmem_limit_bytes=48 << 20),
        name="scan_gated",
    )(intra, state_in, bc_low, sum_cols, second_pre)


def scan_gated_back(out_grads, whole, bc_low, sum_cols, second_pre, gate_at):
    length, inner = whole.shape
    pairs = sum_cols.shape[0]
    wide = inner // pairs
    size = wide // 2
    state_dim = bc_low.shape[1] // 2

    def body(grad_ref, whole_ref, c_ref, col_ref, gate_ref, gate_grad_ref, state_ref):
        gate = gate_ref[...]
        sigmoid = jax.nn.sigmoid(gate)
        grad = grad_ref[...]
        gate_grad_ref[...] = (grad * whole_ref[...] * silu_slope(gate, sigmoid)).astype(jnp.bfloat16)
        inside = grad * (gate * sigmoid)
        grown = [
            inside[:, head * size : (head + 1) * size] * jnp.exp(col_ref[0][:, head : head + 1])
            for head in range(2)
        ]
        state_ref[...] = low_dot(c_ref[...], jnp.concatenate(grown, axis=1), 0, 0).astype(
            jnp.bfloat16
        )

    block = pl.BlockSpec((length, wide), lambda i: (0, i))
    return pl.pallas_call(
        body,
        grid=(pairs,),
        out_shape=(
            jax.ShapeDtypeStruct((length, inner), jnp.bfloat16),
            jax.ShapeDtypeStruct((state_dim, inner), jnp.bfloat16),
        ),
        in_specs=[
            block,
            block,
            pl.BlockSpec((length, state_dim), lambda i: (0, 1)),
            pl.BlockSpec((1, length, 2), lambda i: (i, 0, 0)),
            pl.BlockSpec((length, wide), lambda i: (0, gate_at // wide + i)),
        ],
        out_specs=(block, pl.BlockSpec((state_dim, wide), lambda i: (0, i))),
        compiler_params=pltpu.CompilerParams(vmem_limit_bytes=48 << 20),
        name="scan_gated_back",
    )(out_grads, whole, bc_low, sum_cols, second_pre)


def scan_back(
    first_pre, rims, taps, bc_taps, step_cols, sum_cols, sum_rows,
    out_grads, second_pre, gate_at, state_in, end_grad, bc_low,
):
    length = first_pre.shape[0]
    pairs = step_cols.shape[0]
    state_dim, inner = state_in.shape
    shared = bc_low.shape[1]
    wide = inner // pairs
    size = wide // 2
    part = min(SCAN_ROWS, length)

    def body(
        in_ref, rim_ref, tap_ref, bc_ref, bc_rim_ref, bc_tap_ref, step_ref, col_ref, row_ref,
        grad_ref, gate_ref, state_ref, end_ref, bc_low_ref,
        in_grad_ref, rim_grad_ref, tap_grad_ref, step_grad_ref, sum_grad_ref,
        bc_grad_ref, bc_rim_grad_ref, bc_tap_grad_ref,
        gram_ref, gram_grad_ref, acts_grad_ref, back_ref,
    ):
        b_low = bc_low_ref[:, :state_dim]
        c_low = bc_low_ref[:, state_dim:]

        @pl.when(pl.program_id(0) == 0)
        def _():
            gram_ref[...] = lower_gram(c_low, b_low)
            gram_grad_ref[...] = jnp.zeros_like(gram_grad_ref)
            acts_grad_ref[...] = jnp.zeros_like(acts_grad_ref)

        taps_here = tap_ref[...]
        extended, pre = convolved(rim_ref[...], in_ref[...], taps_here)
        sigmoid = jax.nn.sigmoid(pre)
        acts = pre * sigmoid
        gate = gate_ref[...]
        out_grad = grad_ref[...] * (gate * jax.nn.sigmoid(gate))
        state = state_ref[...]
        end = end_ref[...]
        from_end = low_dot(b_low, end, 1, 0)
        from_start = low_dot(c_low, state, 1, 0)
        state_dot = jnp.sum(
            state.astype(jnp.float32) * end.astype(jnp.float32), axis=0, keepdims=True
        )
        last_row = lax.broadcasted_iota(jnp.int32, (length, 1), 0) == length - 1
        acts_grads, tails, grown_grads = ([], [], [])
        for head in range(2):
            lanes = slice(head * size, (head + 1) * size)
            step = step_ref[0][:, head : head + 1]
            col = col_ref[0][:, head : head + 1]
            row = row_ref[0][head : head + 1, :]
            here = acts[:, lanes]
            stepped = here * step
            stepped_low = stepped.astype(jnp.bfloat16)
            grad = out_grad[:, lanes]
            grad_low = grad.astype(jnp.bfloat16)
            grad_wide = grad_low.astype(jnp.float32)
            back_ref[...] = jnp.zeros_like(back_ref)
            row_terms = []
            for at in range(0, length, part):
                to = at + part
                decay = jnp.exp(jnp.minimum(col[at:to] - row[:, :to], 0.0))
                weights = (decay * gram_ref[at:to, :to]).astype(jnp.bfloat16)
                again = low_dot(weights, stepped_low[:to], 1, 0)
                row_terms.append(jnp.sum(again * grad_wide[at:to], axis=1, keepdims=True))
                back_ref[:to] += low_dot(weights, grad_low[at:to], 0, 0)
                gram_grad_ref[at:to, :to] += decay * low_dot(
                    grad_low[at:to], stepped_low[:to], 1, 1
                )
            back = back_ref[...]
            tail = jnp.exp(col[length - 1 : length] - col)
            growth = jnp.exp(col)
            ended = from_end[:, lanes] * tail
            end_terms = jnp.sum(ended * stepped, axis=1, keepdims=True)
            col_terms = jnp.sum(back * stepped_low.astype(jnp.float32), axis=1, keepdims=True)
            start_terms = growth * jnp.sum(from_start[:, lanes] * grad, axis=1, keepdims=True)
            whole = jnp.sum(end_terms, axis=0, keepdims=True) + growth[
                length - 1 : length
            ] * jnp.sum(state_dot[:, lanes], axis=1, keepdims=True)
            sum_grad_ref[0, :, head : head + 1] = (
                jnp.concatenate(row_terms, axis=0)
                + start_terms
                - col_terms
                - end_terms
                + jnp.where(last_row, whole, 0.0)
            )
            back = back + ended
            step_grad_ref[0, :, head : head + 1] = jnp.sum(back * here, axis=1, keepdims=True)
            acts_grads.append(taps_here[KW + 1 : KW + 2, lanes] * grad + back * step)
            tails.append((stepped * tail).astype(jnp.bfloat16))
            grown_grads.append((grad * growth).astype(jnp.bfloat16))
        acts_grad_ref[:, :state_dim] += low_dot(jnp.concatenate(tails, axis=1), end, 1, 1)
        acts_grad_ref[:, state_dim:] += low_dot(jnp.concatenate(grown_grads, axis=1), state, 1, 1)
        pre_grad = jnp.concatenate(acts_grads, axis=1) * silu_slope(pre, sigmoid)
        total, rows = convolved_back(extended, pre_grad, taps_here)
        rim_grad_ref[...] = total[:8]
        in_grad_ref[...] = total[8:]
        rows.append(jnp.sum(out_grad * acts, axis=0, keepdims=True))
        rows.append(jnp.zeros((8 - len(rows), wide), jnp.float32))
        tap_grad_ref[...] = jnp.concatenate(rows, axis=0)

        @pl.when(pl.program_id(0) == pairs - 1)
        def _():
            gram_grad = gram_grad_ref[...]
            rows_of = lax.broadcasted_iota(jnp.int32, (length, length), 0)
            cols_of = lax.broadcasted_iota(jnp.int32, (length, length), 1)
            gram_grad = jnp.where(rows_of >= cols_of, gram_grad, 0.0).astype(jnp.bfloat16)
            acts_grad_ref[:, :state_dim] += low_dot(gram_grad, c_low, 0, 0)
            acts_grad_ref[:, state_dim:] += low_dot(gram_grad, b_low, 1, 0)
            bc_taps_here = bc_tap_ref[...]
            bc_extended, bc_pre = convolved(bc_rim_ref[...], bc_ref[...], bc_taps_here)
            bc_pre_grad = acts_grad_ref[...] * silu_slope(bc_pre, jax.nn.sigmoid(bc_pre))
            bc_total, bc_rows = convolved_back(bc_extended, bc_pre_grad, bc_taps_here)
            bc_rim_grad_ref[...] = bc_total[:8]
            bc_grad_ref[...] = bc_total[8:]
            bc_rows.append(jnp.zeros((8 - len(bc_rows), shared), jnp.float32))
            bc_tap_grad_ref[...] = jnp.concatenate(bc_rows, axis=0)

    block = pl.BlockSpec((length, wide), lambda i: (0, i))
    eight = pl.BlockSpec((8, wide), lambda i: (0, i))
    table = pl.BlockSpec((1, length, 2), lambda i: (i, 0, 0))
    state_block = pl.BlockSpec((state_dim, wide), lambda i: (0, i))
    bc_block = pl.BlockSpec((length, shared), lambda i: (0, 0))
    bc_eight = pl.BlockSpec((8, shared), lambda i: (0, 0))
    wide_f32 = jax.ShapeDtypeStruct((length, inner), jnp.float32)
    eight_f32 = jax.ShapeDtypeStruct((8, inner), jnp.float32)
    table_f32 = jax.ShapeDtypeStruct(step_cols.shape, jnp.float32)
    bc_f32 = jax.ShapeDtypeStruct((length, shared), jnp.float32)
    bc_eight_f32 = jax.ShapeDtypeStruct((8, shared), jnp.float32)
    return pl.pallas_call(
        body,
        grid=(pairs,),
        out_shape=(
            wide_f32, eight_f32, eight_f32, table_f32, table_f32, bc_f32, bc_eight_f32, bc_eight_f32
        ),
        in_specs=scan_blocks(inner, shared, length, wide)
        + [
            block,
            pl.BlockSpec((length, wide), lambda i: (0, gate_at // wide + i)),
            state_block,
            state_block,
            bc_block,
        ],
        out_specs=(block, eight, eight, table, table, bc_block, bc_eight, bc_eight),
        scratch_shapes=[
            pltpu.VMEM((length, length), jnp.float32),
            pltpu.VMEM((length, length), jnp.float32),
            pltpu.VMEM((length, shared), jnp.float32),
            pltpu.VMEM((length, size), jnp.float32),
        ],
        compiler_params=pltpu.CompilerParams(vmem_limit_bytes=56 << 20),
        name="scan_back",
    )(
        first_pre, rims, taps, first_pre, rims, bc_taps, step_cols, sum_cols, sum_rows,
        out_grads, second_pre, state_in, end_grad, bc_low,
    )


def per_device(
    tokens,
    cotangent,
    mix_norm_gain,
    ssm_gate_proj,
    ssm_input_proj,
    ssm_bc_proj,
    ssm_step_proj,
    conv_in_weight,
    conv_in_bias,
    conv_bc_weight,
    conv_bc_bias,
    step_bias,
    decay_log,
    skip_gain,
    ssm_out_proj,
    query_proj,
    key_proj,
    value_proj,
    attn_out_proj,
    ffn_norm_gain,
    ffn_gate_proj,
    ffn_up_proj,
    ffn_down_proj,
    extra_blocks,
    seq_order,
    pad_rows,
):
    block_rows = tokens.shape[0]
    block_index = lax.axis_index("ctx")
    seq_count = seq_order.shape[0]
    slot_ids = jnp.arange(seq_count, dtype=jnp.int32)
    chosen = (seq_order[:, None] == slot_ids[None, :]).astype(jnp.int32)
    counts = jnp.sum(chosen * extra_blocks[None, :], axis=1) + 1
    slot_pads = jnp.sum(chosen * pad_rows[None, :], axis=1)
    slot_ends = jnp.cumsum(counts)
    starts = slot_ends - counts
    inside = (starts <= block_index) & (block_index < slot_ends)
    within = jnp.sum(jnp.where(inside, block_index - starts, 0))
    pad_here = jnp.sum(jnp.where(inside & (slot_ends - 1 == block_index), slot_pads, 0))
    row_ids = jnp.arange(block_rows, dtype=jnp.int32)
    valid_rows = (row_ids < block_rows - pad_here).astype(jnp.float32)
    positions = within * block_rows + row_ids
    keep_state = (within > 0).astype(jnp.float32)
    devices = lax.axis_size("ctx")
    codes = jnp.asarray(slot_devices(devices), jnp.int32)
    from_whole = jnp.bitwise_xor(codes, block_index)
    to_whole = jnp.argsort(from_whole).astype(jnp.int32)
    rows_here = mix_norm_gain.shape[0]
    misc_here = jnp.concatenate(
        [
            ssm_step_proj,
            mix_norm_gain[:, None],
            ffn_norm_gain[:, None],
            conv_bc_weight.reshape(rows_here, 1),
            jnp.pad(conv_bc_bias, (0, rows_here - conv_bc_bias.shape[0]))[:, None],
        ],
        axis=1,
    )
    steps = ssm_step_proj.shape[1]
    misc_here = jnp.pad(misc_here, ((0, 0), (0, 128 - misc_here.shape[1])))
    inner, shared = (ssm_input_proj.shape[1], ssm_bc_proj.shape[1])
    heads_wide, pair_wide = (query_proj.shape[1], key_proj.shape[1])
    first_weights = gathered(
        jnp.concatenate([ssm_input_proj, ssm_bc_proj, misc_here], axis=1), 0, 1
    )
    second_weights = gathered(
        jnp.concatenate([query_proj, key_proj, value_proj, ssm_gate_proj], axis=1), 0, 2
    )
    out_weights = gathered(jnp.concatenate([ssm_out_proj, attn_out_proj], axis=0), 1, 1)
    ffn_gate_weight = gathered(ffn_gate_proj, 0, 2)
    ffn_up_weight = gathered(ffn_up_proj, 0, 1)
    ffn_down_weight = gathered(ffn_down_proj, 1, 2)
    misc = first_weights[:, inner + shared :]
    mix_gain, gain_two = (misc[:, steps], misc[:, steps + 1])

    def whole_order(column):
        return jnp.take(column.reshape(devices, rows_here), to_whole, axis=0)

    conv_bc_full = whole_order(misc[:, steps + 2]).reshape(shared, KW)
    conv_bc_offset = whole_order(misc[:, steps + 3])[:, : conv_bc_bias.shape[0]].reshape(shared)
    tokens = reordered(tokens, from_whole)
    cotangent = reordered(cotangent, from_whole)
    inputs = tokens.astype(jnp.float32)
    normed_one, norm_one_back = jax.vjp(rms_scale, inputs, mix_gain.astype(jnp.float32))
    normed_low = normed_one.astype(jnp.bfloat16)
    first_pre = plain_product(normed_low, first_weights)
    second_pre = plain_product(normed_low, second_weights)
    step_raw = first_pre[:, inner + shared : inner + shared + steps]
    query_pre = second_pre[:, :heads_wide]
    key_pre = second_pre[:, heads_wide : heads_wide + pair_wide]
    value_pre = second_pre[:, heads_wide + pair_wide : heads_wide + 2 * pair_wide]
    gate_at = heads_wide + 2 * pair_wide
    rim_rows = KW - 1
    edge = shifted(first_pre[block_rows - rim_rows :, : inner + shared], "ctx", 1) * keep_state
    rims = jnp.pad(edge, ((8 - rim_rows, 0), (0, 0)))
    head_dim = inner // steps
    skips = jnp.repeat(skip_gain.astype(jnp.float32), head_dim)[None, :]
    taps = jnp.concatenate(
        [conv_in_weight.astype(jnp.float32).T, conv_in_bias.astype(jnp.float32)[None, :], skips]
    )
    taps = jnp.pad(taps, ((0, 8 - taps.shape[0]), (0, 0)))
    bc_taps = jnp.concatenate(
        [conv_bc_full.astype(jnp.float32).T, conv_bc_offset.astype(jnp.float32)[None, :]]
    )
    bc_taps = jnp.pad(bc_taps, ((0, 8 - bc_taps.shape[0]), (0, 0)))
    step_in = step_raw + step_bias.astype(jnp.float32)[None, :]
    step_size = jax.nn.softplus(step_in)
    rate = -jnp.exp(decay_log.astype(jnp.float32))[None, :]
    lower = (row_ids[:, None] >= row_ids[None, :]).astype(jnp.float32)
    log_decay = jnp.dot(lower, rate * step_size, precision=highest)

    def by_pairs(table):
        return table.reshape(block_rows, steps // 2, 2).transpose(1, 0, 2)

    def from_pairs(table):
        return table.transpose(1, 0, 2).reshape(block_rows, steps)

    step_cols = by_pairs(step_size)
    sum_cols = by_pairs(log_decay)
    sum_rows = log_decay.T.reshape(steps // 2, 2, block_rows)
    intra_out, local_states, bc_low = scan_forward(
        first_pre, rims, taps, bc_taps, step_cols, sum_cols, sum_rows, inner, shared
    )
    decay_row = keep_state * jnp.repeat(jnp.exp(log_decay[block_rows - 1]), head_dim)[None, :]
    keep_low = keep_state.astype(jnp.bfloat16)
    state_in = keep_low * carried_states(local_states, decay_row, False)
    scan_out, ssm_low = scan_gated(intra_out, state_in, bc_low, sum_cols, second_pre, gate_at)
    cos_table, sin_table = rotary_tables(positions)
    query_rot = rotate(
        query_pre.reshape(block_rows, -1, HD), cos_table, sin_table
    ).astype(jnp.bfloat16)
    key_rot = rotate(
        key_pre.reshape(block_rows, -1, HD), cos_table, sin_table
    ).astype(jnp.bfloat16)
    value_low = value_pre.astype(jnp.bfloat16)
    key_heads = key_rot.shape[1]
    own_pair = jnp.concatenate([key_rot.reshape(block_rows, -1), value_low], axis=1)
    earlier_pairs = [shifted(own_pair, "ctx", distance) for distance in range(MAXB - 1, 0, -1)]
    window_pairs = jnp.concatenate(earlier_pairs + [own_pair], axis=0)
    key_window = window_pairs[:, : key_heads * HD].reshape(-1, key_heads, HD)
    value_window = window_pairs[:, key_heads * HD :].reshape(-1, key_heads, HD)
    query_groups = query_rot.reshape(block_rows, key_heads, -1, HD)
    allowed = window_mask(within, pad_here, block_rows)
    score_scale = HD ** (-0.5)
    scores = (
        jnp.einsum("qkgd,skd->kgqs", query_groups, key_window, preferred_element_type=jnp.float32)
        * score_scale
    )
    scores = jnp.where(allowed[None, None], scores, masked_score)
    row_top = jnp.max(scores, axis=-1, keepdims=True)
    exp_scores = jnp.exp(scores - row_top)
    totals = jnp.sum(exp_scores, axis=-1, keepdims=True)
    log_total = row_top + jnp.log(totals)
    probs_low = (exp_scores / totals).astype(jnp.bfloat16)
    attended = jnp.einsum(
        "kgqs,skd->qkgd", probs_low, value_window, preferred_element_type=jnp.float32
    )
    attn_low = attended.reshape(block_rows, -1).astype(jnp.bfloat16)
    mixed_low = jnp.concatenate([ssm_low, attn_low], axis=1)
    mixed_sum = pair_sum(plain_product(mixed_low, out_weights))
    hidden = inputs + mixed_sum
    normed_two, norm_two_back = jax.vjp(rms_scale, hidden, gain_two.astype(jnp.float32))
    normed_two_low = normed_two.astype(jnp.bfloat16)
    ffn_gate = plain_product(normed_two_low, ffn_gate_weight)
    ffn_up = plain_product(normed_two_low, ffn_up_weight)
    ffn_act = (jax.nn.silu(ffn_gate) * ffn_up).astype(jnp.bfloat16)
    ffn_part = plain_product(ffn_act, ffn_down_weight)
    ffn_sum = pair_sum(ffn_part)
    layer_out = ((hidden + ffn_sum) * valid_rows[:, None]).astype(jnp.bfloat16)
    cot_low = (cotangent.astype(jnp.float32) * valid_rows[:, None]).astype(jnp.bfloat16)
    grad_out = cot_low.astype(jnp.float32)
    def in_quarters(value):
        return jnp.split(value, 4, axis=1)

    def rows_grad(left_side, right_side, first):
        return reduced([product_of_cols(part, right_side) for part in in_quarters(left_side)], 0, first)

    def cols_grad(left_side, right_side, first):
        return reduced([product_of_cols(left_side, part) for part in in_quarters(right_side)], 1, first)

    ffn_down_grad = cols_grad(ffn_act, cot_low, 1)
    act_grad = product_by_rows(cot_low, ffn_down_weight)
    gate_sigmoid = jax.nn.sigmoid(ffn_gate)
    ffn_gate_low = (
        act_grad * ffn_up * gate_sigmoid * (1.0 + ffn_gate * (1.0 - gate_sigmoid))
    ).astype(jnp.bfloat16)
    ffn_up_low = (act_grad * jax.nn.silu(ffn_gate)).astype(jnp.bfloat16)
    ffn_gate_grad = rows_grad(normed_two_low, ffn_gate_low, 2)
    ffn_up_grad = rows_grad(normed_two_low, ffn_up_low, 1)
    norm_two_part = product_by_rows(ffn_gate_low, ffn_gate_weight) + product_by_rows(
        ffn_up_low, ffn_up_weight
    )
    norm_two_grad = pair_sum(norm_two_part)
    hidden_norm_grad, gain_two_grad = norm_two_back(norm_two_grad)
    hidden_grad = grad_out + hidden_norm_grad
    hidden_low = hidden_grad.astype(jnp.bfloat16)
    out_grad = cols_grad(mixed_low, hidden_low, 2)
    mixed_grad = product_by_rows(hidden_low, out_weights)
    attn_grad_low = (
        mixed_grad[:, inner:]
        .astype(jnp.bfloat16)
        .reshape(block_rows, key_heads, -1, HD)
    )
    scores_again = (
        jnp.einsum("qkgd,skd->kgqs", query_groups, key_window, preferred_element_type=jnp.float32)
        * score_scale
    )
    probs = jnp.where(allowed[None, None], jnp.exp(scores_again - log_total), 0.0)
    probs_back_low = probs.astype(jnp.bfloat16)
    prob_grad = jnp.einsum(
        "qkgd,skd->kgqs", attn_grad_low, value_window, preferred_element_type=jnp.float32
    )
    row_dots = jnp.sum(probs * prob_grad, axis=-1, keepdims=True)
    score_grad_low = (probs * (prob_grad - row_dots)).astype(jnp.bfloat16)
    query_grad = (
        jnp.einsum("kgqs,skd->qkgd", score_grad_low, key_window, preferred_element_type=jnp.float32)
        * score_scale
    )
    key_grad = (
        jnp.einsum(
            "kgqs,qkgd->skd", score_grad_low, query_groups, preferred_element_type=jnp.float32
        )
        * score_scale
    )
    value_grad = jnp.einsum(
        "kgqs,qkgd->skd", probs_back_low, attn_grad_low, preferred_element_type=jnp.float32
    )
    pair_grad = jnp.concatenate(
        [key_grad.reshape(-1, key_heads * HD), value_grad.reshape(-1, key_heads * HD)], axis=1
    )
    own_pair_grad = pair_grad[(MAXB - 1) * block_rows :]
    for distance in range(1, MAXB):
        pair_piece = pair_grad[(MAXB - 1 - distance) * block_rows : (MAXB - distance) * block_rows]
        own_pair_grad = own_pair_grad + shifted(
            pair_piece.astype(jnp.bfloat16), "ctx", -distance
        ).astype(pair_piece.dtype)
    key_grad_low = (
        rotate(
            own_pair_grad[:, : key_heads * HD].reshape(block_rows, key_heads, HD),
            cos_table,
            -sin_table,
        )
        .reshape(block_rows, -1)
        .astype(jnp.bfloat16)
    )
    value_grad_low = own_pair_grad[:, key_heads * HD :].astype(jnp.bfloat16)
    query_grad_low = (
        rotate(query_grad.reshape(block_rows, -1, HD), cos_table, -sin_table)
        .reshape(block_rows, -1)
        .astype(jnp.bfloat16)
    )
    ssm_gate_low, state_in_grad = scan_gated_back(
        mixed_grad, scan_out, bc_low, sum_cols, second_pre, gate_at
    )
    end_grad = carried_states(keep_low * state_in_grad, decay_row, True)
    in_grad, rim_grad, tap_grad, step_part, sum_part, bc_grad, bc_rim_grad, bc_tap_grad = scan_back(
        first_pre, rims, taps, bc_taps, step_cols, sum_cols, sum_rows,
        mixed_grad, second_pre, gate_at, state_in, end_grad, bc_low,
    )
    edge_grad = jnp.concatenate([rim_grad, bc_rim_grad], axis=1)[8 - rim_rows :]
    edge_back = shifted(keep_state * edge_grad, "ctx", -1)
    edge_back = jnp.pad(edge_back, ((block_rows - rim_rows, 0), (0, 0)))
    input_grad_low = (in_grad + edge_back[:, :inner]).astype(jnp.bfloat16)
    bc_pre_part = bc_grad + edge_back[:, inner:]
    rate_grad = lax.dot_general(
        lower, from_pairs(sum_part), (((0,), (0,)), ((), ())), precision=highest
    )
    step_grad = (from_pairs(step_part) + rate * rate_grad) * jax.nn.sigmoid(step_in)
    step_grad_low = step_grad.astype(jnp.bfloat16)
    tap_sums = [
        tap_grad[:KW].T,
        tap_grad[KW],
        jnp.sum(step_grad, axis=0),
        jnp.sum(rate_grad * rate * step_size, axis=0),
        jnp.sum(tap_grad[KW + 1].reshape(steps, head_dim), axis=1),
    ]
    no_misc = jnp.zeros((block_rows, 128 - steps), jnp.bfloat16)
    first_grads = jnp.concatenate(
        [input_grad_low, bc_pre_part.astype(jnp.bfloat16), step_grad_low, no_misc], axis=1
    )
    second_grads = jnp.concatenate(
        [query_grad_low, key_grad_low, value_grad_low, ssm_gate_low], axis=1
    )
    norm_one_grad = pair_sum(
        product_by_rows(first_grads, first_weights) + product_by_rows(second_grads, second_weights)
    )
    bc_grad_low = pair_sum(bc_pre_part).astype(jnp.bfloat16)
    conv_bc_grads = jnp.concatenate([bc_tap_grad[:KW].T.reshape(-1), bc_tap_grad[KW]])
    conv_bc_grads = conv_bc_grads + swap(conv_bc_grads)
    inputs_norm_grad, gain_one_grad = norm_one_back(norm_one_grad)
    tokens_grad = (hidden_grad + inputs_norm_grad).astype(jnp.bfloat16)
    first_grads = jnp.concatenate([input_grad_low, bc_grad_low, step_grad_low, no_misc], axis=1)
    first_grad = rows_grad(normed_low, first_grads, 1)
    second_grad = rows_grad(normed_low, second_grads, 2)
    small = [
        tap_sums[0].reshape(-1),
        *tap_sums[1:],
        conv_bc_grads,
        whole_order(gain_one_grad).reshape(-1),
        whole_order(gain_two_grad).reshape(-1),
    ]
    packed = jnp.concatenate(small)
    filled = -packed.shape[0] % 1024
    packed = summed(jnp.pad(packed, (0, filled)).reshape(-1, 128)).reshape(-1)
    sums, at = ([], 0)
    for part in small:
        sums.append(packed[at : at + part.shape[0]])
        at += part.shape[0]

    def own(vector, count):
        return lax.dynamic_slice_in_dim(vector, block_index * count, count, 0)

    conv_bc_sums = sums[5]
    conv_rows = conv_bc_weight.shape[0]
    return (
        reordered(layer_out, to_whole),
        reordered(tokens_grad, to_whole),
        own(sums[6], rows_here),
        second_grad[:, heads_wide + 2 * pair_wide :],
        first_grad[:, :inner],
        first_grad[:, inner : inner + shared],
        first_grad[:, inner + shared : inner + shared + steps],
        sums[0].reshape(inner, KW),
        sums[1],
        own(conv_bc_sums[: shared * KW], conv_rows * KW).reshape(conv_rows, KW),
        own(conv_bc_sums[shared * KW :], conv_rows),
        sums[2],
        sums[3],
        sums[4],
        out_grad[:inner],
        second_grad[:, :heads_wide],
        second_grad[:, heads_wide : heads_wide + pair_wide],
        second_grad[:, heads_wide + pair_wide : heads_wide + 2 * pair_wide],
        out_grad[inner:],
        own(sums[7], rows_here),
        ffn_gate_grad,
        ffn_up_grad,
        ffn_down_grad,
    )


def solution(mesh):
    return jax.shard_map(
        per_device,
        mesh=mesh,
        in_specs=(
            P("ctx", None),
            P("ctx", None),
            P("ctx"),
            P("ctx", "wt"),
            P("ctx", "wt"),
            P("ctx", None),
            P("ctx", "wt"),
            P("wt", None),
            P("wt"),
            P("ctx", None),
            P("ctx"),
            P("wt"),
            P("wt"),
            P("wt"),
            P("wt", "ctx"),
            P("ctx", "wt"),
            P("ctx", "wt"),
            P("ctx", "wt"),
            P("wt", "ctx"),
            P("ctx"),
            P("ctx", "wt"),
            P("ctx", "wt"),
            P("wt", "ctx"),
            P(),
            P(),
            P(),
        ),
        out_specs=(
            P("ctx", None),
            P("ctx", None),
            P("ctx"),
            P("ctx", "wt"),
            P("ctx", "wt"),
            P("ctx", None),
            P("ctx", "wt"),
            P("wt", None),
            P("wt"),
            P("ctx", None),
            P("ctx"),
            P("wt"),
            P("wt"),
            P("wt"),
            P("wt", "ctx"),
            P("ctx", "wt"),
            P("ctx", "wt"),
            P("ctx", "wt"),
            P("wt", "ctx"),
            P("ctx"),
            P("ctx", "wt"),
            P("ctx", "wt"),
            P("wt", "ctx"),
        ),
        check_vma=False,
    )
```

```python
import jax
import jax.numpy as jnp
from jax import lax
from jax.experimental import pallas as pl
from jax.experimental.pallas import tpu as pltpu
from jax.sharding import PartitionSpec as P

HD = 128
KW = 4
MAXB = 8
SCAN_ROWS = 128
ATTN_ROWS = 256


epsilon = 1e-05
rope_base = 100000000000.0
highest = lax.Precision.HIGHEST
masked_score = -1e30


def shifted(value, axis, steps):
    count = lax.axis_size(axis)
    leading, last = (max(0, -steps), min(count, count - steps))
    return lax.ppermute(value, axis, [(source, source + steps) for source in range(leading, last)])


def hop(value, code):
    if code == 0:
        return value
    count = lax.axis_size("ctx")
    return lax.ppermute(value, "ctx", [(source, source ^ code) for source in range(count)])


def swap(value):
    return lax.ppermute(value, "wt", [(0, 1), (1, 0)])


def pair_sum(value):
    rounded = lax.reduce_precision(value, 8, 7)
    return rounded + swap(rounded.astype(jnp.bfloat16)).astype(jnp.float32)


def slot_devices(count):
    high = count // 4
    return [4 * (slot % high) + slot // high for slot in range(count)]


def gathered(piece, axis, first):
    high = lax.axis_size("ctx") // 4
    second = 3 - first
    quarter = jnp.concatenate([piece] + [hop(piece, 4 * k) for k in range(1, high)], axis=axis)
    parts = {0: quarter, first: hop(quarter, first)}
    parts[second] = hop(quarter, second)
    parts[3] = hop(parts[first], second)
    return jnp.concatenate([parts[k] for k in range(4)], axis=axis)


def reduced(parts, axis, first):
    high = lax.axis_size("ctx") // 4
    second = 3 - first
    low = [part.astype(jnp.bfloat16) for part in parts]
    near = parts[0] + hop(low[first], first).astype(jnp.float32)
    far = parts[second] + hop(low[3], first).astype(jnp.float32)
    quarter = near + hop(far.astype(jnp.bfloat16), second).astype(jnp.float32)
    blocks = jnp.split(quarter, high, axis=axis)
    total = blocks[0]
    for k in range(1, high):
        total = total + hop(blocks[k].astype(jnp.bfloat16), 4 * k).astype(jnp.float32)
    return total


def summed(value):
    bit = 1
    while bit < lax.axis_size("ctx"):
        value = value + hop(value, bit)
        bit *= 2
    return value


def reordered(value, order):
    blocks = order.shape[0]
    rows, width = value.shape[0], value.shape[1] // blocks
    if width % 128:
        return jnp.take(value.reshape(rows, blocks, width), order, axis=1).reshape(rows, -1)

    def body(order_ref, in_ref, out_ref):
        out_ref[...] = in_ref[...]

    return pl.pallas_call(
        body,
        out_shape=jax.ShapeDtypeStruct(value.shape, value.dtype),
        grid_spec=pltpu.PrefetchScalarGridSpec(
            num_scalar_prefetch=1,
            grid=(blocks,),
            in_specs=[pl.BlockSpec((rows, width), lambda s, order_ref: (0, order_ref[s]))],
            out_specs=pl.BlockSpec((rows, width), lambda s, order_ref: (0, s)),
        ),
        name="reordered",
    )(order, value)


def carried_states(states, decays, reverse):
    me = lax.axis_index("ctx")
    place = me % 4
    width = states.shape[1] // 4
    low = states.astype(jnp.bfloat16)

    def quarter(value, index):
        return lax.dynamic_slice_in_dim(value, index * width, width, 1)

    got = [hop(quarter(low, place ^ k), k) for k in range(4)]
    got_decay = [hop(quarter(decays, place ^ k), k) for k in range(4)]

    def in_order(pieces):
        odd = place % 2 == 1
        pieces = [jnp.where(odd, pieces[k ^ 1], pieces[k]) for k in range(4)]
        upper = place >= 2
        return [jnp.where(upper, pieces[k ^ 2], pieces[k]) for k in range(4)]

    blocks = [piece.astype(jnp.float32) for piece in in_order(got)]
    rates = in_order(got_decay)
    if reverse:
        blocks, rates = (blocks[::-1], rates[::-1])
    total, rate = (blocks[0], rates[0])
    for block, block_rate in zip(blocks[1:], rates[1:]):
        total, rate = (block + block_rate * total, block_rate * rate)
    step = -4 if reverse else 4
    total_low = total.astype(jnp.bfloat16)
    near, near_rate = (shifted(total_low, "ctx", step), shifted(rate, "ctx", step))
    far = shifted(total_low, "ctx", 2 * step)
    state = near.astype(jnp.float32) + near_rate * far.astype(jnp.float32)
    reached = []
    for block, block_rate in zip(blocks, rates):
        reached.append(state.astype(jnp.bfloat16))
        state = block + block_rate * state
    if reverse:
        reached = reached[::-1]
    mine = in_order(reached)
    back = in_order([hop(mine[k], k) for k in range(4)])
    return jnp.concatenate(back, axis=1)


def plain_product(left_side, right_side):
    return jnp.dot(left_side, right_side, preferred_element_type=jnp.float32)


def product_by_rows(left_side, right_side):
    return lax.dot_general(
        left_side, right_side, (((1,), (1,)), ((), ())), preferred_element_type=jnp.float32
    )


def product_of_cols(left_side, right_side):
    return lax.dot_general(
        left_side, right_side, (((0,), (0,)), ((), ())), preferred_element_type=jnp.float32
    )


def rms_scale(values, gain_vec):
    return (
        values * lax.rsqrt(jnp.mean(values * values, axis=-1, keepdims=True) + epsilon) * gain_vec
    )


def rotary_tables(positions):
    exponents = jnp.arange(HD // 2, dtype=jnp.float32) * (2.0 / HD)
    frequency = jnp.power(jnp.float32(rope_base), -exponents)
    angles = positions.astype(jnp.float32)[:, None] * frequency[None, :]
    return (jnp.cos(angles), jnp.sin(angles))


def rotate(values, cos_table, sin_table):
    half_dim = values.shape[-1] // 2
    first_half = values[..., :half_dim]
    second_half = values[..., half_dim:]
    cos_table = cos_table[:, None, :]
    sin_table = sin_table[:, None, :]
    return jnp.concatenate(
        [
            first_half * cos_table - second_half * sin_table,
            second_half * cos_table + first_half * sin_table,
        ],
        axis=-1,
    )


def convolved(rim, block, taps):
    length = block.shape[0]
    extended = jnp.concatenate([rim, block], axis=0)
    first = rim.shape[0] - (KW - 1)
    summed = taps[KW : KW + 1]
    for j in range(KW):
        summed = summed + extended[first + j : first + j + length] * taps[j : j + 1]
    return (extended, summed)


def convolved_back(extended, pre_grad, taps):
    length = pre_grad.shape[0]
    rim_rows = extended.shape[0] - length
    first = rim_rows - (KW - 1)
    zeros = jnp.zeros((8, pre_grad.shape[1]), jnp.float32)
    padded = jnp.concatenate([zeros, pre_grad, zeros], axis=0)
    total = jnp.zeros_like(extended)
    rows = []
    for j in range(KW):
        start = 8 - rim_rows + KW - 1 - j
        total = total + padded[start : start + rim_rows + length] * taps[j : j + 1]
        rows.append(
            jnp.sum(pre_grad * extended[first + j : first + j + length], axis=0, keepdims=True)
        )
    rows.append(jnp.sum(pre_grad, axis=0, keepdims=True))
    return (total, rows)


def silu_slope(value, sigmoid):
    return sigmoid * (1.0 + value * (1.0 - sigmoid))


def low_dot(left_side, right_side, left_axis, right_axis):
    return lax.dot_general(
        left_side.astype(jnp.bfloat16),
        right_side.astype(jnp.bfloat16),
        (((left_axis,), (right_axis,)), ((), ())),
        preferred_element_type=jnp.float32,
    )


def lower_gram(c_low, b_low):
    length = c_low.shape[0]
    gram = low_dot(c_low, b_low, 1, 1)
    rows = lax.broadcasted_iota(jnp.int32, (length, length), 0)
    cols = lax.broadcasted_iota(jnp.int32, (length, length), 1)
    return jnp.where(rows >= cols, gram, 0.0)


def scan_blocks(inner, shared, length, wide):
    return [
        pl.BlockSpec((length, wide), lambda i: (0, i)),
        pl.BlockSpec((8, wide), lambda i: (0, i)),
        pl.BlockSpec((8, wide), lambda i: (0, i)),
        pl.BlockSpec((length, shared), lambda i: (0, inner // shared)),
        pl.BlockSpec((8, shared), lambda i: (0, inner // shared)),
        pl.BlockSpec((8, shared), lambda i: (0, 0)),
        pl.BlockSpec((1, length, 2), lambda i: (i, 0, 0)),
        pl.BlockSpec((1, length, 2), lambda i: (i, 0, 0)),
        pl.BlockSpec((1, 2, length), lambda i: (i, 0, 0)),
    ]


def scan_forward(first_pre, rims, taps, bc_taps, step_cols, sum_cols, sum_rows, inner, shared):
    length = first_pre.shape[0]
    pairs = step_cols.shape[0]
    wide = inner // pairs
    size = wide // 2
    state_dim = shared // 2
    part = min(SCAN_ROWS, length)

    def body(
        in_ref, rim_ref, tap_ref, bc_ref, bc_rim_ref, bc_tap_ref, step_ref, col_ref, row_ref,
        out_ref, state_ref, bc_low_ref, gram_ref,
    ):
        @pl.when(pl.program_id(0) == 0)
        def _():
            _, pre = convolved(bc_rim_ref[...], bc_ref[...], bc_tap_ref[...])
            acts = (pre * jax.nn.sigmoid(pre)).astype(jnp.bfloat16)
            bc_low_ref[...] = acts
            gram_ref[...] = lower_gram(acts[:, state_dim:], acts[:, :state_dim])

        taps_here = tap_ref[...]
        _, pre = convolved(rim_ref[...], in_ref[...], taps_here)
        acts = pre * jax.nn.sigmoid(pre)
        outs, tails = ([], [])
        for head in range(2):
            lanes = slice(head * size, (head + 1) * size)
            step = step_ref[0][:, head : head + 1]
            col = col_ref[0][:, head : head + 1]
            row = row_ref[0][head : head + 1, :]
            stepped = acts[:, lanes] * step
            stepped_low = stepped.astype(jnp.bfloat16)
            for at in range(0, length, part):
                end = at + part
                decay = jnp.exp(jnp.minimum(col[at:end] - row[:, :end], 0.0))
                weights = (decay * gram_ref[at:end, :end]).astype(jnp.bfloat16)
                out_ref[at:end, lanes] = low_dot(weights, stepped_low[:end], 1, 0) + (
                    taps_here[KW + 1 : KW + 2, lanes] * acts[at:end, lanes]
                )
            tails.append(stepped * jnp.exp(col[length - 1 : length] - col))
        tail = jnp.concatenate(tails, axis=1)
        state_ref[...] = low_dot(bc_low_ref[:, :state_dim], tail, 0, 0).astype(jnp.bfloat16)

    return pl.pallas_call(
        body,
        grid=(pairs,),
        out_shape=(
            jax.ShapeDtypeStruct((length, inner), jnp.float32),
            jax.ShapeDtypeStruct((state_dim, inner), jnp.bfloat16),
            jax.ShapeDtypeStruct((length, shared), jnp.bfloat16),
        ),
        in_specs=scan_blocks(inner, shared, length, wide),
        out_specs=(
            pl.BlockSpec((length, wide), lambda i: (0, i)),
            pl.BlockSpec((state_dim, wide), lambda i: (0, i)),
            pl.BlockSpec((length, shared), lambda i: (0, 0)),
        ),
        scratch_shapes=[pltpu.VMEM((length, length), jnp.float32)],
        compiler_params=pltpu.CompilerParams(vmem_limit_bytes=48 << 20),
        name="scan_forward",
    )(first_pre, rims, taps, first_pre, rims, bc_taps, step_cols, sum_cols, sum_rows)


def scan_gated(intra, state_in, bc_low, sum_cols, second_pre, gate_at):
    length, inner = intra.shape
    pairs = sum_cols.shape[0]
    wide = inner // pairs
    size = wide // 2
    state_dim = bc_low.shape[1] // 2

    def body(intra_ref, state_ref, c_ref, col_ref, gate_ref, out_ref, act_ref):
        carried = low_dot(c_ref[...], state_ref[...], 1, 0)
        gate = gate_ref[...]
        silu = gate * jax.nn.sigmoid(gate)
        for head in range(2):
            lanes = slice(head * size, (head + 1) * size)
            growth = jnp.exp(col_ref[0][:, head : head + 1])
            whole = intra_ref[:, lanes] + carried[:, lanes] * growth
            out_ref[:, lanes] = whole
            act_ref[:, lanes] = (whole * silu[:, lanes]).astype(jnp.bfloat16)

    block = pl.BlockSpec((length, wide), lambda i: (0, i))
    return pl.pallas_call(
        body,
        grid=(pairs,),
        out_shape=(
            jax.ShapeDtypeStruct((length, inner), jnp.float32),
            jax.ShapeDtypeStruct((length, inner), jnp.bfloat16),
        ),
        in_specs=[
            block,
            pl.BlockSpec((state_dim, wide), lambda i: (0, i)),
            pl.BlockSpec((length, state_dim), lambda i: (0, 1)),
            pl.BlockSpec((1, length, 2), lambda i: (i, 0, 0)),
            pl.BlockSpec((length, wide), lambda i: (0, gate_at // wide + i)),
        ],
        out_specs=(block, block),
        compiler_params=pltpu.CompilerParams(vmem_limit_bytes=48 << 20),
        name="scan_gated",
    )(intra, state_in, bc_low, sum_cols, second_pre)


def scan_gated_back(out_grads, whole, bc_low, sum_cols, second_pre, gate_at):
    length, inner = whole.shape
    pairs = sum_cols.shape[0]
    wide = inner // pairs
    size = wide // 2
    state_dim = bc_low.shape[1] // 2

    def body(grad_ref, whole_ref, c_ref, col_ref, gate_ref, gate_grad_ref, state_ref):
        gate = gate_ref[...]
        sigmoid = jax.nn.sigmoid(gate)
        grad = grad_ref[...]
        gate_grad_ref[...] = (grad * whole_ref[...] * silu_slope(gate, sigmoid)).astype(jnp.bfloat16)
        inside = grad * (gate * sigmoid)
        grown = [
            inside[:, head * size : (head + 1) * size] * jnp.exp(col_ref[0][:, head : head + 1])
            for head in range(2)
        ]
        state_ref[...] = low_dot(c_ref[...], jnp.concatenate(grown, axis=1), 0, 0).astype(
            jnp.bfloat16
        )

    block = pl.BlockSpec((length, wide), lambda i: (0, i))
    return pl.pallas_call(
        body,
        grid=(pairs,),
        out_shape=(
            jax.ShapeDtypeStruct((length, inner), jnp.bfloat16),
            jax.ShapeDtypeStruct((state_dim, inner), jnp.bfloat16),
        ),
        in_specs=[
            block,
            block,
            pl.BlockSpec((length, state_dim), lambda i: (0, 1)),
            pl.BlockSpec((1, length, 2), lambda i: (i, 0, 0)),
            pl.BlockSpec((length, wide), lambda i: (0, gate_at // wide + i)),
        ],
        out_specs=(block, pl.BlockSpec((state_dim, wide), lambda i: (0, i))),
        compiler_params=pltpu.CompilerParams(vmem_limit_bytes=48 << 20),
        name="scan_gated_back",
    )(out_grads, whole, bc_low, sum_cols, second_pre)


def scan_back(
    first_pre, rims, taps, bc_taps, step_cols, sum_cols, sum_rows,
    out_grads, second_pre, gate_at, state_in, end_grad, bc_low,
):
    length = first_pre.shape[0]
    pairs = step_cols.shape[0]
    state_dim, inner = state_in.shape
    shared = bc_low.shape[1]
    wide = inner // pairs
    size = wide // 2
    part = min(SCAN_ROWS, length)

    def body(
        in_ref, rim_ref, tap_ref, bc_ref, bc_rim_ref, bc_tap_ref, step_ref, col_ref, row_ref,
        grad_ref, gate_ref, state_ref, end_ref, bc_low_ref,
        in_grad_ref, rim_grad_ref, tap_grad_ref, step_grad_ref, sum_grad_ref,
        bc_grad_ref, bc_rim_grad_ref, bc_tap_grad_ref,
        gram_ref, gram_grad_ref, acts_grad_ref, back_ref,
    ):
        b_low = bc_low_ref[:, :state_dim]
        c_low = bc_low_ref[:, state_dim:]

        @pl.when(pl.program_id(0) == 0)
        def _():
            gram_ref[...] = lower_gram(c_low, b_low)
            gram_grad_ref[...] = jnp.zeros_like(gram_grad_ref)
            acts_grad_ref[...] = jnp.zeros_like(acts_grad_ref)

        taps_here = tap_ref[...]
        extended, pre = convolved(rim_ref[...], in_ref[...], taps_here)
        sigmoid = jax.nn.sigmoid(pre)
        acts = pre * sigmoid
        gate = gate_ref[...]
        out_grad = grad_ref[...] * (gate * jax.nn.sigmoid(gate))
        state = state_ref[...]
        end = end_ref[...]
        from_end = low_dot(b_low, end, 1, 0)
        from_start = low_dot(c_low, state, 1, 0)
        state_dot = jnp.sum(
            state.astype(jnp.float32) * end.astype(jnp.float32), axis=0, keepdims=True
        )
        last_row = lax.broadcasted_iota(jnp.int32, (length, 1), 0) == length - 1
        acts_grads, tails, grown_grads = ([], [], [])
        for head in range(2):
            lanes = slice(head * size, (head + 1) * size)
            step = step_ref[0][:, head : head + 1]
            col = col_ref[0][:, head : head + 1]
            row = row_ref[0][head : head + 1, :]
            here = acts[:, lanes]
            stepped = here * step
            stepped_low = stepped.astype(jnp.bfloat16)
            grad = out_grad[:, lanes]
            grad_low = grad.astype(jnp.bfloat16)
            grad_wide = grad_low.astype(jnp.float32)
            back_ref[...] = jnp.zeros_like(back_ref)
            row_terms = []
            for at in range(0, length, part):
                to = at + part
                decay = jnp.exp(jnp.minimum(col[at:to] - row[:, :to], 0.0))
                weights = (decay * gram_ref[at:to, :to]).astype(jnp.bfloat16)
                again = low_dot(weights, stepped_low[:to], 1, 0)
                row_terms.append(jnp.sum(again * grad_wide[at:to], axis=1, keepdims=True))
                back_ref[:to] += low_dot(weights, grad_low[at:to], 0, 0)
                gram_grad_ref[at:to, :to] += decay * low_dot(
                    grad_low[at:to], stepped_low[:to], 1, 1
                )
            back = back_ref[...]
            tail = jnp.exp(col[length - 1 : length] - col)
            growth = jnp.exp(col)
            ended = from_end[:, lanes] * tail
            end_terms = jnp.sum(ended * stepped, axis=1, keepdims=True)
            col_terms = jnp.sum(back * stepped_low.astype(jnp.float32), axis=1, keepdims=True)
            start_terms = growth * jnp.sum(from_start[:, lanes] * grad, axis=1, keepdims=True)
            whole = jnp.sum(end_terms, axis=0, keepdims=True) + growth[
                length - 1 : length
            ] * jnp.sum(state_dot[:, lanes], axis=1, keepdims=True)
            sum_grad_ref[0, :, head : head + 1] = (
                jnp.concatenate(row_terms, axis=0)
                + start_terms
                - col_terms
                - end_terms
                + jnp.where(last_row, whole, 0.0)
            )
            back = back + ended
            step_grad_ref[0, :, head : head + 1] = jnp.sum(back * here, axis=1, keepdims=True)
            acts_grads.append(taps_here[KW + 1 : KW + 2, lanes] * grad + back * step)
            tails.append((stepped * tail).astype(jnp.bfloat16))
            grown_grads.append((grad * growth).astype(jnp.bfloat16))
        acts_grad_ref[:, :state_dim] += low_dot(jnp.concatenate(tails, axis=1), end, 1, 1)
        acts_grad_ref[:, state_dim:] += low_dot(jnp.concatenate(grown_grads, axis=1), state, 1, 1)
        pre_grad = jnp.concatenate(acts_grads, axis=1) * silu_slope(pre, sigmoid)
        total, rows = convolved_back(extended, pre_grad, taps_here)
        rim_grad_ref[...] = total[:8]
        in_grad_ref[...] = total[8:]
        rows.append(jnp.sum(out_grad * acts, axis=0, keepdims=True))
        rows.append(jnp.zeros((8 - len(rows), wide), jnp.float32))
        tap_grad_ref[...] = jnp.concatenate(rows, axis=0)

        @pl.when(pl.program_id(0) == pairs - 1)
        def _():
            gram_grad = gram_grad_ref[...]
            rows_of = lax.broadcasted_iota(jnp.int32, (length, length), 0)
            cols_of = lax.broadcasted_iota(jnp.int32, (length, length), 1)
            gram_grad = jnp.where(rows_of >= cols_of, gram_grad, 0.0).astype(jnp.bfloat16)
            acts_grad_ref[:, :state_dim] += low_dot(gram_grad, c_low, 0, 0)
            acts_grad_ref[:, state_dim:] += low_dot(gram_grad, b_low, 1, 0)
            bc_taps_here = bc_tap_ref[...]
            bc_extended, bc_pre = convolved(bc_rim_ref[...], bc_ref[...], bc_taps_here)
            bc_pre_grad = acts_grad_ref[...] * silu_slope(bc_pre, jax.nn.sigmoid(bc_pre))
            bc_total, bc_rows = convolved_back(bc_extended, bc_pre_grad, bc_taps_here)
            bc_rim_grad_ref[...] = bc_total[:8]
            bc_grad_ref[...] = bc_total[8:]
            bc_rows.append(jnp.zeros((8 - len(bc_rows), shared), jnp.float32))
            bc_tap_grad_ref[...] = jnp.concatenate(bc_rows, axis=0)

    block = pl.BlockSpec((length, wide), lambda i: (0, i))
    eight = pl.BlockSpec((8, wide), lambda i: (0, i))
    table = pl.BlockSpec((1, length, 2), lambda i: (i, 0, 0))
    state_block = pl.BlockSpec((state_dim, wide), lambda i: (0, i))
    bc_block = pl.BlockSpec((length, shared), lambda i: (0, 0))
    bc_eight = pl.BlockSpec((8, shared), lambda i: (0, 0))
    wide_f32 = jax.ShapeDtypeStruct((length, inner), jnp.float32)
    eight_f32 = jax.ShapeDtypeStruct((8, inner), jnp.float32)
    table_f32 = jax.ShapeDtypeStruct(step_cols.shape, jnp.float32)
    bc_f32 = jax.ShapeDtypeStruct((length, shared), jnp.float32)
    bc_eight_f32 = jax.ShapeDtypeStruct((8, shared), jnp.float32)
    return pl.pallas_call(
        body,
        grid=(pairs,),
        out_shape=(
            wide_f32, eight_f32, eight_f32, table_f32, table_f32, bc_f32, bc_eight_f32, bc_eight_f32
        ),
        in_specs=scan_blocks(inner, shared, length, wide)
        + [
            block,
            pl.BlockSpec((length, wide), lambda i: (0, gate_at // wide + i)),
            state_block,
            state_block,
            bc_block,
        ],
        out_specs=(block, eight, eight, table, table, bc_block, bc_eight, bc_eight),
        scratch_shapes=[
            pltpu.VMEM((length, length), jnp.float32),
            pltpu.VMEM((length, length), jnp.float32),
            pltpu.VMEM((length, shared), jnp.float32),
            pltpu.VMEM((length, size), jnp.float32),
        ],
        compiler_params=pltpu.CompilerParams(vmem_limit_bytes=56 << 20),
        name="scan_back",
    )(
        first_pre, rims, taps, first_pre, rims, bc_taps, step_cols, sum_cols, sum_rows,
        out_grads, second_pre, state_in, end_grad, bc_low,
    )


def turned(values, cos_wide, sin_wide):
    return values * cos_wide + pltpu.roll(values, values.shape[1] // 2, 1) * sin_wide


def own_mask(at, rows, keys, limit):
    query_row = lax.broadcasted_iota(jnp.int32, (rows, keys), 0) + at
    key_row = lax.broadcasted_iota(jnp.int32, (rows, keys), 1)
    return (key_row <= query_row) & (key_row < limit)


def attention_forward(layout, second_pre, window, cos_wide, sin_wide, heads):
    length = second_pre.shape[0]
    part = min(ATTN_ROWS, length)
    own_at = window.shape[0] - length
    scale = HD ** (-0.5)

    def body(layout_ref, query_ref, window_ref, cos_ref, sin_ref, out_ref, turned_ref, total_ref):
        query = turned(query_ref[...], cos_ref[...], sin_ref[...]).astype(jnp.bfloat16)
        turned_ref[...] = query
        for at in range(0, length, part):
            to = at + part
            here = query[at:to]

            def scores_of(keys):
                return scale * low_dot(here, keys, 1, 1)

            keys = window_ref[own_at : own_at + to, :HD]
            values = window_ref[own_at : own_at + to, HD:]
            scores = jnp.where(
                own_mask(at, part, to, layout_ref[1]), scores_of(keys), masked_score
            )
            top = jnp.max(scores, axis=1, keepdims=True)
            shares = jnp.exp(scores - top)
            total = jnp.sum(shares, axis=1, keepdims=True)
            acc = low_dot(shares, values, 1, 0)

            def earlier(distance, carry):
                top, total, acc = carry
                start = pl.multiple_of(own_at - distance * length, length)
                scores = scores_of(window_ref[pl.ds(start, length), :HD])
                new_top = jnp.maximum(top, jnp.max(scores, axis=1, keepdims=True))
                fade = jnp.exp(top - new_top)
                shares = jnp.exp(scores - new_top)
                total = fade * total + jnp.sum(shares, axis=1, keepdims=True)
                acc = fade * acc + low_dot(shares, window_ref[pl.ds(start, length), HD:], 1, 0)
                return (new_top, total, acc)

            top, total, acc = lax.fori_loop(1, layout_ref[0] + 1, earlier, (top, total, acc))
            out_ref[at:to] = (acc / total).astype(jnp.bfloat16)
            total_ref[0, at:to] = top + jnp.log(total)

    head = pl.BlockSpec((length, HD), lambda i, layout_ref: (0, i))
    whole = pl.BlockSpec((length, HD), lambda i, layout_ref: (0, 0))
    return pl.pallas_call(
        body,
        out_shape=(
            jax.ShapeDtypeStruct((length, heads * HD), jnp.bfloat16),
            jax.ShapeDtypeStruct((length, heads * HD), jnp.bfloat16),
            jax.ShapeDtypeStruct((heads, length, 1), jnp.float32),
        ),
        grid_spec=pltpu.PrefetchScalarGridSpec(
            num_scalar_prefetch=1,
            grid=(heads,),
            in_specs=[
                head,
                pl.BlockSpec(window.shape, lambda i, layout_ref: (0, 0)),
                whole,
                whole,
            ],
            out_specs=(
                head,
                head,
                pl.BlockSpec((1, length, 1), lambda i, layout_ref: (i, 0, 0)),
            ),
        ),
        compiler_params=pltpu.CompilerParams(vmem_limit_bytes=48 << 20),
        name="attention_forward",
    )(layout, second_pre, window, cos_wide, sin_wide)


def attention_back(layout, query, window, out, totals, mixed_grad, grad_at, cos_wide, sin_wide):
    length = query.shape[0]
    heads = query.shape[1] // HD
    part = min(ATTN_ROWS, length)
    own_at = window.shape[0] - length
    scale = HD ** (-0.5)

    def body(
        layout_ref, query_ref, window_ref, out_in_ref, total_ref, grad_ref, cos_ref, sin_ref,
        query_grad_ref, window_grad_ref, own_grad_ref, sum_ref, acc_ref,
    ):
        @pl.when(pl.program_id(0) == 0)
        def _():
            sum_ref[...] = jnp.zeros_like(sum_ref)

        for at in range(0, length, part):
            to = at + part
            here = query_ref[at:to]
            grad = grad_ref[at:to].astype(jnp.bfloat16)
            dots = jnp.sum(
                grad.astype(jnp.float32) * out_in_ref[at:to].astype(jnp.float32),
                axis=1,
                keepdims=True,
            )
            total = total_ref[0, at:to]

            def step(start, count, mask):
                keys = window_ref[pl.ds(start, count), :HD]
                values = window_ref[pl.ds(start, count), HD:]
                probs = jnp.exp(scale * low_dot(here, keys, 1, 1) - total)
                if mask is not None:
                    probs = jnp.where(mask, probs, 0.0)
                score_grad = (probs * (low_dot(grad, values, 1, 1) - dots)).astype(jnp.bfloat16)
                sum_ref[pl.ds(start, count), :HD] += low_dot(score_grad, here, 0, 0)
                sum_ref[pl.ds(start, count), HD:] += low_dot(probs, grad, 0, 0)
                return low_dot(score_grad, keys, 1, 0)

            acc_ref[...] = step(own_at, to, own_mask(at, part, to, layout_ref[1]))

            def earlier(distance, carry):
                start = pl.multiple_of(own_at - distance * length, length)
                acc_ref[...] += step(start, length, None)
                return carry

            lax.fori_loop(1, layout_ref[0] + 1, earlier, 0)
            query_grad_ref[at:to] = turned(
                acc_ref[...] * scale, cos_ref[at:to], -sin_ref[at:to]
            ).astype(jnp.bfloat16)

        @pl.when(pl.program_id(0) == heads - 1)
        def _():
            own_grad_ref[:, :HD] = sum_ref[own_at:, :HD] * scale
            own_grad_ref[:, HD:] = sum_ref[own_at:, HD:]
            window_grad_ref[:, :HD] = (sum_ref[:own_at, :HD] * scale).astype(jnp.bfloat16)
            window_grad_ref[:, HD:] = sum_ref[:own_at, HD:].astype(jnp.bfloat16)

    head = pl.BlockSpec((length, HD), lambda i, layout_ref: (0, i))
    whole = pl.BlockSpec((length, HD), lambda i, layout_ref: (0, 0))
    return pl.pallas_call(
        body,
        out_shape=(
            jax.ShapeDtypeStruct(query.shape, jnp.bfloat16),
            jax.ShapeDtypeStruct((own_at, 2 * HD), jnp.bfloat16),
            jax.ShapeDtypeStruct((length, 2 * HD), jnp.float32),
        ),
        grid_spec=pltpu.PrefetchScalarGridSpec(
            num_scalar_prefetch=1,
            grid=(heads,),
            in_specs=[
                head,
                pl.BlockSpec(window.shape, lambda i, layout_ref: (0, 0)),
                head,
                pl.BlockSpec((1, length, 1), lambda i, layout_ref: (i, 0, 0)),
                pl.BlockSpec((length, HD), lambda i, layout_ref: (0, grad_at // HD + i)),
                whole,
                whole,
            ],
            out_specs=(
                head,
                pl.BlockSpec((own_at, 2 * HD), lambda i, layout_ref: (0, 0)),
                pl.BlockSpec((length, 2 * HD), lambda i, layout_ref: (0, 0)),
            ),
            scratch_shapes=[
                pltpu.VMEM(window.shape, jnp.float32),
                pltpu.VMEM((part, HD), jnp.float32),
            ],
        ),
        compiler_params=pltpu.CompilerParams(vmem_limit_bytes=56 << 20),
        name="attention_back",
    )(layout, query, window, out, totals, mixed_grad, cos_wide, sin_wide)


def per_device(
    tokens,
    cotangent,
    mix_norm_gain,
    ssm_gate_proj,
    ssm_input_proj,
    ssm_bc_proj,
    ssm_step_proj,
    conv_in_weight,
    conv_in_bias,
    conv_bc_weight,
    conv_bc_bias,
    step_bias,
    decay_log,
    skip_gain,
    ssm_out_proj,
    query_proj,
    key_proj,
    value_proj,
    attn_out_proj,
    ffn_norm_gain,
    ffn_gate_proj,
    ffn_up_proj,
    ffn_down_proj,
    extra_blocks,
    seq_order,
    pad_rows,
):
    block_rows = tokens.shape[0]
    block_index = lax.axis_index("ctx")
    seq_count = seq_order.shape[0]
    slot_ids = jnp.arange(seq_count, dtype=jnp.int32)
    chosen = (seq_order[:, None] == slot_ids[None, :]).astype(jnp.int32)
    counts = jnp.sum(chosen * extra_blocks[None, :], axis=1) + 1
    slot_pads = jnp.sum(chosen * pad_rows[None, :], axis=1)
    slot_ends = jnp.cumsum(counts)
    starts = slot_ends - counts
    inside = (starts <= block_index) & (block_index < slot_ends)
    within = jnp.sum(jnp.where(inside, block_index - starts, 0))
    pad_here = jnp.sum(jnp.where(inside & (slot_ends - 1 == block_index), slot_pads, 0))
    row_ids = jnp.arange(block_rows, dtype=jnp.int32)
    valid_rows = (row_ids < block_rows - pad_here).astype(jnp.float32)
    positions = within * block_rows + row_ids
    keep_state = (within > 0).astype(jnp.float32)
    devices = lax.axis_size("ctx")
    codes = jnp.asarray(slot_devices(devices), jnp.int32)
    from_whole = jnp.bitwise_xor(codes, block_index)
    to_whole = jnp.argsort(from_whole).astype(jnp.int32)
    rows_here = mix_norm_gain.shape[0]
    misc_here = jnp.concatenate(
        [
            ssm_step_proj,
            mix_norm_gain[:, None],
            ffn_norm_gain[:, None],
            conv_bc_weight.reshape(rows_here, 1),
            jnp.pad(conv_bc_bias, (0, rows_here - conv_bc_bias.shape[0]))[:, None],
        ],
        axis=1,
    )
    steps = ssm_step_proj.shape[1]
    misc_here = jnp.pad(misc_here, ((0, 0), (0, 128 - misc_here.shape[1])))
    inner, shared = (ssm_input_proj.shape[1], ssm_bc_proj.shape[1])
    heads_wide, pair_wide = (query_proj.shape[1], key_proj.shape[1])
    first_weights = gathered(
        jnp.concatenate([ssm_input_proj, ssm_bc_proj, misc_here], axis=1), 0, 1
    )
    second_weights = gathered(
        jnp.concatenate([query_proj, key_proj, value_proj, ssm_gate_proj], axis=1), 0, 2
    )
    out_weights = gathered(jnp.concatenate([ssm_out_proj, attn_out_proj], axis=0), 1, 1)
    ffn_gate_weight = gathered(ffn_gate_proj, 0, 2)
    ffn_up_weight = gathered(ffn_up_proj, 0, 1)
    ffn_down_weight = gathered(ffn_down_proj, 1, 2)
    misc = first_weights[:, inner + shared :]
    mix_gain, gain_two = (misc[:, steps], misc[:, steps + 1])

    def whole_order(column):
        return jnp.take(column.reshape(devices, rows_here), to_whole, axis=0)

    conv_bc_full = whole_order(misc[:, steps + 2]).reshape(shared, KW)
    conv_bc_offset = whole_order(misc[:, steps + 3])[:, : conv_bc_bias.shape[0]].reshape(shared)
    tokens = reordered(tokens, from_whole)
    cotangent = reordered(cotangent, from_whole)
    inputs = tokens.astype(jnp.float32)
    normed_one, norm_one_back = jax.vjp(rms_scale, inputs, mix_gain.astype(jnp.float32))
    normed_low = normed_one.astype(jnp.bfloat16)
    first_pre = plain_product(normed_low, first_weights)
    second_pre = plain_product(normed_low, second_weights)
    step_raw = first_pre[:, inner + shared : inner + shared + steps]
    query_pre = second_pre[:, :heads_wide]
    key_pre = second_pre[:, heads_wide : heads_wide + pair_wide]
    value_pre = second_pre[:, heads_wide + pair_wide : heads_wide + 2 * pair_wide]
    gate_at = heads_wide + 2 * pair_wide
    rim_rows = KW - 1
    edge = shifted(first_pre[block_rows - rim_rows :, : inner + shared], "ctx", 1) * keep_state
    rims = jnp.pad(edge, ((8 - rim_rows, 0), (0, 0)))
    head_dim = inner // steps
    skips = jnp.repeat(skip_gain.astype(jnp.float32), head_dim)[None, :]
    taps = jnp.concatenate(
        [conv_in_weight.astype(jnp.float32).T, conv_in_bias.astype(jnp.float32)[None, :], skips]
    )
    taps = jnp.pad(taps, ((0, 8 - taps.shape[0]), (0, 0)))
    bc_taps = jnp.concatenate(
        [conv_bc_full.astype(jnp.float32).T, conv_bc_offset.astype(jnp.float32)[None, :]]
    )
    bc_taps = jnp.pad(bc_taps, ((0, 8 - bc_taps.shape[0]), (0, 0)))
    step_in = step_raw + step_bias.astype(jnp.float32)[None, :]
    step_size = jax.nn.softplus(step_in)
    rate = -jnp.exp(decay_log.astype(jnp.float32))[None, :]
    lower = (row_ids[:, None] >= row_ids[None, :]).astype(jnp.float32)
    log_decay = jnp.dot(lower, rate * step_size, precision=highest)

    def by_pairs(table):
        return table.reshape(block_rows, steps // 2, 2).transpose(1, 0, 2)

    def from_pairs(table):
        return table.transpose(1, 0, 2).reshape(block_rows, steps)

    step_cols = by_pairs(step_size)
    sum_cols = by_pairs(log_decay)
    sum_rows = log_decay.T.reshape(steps // 2, 2, block_rows)
    intra_out, local_states, bc_low = scan_forward(
        first_pre, rims, taps, bc_taps, step_cols, sum_cols, sum_rows, inner, shared
    )
    decay_row = keep_state * jnp.repeat(jnp.exp(log_decay[block_rows - 1]), head_dim)[None, :]
    keep_low = keep_state.astype(jnp.bfloat16)
    state_in = keep_low * carried_states(local_states, decay_row, False)
    scan_out, ssm_low = scan_gated(intra_out, state_in, bc_low, sum_cols, second_pre, gate_at)
    cos_table, sin_table = rotary_tables(positions)
    cos_wide = jnp.concatenate([cos_table, cos_table], axis=1)
    sin_wide = jnp.concatenate([-sin_table, sin_table], axis=1)
    key_rot = rotate(key_pre.reshape(block_rows, -1, HD), cos_table, sin_table)
    own_pair = jnp.concatenate(
        [key_rot.reshape(block_rows, HD).astype(jnp.bfloat16), value_pre.astype(jnp.bfloat16)],
        axis=1,
    )
    earlier_pairs = [shifted(own_pair, "ctx", distance) for distance in range(MAXB - 1, 0, -1)]
    window = jnp.concatenate(earlier_pairs + [own_pair], axis=0)
    layout = jnp.stack([within, block_rows - pad_here]).astype(jnp.int32)
    attn_low, query_rot, log_totals = attention_forward(
        layout, second_pre, window, cos_wide, sin_wide, heads_wide // HD
    )
    mixed_low = jnp.concatenate([ssm_low, attn_low], axis=1)
    mixed_sum = pair_sum(plain_product(mixed_low, out_weights))
    hidden = inputs + mixed_sum
    normed_two, norm_two_back = jax.vjp(rms_scale, hidden, gain_two.astype(jnp.float32))
    normed_two_low = normed_two.astype(jnp.bfloat16)
    ffn_gate = plain_product(normed_two_low, ffn_gate_weight)
    ffn_up = plain_product(normed_two_low, ffn_up_weight)
    ffn_act = (jax.nn.silu(ffn_gate) * ffn_up).astype(jnp.bfloat16)
    ffn_part = plain_product(ffn_act, ffn_down_weight)
    ffn_sum = pair_sum(ffn_part)
    layer_out = ((hidden + ffn_sum) * valid_rows[:, None]).astype(jnp.bfloat16)
    cot_low = (cotangent.astype(jnp.float32) * valid_rows[:, None]).astype(jnp.bfloat16)
    grad_out = cot_low.astype(jnp.float32)
    def in_quarters(value):
        return jnp.split(value, 4, axis=1)

    def rows_grad(left_side, right_side, first):
        return reduced([product_of_cols(part, right_side) for part in in_quarters(left_side)], 0, first)

    def cols_grad(left_side, right_side, first):
        return reduced([product_of_cols(left_side, part) for part in in_quarters(right_side)], 1, first)

    ffn_down_grad = cols_grad(ffn_act, cot_low, 1)
    act_grad = product_by_rows(cot_low, ffn_down_weight)
    gate_sigmoid = jax.nn.sigmoid(ffn_gate)
    ffn_gate_low = (
        act_grad * ffn_up * gate_sigmoid * (1.0 + ffn_gate * (1.0 - gate_sigmoid))
    ).astype(jnp.bfloat16)
    ffn_up_low = (act_grad * jax.nn.silu(ffn_gate)).astype(jnp.bfloat16)
    ffn_gate_grad = rows_grad(normed_two_low, ffn_gate_low, 2)
    ffn_up_grad = rows_grad(normed_two_low, ffn_up_low, 1)
    norm_two_part = product_by_rows(ffn_gate_low, ffn_gate_weight) + product_by_rows(
        ffn_up_low, ffn_up_weight
    )
    norm_two_grad = pair_sum(norm_two_part)
    hidden_norm_grad, gain_two_grad = norm_two_back(norm_two_grad)
    hidden_grad = grad_out + hidden_norm_grad
    hidden_low = hidden_grad.astype(jnp.bfloat16)
    out_grad = cols_grad(mixed_low, hidden_low, 2)
    mixed_grad = product_by_rows(hidden_low, out_weights)
    query_grad_low, window_grad, own_pair_grad = attention_back(
        layout, query_rot, window, attn_low, log_totals, mixed_grad, inner, cos_wide, sin_wide
    )
    for distance in range(1, MAXB):
        at = (MAXB - 1 - distance) * block_rows
        own_pair_grad = own_pair_grad + shifted(
            window_grad[at : at + block_rows], "ctx", -distance
        ).astype(jnp.float32)
    key_grad_low = (
        rotate(own_pair_grad[:, :HD].reshape(block_rows, 1, HD), cos_table, -sin_table)
        .reshape(block_rows, HD)
        .astype(jnp.bfloat16)
    )
    value_grad_low = own_pair_grad[:, HD:].astype(jnp.bfloat16)
    ssm_gate_low, state_in_grad = scan_gated_back(
        mixed_grad, scan_out, bc_low, sum_cols, second_pre, gate_at
    )
    end_grad = carried_states(keep_low * state_in_grad, decay_row, True)
    in_grad, rim_grad, tap_grad, step_part, sum_part, bc_grad, bc_rim_grad, bc_tap_grad = scan_back(
        first_pre, rims, taps, bc_taps, step_cols, sum_cols, sum_rows,
        mixed_grad, second_pre, gate_at, state_in, end_grad, bc_low,
    )
    edge_grad = jnp.concatenate([rim_grad, bc_rim_grad], axis=1)[8 - rim_rows :]
    edge_back = shifted(keep_state * edge_grad, "ctx", -1)
    edge_back = jnp.pad(edge_back, ((block_rows - rim_rows, 0), (0, 0)))
    input_grad_low = (in_grad + edge_back[:, :inner]).astype(jnp.bfloat16)
    bc_pre_part = bc_grad + edge_back[:, inner:]
    rate_grad = lax.dot_general(
        lower, from_pairs(sum_part), (((0,), (0,)), ((), ())), precision=highest
    )
    step_grad = (from_pairs(step_part) + rate * rate_grad) * jax.nn.sigmoid(step_in)
    step_grad_low = step_grad.astype(jnp.bfloat16)
    tap_sums = [
        tap_grad[:KW].T,
        tap_grad[KW],
        jnp.sum(step_grad, axis=0),
        jnp.sum(rate_grad * rate * step_size, axis=0),
        jnp.sum(tap_grad[KW + 1].reshape(steps, head_dim), axis=1),
    ]
    no_misc = jnp.zeros((block_rows, 128 - steps), jnp.bfloat16)
    first_grads = jnp.concatenate(
        [input_grad_low, bc_pre_part.astype(jnp.bfloat16), step_grad_low, no_misc], axis=1
    )
    second_grads = jnp.concatenate(
        [query_grad_low, key_grad_low, value_grad_low, ssm_gate_low], axis=1
    )
    norm_one_grad = pair_sum(
        product_by_rows(first_grads, first_weights) + product_by_rows(second_grads, second_weights)
    )
    bc_grad_low = pair_sum(bc_pre_part).astype(jnp.bfloat16)
    conv_bc_grads = jnp.concatenate([bc_tap_grad[:KW].T.reshape(-1), bc_tap_grad[KW]])
    conv_bc_grads = conv_bc_grads + swap(conv_bc_grads)
    inputs_norm_grad, gain_one_grad = norm_one_back(norm_one_grad)
    tokens_grad = (hidden_grad + inputs_norm_grad).astype(jnp.bfloat16)
    first_grads = jnp.concatenate([input_grad_low, bc_grad_low, step_grad_low, no_misc], axis=1)
    first_grad = rows_grad(normed_low, first_grads, 1)
    second_grad = rows_grad(normed_low, second_grads, 2)
    small = [
        tap_sums[0].reshape(-1),
        *tap_sums[1:],
        conv_bc_grads,
        whole_order(gain_one_grad).reshape(-1),
        whole_order(gain_two_grad).reshape(-1),
    ]
    packed = jnp.concatenate(small)
    filled = -packed.shape[0] % 1024
    packed = summed(jnp.pad(packed, (0, filled)).reshape(-1, 128)).reshape(-1)
    sums, at = ([], 0)
    for part in small:
        sums.append(packed[at : at + part.shape[0]])
        at += part.shape[0]

    def own(vector, count):
        return lax.dynamic_slice_in_dim(vector, block_index * count, count, 0)

    conv_bc_sums = sums[5]
    conv_rows = conv_bc_weight.shape[0]
    return (
        reordered(layer_out, to_whole),
        reordered(tokens_grad, to_whole),
        own(sums[6], rows_here),
        second_grad[:, heads_wide + 2 * pair_wide :],
        first_grad[:, :inner],
        first_grad[:, inner : inner + shared],
        first_grad[:, inner + shared : inner + shared + steps],
        sums[0].reshape(inner, KW),
        sums[1],
        own(conv_bc_sums[: shared * KW], conv_rows * KW).reshape(conv_rows, KW),
        own(conv_bc_sums[shared * KW :], conv_rows),
        sums[2],
        sums[3],
        sums[4],
        out_grad[:inner],
        second_grad[:, :heads_wide],
        second_grad[:, heads_wide : heads_wide + pair_wide],
        second_grad[:, heads_wide + pair_wide : heads_wide + 2 * pair_wide],
        out_grad[inner:],
        own(sums[7], rows_here),
        ffn_gate_grad,
        ffn_up_grad,
        ffn_down_grad,
    )


def solution(mesh):
    return jax.shard_map(
        per_device,
        mesh=mesh,
        in_specs=(
            P("ctx", None),
            P("ctx", None),
            P("ctx"),
            P("ctx", "wt"),
            P("ctx", "wt"),
            P("ctx", None),
            P("ctx", "wt"),
            P("wt", None),
            P("wt"),
            P("ctx", None),
            P("ctx"),
            P("wt"),
            P("wt"),
            P("wt"),
            P("wt", "ctx"),
            P("ctx", "wt"),
            P("ctx", "wt"),
            P("ctx", "wt"),
            P("wt", "ctx"),
            P("ctx"),
            P("ctx", "wt"),
            P("ctx", "wt"),
            P("wt", "ctx"),
            P(),
            P(),
            P(),
        ),
        out_specs=(
            P("ctx", None),
            P("ctx", None),
            P("ctx"),
            P("ctx", "wt"),
            P("ctx", "wt"),
            P("ctx", None),
            P("ctx", "wt"),
            P("wt", None),
            P("wt"),
            P("ctx", None),
            P("ctx"),
            P("wt"),
            P("wt"),
            P("wt"),
            P("wt", "ctx"),
            P("ctx", "wt"),
            P("ctx", "wt"),
            P("ctx", "wt"),
            P("wt", "ctx"),
            P("ctx"),
            P("ctx", "wt"),
            P("ctx", "wt"),
            P("wt", "ctx"),
        ),
        check_vma=False,
    )
```

```python
import jax
import jax.numpy as jnp
from jax import lax
from jax.experimental import pallas as pl
from jax.experimental.pallas import tpu as pltpu
from jax.sharding import PartitionSpec as P

HD = 128
KW = 4
MAXB = 8
SCAN_ROWS = 128
ATTN_ROWS = 256


epsilon = 1e-05
rope_base = 100000000000.0
highest = lax.Precision.HIGHEST
masked_score = -1e30


def shifted(value, axis, steps):
    count = lax.axis_size(axis)
    leading, last = (max(0, -steps), min(count, count - steps))
    return lax.ppermute(value, axis, [(source, source + steps) for source in range(leading, last)])


def hop(value, code):
    if code == 0:
        return value
    count = lax.axis_size("ctx")
    return lax.ppermute(value, "ctx", [(source, source ^ code) for source in range(count)])


def swap(value):
    return lax.ppermute(value, "wt", [(0, 1), (1, 0)])


def pair_sum(value):
    rounded = lax.reduce_precision(value, 8, 7)
    return rounded + swap(rounded.astype(jnp.bfloat16)).astype(jnp.float32)


def slot_devices(count):
    high = count // 4
    return [4 * (slot % high) + slot // high for slot in range(count)]


def after(value, *gates):
    return lax.optimization_barrier((value, *gates))[0]


def spread(held, axis, codes, gates=(), merge=False):
    if merge:
        every = [code for here, _ in held for code in here]
        held = [(every, jnp.concatenate([array for _, array in held], axis=axis))]
    taken = list(held)
    for here, array in held:
        operand = after(array, *gates) if gates else array
        for code in codes:
            taken.append(([one ^ code for one in here], hop(operand, code)))
    return taken


def joined(held, axis):
    size = sum(array.shape[axis] for _, array in held) // sum(len(here) for here, _ in held)
    found = {code: (i, at) for i, (here, _) in enumerate(held) for at, code in enumerate(here)}
    runs = []
    for code in slot_devices(len(found)):
        i, at = found[code]
        if runs and runs[-1][0] == i and runs[-1][2] == at:
            runs[-1][2] = at + 1
        else:
            runs.append([i, at, at + 1])
    return jnp.concatenate(
        [lax.slice_in_dim(held[i][1], at * size, to * size, axis=axis) for i, at, to in runs],
        axis=axis,
    )


class Reduction:
    def __init__(self, parts, axis, first, gates=()):
        self.axis, self.second = (axis, 3 - first)
        self.near, self.far = (parts[0], parts[3 - first])
        low = [parts[k].astype(jnp.bfloat16) for k in (first, 3)]
        if gates:
            low = lax.optimization_barrier((*low, *gates))[:2]
        self.got = [hop(part, first) for part in low]

    def onward(self, *gates):
        far = self.far + self.got[1].astype(jnp.float32)
        self.far_low = far.astype(jnp.bfloat16)
        operand = after(self.far_low, *gates) if gates else self.far_low
        self.near = self.near + self.got[0].astype(jnp.float32)
        self.got = [hop(operand, self.second)]

    def last(self, *gates):
        high = lax.axis_size("ctx") // 4
        quarter = self.near + self.got[0].astype(jnp.float32)
        blocks = jnp.split(quarter, high, axis=self.axis)
        self.block = blocks[0]
        self.blocks_low = [block.astype(jnp.bfloat16) for block in blocks[1:]]
        operands = self.blocks_low
        if gates:
            operands = lax.optimization_barrier((*operands, *gates))[: len(operands)]
        self.got = [hop(block, 4 * (k + 1)) for k, block in enumerate(operands)]

    def total(self):
        total = self.block
        for got in self.got:
            total = total + got.astype(jnp.float32)
        return total


def summed(value):
    bit = 1
    while bit < lax.axis_size("ctx"):
        value = value + hop(value, bit)
        bit *= 2
    return value


def reordered(value, order):
    blocks = order.shape[0]
    rows, width = value.shape[0], value.shape[1] // blocks
    if width % 128:
        return jnp.take(value.reshape(rows, blocks, width), order, axis=1).reshape(rows, -1)

    def body(order_ref, in_ref, out_ref):
        out_ref[...] = in_ref[...]

    return pl.pallas_call(
        body,
        out_shape=jax.ShapeDtypeStruct(value.shape, value.dtype),
        grid_spec=pltpu.PrefetchScalarGridSpec(
            num_scalar_prefetch=1,
            grid=(blocks,),
            in_specs=[pl.BlockSpec((rows, width), lambda s, order_ref: (0, order_ref[s]))],
            out_specs=pl.BlockSpec((rows, width), lambda s, order_ref: (0, s)),
        ),
        name="reordered",
    )(order, value)


def carried_states(states, decays, reverse):
    me = lax.axis_index("ctx")
    place = me % 4
    width = states.shape[1] // 4
    low = states.astype(jnp.bfloat16)

    def quarter(value, index):
        return lax.dynamic_slice_in_dim(value, index * width, width, 1)

    got = [hop(quarter(low, place ^ k), k) for k in range(4)]
    got_decay = [hop(quarter(decays, place ^ k), k) for k in range(4)]

    def in_order(pieces):
        odd = place % 2 == 1
        pieces = [jnp.where(odd, pieces[k ^ 1], pieces[k]) for k in range(4)]
        upper = place >= 2
        return [jnp.where(upper, pieces[k ^ 2], pieces[k]) for k in range(4)]

    blocks = [piece.astype(jnp.float32) for piece in in_order(got)]
    rates = in_order(got_decay)
    if reverse:
        blocks, rates = (blocks[::-1], rates[::-1])
    total, rate = (blocks[0], rates[0])
    for block, block_rate in zip(blocks[1:], rates[1:]):
        total, rate = (block + block_rate * total, block_rate * rate)
    step = -4 if reverse else 4
    total_low = total.astype(jnp.bfloat16)
    near, near_rate = (shifted(total_low, "ctx", step), shifted(rate, "ctx", step))
    far = shifted(total_low, "ctx", 2 * step)
    state = near.astype(jnp.float32) + near_rate * far.astype(jnp.float32)
    reached = []
    for block, block_rate in zip(blocks, rates):
        reached.append(state.astype(jnp.bfloat16))
        state = block + block_rate * state
    if reverse:
        reached = reached[::-1]
    mine = in_order(reached)
    back = in_order([hop(mine[k], k) for k in range(4)])
    return jnp.concatenate(back, axis=1)


def plain_product(left_side, right_side):
    return jnp.dot(left_side, right_side, preferred_element_type=jnp.float32)


def product_by_rows(left_side, right_side):
    return lax.dot_general(
        left_side, right_side, (((1,), (1,)), ((), ())), preferred_element_type=jnp.float32
    )


def product_of_cols(left_side, right_side):
    return lax.dot_general(
        left_side, right_side, (((0,), (0,)), ((), ())), preferred_element_type=jnp.float32
    )


def rms_scale(values, gain_vec):
    return (
        values * lax.rsqrt(jnp.mean(values * values, axis=-1, keepdims=True) + epsilon) * gain_vec
    )


def rotary_tables(positions):
    exponents = jnp.arange(HD // 2, dtype=jnp.float32) * (2.0 / HD)
    frequency = jnp.power(jnp.float32(rope_base), -exponents)
    angles = positions.astype(jnp.float32)[:, None] * frequency[None, :]
    return (jnp.cos(angles), jnp.sin(angles))


def rotate(values, cos_table, sin_table):
    half_dim = values.shape[-1] // 2
    first_half = values[..., :half_dim]
    second_half = values[..., half_dim:]
    cos_table = cos_table[:, None, :]
    sin_table = sin_table[:, None, :]
    return jnp.concatenate(
        [
            first_half * cos_table - second_half * sin_table,
            second_half * cos_table + first_half * sin_table,
        ],
        axis=-1,
    )


def convolved(rim, block, taps):
    length = block.shape[0]
    extended = jnp.concatenate([rim, block], axis=0)
    first = rim.shape[0] - (KW - 1)
    summed = taps[KW : KW + 1]
    for j in range(KW):
        summed = summed + extended[first + j : first + j + length] * taps[j : j + 1]
    return (extended, summed)


def convolved_back(extended, pre_grad, taps):
    length = pre_grad.shape[0]
    rim_rows = extended.shape[0] - length
    first = rim_rows - (KW - 1)
    zeros = jnp.zeros((8, pre_grad.shape[1]), jnp.float32)
    padded = jnp.concatenate([zeros, pre_grad, zeros], axis=0)
    total = jnp.zeros_like(extended)
    rows = []
    for j in range(KW):
        start = 8 - rim_rows + KW - 1 - j
        total = total + padded[start : start + rim_rows + length] * taps[j : j + 1]
        rows.append(
            jnp.sum(pre_grad * extended[first + j : first + j + length], axis=0, keepdims=True)
        )
    rows.append(jnp.sum(pre_grad, axis=0, keepdims=True))
    return (total, rows)


def silu_slope(value, sigmoid):
    return sigmoid * (1.0 + value * (1.0 - sigmoid))


def low_dot(left_side, right_side, left_axis, right_axis):
    return lax.dot_general(
        left_side.astype(jnp.bfloat16),
        right_side.astype(jnp.bfloat16),
        (((left_axis,), (right_axis,)), ((), ())),
        preferred_element_type=jnp.float32,
    )


def lower_gram(c_low, b_low):
    length = c_low.shape[0]
    gram = low_dot(c_low, b_low, 1, 1)
    rows = lax.broadcasted_iota(jnp.int32, (length, length), 0)
    cols = lax.broadcasted_iota(jnp.int32, (length, length), 1)
    return jnp.where(rows >= cols, gram, 0.0)


def scan_blocks(inner, shared, length, wide):
    return [
        pl.BlockSpec((length, wide), lambda i: (0, i)),
        pl.BlockSpec((8, wide), lambda i: (0, i)),
        pl.BlockSpec((8, wide), lambda i: (0, i)),
        pl.BlockSpec((length, shared), lambda i: (0, 0)),
        pl.BlockSpec((8, shared), lambda i: (0, inner // shared)),
        pl.BlockSpec((8, shared), lambda i: (0, 0)),
        pl.BlockSpec((1, length, 2), lambda i: (i, 0, 0)),
        pl.BlockSpec((1, length, 2), lambda i: (i, 0, 0)),
        pl.BlockSpec((1, 2, length), lambda i: (i, 0, 0)),
    ]


def scan_forward(first_pre, mix_pre, rims, taps, bc_taps, step_cols, sum_cols, sum_rows, inner, shared):
    length = first_pre.shape[0]
    pairs = step_cols.shape[0]
    wide = inner // pairs
    size = wide // 2
    state_dim = shared // 2
    part = min(SCAN_ROWS, length)

    def body(
        in_ref, rim_ref, tap_ref, bc_ref, bc_rim_ref, bc_tap_ref, step_ref, col_ref, row_ref,
        out_ref, state_ref, bc_low_ref, gram_ref,
    ):
        @pl.when(pl.program_id(0) == 0)
        def _():
            _, pre = convolved(bc_rim_ref[...], bc_ref[...], bc_tap_ref[...])
            acts = (pre * jax.nn.sigmoid(pre)).astype(jnp.bfloat16)
            bc_low_ref[...] = acts
            gram_ref[...] = lower_gram(acts[:, state_dim:], acts[:, :state_dim])

        taps_here = tap_ref[...]
        _, pre = convolved(rim_ref[...], in_ref[...], taps_here)
        acts = pre * jax.nn.sigmoid(pre)
        outs, tails = ([], [])
        for head in range(2):
            lanes = slice(head * size, (head + 1) * size)
            step = step_ref[0][:, head : head + 1]
            col = col_ref[0][:, head : head + 1]
            row = row_ref[0][head : head + 1, :]
            stepped = acts[:, lanes] * step
            stepped_low = stepped.astype(jnp.bfloat16)
            for at in range(0, length, part):
                end = at + part
                decay = jnp.exp(jnp.minimum(col[at:end] - row[:, :end], 0.0))
                weights = (decay * gram_ref[at:end, :end]).astype(jnp.bfloat16)
                out_ref[at:end, lanes] = low_dot(weights, stepped_low[:end], 1, 0) + (
                    taps_here[KW + 1 : KW + 2, lanes] * acts[at:end, lanes]
                )
            tails.append(stepped * jnp.exp(col[length - 1 : length] - col))
        tail = jnp.concatenate(tails, axis=1)
        state_ref[...] = low_dot(bc_low_ref[:, :state_dim], tail, 0, 0).astype(jnp.bfloat16)

    return pl.pallas_call(
        body,
        grid=(pairs,),
        out_shape=(
            jax.ShapeDtypeStruct((length, inner), jnp.float32),
            jax.ShapeDtypeStruct((state_dim, inner), jnp.bfloat16),
            jax.ShapeDtypeStruct((length, shared), jnp.bfloat16),
        ),
        in_specs=scan_blocks(inner, shared, length, wide),
        out_specs=(
            pl.BlockSpec((length, wide), lambda i: (0, i)),
            pl.BlockSpec((state_dim, wide), lambda i: (0, i)),
            pl.BlockSpec((length, shared), lambda i: (0, 0)),
        ),
        scratch_shapes=[pltpu.VMEM((length, length), jnp.float32)],
        compiler_params=pltpu.CompilerParams(vmem_limit_bytes=48 << 20),
        name="scan_forward",
    )(first_pre, rims, taps, mix_pre, rims, bc_taps, step_cols, sum_cols, sum_rows)


def scan_gated(intra, state_in, bc_low, sum_cols, second_pre, gate_at):
    length, inner = intra.shape
    pairs = sum_cols.shape[0]
    wide = inner // pairs
    size = wide // 2
    state_dim = bc_low.shape[1] // 2

    def body(intra_ref, state_ref, c_ref, col_ref, gate_ref, out_ref, act_ref):
        carried = low_dot(c_ref[...], state_ref[...], 1, 0)
        gate = gate_ref[...]
        silu = gate * jax.nn.sigmoid(gate)
        for head in range(2):
            lanes = slice(head * size, (head + 1) * size)
            growth = jnp.exp(col_ref[0][:, head : head + 1])
            whole = intra_ref[:, lanes] + carried[:, lanes] * growth
            out_ref[:, lanes] = whole
            act_ref[:, lanes] = (whole * silu[:, lanes]).astype(jnp.bfloat16)

    block = pl.BlockSpec((length, wide), lambda i: (0, i))
    return pl.pallas_call(
        body,
        grid=(pairs,),
        out_shape=(
            jax.ShapeDtypeStruct((length, inner), jnp.float32),
            jax.ShapeDtypeStruct((length, inner), jnp.bfloat16),
        ),
        in_specs=[
            block,
            pl.BlockSpec((state_dim, wide), lambda i: (0, i)),
            pl.BlockSpec((length, state_dim), lambda i: (0, 1)),
            pl.BlockSpec((1, length, 2), lambda i: (i, 0, 0)),
            pl.BlockSpec((length, wide), lambda i: (0, gate_at // wide + i)),
        ],
        out_specs=(block, block),
        compiler_params=pltpu.CompilerParams(vmem_limit_bytes=48 << 20),
        name="scan_gated",
    )(intra, state_in, bc_low, sum_cols, second_pre)


def scan_gated_back(out_grads, whole, bc_low, sum_cols, second_pre, gate_at):
    length, inner = whole.shape
    pairs = sum_cols.shape[0]
    wide = inner // pairs
    size = wide // 2
    state_dim = bc_low.shape[1] // 2

    def body(grad_ref, whole_ref, c_ref, col_ref, gate_ref, gate_grad_ref, state_ref):
        gate = gate_ref[...]
        sigmoid = jax.nn.sigmoid(gate)
        grad = grad_ref[...]
        gate_grad_ref[...] = (grad * whole_ref[...] * silu_slope(gate, sigmoid)).astype(jnp.bfloat16)
        inside = grad * (gate * sigmoid)
        grown = [
            inside[:, head * size : (head + 1) * size] * jnp.exp(col_ref[0][:, head : head + 1])
            for head in range(2)
        ]
        state_ref[...] = low_dot(c_ref[...], jnp.concatenate(grown, axis=1), 0, 0).astype(
            jnp.bfloat16
        )

    block = pl.BlockSpec((length, wide), lambda i: (0, i))
    return pl.pallas_call(
        body,
        grid=(pairs,),
        out_shape=(
            jax.ShapeDtypeStruct((length, inner), jnp.bfloat16),
            jax.ShapeDtypeStruct((state_dim, inner), jnp.bfloat16),
        ),
        in_specs=[
            block,
            block,
            pl.BlockSpec((length, state_dim), lambda i: (0, 1)),
            pl.BlockSpec((1, length, 2), lambda i: (i, 0, 0)),
            pl.BlockSpec((length, wide), lambda i: (0, gate_at // wide + i)),
        ],
        out_specs=(block, pl.BlockSpec((state_dim, wide), lambda i: (0, i))),
        compiler_params=pltpu.CompilerParams(vmem_limit_bytes=48 << 20),
        name="scan_gated_back",
    )(out_grads, whole, bc_low, sum_cols, second_pre)


def scan_back(
    first_pre, mix_pre, rims, taps, bc_taps, step_cols, sum_cols, sum_rows,
    out_grads, second_pre, gate_at, state_in, end_grad, bc_low,
):
    length = first_pre.shape[0]
    pairs = step_cols.shape[0]
    state_dim, inner = state_in.shape
    shared = bc_low.shape[1]
    wide = inner // pairs
    size = wide // 2
    part = min(SCAN_ROWS, length)

    def body(
        in_ref, rim_ref, tap_ref, bc_ref, bc_rim_ref, bc_tap_ref, step_ref, col_ref, row_ref,
        grad_ref, gate_ref, state_ref, end_ref, bc_low_ref,
        in_grad_ref, rim_grad_ref, tap_grad_ref, step_grad_ref, sum_grad_ref,
        bc_grad_ref, bc_rim_grad_ref, bc_tap_grad_ref,
        gram_ref, gram_grad_ref, acts_grad_ref, back_ref,
    ):
        b_low = bc_low_ref[:, :state_dim]
        c_low = bc_low_ref[:, state_dim:]

        @pl.when(pl.program_id(0) == 0)
        def _():
            gram_ref[...] = lower_gram(c_low, b_low)
            gram_grad_ref[...] = jnp.zeros_like(gram_grad_ref)
            acts_grad_ref[...] = jnp.zeros_like(acts_grad_ref)

        taps_here = tap_ref[...]
        extended, pre = convolved(rim_ref[...], in_ref[...], taps_here)
        sigmoid = jax.nn.sigmoid(pre)
        acts = pre * sigmoid
        gate = gate_ref[...]
        out_grad = grad_ref[...] * (gate * jax.nn.sigmoid(gate))
        state = state_ref[...]
        end = end_ref[...]
        from_end = low_dot(b_low, end, 1, 0)
        from_start = low_dot(c_low, state, 1, 0)
        state_dot = jnp.sum(
            state.astype(jnp.float32) * end.astype(jnp.float32), axis=0, keepdims=True
        )
        last_row = lax.broadcasted_iota(jnp.int32, (length, 1), 0) == length - 1
        acts_grads, tails, grown_grads = ([], [], [])
        for head in range(2):
            lanes = slice(head * size, (head + 1) * size)
            step = step_ref[0][:, head : head + 1]
            col = col_ref[0][:, head : head + 1]
            row = row_ref[0][head : head + 1, :]
            here = acts[:, lanes]
            stepped = here * step
            stepped_low = stepped.astype(jnp.bfloat16)
            grad = out_grad[:, lanes]
            grad_low = grad.astype(jnp.bfloat16)
            grad_wide = grad_low.astype(jnp.float32)
            back_ref[...] = jnp.zeros_like(back_ref)
            row_terms = []
            for at in range(0, length, part):
                to = at + part
                decay = jnp.exp(jnp.minimum(col[at:to] - row[:, :to], 0.0))
                weights = (decay * gram_ref[at:to, :to]).astype(jnp.bfloat16)
                again = low_dot(weights, stepped_low[:to], 1, 0)
                row_terms.append(jnp.sum(again * grad_wide[at:to], axis=1, keepdims=True))
                back_ref[:to] += low_dot(weights, grad_low[at:to], 0, 0)
                gram_grad_ref[at:to, :to] += decay * low_dot(
                    grad_low[at:to], stepped_low[:to], 1, 1
                )
            back = back_ref[...]
            tail = jnp.exp(col[length - 1 : length] - col)
            growth = jnp.exp(col)
            ended = from_end[:, lanes] * tail
            end_terms = jnp.sum(ended * stepped, axis=1, keepdims=True)
            col_terms = jnp.sum(back * stepped_low.astype(jnp.float32), axis=1, keepdims=True)
            start_terms = growth * jnp.sum(from_start[:, lanes] * grad, axis=1, keepdims=True)
            whole = jnp.sum(end_terms, axis=0, keepdims=True) + growth[
                length - 1 : length
            ] * jnp.sum(state_dot[:, lanes], axis=1, keepdims=True)
            sum_grad_ref[0, :, head : head + 1] = (
                jnp.concatenate(row_terms, axis=0)
                + start_terms
                - col_terms
                - end_terms
                + jnp.where(last_row, whole, 0.0)
            )
            back = back + ended
            step_grad_ref[0, :, head : head + 1] = jnp.sum(back * here, axis=1, keepdims=True)
            acts_grads.append(taps_here[KW + 1 : KW + 2, lanes] * grad + back * step)
            tails.append((stepped * tail).astype(jnp.bfloat16))
            grown_grads.append((grad * growth).astype(jnp.bfloat16))
        acts_grad_ref[:, :state_dim] += low_dot(jnp.concatenate(tails, axis=1), end, 1, 1)
        acts_grad_ref[:, state_dim:] += low_dot(jnp.concatenate(grown_grads, axis=1), state, 1, 1)
        pre_grad = jnp.concatenate(acts_grads, axis=1) * silu_slope(pre, sigmoid)
        total, rows = convolved_back(extended, pre_grad, taps_here)
        rim_grad_ref[...] = total[:8]
        in_grad_ref[...] = total[8:]
        rows.append(jnp.sum(out_grad * acts, axis=0, keepdims=True))
        rows.append(jnp.zeros((8 - len(rows), wide), jnp.float32))
        tap_grad_ref[...] = jnp.concatenate(rows, axis=0)

        @pl.when(pl.program_id(0) == pairs - 1)
        def _():
            gram_grad = gram_grad_ref[...]
            rows_of = lax.broadcasted_iota(jnp.int32, (length, length), 0)
            cols_of = lax.broadcasted_iota(jnp.int32, (length, length), 1)
            gram_grad = jnp.where(rows_of >= cols_of, gram_grad, 0.0).astype(jnp.bfloat16)
            acts_grad_ref[:, :state_dim] += low_dot(gram_grad, c_low, 0, 0)
            acts_grad_ref[:, state_dim:] += low_dot(gram_grad, b_low, 1, 0)
            bc_taps_here = bc_tap_ref[...]
            bc_extended, bc_pre = convolved(bc_rim_ref[...], bc_ref[...], bc_taps_here)
            bc_pre_grad = acts_grad_ref[...] * silu_slope(bc_pre, jax.nn.sigmoid(bc_pre))
            bc_total, bc_rows = convolved_back(bc_extended, bc_pre_grad, bc_taps_here)
            bc_rim_grad_ref[...] = bc_total[:8]
            bc_grad_ref[...] = bc_total[8:]
            bc_rows.append(jnp.zeros((8 - len(bc_rows), shared), jnp.float32))
            bc_tap_grad_ref[...] = jnp.concatenate(bc_rows, axis=0)

    block = pl.BlockSpec((length, wide), lambda i: (0, i))
    eight = pl.BlockSpec((8, wide), lambda i: (0, i))
    table = pl.BlockSpec((1, length, 2), lambda i: (i, 0, 0))
    state_block = pl.BlockSpec((state_dim, wide), lambda i: (0, i))
    bc_block = pl.BlockSpec((length, shared), lambda i: (0, 0))
    bc_eight = pl.BlockSpec((8, shared), lambda i: (0, 0))
    wide_f32 = jax.ShapeDtypeStruct((length, inner), jnp.float32)
    eight_f32 = jax.ShapeDtypeStruct((8, inner), jnp.float32)
    table_f32 = jax.ShapeDtypeStruct(step_cols.shape, jnp.float32)
    bc_f32 = jax.ShapeDtypeStruct((length, shared), jnp.float32)
    bc_eight_f32 = jax.ShapeDtypeStruct((8, shared), jnp.float32)
    return pl.pallas_call(
        body,
        grid=(pairs,),
        out_shape=(
            wide_f32, eight_f32, eight_f32, table_f32, table_f32, bc_f32, bc_eight_f32, bc_eight_f32
        ),
        in_specs=scan_blocks(inner, shared, length, wide)
        + [
            block,
            pl.BlockSpec((length, wide), lambda i: (0, gate_at // wide + i)),
            state_block,
            state_block,
            bc_block,
        ],
        out_specs=(block, eight, eight, table, table, bc_block, bc_eight, bc_eight),
        scratch_shapes=[
            pltpu.VMEM((length, length), jnp.float32),
            pltpu.VMEM((length, length), jnp.float32),
            pltpu.VMEM((length, shared), jnp.float32),
            pltpu.VMEM((length, size), jnp.float32),
        ],
        compiler_params=pltpu.CompilerParams(vmem_limit_bytes=56 << 20),
        name="scan_back",
    )(
        first_pre, rims, taps, mix_pre, rims, bc_taps, step_cols, sum_cols, sum_rows,
        out_grads, second_pre, state_in, end_grad, bc_low,
    )


def turned(values, cos_wide, sin_wide):
    return values * cos_wide + pltpu.roll(values, values.shape[1] // 2, 1) * sin_wide


def own_mask(at, rows, keys, limit):
    query_row = lax.broadcasted_iota(jnp.int32, (rows, keys), 0) + at
    key_row = lax.broadcasted_iota(jnp.int32, (rows, keys), 1)
    return (key_row <= query_row) & (key_row < limit)


def attention_forward(layout, second_pre, query_at, window, cos_wide, sin_wide, heads):
    length = second_pre.shape[0]
    part = min(ATTN_ROWS, length)
    own_at = window.shape[0] - length
    scale = HD ** (-0.5)

    def body(layout_ref, query_ref, window_ref, cos_ref, sin_ref, out_ref, turned_ref, total_ref):
        query = turned(query_ref[...], cos_ref[...], sin_ref[...]).astype(jnp.bfloat16)
        turned_ref[...] = query
        for at in range(0, length, part):
            to = at + part
            here = query[at:to]

            def scores_of(keys):
                return scale * low_dot(here, keys, 1, 1)

            keys = window_ref[own_at : own_at + to, :HD]
            values = window_ref[own_at : own_at + to, HD:]
            scores = jnp.where(
                own_mask(at, part, to, layout_ref[1]), scores_of(keys), masked_score
            )
            top = jnp.max(scores, axis=1, keepdims=True)
            shares = jnp.exp(scores - top)
            total = jnp.sum(shares, axis=1, keepdims=True)
            acc = low_dot(shares, values, 1, 0)

            def earlier(distance, carry):
                top, total, acc = carry
                start = pl.multiple_of(own_at - distance * length, length)
                scores = scores_of(window_ref[pl.ds(start, length), :HD])
                new_top = jnp.maximum(top, jnp.max(scores, axis=1, keepdims=True))
                fade = jnp.exp(top - new_top)
                shares = jnp.exp(scores - new_top)
                total = fade * total + jnp.sum(shares, axis=1, keepdims=True)
                acc = fade * acc + low_dot(shares, window_ref[pl.ds(start, length), HD:], 1, 0)
                return (new_top, total, acc)

            top, total, acc = lax.fori_loop(1, layout_ref[0] + 1, earlier, (top, total, acc))
            out_ref[at:to] = (acc / total).astype(jnp.bfloat16)
            total_ref[0, at:to] = top + jnp.log(total)

    head = pl.BlockSpec((length, HD), lambda i, layout_ref: (0, i))
    whole = pl.BlockSpec((length, HD), lambda i, layout_ref: (0, 0))
    return pl.pallas_call(
        body,
        out_shape=(
            jax.ShapeDtypeStruct((length, heads * HD), jnp.bfloat16),
            jax.ShapeDtypeStruct((length, heads * HD), jnp.bfloat16),
            jax.ShapeDtypeStruct((heads, length, 1), jnp.float32),
        ),
        grid_spec=pltpu.PrefetchScalarGridSpec(
            num_scalar_prefetch=1,
            grid=(heads,),
            in_specs=[
                pl.BlockSpec((length, HD), lambda i, layout_ref: (0, query_at // HD + i)),
                pl.BlockSpec(window.shape, lambda i, layout_ref: (0, 0)),
                whole,
                whole,
            ],
            out_specs=(
                head,
                head,
                pl.BlockSpec((1, length, 1), lambda i, layout_ref: (i, 0, 0)),
            ),
        ),
        compiler_params=pltpu.CompilerParams(vmem_limit_bytes=48 << 20),
        name="attention_forward",
    )(layout, second_pre, window, cos_wide, sin_wide)


def attention_back(layout, query, window, out, totals, mixed_grad, grad_at, cos_wide, sin_wide):
    length = query.shape[0]
    heads = query.shape[1] // HD
    part = min(ATTN_ROWS, length)
    own_at = window.shape[0] - length
    scale = HD ** (-0.5)

    def body(
        layout_ref, query_ref, window_ref, out_in_ref, total_ref, grad_ref, cos_ref, sin_ref,
        query_grad_ref, window_grad_ref, own_grad_ref, sum_ref, acc_ref,
    ):
        @pl.when(pl.program_id(0) == 0)
        def _():
            sum_ref[...] = jnp.zeros_like(sum_ref)

        for at in range(0, length, part):
            to = at + part
            here = query_ref[at:to]
            grad = grad_ref[at:to].astype(jnp.bfloat16)
            dots = jnp.sum(
                grad.astype(jnp.float32) * out_in_ref[at:to].astype(jnp.float32),
                axis=1,
                keepdims=True,
            )
            total = total_ref[0, at:to]

            def step(start, count, mask):
                keys = window_ref[pl.ds(start, count), :HD]
                values = window_ref[pl.ds(start, count), HD:]
                probs = jnp.exp(scale * low_dot(here, keys, 1, 1) - total)
                if mask is not None:
                    probs = jnp.where(mask, probs, 0.0)
                score_grad = (probs * (low_dot(grad, values, 1, 1) - dots)).astype(jnp.bfloat16)
                sum_ref[pl.ds(start, count), :HD] += low_dot(score_grad, here, 0, 0)
                sum_ref[pl.ds(start, count), HD:] += low_dot(probs, grad, 0, 0)
                return low_dot(score_grad, keys, 1, 0)

            acc_ref[...] = step(own_at, to, own_mask(at, part, to, layout_ref[1]))

            def earlier(distance, carry):
                start = pl.multiple_of(own_at - distance * length, length)
                acc_ref[...] += step(start, length, None)
                return carry

            lax.fori_loop(1, layout_ref[0] + 1, earlier, 0)
            query_grad_ref[at:to] = turned(
                acc_ref[...] * scale, cos_ref[at:to], -sin_ref[at:to]
            ).astype(jnp.bfloat16)

        @pl.when(pl.program_id(0) == heads - 1)
        def _():
            own_grad_ref[:, :HD] = sum_ref[own_at:, :HD] * scale
            own_grad_ref[:, HD:] = sum_ref[own_at:, HD:]
            window_grad_ref[:, :HD] = (sum_ref[:own_at, :HD] * scale).astype(jnp.bfloat16)
            window_grad_ref[:, HD:] = sum_ref[:own_at, HD:].astype(jnp.bfloat16)

    head = pl.BlockSpec((length, HD), lambda i, layout_ref: (0, i))
    whole = pl.BlockSpec((length, HD), lambda i, layout_ref: (0, 0))
    return pl.pallas_call(
        body,
        out_shape=(
            jax.ShapeDtypeStruct(query.shape, jnp.bfloat16),
            jax.ShapeDtypeStruct((own_at, 2 * HD), jnp.bfloat16),
            jax.ShapeDtypeStruct((length, 2 * HD), jnp.float32),
        ),
        grid_spec=pltpu.PrefetchScalarGridSpec(
            num_scalar_prefetch=1,
            grid=(heads,),
            in_specs=[
                head,
                pl.BlockSpec(window.shape, lambda i, layout_ref: (0, 0)),
                head,
                pl.BlockSpec((1, length, 1), lambda i, layout_ref: (i, 0, 0)),
                pl.BlockSpec((length, HD), lambda i, layout_ref: (0, grad_at // HD + i)),
                whole,
                whole,
            ],
            out_specs=(
                head,
                pl.BlockSpec((own_at, 2 * HD), lambda i, layout_ref: (0, 0)),
                pl.BlockSpec((length, 2 * HD), lambda i, layout_ref: (0, 0)),
            ),
            scratch_shapes=[
                pltpu.VMEM(window.shape, jnp.float32),
                pltpu.VMEM((part, HD), jnp.float32),
            ],
        ),
        compiler_params=pltpu.CompilerParams(vmem_limit_bytes=56 << 20),
        name="attention_back",
    )(layout, query, window, out, totals, mixed_grad, cos_wide, sin_wide)


def per_device(
    tokens,
    cotangent,
    mix_norm_gain,
    ssm_gate_proj,
    ssm_input_proj,
    ssm_bc_proj,
    ssm_step_proj,
    conv_in_weight,
    conv_in_bias,
    conv_bc_weight,
    conv_bc_bias,
    step_bias,
    decay_log,
    skip_gain,
    ssm_out_proj,
    query_proj,
    key_proj,
    value_proj,
    attn_out_proj,
    ffn_norm_gain,
    ffn_gate_proj,
    ffn_up_proj,
    ffn_down_proj,
    extra_blocks,
    seq_order,
    pad_rows,
):
    block_rows = tokens.shape[0]
    block_index = lax.axis_index("ctx")
    seq_count = seq_order.shape[0]
    slot_ids = jnp.arange(seq_count, dtype=jnp.int32)
    chosen = (seq_order[:, None] == slot_ids[None, :]).astype(jnp.int32)
    counts = jnp.sum(chosen * extra_blocks[None, :], axis=1) + 1
    slot_pads = jnp.sum(chosen * pad_rows[None, :], axis=1)
    slot_ends = jnp.cumsum(counts)
    starts = slot_ends - counts
    inside = (starts <= block_index) & (block_index < slot_ends)
    within = jnp.sum(jnp.where(inside, block_index - starts, 0))
    pad_here = jnp.sum(jnp.where(inside & (slot_ends - 1 == block_index), slot_pads, 0))
    row_ids = jnp.arange(block_rows, dtype=jnp.int32)
    valid_rows = (row_ids < block_rows - pad_here).astype(jnp.float32)
    positions = within * block_rows + row_ids
    keep_state = (within > 0).astype(jnp.float32)
    devices = lax.axis_size("ctx")
    codes = jnp.asarray(slot_devices(devices), jnp.int32)
    from_whole = jnp.bitwise_xor(codes, block_index)
    to_whole = jnp.argsort(from_whole).astype(jnp.int32)
    rows_here = mix_norm_gain.shape[0]
    misc_here = jnp.concatenate(
        [
            ssm_step_proj,
            mix_norm_gain[:, None],
            ffn_norm_gain[:, None],
            conv_bc_weight.reshape(rows_here, 1),
            jnp.pad(conv_bc_bias, (0, rows_here - conv_bc_bias.shape[0]))[:, None],
        ],
        axis=1,
    )
    steps = ssm_step_proj.shape[1]
    misc_here = jnp.pad(misc_here, ((0, 0), (0, 128 - misc_here.shape[1])))
    inner, shared = (ssm_input_proj.shape[1], ssm_bc_proj.shape[1])
    heads_wide, pair_wide = (query_proj.shape[1], key_proj.shape[1])
    across = [4 * k for k in range(1, devices // 4)]
    mix_here = jnp.concatenate([ssm_bc_proj, misc_here, query_proj, key_proj, value_proj], axis=1)
    out_here = jnp.concatenate([ssm_out_proj, attn_out_proj], axis=0)
    down_half = ffn_down_proj.shape[0] // 2
    input_held = spread([([0], ssm_input_proj)], 0, across)
    mix_held = spread([([0], mix_here)], 0, across)
    out_held = spread([([0], out_here)], 1, [1])
    swish_held = spread([([0], ffn_gate_proj)], 0, [2])
    gate_held = spread([([0], ssm_gate_proj)], 0, across, (input_held[-1][1],))
    out_held = spread(out_held, 1, across, (mix_held[-1][1],), merge=True)
    input_held = spread(input_held, 0, [1], merge=True)
    mix_held = spread(mix_held, 0, [2], merge=True)
    input_held = spread(input_held, 0, [2])
    mix_held = spread(mix_held, 0, [1])
    input_weight = joined(input_held, 0)
    mix_weights = joined(mix_held, 0)
    arrived = (input_held[-1][1], mix_held[-1][1])
    misc = mix_weights[:, shared : shared + 128]
    mix_gain, gain_two = (misc[:, steps], misc[:, steps + 1])

    def whole_order(column):
        return jnp.take(column.reshape(devices, rows_here), to_whole, axis=0)

    conv_bc_full = whole_order(misc[:, steps + 2]).reshape(shared, KW)
    conv_bc_offset = whole_order(misc[:, steps + 3])[:, : conv_bc_bias.shape[0]].reshape(shared)
    tokens = reordered(tokens, from_whole)
    cotangent = reordered(cotangent, from_whole)
    inputs = tokens.astype(jnp.float32)
    normed_one, norm_one_back = jax.vjp(rms_scale, inputs, mix_gain.astype(jnp.float32))
    normed_low = normed_one.astype(jnp.bfloat16)
    first_pre = plain_product(normed_low, input_weight)
    mix_pre = plain_product(normed_low, mix_weights)
    step_raw = mix_pre[:, shared : shared + steps]
    query_at = shared + 128
    key_at = query_at + heads_wide
    key_pre = mix_pre[:, key_at : key_at + pair_wide]
    value_pre = mix_pre[:, key_at + pair_wide :]
    gate_held = spread(gate_held, 0, [2], arrived, merge=True)
    rim_rows = KW - 1
    edge = jnp.concatenate(
        [first_pre[block_rows - rim_rows :], mix_pre[block_rows - rim_rows :, :shared]], axis=1
    )
    edge = shifted(edge, "ctx", 1) * keep_state
    rims = jnp.pad(edge, ((8 - rim_rows, 0), (0, 0)))
    head_dim = inner // steps
    skips = jnp.repeat(skip_gain.astype(jnp.float32), head_dim)[None, :]
    taps = jnp.concatenate(
        [conv_in_weight.astype(jnp.float32).T, conv_in_bias.astype(jnp.float32)[None, :], skips]
    )
    taps = jnp.pad(taps, ((0, 8 - taps.shape[0]), (0, 0)))
    bc_taps = jnp.concatenate(
        [conv_bc_full.astype(jnp.float32).T, conv_bc_offset.astype(jnp.float32)[None, :]]
    )
    bc_taps = jnp.pad(bc_taps, ((0, 8 - bc_taps.shape[0]), (0, 0)))
    step_in = step_raw + step_bias.astype(jnp.float32)[None, :]
    step_size = jax.nn.softplus(step_in)
    rate = -jnp.exp(decay_log.astype(jnp.float32))[None, :]
    lower = (row_ids[:, None] >= row_ids[None, :]).astype(jnp.float32)
    log_decay = jnp.dot(lower, rate * step_size, precision=highest)

    def by_pairs(table):
        return table.reshape(block_rows, steps // 2, 2).transpose(1, 0, 2)

    def from_pairs(table):
        return table.transpose(1, 0, 2).reshape(block_rows, steps)

    step_cols = by_pairs(step_size)
    sum_cols = by_pairs(log_decay)
    sum_rows = log_decay.T.reshape(steps // 2, 2, block_rows)
    intra_out, local_states, bc_low = scan_forward(
        first_pre, mix_pre, rims, taps, bc_taps, step_cols, sum_cols, sum_rows, inner, shared
    )
    decay_row = keep_state * jnp.repeat(jnp.exp(log_decay[block_rows - 1]), head_dim)[None, :]
    keep_low = keep_state.astype(jnp.bfloat16)
    state_in = keep_low * carried_states(local_states, decay_row, False)
    gate_held = spread(gate_held, 0, [1], (local_states,))
    out_held = spread(out_held, 1, [2], (local_states,))
    swish_held = spread(swish_held, 0, across, (local_states,), merge=True)
    cos_table, sin_table = rotary_tables(positions)
    cos_wide = jnp.concatenate([cos_table, cos_table], axis=1)
    sin_wide = jnp.concatenate([-sin_table, sin_table], axis=1)
    key_rot = rotate(key_pre.reshape(block_rows, -1, HD), cos_table, sin_table)
    own_pair = jnp.concatenate(
        [key_rot.reshape(block_rows, HD).astype(jnp.bfloat16), value_pre.astype(jnp.bfloat16)],
        axis=1,
    )
    earlier_pairs = [shifted(own_pair, "ctx", distance) for distance in range(MAXB - 1, 0, -1)]
    window = jnp.concatenate(earlier_pairs + [own_pair], axis=0)
    layout = jnp.stack([within, block_rows - pad_here]).astype(jnp.int32)
    attn_low, query_rot, log_totals = attention_forward(
        layout, mix_pre, query_at, window, cos_wide, sin_wide, heads_wide // HD
    )
    up_held = spread([([0], ffn_up_proj)], 0, across, (attn_low,))
    gate_pre = plain_product(normed_low, joined(gate_held, 0))
    scan_out, ssm_low = scan_gated(intra_out, state_in, bc_low, sum_cols, gate_pre, 0)
    swish_held = spread(swish_held, 0, [1], (ssm_low,))
    down_held = [
        spread([([0], ffn_down_proj[:down_half])], 1, across, (ssm_low,)),
        spread([([0], ffn_down_proj[down_half:])], 1, across, (ssm_low,)),
    ]
    out_weights = joined(out_held, 1)
    mixed_low = jnp.concatenate([ssm_low, attn_low], axis=1)
    mixed_part = plain_product(mixed_low, out_weights)
    up_held = spread(up_held, 0, [2], (mixed_part,), merge=True)
    hidden = inputs + pair_sum(mixed_part)
    up_held = spread(up_held, 0, [1])
    down_held[0] = spread(down_held[0], 1, [1], (hidden,), merge=True)
    down_held[1] = spread(down_held[1], 1, [2], (hidden,), merge=True)
    normed_two, norm_two_back = jax.vjp(rms_scale, hidden, gain_two.astype(jnp.float32))
    normed_two_low = normed_two.astype(jnp.bfloat16)
    ffn_gate_weight = joined(swish_held, 0)
    ffn_up_weight = joined(up_held, 0)
    ffn_gate = plain_product(normed_two_low, ffn_gate_weight)
    down_held[0] = spread(down_held[0], 1, [2], (ffn_gate,))
    down_held[1] = spread(down_held[1], 1, [1], (ffn_gate,))
    ffn_up = plain_product(normed_two_low, ffn_up_weight)
    ffn_act = (jax.nn.silu(ffn_gate) * ffn_up).astype(jnp.bfloat16)
    ffn_down_weight = jnp.concatenate([joined(held, 1) for held in down_held], axis=0)
    ffn_part = plain_product(ffn_act, ffn_down_weight)
    ffn_sum = pair_sum(ffn_part)
    layer_out = ((hidden + ffn_sum) * valid_rows[:, None]).astype(jnp.bfloat16)
    cot_low = (cotangent.astype(jnp.float32) * valid_rows[:, None]).astype(jnp.bfloat16)
    grad_out = cot_low.astype(jnp.float32)
    def in_quarters(value):
        return jnp.split(value, 4, axis=1)

    def rows_grad(left_side, right_side, first, gates=()):
        parts = [product_of_cols(part, right_side) for part in in_quarters(left_side)]
        return Reduction(parts, 0, first, gates)

    def cols_grad(left_side, right_side, first, gates=()):
        parts = [product_of_cols(left_side, part) for part in in_quarters(right_side)]
        return Reduction(parts, 1, first, gates)

    down_sum = cols_grad(ffn_act, cot_low, 2)
    act_grad = product_by_rows(cot_low, ffn_down_weight)
    gate_sigmoid = jax.nn.sigmoid(ffn_gate)
    ffn_gate_low = (
        act_grad * ffn_up * gate_sigmoid * (1.0 + ffn_gate * (1.0 - gate_sigmoid))
    ).astype(jnp.bfloat16)
    ffn_up_low = (act_grad * jax.nn.silu(ffn_gate)).astype(jnp.bfloat16)
    swish_sum = rows_grad(normed_two_low, ffn_gate_low, 1)
    norm_two_part = product_by_rows(ffn_gate_low, ffn_gate_weight) + product_by_rows(
        ffn_up_low, ffn_up_weight
    )
    norm_two_grad = pair_sum(norm_two_part)
    hidden_norm_grad, gain_two_grad = norm_two_back(norm_two_grad)
    hidden_grad = grad_out + hidden_norm_grad
    hidden_low = hidden_grad.astype(jnp.bfloat16)
    mixed_grad = product_by_rows(hidden_low, out_weights)
    down_sum.onward()
    swish_sum.onward()
    up_sum = rows_grad(normed_two_low, ffn_up_low, 2, (down_sum.far_low,))
    out_sum = cols_grad(mixed_low, hidden_low, 1, (swish_sum.far_low,))
    ssm_gate_low, state_in_grad = scan_gated_back(
        mixed_grad, scan_out, bc_low, sum_cols, gate_pre, 0
    )
    layout = after(layout, down_sum.far_low, swish_sum.far_low, ssm_gate_low)
    query_grad_low, window_grad, own_pair_grad = attention_back(
        layout, query_rot, window, attn_low, log_totals, mixed_grad, inner, cos_wide, sin_wide
    )
    for distance in range(1, MAXB):
        at = (MAXB - 1 - distance) * block_rows
        own_pair_grad = own_pair_grad + shifted(
            window_grad[at : at + block_rows], "ctx", -distance
        ).astype(jnp.float32)
    down_sum.last(query_grad_low)
    swish_sum.last(query_grad_low)
    up_sum.onward(query_grad_low)
    out_sum.onward(query_grad_low)
    gate_sum = rows_grad(normed_low, ssm_gate_low, 2, (up_sum.far_low, out_sum.far_low))
    key_grad_low = (
        rotate(own_pair_grad[:, :HD].reshape(block_rows, 1, HD), cos_table, -sin_table)
        .reshape(block_rows, HD)
        .astype(jnp.bfloat16)
    )
    value_grad_low = own_pair_grad[:, HD:].astype(jnp.bfloat16)
    end_grad = carried_states(keep_low * state_in_grad, decay_row, True)
    in_grad, rim_grad, tap_grad, step_part, sum_part, bc_grad, bc_rim_grad, bc_tap_grad = scan_back(
        first_pre, mix_pre, rims, after(taps, up_sum.far_low, out_sum.far_low, *down_sum.blocks_low),
        bc_taps, step_cols, sum_cols, sum_rows,
        mixed_grad, gate_pre, 0, state_in, end_grad, bc_low,
    )
    up_sum.last(in_grad)
    out_sum.last(in_grad)
    gate_sum.onward(in_grad)
    edge_grad = jnp.concatenate([rim_grad, bc_rim_grad], axis=1)[8 - rim_rows :]
    edge_back = shifted(keep_state * edge_grad, "ctx", -1)
    edge_back = jnp.pad(edge_back, ((block_rows - rim_rows, 0), (0, 0)))
    input_grad_low = (in_grad + edge_back[:, :inner]).astype(jnp.bfloat16)
    bc_pre_part = bc_grad + edge_back[:, inner:]
    rate_grad = lax.dot_general(
        lower, from_pairs(sum_part), (((0,), (0,)), ((), ())), precision=highest
    )
    step_grad = (from_pairs(step_part) + rate * rate_grad) * jax.nn.sigmoid(step_in)
    step_grad_low = step_grad.astype(jnp.bfloat16)
    tap_sums = [
        tap_grad[:KW].T,
        tap_grad[KW],
        jnp.sum(step_grad, axis=0),
        jnp.sum(rate_grad * rate * step_size, axis=0),
        jnp.sum(tap_grad[KW + 1].reshape(steps, head_dim), axis=1),
    ]
    no_misc = jnp.zeros((block_rows, 128 - steps), jnp.bfloat16)
    mix_grads = [step_grad_low, no_misc, query_grad_low, key_grad_low, value_grad_low]
    bc_grad_low = pair_sum(bc_pre_part).astype(jnp.bfloat16)
    input_sum = rows_grad(normed_low, input_grad_low, 1)
    mix_sum = rows_grad(normed_low, jnp.concatenate([bc_grad_low] + mix_grads, axis=1), 2)
    mix_grads = jnp.concatenate([bc_pre_part.astype(jnp.bfloat16)] + mix_grads, axis=1)
    norm_one_part = (
        product_by_rows(input_grad_low, input_weight)
        + product_by_rows(mix_grads, mix_weights)
        + product_by_rows(ssm_gate_low, joined(gate_held, 0))
    )
    input_sum.onward(norm_one_part)
    mix_sum.onward(norm_one_part)
    gate_sum.last(norm_one_part)
    norm_one_grad = pair_sum(norm_one_part)
    conv_bc_grads = jnp.concatenate([bc_tap_grad[:KW].T.reshape(-1), bc_tap_grad[KW]])
    conv_bc_grads = conv_bc_grads + swap(conv_bc_grads)
    inputs_norm_grad, gain_one_grad = norm_one_back(norm_one_grad)
    tokens_grad = (hidden_grad + inputs_norm_grad).astype(jnp.bfloat16)
    small = [
        tap_sums[0].reshape(-1),
        *tap_sums[1:],
        conv_bc_grads,
        whole_order(gain_one_grad).reshape(-1),
        whole_order(gain_two_grad).reshape(-1),
    ]
    packed = jnp.concatenate(small)
    filled = -packed.shape[0] % 1024
    packed = summed(jnp.pad(packed, (0, filled)).reshape(-1, 128)).reshape(-1)
    sums, at = ([], 0)
    for part in small:
        sums.append(packed[at : at + part.shape[0]])
        at += part.shape[0]

    def own(vector, count):
        return lax.dynamic_slice_in_dim(vector, block_index * count, count, 0)

    input_sum.last()
    mix_sum.last()
    mix_grad = mix_sum.total()
    out_grad = out_sum.total()
    conv_bc_sums = sums[5]
    conv_rows = conv_bc_weight.shape[0]
    return (
        reordered(layer_out, to_whole),
        reordered(tokens_grad, to_whole),
        own(sums[6], rows_here),
        gate_sum.total(),
        input_sum.total(),
        mix_grad[:, :shared],
        mix_grad[:, shared : shared + steps],
        sums[0].reshape(inner, KW),
        sums[1],
        own(conv_bc_sums[: shared * KW], conv_rows * KW).reshape(conv_rows, KW),
        own(conv_bc_sums[shared * KW :], conv_rows),
        sums[2],
        sums[3],
        sums[4],
        out_grad[:inner],
        mix_grad[:, query_at:key_at],
        mix_grad[:, key_at : key_at + pair_wide],
        mix_grad[:, key_at + pair_wide :],
        out_grad[inner:],
        own(sums[7], rows_here),
        swish_sum.total(),
        up_sum.total(),
        down_sum.total(),
    )


def solution(mesh):
    return jax.shard_map(
        per_device,
        mesh=mesh,
        in_specs=(
            P("ctx", None),
            P("ctx", None),
            P("ctx"),
            P("ctx", "wt"),
            P("ctx", "wt"),
            P("ctx", None),
            P("ctx", "wt"),
            P("wt", None),
            P("wt"),
            P("ctx", None),
            P("ctx"),
            P("wt"),
            P("wt"),
            P("wt"),
            P("wt", "ctx"),
            P("ctx", "wt"),
            P("ctx", "wt"),
            P("ctx", "wt"),
            P("wt", "ctx"),
            P("ctx"),
            P("ctx", "wt"),
            P("ctx", "wt"),
            P("wt", "ctx"),
            P(),
            P(),
            P(),
        ),
        out_specs=(
            P("ctx", None),
            P("ctx", None),
            P("ctx"),
            P("ctx", "wt"),
            P("ctx", "wt"),
            P("ctx", None),
            P("ctx", "wt"),
            P("wt", None),
            P("wt"),
            P("ctx", None),
            P("ctx"),
            P("wt"),
            P("wt"),
            P("wt"),
            P("wt", "ctx"),
            P("ctx", "wt"),
            P("ctx", "wt"),
            P("ctx", "wt"),
            P("wt", "ctx"),
            P("ctx"),
            P("ctx", "wt"),
            P("ctx", "wt"),
            P("wt", "ctx"),
        ),
        check_vma=False,
    )
```

```python
import jax
import jax.numpy as jnp
from jax import lax
from jax.experimental import pallas as pl
from jax.experimental.pallas import tpu as pltpu
from jax.sharding import PartitionSpec as P

HD = 128
KW = 4
MAXB = 8
SCAN_ROWS = 128
ATTN_ROWS = 256


epsilon = 1e-05
rope_base = 100000000000.0
highest = lax.Precision.HIGHEST
masked_score = -1e30


def shifted(value, axis, steps):
    count = lax.axis_size(axis)
    leading, last = (max(0, -steps), min(count, count - steps))
    return lax.ppermute(value, axis, [(source, source + steps) for source in range(leading, last)])


def hop(value, code):
    if code == 0:
        return value
    count = lax.axis_size("ctx")
    return lax.ppermute(value, "ctx", [(source, source ^ code) for source in range(count)])


def swap(value):
    return lax.ppermute(value, "wt", [(0, 1), (1, 0)])


def pair_sum(value):
    rounded = lax.reduce_precision(value, 8, 7)
    return rounded + swap(rounded.astype(jnp.bfloat16)).astype(jnp.float32)


def slot_devices(count):
    high = count // 4
    return [4 * (slot % high) + slot // high for slot in range(count)]


def after(value, *gates):
    return lax.optimization_barrier((value, *gates))[0]


def spread(held, axis, codes, gates=(), merge=False):
    if merge:
        every = [code for here, _ in held for code in here]
        held = [(every, jnp.concatenate([array for _, array in held], axis=axis))]
    taken = list(held)
    for here, array in held:
        operand = after(array, *gates) if gates else array
        for code in codes:
            taken.append(([one ^ code for one in here], hop(operand, code)))
    return taken


def joined(held, axis):
    size = sum(array.shape[axis] for _, array in held) // sum(len(here) for here, _ in held)
    found = {code: (i, at) for i, (here, _) in enumerate(held) for at, code in enumerate(here)}
    runs = []
    for code in slot_devices(len(found)):
        i, at = found[code]
        if runs and runs[-1][0] == i and runs[-1][2] == at:
            runs[-1][2] = at + 1
        else:
            runs.append([i, at, at + 1])
    return jnp.concatenate(
        [lax.slice_in_dim(held[i][1], at * size, to * size, axis=axis) for i, at, to in runs],
        axis=axis,
    )


class Reduction:
    def __init__(self, parts, axis, first, gates=()):
        self.axis, self.second = (axis, 3 - first)
        self.near, self.far = (parts[0], parts[3 - first])
        low = [parts[k].astype(jnp.bfloat16) for k in (first, 3)]
        if gates:
            low = lax.optimization_barrier((*low, *gates))[:2]
        self.got = [hop(part, first) for part in low]

    def onward(self, *gates):
        far = self.far + self.got[1].astype(jnp.float32)
        self.far_low = far.astype(jnp.bfloat16)
        operand = after(self.far_low, *gates) if gates else self.far_low
        self.near = self.near + self.got[0].astype(jnp.float32)
        self.got = [hop(operand, self.second)]

    def last(self, *gates):
        high = lax.axis_size("ctx") // 4
        quarter = self.near + self.got[0].astype(jnp.float32)
        blocks = jnp.split(quarter, high, axis=self.axis)
        self.block = blocks[0]
        self.blocks_low = [block.astype(jnp.bfloat16) for block in blocks[1:]]
        operands = self.blocks_low
        if gates:
            operands = lax.optimization_barrier((*operands, *gates))[: len(operands)]
        self.got = [hop(block, 4 * (k + 1)) for k, block in enumerate(operands)]

    def total(self):
        total = self.block
        for got in self.got:
            total = total + got.astype(jnp.float32)
        return total


def summed(value):
    bit = 1
    while bit < lax.axis_size("ctx"):
        value = value + hop(value, bit)
        bit *= 2
    return value


def reordered(value, order):
    blocks = order.shape[0]
    rows, width = value.shape[0], value.shape[1] // blocks
    if width % 128:
        return jnp.take(value.reshape(rows, blocks, width), order, axis=1).reshape(rows, -1)

    part = rows // 4

    def body(order_ref, in_ref, out_ref):
        for slot in range(blocks):
            start = pl.multiple_of(order_ref[slot] * width, width)
            out_ref[:, slot * width : (slot + 1) * width] = in_ref[:, pl.ds(start, width)]

    block = pl.BlockSpec((part, value.shape[1]), lambda i, order_ref: (i, 0))
    return pl.pallas_call(
        body,
        out_shape=jax.ShapeDtypeStruct(value.shape, value.dtype),
        grid_spec=pltpu.PrefetchScalarGridSpec(
            num_scalar_prefetch=1, grid=(4,), in_specs=[block], out_specs=block
        ),
        name="reordered",
    )(order, value)


def carried_states(states, decays, reverse):
    me = lax.axis_index("ctx")
    place = me % 4
    width = states.shape[1] // 4
    low = states.astype(jnp.bfloat16)

    def quarter(value, index):
        return lax.dynamic_slice_in_dim(value, index * width, width, 1)

    got = [hop(quarter(low, place ^ k), k) for k in range(4)]
    got_decay = [hop(quarter(decays, place ^ k), k) for k in range(4)]

    def in_order(pieces):
        odd = place % 2 == 1
        pieces = [jnp.where(odd, pieces[k ^ 1], pieces[k]) for k in range(4)]
        upper = place >= 2
        return [jnp.where(upper, pieces[k ^ 2], pieces[k]) for k in range(4)]

    blocks = [piece.astype(jnp.float32) for piece in in_order(got)]
    rates = in_order(got_decay)
    if reverse:
        blocks, rates = (blocks[::-1], rates[::-1])
    total, rate = (blocks[0], rates[0])
    for block, block_rate in zip(blocks[1:], rates[1:]):
        total, rate = (block + block_rate * total, block_rate * rate)
    step = -4 if reverse else 4
    total_low = total.astype(jnp.bfloat16)
    near, near_rate = (shifted(total_low, "ctx", step), shifted(rate, "ctx", step))
    far = shifted(total_low, "ctx", 2 * step)
    state = near.astype(jnp.float32) + near_rate * far.astype(jnp.float32)
    reached = []
    for block, block_rate in zip(blocks, rates):
        reached.append(state.astype(jnp.bfloat16))
        state = block + block_rate * state
    if reverse:
        reached = reached[::-1]
    mine = in_order(reached)
    back = in_order([hop(mine[k], k) for k in range(4)])
    return (jnp.concatenate(back, axis=1), mine[1])


def plain_product(left_side, right_side):
    return jnp.dot(left_side, right_side, preferred_element_type=jnp.float32)


def product_by_rows(left_side, right_side):
    return lax.dot_general(
        left_side, right_side, (((1,), (1,)), ((), ())), preferred_element_type=jnp.float32
    )


def product_of_cols(left_side, right_side):
    return lax.dot_general(
        left_side, right_side, (((0,), (0,)), ((), ())), preferred_element_type=jnp.float32
    )


def rms_scale(values, gain_vec):
    return (
        values * lax.rsqrt(jnp.mean(values * values, axis=-1, keepdims=True) + epsilon) * gain_vec
    )


def rotary_tables(positions):
    exponents = jnp.arange(HD // 2, dtype=jnp.float32) * (2.0 / HD)
    frequency = jnp.power(jnp.float32(rope_base), -exponents)
    angles = positions.astype(jnp.float32)[:, None] * frequency[None, :]
    return (jnp.cos(angles), jnp.sin(angles))


def rotate(values, cos_table, sin_table):
    half_dim = values.shape[-1] // 2
    first_half = values[..., :half_dim]
    second_half = values[..., half_dim:]
    cos_table = cos_table[:, None, :]
    sin_table = sin_table[:, None, :]
    return jnp.concatenate(
        [
            first_half * cos_table - second_half * sin_table,
            second_half * cos_table + first_half * sin_table,
        ],
        axis=-1,
    )


def convolved(rim, block, taps):
    length = block.shape[0]
    extended = jnp.concatenate([rim, block], axis=0)
    first = rim.shape[0] - (KW - 1)
    summed = taps[KW : KW + 1]
    for j in range(KW):
        summed = summed + extended[first + j : first + j + length] * taps[j : j + 1]
    return (extended, summed)


def convolved_back(extended, pre_grad, taps):
    length = pre_grad.shape[0]
    rim_rows = extended.shape[0] - length
    first = rim_rows - (KW - 1)
    zeros = jnp.zeros((8, pre_grad.shape[1]), jnp.float32)
    padded = jnp.concatenate([zeros, pre_grad, zeros], axis=0)
    total = jnp.zeros_like(extended)
    rows = []
    for j in range(KW):
        start = 8 - rim_rows + KW - 1 - j
        total = total + padded[start : start + rim_rows + length] * taps[j : j + 1]
        rows.append(
            jnp.sum(pre_grad * extended[first + j : first + j + length], axis=0, keepdims=True)
        )
    rows.append(jnp.sum(pre_grad, axis=0, keepdims=True))
    return (total, rows)


def silu_slope(value, sigmoid):
    return sigmoid * (1.0 + value * (1.0 - sigmoid))


def low_dot(left_side, right_side, left_axis, right_axis):
    return lax.dot_general(
        left_side.astype(jnp.bfloat16),
        right_side.astype(jnp.bfloat16),
        (((left_axis,), (right_axis,)), ((), ())),
        preferred_element_type=jnp.float32,
    )


def lower_gram(c_low, b_low):
    length = c_low.shape[0]
    gram = low_dot(c_low, b_low, 1, 1)
    rows = lax.broadcasted_iota(jnp.int32, (length, length), 0)
    cols = lax.broadcasted_iota(jnp.int32, (length, length), 1)
    return jnp.where(rows >= cols, gram, 0.0)


def scan_blocks(inner, shared, length, wide):
    return [
        pl.BlockSpec((length, wide), lambda i: (0, i)),
        pl.BlockSpec((8, wide), lambda i: (0, i)),
        pl.BlockSpec((8, wide), lambda i: (0, i)),
        pl.BlockSpec((length, shared), lambda i: (0, 0)),
        pl.BlockSpec((8, shared), lambda i: (0, inner // shared)),
        pl.BlockSpec((8, shared), lambda i: (0, 0)),
        pl.BlockSpec((1, length, 2), lambda i: (i, 0, 0)),
        pl.BlockSpec((1, length, 2), lambda i: (i, 0, 0)),
        pl.BlockSpec((1, 2, length), lambda i: (i, 0, 0)),
    ]


def scan_forward(first_pre, mix_pre, rims, taps, bc_taps, step_cols, sum_cols, sum_rows, inner, shared):
    length = first_pre.shape[0]
    pairs = step_cols.shape[0]
    wide = inner // pairs
    size = wide // 2
    state_dim = shared // 2
    part = min(SCAN_ROWS, length)

    def body(
        in_ref, rim_ref, tap_ref, bc_ref, bc_rim_ref, bc_tap_ref, step_ref, col_ref, row_ref,
        out_ref, state_ref, bc_low_ref, gram_ref,
    ):
        @pl.when(pl.program_id(0) == 0)
        def _():
            _, pre = convolved(bc_rim_ref[...], bc_ref[...], bc_tap_ref[...])
            acts = (pre * jax.nn.sigmoid(pre)).astype(jnp.bfloat16)
            bc_low_ref[...] = acts
            gram_ref[...] = lower_gram(acts[:, state_dim:], acts[:, :state_dim])

        taps_here = tap_ref[...]
        _, pre = convolved(rim_ref[...], in_ref[...], taps_here)
        acts = pre * jax.nn.sigmoid(pre)
        outs, tails = ([], [])
        for head in range(2):
            lanes = slice(head * size, (head + 1) * size)
            step = step_ref[0][:, head : head + 1]
            col = col_ref[0][:, head : head + 1]
            row = row_ref[0][head : head + 1, :]
            stepped = acts[:, lanes] * step
            stepped_low = stepped.astype(jnp.bfloat16)
            for at in range(0, length, part):
                end = at + part
                decay = jnp.exp(jnp.minimum(col[at:end] - row[:, :end], 0.0))
                weights = (decay * gram_ref[at:end, :end]).astype(jnp.bfloat16)
                out_ref[at:end, lanes] = low_dot(weights, stepped_low[:end], 1, 0) + (
                    taps_here[KW + 1 : KW + 2, lanes] * acts[at:end, lanes]
                )
            tails.append(stepped * jnp.exp(col[length - 1 : length] - col))
        tail = jnp.concatenate(tails, axis=1)
        state_ref[...] = low_dot(bc_low_ref[:, :state_dim], tail, 0, 0).astype(jnp.bfloat16)

    return pl.pallas_call(
        body,
        grid=(pairs,),
        out_shape=(
            jax.ShapeDtypeStruct((length, inner), jnp.float32),
            jax.ShapeDtypeStruct((state_dim, inner), jnp.bfloat16),
            jax.ShapeDtypeStruct((length, shared), jnp.bfloat16),
        ),
        in_specs=scan_blocks(inner, shared, length, wide),
        out_specs=(
            pl.BlockSpec((length, wide), lambda i: (0, i)),
            pl.BlockSpec((state_dim, wide), lambda i: (0, i)),
            pl.BlockSpec((length, shared), lambda i: (0, 0)),
        ),
        scratch_shapes=[pltpu.VMEM((length, length), jnp.float32)],
        compiler_params=pltpu.CompilerParams(vmem_limit_bytes=48 << 20),
        name="scan_forward",
    )(first_pre, rims, taps, mix_pre, rims, bc_taps, step_cols, sum_cols, sum_rows)


def scan_gated(intra, state_in, bc_low, sum_cols, second_pre, gate_at):
    length, inner = intra.shape
    pairs = sum_cols.shape[0]
    wide = inner // pairs
    size = wide // 2
    state_dim = bc_low.shape[1] // 2

    def body(intra_ref, state_ref, c_ref, col_ref, gate_ref, out_ref, act_ref):
        carried = low_dot(c_ref[...], state_ref[...], 1, 0)
        gate = gate_ref[...]
        silu = gate * jax.nn.sigmoid(gate)
        for head in range(2):
            lanes = slice(head * size, (head + 1) * size)
            growth = jnp.exp(col_ref[0][:, head : head + 1])
            whole = intra_ref[:, lanes] + carried[:, lanes] * growth
            out_ref[:, lanes] = whole
            act_ref[:, lanes] = (whole * silu[:, lanes]).astype(jnp.bfloat16)

    block = pl.BlockSpec((length, wide), lambda i: (0, i))
    return pl.pallas_call(
        body,
        grid=(pairs,),
        out_shape=(
            jax.ShapeDtypeStruct((length, inner), jnp.float32),
            jax.ShapeDtypeStruct((length, inner), jnp.bfloat16),
        ),
        in_specs=[
            block,
            pl.BlockSpec((state_dim, wide), lambda i: (0, i)),
            pl.BlockSpec((length, state_dim), lambda i: (0, 1)),
            pl.BlockSpec((1, length, 2), lambda i: (i, 0, 0)),
            pl.BlockSpec((length, wide), lambda i: (0, gate_at // wide + i)),
        ],
        out_specs=(block, block),
        compiler_params=pltpu.CompilerParams(vmem_limit_bytes=48 << 20),
        name="scan_gated",
    )(intra, state_in, bc_low, sum_cols, second_pre)


def scan_gated_back(out_grads, whole, bc_low, sum_cols, second_pre, gate_at):
    length, inner = whole.shape
    pairs = sum_cols.shape[0]
    wide = inner // pairs
    size = wide // 2
    state_dim = bc_low.shape[1] // 2

    def body(grad_ref, whole_ref, c_ref, col_ref, gate_ref, gate_grad_ref, state_ref):
        gate = gate_ref[...]
        sigmoid = jax.nn.sigmoid(gate)
        grad = grad_ref[...]
        gate_grad_ref[...] = (grad * whole_ref[...] * silu_slope(gate, sigmoid)).astype(jnp.bfloat16)
        inside = grad * (gate * sigmoid)
        grown = [
            inside[:, head * size : (head + 1) * size] * jnp.exp(col_ref[0][:, head : head + 1])
            for head in range(2)
        ]
        state_ref[...] = low_dot(c_ref[...], jnp.concatenate(grown, axis=1), 0, 0).astype(
            jnp.bfloat16
        )

    block = pl.BlockSpec((length, wide), lambda i: (0, i))
    return pl.pallas_call(
        body,
        grid=(pairs,),
        out_shape=(
            jax.ShapeDtypeStruct((length, inner), jnp.bfloat16),
            jax.ShapeDtypeStruct((state_dim, inner), jnp.bfloat16),
        ),
        in_specs=[
            block,
            block,
            pl.BlockSpec((length, state_dim), lambda i: (0, 1)),
            pl.BlockSpec((1, length, 2), lambda i: (i, 0, 0)),
            pl.BlockSpec((length, wide), lambda i: (0, gate_at // wide + i)),
        ],
        out_specs=(block, pl.BlockSpec((state_dim, wide), lambda i: (0, i))),
        compiler_params=pltpu.CompilerParams(vmem_limit_bytes=48 << 20),
        name="scan_gated_back",
    )(out_grads, whole, bc_low, sum_cols, second_pre)


def scan_back(
    first_pre, mix_pre, rims, taps, bc_taps, step_cols, sum_cols, sum_rows,
    out_grads, second_pre, gate_at, state_in, end_grad, bc_low,
):
    length = first_pre.shape[0]
    pairs = step_cols.shape[0]
    state_dim, inner = state_in.shape
    shared = bc_low.shape[1]
    wide = inner // pairs
    size = wide // 2
    part = min(SCAN_ROWS, length)

    def body(
        in_ref, rim_ref, tap_ref, bc_ref, bc_rim_ref, bc_tap_ref, step_ref, col_ref, row_ref,
        grad_ref, gate_ref, state_ref, end_ref, bc_low_ref,
        in_grad_ref, rim_grad_ref, tap_grad_ref, step_grad_ref, sum_grad_ref,
        bc_grad_ref, bc_rim_grad_ref, bc_tap_grad_ref,
        gram_ref, gram_grad_ref, acts_grad_ref, back_ref,
    ):
        b_low = bc_low_ref[:, :state_dim]
        c_low = bc_low_ref[:, state_dim:]

        @pl.when(pl.program_id(0) == 0)
        def _():
            gram_ref[...] = lower_gram(c_low, b_low)
            gram_grad_ref[...] = jnp.zeros_like(gram_grad_ref)
            acts_grad_ref[...] = jnp.zeros_like(acts_grad_ref)

        taps_here = tap_ref[...]
        extended, pre = convolved(rim_ref[...], in_ref[...], taps_here)
        sigmoid = jax.nn.sigmoid(pre)
        acts = pre * sigmoid
        gate = gate_ref[...]
        out_grad = grad_ref[...] * (gate * jax.nn.sigmoid(gate))
        state = state_ref[...]
        end = end_ref[...]
        from_end = low_dot(b_low, end, 1, 0)
        from_start = low_dot(c_low, state, 1, 0)
        state_dot = jnp.sum(
            state.astype(jnp.float32) * end.astype(jnp.float32), axis=0, keepdims=True
        )
        last_row = lax.broadcasted_iota(jnp.int32, (length, 1), 0) == length - 1
        acts_grads, tails, grown_grads = ([], [], [])
        for head in range(2):
            lanes = slice(head * size, (head + 1) * size)
            step = step_ref[0][:, head : head + 1]
            col = col_ref[0][:, head : head + 1]
            row = row_ref[0][head : head + 1, :]
            here = acts[:, lanes]
            stepped = here * step
            stepped_low = stepped.astype(jnp.bfloat16)
            grad = out_grad[:, lanes]
            grad_low = grad.astype(jnp.bfloat16)
            grad_wide = grad_low.astype(jnp.float32)
            back_ref[...] = jnp.zeros_like(back_ref)
            row_terms = []
            for at in range(0, length, part):
                to = at + part
                decay = jnp.exp(jnp.minimum(col[at:to] - row[:, :to], 0.0))
                weights = (decay * gram_ref[at:to, :to]).astype(jnp.bfloat16)
                again = low_dot(weights, stepped_low[:to], 1, 0)
                row_terms.append(jnp.sum(again * grad_wide[at:to], axis=1, keepdims=True))
                back_ref[:to] += low_dot(weights, grad_low[at:to], 0, 0)
                gram_grad_ref[at:to, :to] += decay * low_dot(
                    grad_low[at:to], stepped_low[:to], 1, 1
                )
            back = back_ref[...]
            tail = jnp.exp(col[length - 1 : length] - col)
            growth = jnp.exp(col)
            ended = from_end[:, lanes] * tail
            end_terms = jnp.sum(ended * stepped, axis=1, keepdims=True)
            col_terms = jnp.sum(back * stepped_low.astype(jnp.float32), axis=1, keepdims=True)
            start_terms = growth * jnp.sum(from_start[:, lanes] * grad, axis=1, keepdims=True)
            whole = jnp.sum(end_terms, axis=0, keepdims=True) + growth[
                length - 1 : length
            ] * jnp.sum(state_dot[:, lanes], axis=1, keepdims=True)
            sum_grad_ref[0, :, head : head + 1] = (
                jnp.concatenate(row_terms, axis=0)
                + start_terms
                - col_terms
                - end_terms
                + jnp.where(last_row, whole, 0.0)
            )
            back = back + ended
            step_grad_ref[0, :, head : head + 1] = jnp.sum(back * here, axis=1, keepdims=True)
            acts_grads.append(taps_here[KW + 1 : KW + 2, lanes] * grad + back * step)
            tails.append((stepped * tail).astype(jnp.bfloat16))
            grown_grads.append((grad * growth).astype(jnp.bfloat16))
        acts_grad_ref[:, :state_dim] += low_dot(jnp.concatenate(tails, axis=1), end, 1, 1)
        acts_grad_ref[:, state_dim:] += low_dot(jnp.concatenate(grown_grads, axis=1), state, 1, 1)
        pre_grad = jnp.concatenate(acts_grads, axis=1) * silu_slope(pre, sigmoid)
        total, rows = convolved_back(extended, pre_grad, taps_here)
        rim_grad_ref[...] = total[:8]
        in_grad_ref[...] = total[8:]
        rows.append(jnp.sum(out_grad * acts, axis=0, keepdims=True))
        rows.append(jnp.zeros((8 - len(rows), wide), jnp.float32))
        tap_grad_ref[...] = jnp.concatenate(rows, axis=0)

        @pl.when(pl.program_id(0) == pairs - 1)
        def _():
            gram_grad = gram_grad_ref[...]
            rows_of = lax.broadcasted_iota(jnp.int32, (length, length), 0)
            cols_of = lax.broadcasted_iota(jnp.int32, (length, length), 1)
            gram_grad = jnp.where(rows_of >= cols_of, gram_grad, 0.0).astype(jnp.bfloat16)
            acts_grad_ref[:, :state_dim] += low_dot(gram_grad, c_low, 0, 0)
            acts_grad_ref[:, state_dim:] += low_dot(gram_grad, b_low, 1, 0)
            bc_taps_here = bc_tap_ref[...]
            bc_extended, bc_pre = convolved(bc_rim_ref[...], bc_ref[...], bc_taps_here)
            bc_pre_grad = acts_grad_ref[...] * silu_slope(bc_pre, jax.nn.sigmoid(bc_pre))
            bc_total, bc_rows = convolved_back(bc_extended, bc_pre_grad, bc_taps_here)
            bc_rim_grad_ref[...] = bc_total[:8]
            bc_grad_ref[...] = bc_total[8:]
            bc_rows.append(jnp.zeros((8 - len(bc_rows), shared), jnp.float32))
            bc_tap_grad_ref[...] = jnp.concatenate(bc_rows, axis=0)

    block = pl.BlockSpec((length, wide), lambda i: (0, i))
    eight = pl.BlockSpec((8, wide), lambda i: (0, i))
    table = pl.BlockSpec((1, length, 2), lambda i: (i, 0, 0))
    state_block = pl.BlockSpec((state_dim, wide), lambda i: (0, i))
    bc_block = pl.BlockSpec((length, shared), lambda i: (0, 0))
    bc_eight = pl.BlockSpec((8, shared), lambda i: (0, 0))
    wide_f32 = jax.ShapeDtypeStruct((length, inner), jnp.float32)
    eight_f32 = jax.ShapeDtypeStruct((8, inner), jnp.float32)
    table_f32 = jax.ShapeDtypeStruct(step_cols.shape, jnp.float32)
    bc_f32 = jax.ShapeDtypeStruct((length, shared), jnp.float32)
    bc_eight_f32 = jax.ShapeDtypeStruct((8, shared), jnp.float32)
    return pl.pallas_call(
        body,
        grid=(pairs,),
        out_shape=(
            wide_f32, eight_f32, eight_f32, table_f32, table_f32, bc_f32, bc_eight_f32, bc_eight_f32
        ),
        in_specs=scan_blocks(inner, shared, length, wide)
        + [
            block,
            pl.BlockSpec((length, wide), lambda i: (0, gate_at // wide + i)),
            state_block,
            state_block,
            bc_block,
        ],
        out_specs=(block, eight, eight, table, table, bc_block, bc_eight, bc_eight),
        scratch_shapes=[
            pltpu.VMEM((length, length), jnp.float32),
            pltpu.VMEM((length, length), jnp.float32),
            pltpu.VMEM((length, shared), jnp.float32),
            pltpu.VMEM((length, size), jnp.float32),
        ],
        compiler_params=pltpu.CompilerParams(vmem_limit_bytes=56 << 20),
        name="scan_back",
    )(
        first_pre, rims, taps, mix_pre, rims, bc_taps, step_cols, sum_cols, sum_rows,
        out_grads, second_pre, state_in, end_grad, bc_low,
    )


def turned(values, cos_wide, sin_wide):
    return values * cos_wide + pltpu.roll(values, values.shape[1] // 2, 1) * sin_wide


def own_mask(at, rows, keys, limit):
    query_row = lax.broadcasted_iota(jnp.int32, (rows, keys), 0) + at
    key_row = lax.broadcasted_iota(jnp.int32, (rows, keys), 1)
    return (key_row <= query_row) & (key_row < limit)


def attention_forward(layout, second_pre, query_at, window, cos_wide, sin_wide, heads):
    length = second_pre.shape[0]
    part = min(ATTN_ROWS, length)
    own_at = window.shape[0] - length
    scale = HD ** (-0.5)

    def body(layout_ref, query_ref, window_ref, cos_ref, sin_ref, out_ref, turned_ref, total_ref):
        query = turned(query_ref[...], cos_ref[...], sin_ref[...]).astype(jnp.bfloat16)
        turned_ref[...] = query
        for at in range(0, length, part):
            to = at + part
            here = query[at:to]

            def scores_of(keys):
                return scale * low_dot(here, keys, 1, 1)

            keys = window_ref[own_at : own_at + to, :HD]
            values = window_ref[own_at : own_at + to, HD:]
            scores = jnp.where(
                own_mask(at, part, to, layout_ref[1]), scores_of(keys), masked_score
            )
            top = jnp.max(scores, axis=1, keepdims=True)
            shares = jnp.exp(scores - top)
            total = jnp.sum(shares, axis=1, keepdims=True)
            acc = low_dot(shares, values, 1, 0)

            def earlier(distance, carry):
                top, total, acc = carry
                start = pl.multiple_of(own_at - distance * length, length)
                scores = scores_of(window_ref[pl.ds(start, length), :HD])
                new_top = jnp.maximum(top, jnp.max(scores, axis=1, keepdims=True))
                fade = jnp.exp(top - new_top)
                shares = jnp.exp(scores - new_top)
                total = fade * total + jnp.sum(shares, axis=1, keepdims=True)
                acc = fade * acc + low_dot(shares, window_ref[pl.ds(start, length), HD:], 1, 0)
                return (new_top, total, acc)

            top, total, acc = lax.fori_loop(1, layout_ref[0] + 1, earlier, (top, total, acc))
            out_ref[at:to] = (acc / total).astype(jnp.bfloat16)
            total_ref[0, at:to] = top + jnp.log(total)

    head = pl.BlockSpec((length, HD), lambda i, layout_ref: (0, i))
    whole = pl.BlockSpec((length, HD), lambda i, layout_ref: (0, 0))
    return pl.pallas_call(
        body,
        out_shape=(
            jax.ShapeDtypeStruct((length, heads * HD), jnp.bfloat16),
            jax.ShapeDtypeStruct((length, heads * HD), jnp.bfloat16),
            jax.ShapeDtypeStruct((heads, length, 1), jnp.float32),
        ),
        grid_spec=pltpu.PrefetchScalarGridSpec(
            num_scalar_prefetch=1,
            grid=(heads,),
            in_specs=[
                pl.BlockSpec((length, HD), lambda i, layout_ref: (0, query_at // HD + i)),
                pl.BlockSpec(window.shape, lambda i, layout_ref: (0, 0)),
                whole,
                whole,
            ],
            out_specs=(
                head,
                head,
                pl.BlockSpec((1, length, 1), lambda i, layout_ref: (i, 0, 0)),
            ),
        ),
        compiler_params=pltpu.CompilerParams(vmem_limit_bytes=48 << 20),
        name="attention_forward",
    )(layout, second_pre, window, cos_wide, sin_wide)


def attention_back(layout, query, window, out, totals, mixed_grad, grad_at, cos_wide, sin_wide):
    length = query.shape[0]
    heads = query.shape[1] // HD
    part = min(ATTN_ROWS, length)
    own_at = window.shape[0] - length
    scale = HD ** (-0.5)

    def body(
        layout_ref, query_ref, window_ref, out_in_ref, total_ref, grad_ref, cos_ref, sin_ref,
        query_grad_ref, window_grad_ref, own_grad_ref, sum_ref, acc_ref,
    ):
        @pl.when(pl.program_id(0) == 0)
        def _():
            sum_ref[...] = jnp.zeros_like(sum_ref)

        for at in range(0, length, part):
            to = at + part
            here = query_ref[at:to]
            grad = grad_ref[at:to].astype(jnp.bfloat16)
            dots = jnp.sum(
                grad.astype(jnp.float32) * out_in_ref[at:to].astype(jnp.float32),
                axis=1,
                keepdims=True,
            )
            total = total_ref[0, at:to]

            def step(start, count, mask):
                keys = window_ref[pl.ds(start, count), :HD]
                values = window_ref[pl.ds(start, count), HD:]
                probs = jnp.exp(scale * low_dot(here, keys, 1, 1) - total)
                if mask is not None:
                    probs = jnp.where(mask, probs, 0.0)
                score_grad = (probs * (low_dot(grad, values, 1, 1) - dots)).astype(jnp.bfloat16)
                sum_ref[pl.ds(start, count), :HD] += low_dot(score_grad, here, 0, 0)
                sum_ref[pl.ds(start, count), HD:] += low_dot(probs, grad, 0, 0)
                return low_dot(score_grad, keys, 1, 0)

            acc_ref[...] = step(own_at, to, own_mask(at, part, to, layout_ref[1]))

            def earlier(distance, carry):
                start = pl.multiple_of(own_at - distance * length, length)
                acc_ref[...] += step(start, length, None)
                return carry

            lax.fori_loop(1, layout_ref[0] + 1, earlier, 0)
            query_grad_ref[at:to] = turned(
                acc_ref[...] * scale, cos_ref[at:to], -sin_ref[at:to]
            ).astype(jnp.bfloat16)

        @pl.when(pl.program_id(0) == heads - 1)
        def _():
            own_grad_ref[:, :HD] = sum_ref[own_at:, :HD] * scale
            own_grad_ref[:, HD:] = sum_ref[own_at:, HD:]
            window_grad_ref[:, :HD] = (sum_ref[:own_at, :HD] * scale).astype(jnp.bfloat16)
            window_grad_ref[:, HD:] = sum_ref[:own_at, HD:].astype(jnp.bfloat16)

    head = pl.BlockSpec((length, HD), lambda i, layout_ref: (0, i))
    whole = pl.BlockSpec((length, HD), lambda i, layout_ref: (0, 0))
    return pl.pallas_call(
        body,
        out_shape=(
            jax.ShapeDtypeStruct(query.shape, jnp.bfloat16),
            jax.ShapeDtypeStruct((own_at, 2 * HD), jnp.bfloat16),
            jax.ShapeDtypeStruct((length, 2 * HD), jnp.float32),
        ),
        grid_spec=pltpu.PrefetchScalarGridSpec(
            num_scalar_prefetch=1,
            grid=(heads,),
            in_specs=[
                head,
                pl.BlockSpec(window.shape, lambda i, layout_ref: (0, 0)),
                head,
                pl.BlockSpec((1, length, 1), lambda i, layout_ref: (i, 0, 0)),
                pl.BlockSpec((length, HD), lambda i, layout_ref: (0, grad_at // HD + i)),
                whole,
                whole,
            ],
            out_specs=(
                head,
                pl.BlockSpec((own_at, 2 * HD), lambda i, layout_ref: (0, 0)),
                pl.BlockSpec((length, 2 * HD), lambda i, layout_ref: (0, 0)),
            ),
            scratch_shapes=[
                pltpu.VMEM(window.shape, jnp.float32),
                pltpu.VMEM((part, HD), jnp.float32),
            ],
        ),
        compiler_params=pltpu.CompilerParams(vmem_limit_bytes=56 << 20),
        name="attention_back",
    )(layout, query, window, out, totals, mixed_grad, cos_wide, sin_wide)


def per_device(
    tokens,
    cotangent,
    mix_norm_gain,
    ssm_gate_proj,
    ssm_input_proj,
    ssm_bc_proj,
    ssm_step_proj,
    conv_in_weight,
    conv_in_bias,
    conv_bc_weight,
    conv_bc_bias,
    step_bias,
    decay_log,
    skip_gain,
    ssm_out_proj,
    query_proj,
    key_proj,
    value_proj,
    attn_out_proj,
    ffn_norm_gain,
    ffn_gate_proj,
    ffn_up_proj,
    ffn_down_proj,
    extra_blocks,
    seq_order,
    pad_rows,
):
    block_rows = tokens.shape[0]
    block_index = lax.axis_index("ctx")
    seq_count = seq_order.shape[0]
    slot_ids = jnp.arange(seq_count, dtype=jnp.int32)
    chosen = (seq_order[:, None] == slot_ids[None, :]).astype(jnp.int32)
    counts = jnp.sum(chosen * extra_blocks[None, :], axis=1) + 1
    slot_pads = jnp.sum(chosen * pad_rows[None, :], axis=1)
    slot_ends = jnp.cumsum(counts)
    starts = slot_ends - counts
    inside = (starts <= block_index) & (block_index < slot_ends)
    within = jnp.sum(jnp.where(inside, block_index - starts, 0))
    pad_here = jnp.sum(jnp.where(inside & (slot_ends - 1 == block_index), slot_pads, 0))
    row_ids = jnp.arange(block_rows, dtype=jnp.int32)
    valid_rows = (row_ids < block_rows - pad_here).astype(jnp.float32)
    positions = within * block_rows + row_ids
    keep_state = (within > 0).astype(jnp.float32)
    devices = lax.axis_size("ctx")
    codes = jnp.asarray(slot_devices(devices), jnp.int32)
    from_whole = jnp.bitwise_xor(codes, block_index)
    to_whole = jnp.argsort(from_whole).astype(jnp.int32)
    rows_here = mix_norm_gain.shape[0]
    misc_here = jnp.concatenate(
        [
            ssm_step_proj,
            mix_norm_gain[:, None],
            ffn_norm_gain[:, None],
            conv_bc_weight.reshape(rows_here, 1),
            jnp.pad(conv_bc_bias, (0, rows_here - conv_bc_bias.shape[0]))[:, None],
        ],
        axis=1,
    )
    steps = ssm_step_proj.shape[1]
    misc_here = jnp.pad(misc_here, ((0, 0), (0, 128 - misc_here.shape[1])))
    inner, shared = (ssm_input_proj.shape[1], ssm_bc_proj.shape[1])
    heads_wide, pair_wide = (query_proj.shape[1], key_proj.shape[1])
    across = [4 * k for k in range(1, devices // 4)]
    mix_here = jnp.concatenate([ssm_bc_proj, misc_here, query_proj, key_proj, value_proj], axis=1)
    out_here = jnp.concatenate([ssm_out_proj, attn_out_proj], axis=0)
    ffn_gate_weight = lax.all_gather(ffn_gate_proj, "ctx", axis=0, tiled=True)
    ffn_up_weight = lax.all_gather(ffn_up_proj, "ctx", axis=0, tiled=True)
    ffn_down_weight = lax.all_gather(ffn_down_proj, "ctx", axis=1, tiled=True)
    both_held = spread([([0], jnp.concatenate([ssm_input_proj, mix_here], axis=1))], 0, across)
    input_held = spread([(here, piece[:, :inner]) for here, piece in both_held], 0, [1], merge=True)
    mix_held = spread([(here, piece[:, inner:]) for here, piece in both_held], 0, [2], merge=True)
    near = (input_held[-1][1], mix_held[-1][1])
    input_held = spread(input_held, 0, [2])
    mix_held = spread(mix_held, 0, [1])
    gate_held = spread([([0], ssm_gate_proj)], 0, across, near)
    out_held = spread([([0], out_here)], 1, across, near)
    input_weight = joined(input_held, 0)
    mix_weights = joined(mix_held, 0)
    misc = mix_weights[:, shared : shared + 128]
    mix_gain = misc[:, steps].astype(jnp.float32)

    def whole_order(column):
        return jnp.take(column.reshape(devices, rows_here), to_whole, axis=0)

    conv_bc_full = whole_order(misc[:, steps + 2]).reshape(shared, KW)
    conv_bc_offset = whole_order(misc[:, steps + 3])[:, : conv_bc_bias.shape[0]].reshape(shared)
    gain_two = whole_order(misc[:, steps + 1]).reshape(-1)
    inputs = tokens.astype(jnp.float32)
    normed_one, norm_one_back = jax.vjp(
        rms_scale, reordered(tokens, from_whole).astype(jnp.float32), mix_gain
    )
    normed_low = normed_one.astype(jnp.bfloat16)
    first_pre = plain_product(normed_low, input_weight)
    mix_pre = plain_product(normed_low, mix_weights)
    step_raw = mix_pre[:, shared : shared + steps]
    query_at = shared + 128
    key_at = query_at + heads_wide
    key_pre = mix_pre[:, key_at : key_at + pair_wide]
    value_pre = mix_pre[:, key_at + pair_wide :]
    rim_rows = KW - 1
    edge = jnp.concatenate(
        [first_pre[block_rows - rim_rows :], mix_pre[block_rows - rim_rows :, :shared]], axis=1
    )
    edge = shifted(edge, "ctx", 1) * keep_state
    rims = jnp.pad(edge, ((8 - rim_rows, 0), (0, 0)))
    gate_held = spread(gate_held, 0, [2], (rims,), merge=True)
    out_held = spread(out_held, 1, [1], (rims,), merge=True)
    head_dim = inner // steps
    skips = jnp.repeat(skip_gain.astype(jnp.float32), head_dim)[None, :]
    taps = jnp.concatenate(
        [conv_in_weight.astype(jnp.float32).T, conv_in_bias.astype(jnp.float32)[None, :], skips]
    )
    taps = jnp.pad(taps, ((0, 8 - taps.shape[0]), (0, 0)))
    bc_taps = jnp.concatenate(
        [conv_bc_full.astype(jnp.float32).T, conv_bc_offset.astype(jnp.float32)[None, :]]
    )
    bc_taps = jnp.pad(bc_taps, ((0, 8 - bc_taps.shape[0]), (0, 0)))
    step_in = step_raw + step_bias.astype(jnp.float32)[None, :]
    step_size = jax.nn.softplus(step_in)
    rate = -jnp.exp(decay_log.astype(jnp.float32))[None, :]
    lower = (row_ids[:, None] >= row_ids[None, :]).astype(jnp.float32)
    log_decay = jnp.dot(lower, rate * step_size, precision=highest)

    def by_pairs(table):
        return table.reshape(block_rows, steps // 2, 2).transpose(1, 0, 2)

    def from_pairs(table):
        return table.transpose(1, 0, 2).reshape(block_rows, steps)

    step_cols = by_pairs(step_size)
    sum_cols = by_pairs(log_decay)
    sum_rows = log_decay.T.reshape(steps // 2, 2, block_rows)
    intra_out, local_states, bc_low = scan_forward(
        first_pre, mix_pre, rims, taps, bc_taps, step_cols, sum_cols, sum_rows, inner, shared
    )
    decay_row = keep_state * jnp.repeat(jnp.exp(log_decay[block_rows - 1]), head_dim)[None, :]
    keep_low = keep_state.astype(jnp.bfloat16)
    reached, returned = carried_states(local_states, decay_row, False)
    state_in = keep_low * reached
    gate_held = spread(gate_held, 0, [1], (returned,))
    out_held = spread(out_held, 1, [2], (returned,))
    cos_table, sin_table = rotary_tables(positions)
    cos_wide = jnp.concatenate([cos_table, cos_table], axis=1)
    sin_wide = jnp.concatenate([-sin_table, sin_table], axis=1)
    key_rot = rotate(key_pre.reshape(block_rows, -1, HD), cos_table, sin_table)
    own_pair = jnp.concatenate(
        [key_rot.reshape(block_rows, HD).astype(jnp.bfloat16), value_pre.astype(jnp.bfloat16)],
        axis=1,
    )
    earlier_pairs = [shifted(own_pair, "ctx", distance) for distance in range(MAXB - 1, 0, -1)]
    window = jnp.concatenate(earlier_pairs + [own_pair], axis=0)
    layout = jnp.stack([within, block_rows - pad_here]).astype(jnp.int32)
    attn_low, query_rot, log_totals = attention_forward(
        layout, mix_pre, query_at, window, cos_wide, sin_wide, heads_wide // HD
    )
    gate_weight = joined(gate_held, 0)
    gate_pre = plain_product(normed_low, gate_weight)
    scan_out, ssm_low = scan_gated(intra_out, state_in, bc_low, sum_cols, gate_pre, 0)
    out_weights = joined(out_held, 1)
    mixed_low = jnp.concatenate([ssm_low, attn_low], axis=1)
    mixed_part = plain_product(mixed_low, out_weights)
    hidden = inputs + reordered(pair_sum(mixed_part), to_whole)
    normed_two, norm_two_back = jax.vjp(rms_scale, hidden, gain_two.astype(jnp.float32))
    normed_two_low = normed_two.astype(jnp.bfloat16)
    ffn_gate = plain_product(normed_two_low, ffn_gate_weight)
    ffn_up = plain_product(normed_two_low, ffn_up_weight)
    ffn_act = (jax.nn.silu(ffn_gate) * ffn_up).astype(jnp.bfloat16)
    ffn_part = plain_product(ffn_act, ffn_down_weight)
    ffn_sum = pair_sum(ffn_part)
    layer_out = ((hidden + ffn_sum) * valid_rows[:, None]).astype(jnp.bfloat16)
    cot_low = (cotangent.astype(jnp.float32) * valid_rows[:, None]).astype(jnp.bfloat16)
    grad_out = cot_low.astype(jnp.float32)

    def in_quarters(value):
        return jnp.split(value, 4, axis=1)

    def rows_grad(left_side, right_side, first, gates=()):
        parts = [product_of_cols(part, right_side) for part in in_quarters(left_side)]
        return Reduction(parts, 0, first, gates)

    def cols_grad(left_side, right_side, first, gates=()):
        parts = [product_of_cols(left_side, part) for part in in_quarters(right_side)]
        return Reduction(parts, 1, first, gates)

    ffn_down_grad = lax.psum_scatter(
        product_of_cols(ffn_act, cot_low).astype(jnp.bfloat16), "ctx", scatter_dimension=1, tiled=True
    )
    act_grad = product_by_rows(cot_low, ffn_down_weight)
    gate_sigmoid = jax.nn.sigmoid(ffn_gate)
    ffn_gate_low = (
        act_grad * ffn_up * gate_sigmoid * (1.0 + ffn_gate * (1.0 - gate_sigmoid))
    ).astype(jnp.bfloat16)
    ffn_up_low = (act_grad * jax.nn.silu(ffn_gate)).astype(jnp.bfloat16)
    up_sum = rows_grad(reordered(normed_two_low, from_whole), ffn_up_low, 1)
    ffn_gate_grad = lax.psum_scatter(
        product_of_cols(normed_two_low, ffn_gate_low).astype(jnp.bfloat16),
        "ctx",
        scatter_dimension=0,
        tiled=True,
    )
    norm_two_part = product_by_rows(ffn_gate_low, ffn_gate_weight) + product_by_rows(
        ffn_up_low, ffn_up_weight
    )
    norm_two_grad = pair_sum(norm_two_part)
    hidden_norm_grad, gain_two_grad = norm_two_back(norm_two_grad)
    hidden_grad = grad_out + hidden_norm_grad
    hidden_low = reordered(hidden_grad.astype(jnp.bfloat16), from_whole)
    mixed_grad = product_by_rows(hidden_low, out_weights)
    ssm_gate_low, state_in_grad = scan_gated_back(
        mixed_grad, scan_out, bc_low, sum_cols, gate_pre, 0
    )
    end_grad, returned = carried_states(keep_low * state_in_grad, decay_row, True)
    layout = after(layout, ssm_gate_low)
    query_grad_low, window_grad, own_pair_grad = attention_back(
        layout, query_rot, window, attn_low, log_totals, mixed_grad, inner, cos_wide, sin_wide
    )
    for distance in range(1, MAXB):
        at = (MAXB - 1 - distance) * block_rows
        own_pair_grad = own_pair_grad + shifted(
            window_grad[at : at + block_rows], "ctx", -distance
        ).astype(jnp.float32)
    up_sum.onward(returned)
    out_sum = cols_grad(mixed_low, hidden_low, 1, (returned,))
    gate_sum = rows_grad(normed_low, ssm_gate_low, 2, (returned,))
    key_grad_low = (
        rotate(own_pair_grad[:, :HD].reshape(block_rows, 1, HD), cos_table, -sin_table)
        .reshape(block_rows, HD)
        .astype(jnp.bfloat16)
    )
    value_grad_low = own_pair_grad[:, HD:].astype(jnp.bfloat16)
    in_grad, rim_grad, tap_grad, step_part, sum_part, bc_grad, bc_rim_grad, bc_tap_grad = scan_back(
        first_pre, mix_pre, rims, after(taps, up_sum.far_low),
        bc_taps, step_cols, sum_cols, sum_rows,
        mixed_grad, gate_pre, 0, state_in, end_grad, bc_low,
    )
    up_sum.last(in_grad)
    out_sum.onward(in_grad)
    gate_sum.onward(in_grad)
    edge_grad = jnp.concatenate([rim_grad, bc_rim_grad], axis=1)[8 - rim_rows :]
    edge_back = shifted(keep_state * edge_grad, "ctx", -1)
    edge_back = jnp.pad(edge_back, ((block_rows - rim_rows, 0), (0, 0)))
    input_grad_low = (in_grad + edge_back[:, :inner]).astype(jnp.bfloat16)
    bc_pre_part = bc_grad + edge_back[:, inner:]
    rate_grad = lax.dot_general(
        lower, from_pairs(sum_part), (((0,), (0,)), ((), ())), precision=highest
    )
    step_grad = (from_pairs(step_part) + rate * rate_grad) * jax.nn.sigmoid(step_in)
    step_grad_low = step_grad.astype(jnp.bfloat16)
    tap_sums = [
        tap_grad[:KW].T,
        tap_grad[KW],
        jnp.sum(step_grad, axis=0),
        jnp.sum(rate_grad * rate * step_size, axis=0),
        jnp.sum(tap_grad[KW + 1].reshape(steps, head_dim), axis=1),
    ]
    no_misc = jnp.zeros((block_rows, 128 - steps), jnp.bfloat16)
    mix_grads = [step_grad_low, no_misc, query_grad_low, key_grad_low, value_grad_low]
    bc_grad_low = pair_sum(bc_pre_part).astype(jnp.bfloat16)
    input_sum = rows_grad(normed_low, input_grad_low, 1)
    mix_sum = rows_grad(normed_low, jnp.concatenate([bc_grad_low] + mix_grads, axis=1), 2)
    mix_grads = jnp.concatenate([bc_pre_part.astype(jnp.bfloat16)] + mix_grads, axis=1)
    norm_one_part = (
        product_by_rows(input_grad_low, input_weight)
        + product_by_rows(mix_grads, mix_weights)
        + product_by_rows(ssm_gate_low, gate_weight)
    )
    out_sum.last(norm_one_part)
    gate_sum.last(norm_one_part)
    input_sum.onward(norm_one_part)
    mix_sum.onward(norm_one_part)
    norm_one_grad = pair_sum(norm_one_part)
    conv_bc_grads = jnp.concatenate([bc_tap_grad[:KW].T.reshape(-1), bc_tap_grad[KW]])
    conv_bc_grads = conv_bc_grads + swap(conv_bc_grads)
    inputs_norm_grad, gain_one_grad = norm_one_back(norm_one_grad)
    tokens_grad = hidden_grad + reordered(inputs_norm_grad, to_whole)
    small = [
        tap_sums[0].reshape(-1),
        *tap_sums[1:],
        conv_bc_grads,
        whole_order(gain_one_grad).reshape(-1),
        gain_two_grad,
    ]
    packed = jnp.concatenate(small)
    filled = -packed.shape[0] % 1024
    packed = summed(jnp.pad(packed, (0, filled)).reshape(-1, 128)).reshape(-1)
    sums, at = ([], 0)
    for part in small:
        sums.append(packed[at : at + part.shape[0]])
        at += part.shape[0]

    def own(vector, count):
        return lax.dynamic_slice_in_dim(vector, block_index * count, count, 0)

    input_sum.last()
    mix_sum.last()
    mix_grad = mix_sum.total()
    out_grad = out_sum.total()
    conv_bc_sums = sums[5]
    conv_rows = conv_bc_weight.shape[0]
    return (
        layer_out,
        tokens_grad.astype(jnp.bfloat16),
        own(sums[6], rows_here),
        gate_sum.total(),
        input_sum.total(),
        mix_grad[:, :shared],
        mix_grad[:, shared : shared + steps],
        sums[0].reshape(inner, KW),
        sums[1],
        own(conv_bc_sums[: shared * KW], conv_rows * KW).reshape(conv_rows, KW),
        own(conv_bc_sums[shared * KW :], conv_rows),
        sums[2],
        sums[3],
        sums[4],
        out_grad[:inner],
        mix_grad[:, query_at:key_at],
        mix_grad[:, key_at : key_at + pair_wide],
        mix_grad[:, key_at + pair_wide :],
        out_grad[inner:],
        own(sums[7], rows_here),
        ffn_gate_grad.astype(jnp.float32),
        up_sum.total(),
        ffn_down_grad.astype(jnp.float32),
    )


def solution(mesh):
    return jax.shard_map(
        per_device,
        mesh=mesh,
        in_specs=(
            P("ctx", None),
            P("ctx", None),
            P("ctx"),
            P("ctx", "wt"),
            P("ctx", "wt"),
            P("ctx", None),
            P("ctx", "wt"),
            P("wt", None),
            P("wt"),
            P("ctx", None),
            P("ctx"),
            P("wt"),
            P("wt"),
            P("wt"),
            P("wt", "ctx"),
            P("ctx", "wt"),
            P("ctx", "wt"),
            P("ctx", "wt"),
            P("wt", "ctx"),
            P("ctx"),
            P("ctx", "wt"),
            P("ctx", "wt"),
            P("wt", "ctx"),
            P(),
            P(),
            P(),
        ),
        out_specs=(
            P("ctx", None),
            P("ctx", None),
            P("ctx"),
            P("ctx", "wt"),
            P("ctx", "wt"),
            P("ctx", None),
            P("ctx", "wt"),
            P("wt", None),
            P("wt"),
            P("ctx", None),
            P("ctx"),
            P("wt"),
            P("wt"),
            P("wt"),
            P("wt", "ctx"),
            P("ctx", "wt"),
            P("ctx", "wt"),
            P("ctx", "wt"),
            P("wt", "ctx"),
            P("ctx"),
            P("ctx", "wt"),
            P("ctx", "wt"),
            P("wt", "ctx"),
        ),
        check_vma=False,
    )
```

```python
import jax
import jax.numpy as jnp
from jax import lax
from jax.experimental import pallas as pl
from jax.experimental.pallas import tpu as pltpu
from jax.sharding import PartitionSpec as P


HD = 128
KW = 4
MAXB = 8
EXTRA = 16
SCAN_ROWS = 128
ATTN_ROWS = 256


epsilon = 1e-05
rope_base = 100000000000.0
highest = lax.Precision.HIGHEST
masked_score = -1e30


def shifted(value, axis, steps):
    count = lax.axis_size(axis)
    leading, last = (max(0, -steps), min(count, count - steps))
    return lax.ppermute(value, axis, [(source, source + steps) for source in range(leading, last)])


def hop(value, code):
    if code == 0:
        return value
    count = lax.axis_size("ctx")
    return lax.ppermute(value, "ctx", [(source, source ^ code) for source in range(count)])


def swap(value):
    return lax.ppermute(value, "wt", [(0, 1), (1, 0)])


def pair_sum(value):
    rounded = lax.reduce_precision(value, 8, 7)
    return rounded + swap(rounded.astype(jnp.bfloat16)).astype(jnp.float32)


def slot_devices(count):
    high = count // 4
    return [4 * (slot % high) + slot // high for slot in range(count)]


def after(value, *gates):
    return lax.optimization_barrier((value, *gates))[0]


def spread(held, axis, codes, gates=(), merge=False):
    if merge:
        every = [code for here, _ in held for code in here]
        held = [(every, jnp.concatenate([array for _, array in held], axis=axis))]
    taken = list(held)
    for here, array in held:
        operand = after(array, *gates) if gates else array
        for code in codes:
            taken.append(([one ^ code for one in here], hop(operand, code)))
    return taken


def joined(held, axis):
    size = sum(array.shape[axis] for _, array in held) // sum(len(here) for here, _ in held)
    found = {code: (i, at) for i, (here, _) in enumerate(held) for at, code in enumerate(here)}
    runs = []
    for code in slot_devices(len(found)):
        i, at = found[code]
        if runs and runs[-1][0] == i and runs[-1][2] == at:
            runs[-1][2] = at + 1
        else:
            runs.append([i, at, at + 1])
    return jnp.concatenate(
        [lax.slice_in_dim(held[i][1], at * size, to * size, axis=axis) for i, at, to in runs],
        axis=axis,
    )


class Reduction:
    def __init__(self, parts, axis, first, gates=()):
        self.axis, self.second = (axis, 3 - first)
        self.near, self.far = (parts[0], parts[3 - first])
        low = [parts[k].astype(jnp.bfloat16) for k in (first, 3)]
        if gates:
            low = lax.optimization_barrier((*low, *gates))[:2]
        self.got = [hop(part, first) for part in low]

    def onward(self, *gates):
        far = self.far + self.got[1].astype(jnp.float32)
        self.far_low = far.astype(jnp.bfloat16)
        operand = after(self.far_low, *gates) if gates else self.far_low
        self.near = self.near + self.got[0].astype(jnp.float32)
        self.got = [hop(operand, self.second)]

    def last(self, *gates):
        high = lax.axis_size("ctx") // 4
        quarter = self.near + self.got[0].astype(jnp.float32)
        blocks = jnp.split(quarter, high, axis=self.axis)
        self.block = blocks[0]
        self.blocks_low = [block.astype(jnp.bfloat16) for block in blocks[1:]]
        operands = self.blocks_low
        if gates:
            operands = lax.optimization_barrier((*operands, *gates))[: len(operands)]
        self.got = [hop(block, 4 * (k + 1)) for k, block in enumerate(operands)]

    def total(self):
        total = self.block
        for got in self.got:
            total = total + got.astype(jnp.float32)
        return total


def summed(value):
    bit = 1
    while bit < lax.axis_size("ctx"):
        value = value + hop(value, bit)
        bit *= 2
    return value


def reordered(value, order):
    blocks = order.shape[0]
    rows, width = value.shape[0], value.shape[1] // blocks
    if width % 128:
        return jnp.take(value.reshape(rows, blocks, width), order, axis=1).reshape(rows, -1)

    steps = 4 if rows % 64 == 0 else 3
    part = rows // steps

    def body(order_ref, in_ref, out_ref):
        for slot in range(blocks):
            start = pl.multiple_of(order_ref[slot] * width, width)
            out_ref[:, slot * width : (slot + 1) * width] = in_ref[:, pl.ds(start, width)]

    block = pl.BlockSpec((part, value.shape[1]), lambda i, order_ref: (i, 0))
    return pl.pallas_call(
        body,
        out_shape=jax.ShapeDtypeStruct(value.shape, value.dtype),
        grid_spec=pltpu.PrefetchScalarGridSpec(
            num_scalar_prefetch=1, grid=(steps,), in_specs=[block], out_specs=block
        ),
        name="reordered",
    )(order, value)


def carried_states(states, decays, reverse):
    me = lax.axis_index("ctx")
    place = me % 4
    width = states.shape[1] // 4
    low = states.astype(jnp.bfloat16)

    def quarter(value, index):
        return lax.dynamic_slice_in_dim(value, index * width, width, 1)

    got = [hop(quarter(low, place ^ k), k) for k in range(4)]
    got_decay = [hop(quarter(decays, place ^ k), k) for k in range(4)]

    def in_order(pieces):
        odd = place % 2 == 1
        pieces = [jnp.where(odd, pieces[k ^ 1], pieces[k]) for k in range(4)]
        upper = place >= 2
        return [jnp.where(upper, pieces[k ^ 2], pieces[k]) for k in range(4)]

    blocks = [piece.astype(jnp.float32) for piece in in_order(got)]
    rates = in_order(got_decay)
    if reverse:
        blocks, rates = (blocks[::-1], rates[::-1])
    total, rate = (blocks[0], rates[0])
    for block, block_rate in zip(blocks[1:], rates[1:]):
        total, rate = (block + block_rate * total, block_rate * rate)
    step = -4 if reverse else 4
    total_low = total.astype(jnp.bfloat16)
    near, near_rate = (shifted(total_low, "ctx", step), shifted(rate, "ctx", step))
    far = shifted(total_low, "ctx", 2 * step)
    state = near.astype(jnp.float32) + near_rate * far.astype(jnp.float32)
    reached = []
    for block, block_rate in zip(blocks, rates):
        reached.append(state.astype(jnp.bfloat16))
        state = block + block_rate * state
    if reverse:
        reached = reached[::-1]
    mine = in_order(reached)
    back = in_order([hop(mine[k], k) for k in range(4)])
    return (jnp.concatenate(back, axis=1), mine[1])


def plain_product(left_side, right_side):
    return jnp.dot(left_side, right_side, preferred_element_type=jnp.float32)


def product_by_rows(left_side, right_side):
    return lax.dot_general(
        left_side, right_side, (((1,), (1,)), ((), ())), preferred_element_type=jnp.float32
    )


def product_of_cols(left_side, right_side):
    return lax.dot_general(
        left_side, right_side, (((0,), (0,)), ((), ())), preferred_element_type=jnp.float32
    )


def rms_scale(values, gain_vec):
    return (
        values * lax.rsqrt(jnp.mean(values * values, axis=-1, keepdims=True) + epsilon) * gain_vec
    )


def rotary_tables(positions):
    exponents = jnp.arange(HD // 2, dtype=jnp.float32) * (2.0 / HD)
    frequency = jnp.power(jnp.float32(rope_base), -exponents)
    angles = positions.astype(jnp.float32)[:, None] * frequency[None, :]
    return (jnp.cos(angles), jnp.sin(angles))


def rotate(values, cos_table, sin_table):
    half_dim = values.shape[-1] // 2
    first_half = values[..., :half_dim]
    second_half = values[..., half_dim:]
    cos_table = cos_table[:, None, :]
    sin_table = sin_table[:, None, :]
    return jnp.concatenate(
        [
            first_half * cos_table - second_half * sin_table,
            second_half * cos_table + first_half * sin_table,
        ],
        axis=-1,
    )


def convolved(rim, block, taps):
    length = block.shape[0]
    extended = jnp.concatenate([rim, block], axis=0)
    first = rim.shape[0] - (KW - 1)
    summed = taps[KW : KW + 1]
    for j in range(KW):
        summed = summed + extended[first + j : first + j + length] * taps[j : j + 1]
    return (extended, summed)


def convolved_back(extended, pre_grad, taps):
    length = pre_grad.shape[0]
    rim_rows = extended.shape[0] - length
    first = rim_rows - (KW - 1)
    zeros = jnp.zeros((8, pre_grad.shape[1]), jnp.float32)
    padded = jnp.concatenate([zeros, pre_grad, zeros], axis=0)
    total = jnp.zeros_like(extended)
    rows = []
    for j in range(KW):
        start = 8 - rim_rows + KW - 1 - j
        total = total + padded[start : start + rim_rows + length] * taps[j : j + 1]
        rows.append(
            jnp.sum(pre_grad * extended[first + j : first + j + length], axis=0, keepdims=True)
        )
    rows.append(jnp.sum(pre_grad, axis=0, keepdims=True))
    return (total, rows)


def silu_slope(value, sigmoid):
    return sigmoid * (1.0 + value * (1.0 - sigmoid))


def low_dot(left_side, right_side, left_axis, right_axis):
    return lax.dot_general(
        left_side.astype(jnp.bfloat16),
        right_side.astype(jnp.bfloat16),
        (((left_axis,), (right_axis,)), ((), ())),
        preferred_element_type=jnp.float32,
    )


def lower_gram(c_low, b_low):
    length = c_low.shape[0]
    gram = low_dot(c_low, b_low, 1, 1)
    rows = lax.broadcasted_iota(jnp.int32, (length, length), 0)
    cols = lax.broadcasted_iota(jnp.int32, (length, length), 1)
    return jnp.where(rows >= cols, gram, 0.0)


def scan_blocks(shared, length, wide):
    return [
        pl.BlockSpec((length, wide), lambda i: (0, i)),
        pl.BlockSpec((8, wide), lambda i: ((length + EXTRA) // 8 - 1, i)),
        pl.BlockSpec((8, wide), lambda i: (0, i)),
        pl.BlockSpec((length, shared), lambda i: (0, 0)),
        pl.BlockSpec((8, shared), lambda i: ((length + EXTRA) // 8 - 1, 0)),
        pl.BlockSpec((8, shared), lambda i: (0, 0)),
        pl.BlockSpec((1, length, 2), lambda i: (i, 0, 0)),
        pl.BlockSpec((1, length, 2), lambda i: (i, 0, 0)),
        pl.BlockSpec((1, 2, length), lambda i: (i, 0, 0)),
    ]


def scan_forward(first_pre, mix_pre, taps, bc_taps, step_cols, sum_cols, sum_rows, inner, shared):
    length = first_pre.shape[0] - EXTRA
    pairs = step_cols.shape[0]
    wide = inner // pairs
    size = wide // 2
    state_dim = shared // 2
    part = min(SCAN_ROWS, length)

    def body(
        in_ref, rim_ref, tap_ref, bc_ref, bc_rim_ref, bc_tap_ref, step_ref, col_ref, row_ref,
        out_ref, state_ref, bc_low_ref, gram_ref,
    ):
        @pl.when(pl.program_id(0) == 0)
        def _():
            _, pre = convolved(bc_rim_ref[...], bc_ref[...], bc_tap_ref[...])
            acts = (pre * jax.nn.sigmoid(pre)).astype(jnp.bfloat16)
            bc_low_ref[...] = acts
            gram_ref[...] = lower_gram(acts[:, state_dim:], acts[:, :state_dim])

        taps_here = tap_ref[...]
        _, pre = convolved(rim_ref[...], in_ref[...], taps_here)
        acts = pre * jax.nn.sigmoid(pre)
        tails = []
        for head in range(2):
            lanes = slice(head * size, (head + 1) * size)
            step = step_ref[0][:, head : head + 1]
            col = col_ref[0][:, head : head + 1]
            row = row_ref[0][head : head + 1, :]
            stepped = acts[:, lanes] * step
            stepped_low = stepped.astype(jnp.bfloat16)
            for at in range(0, length, part):
                end = at + part
                decay = jnp.exp(jnp.minimum(col[at:end] - row[:, :end], 0.0))
                weights = (decay * gram_ref[at:end, :end]).astype(jnp.bfloat16)
                out_ref[at:end, lanes] = low_dot(weights, stepped_low[:end], 1, 0) + (
                    taps_here[KW + 1 : KW + 2, lanes] * acts[at:end, lanes]
                )
            tails.append(stepped * jnp.exp(col[length - 1 : length] - col))
        tail = jnp.concatenate(tails, axis=1)
        state_ref[...] = low_dot(bc_low_ref[:, :state_dim], tail, 0, 0).astype(jnp.bfloat16)

    return pl.pallas_call(
        body,
        grid=(pairs,),
        out_shape=(
            jax.ShapeDtypeStruct((length, inner), jnp.float32),
            jax.ShapeDtypeStruct((state_dim, inner), jnp.bfloat16),
            jax.ShapeDtypeStruct((length, shared), jnp.bfloat16),
        ),
        in_specs=scan_blocks(shared, length, wide),
        out_specs=(
            pl.BlockSpec((length, wide), lambda i: (0, i)),
            pl.BlockSpec((state_dim, wide), lambda i: (0, i)),
            pl.BlockSpec((length, shared), lambda i: (0, 0)),
        ),
        scratch_shapes=[pltpu.VMEM((length, length), jnp.float32)],
        compiler_params=pltpu.CompilerParams(vmem_limit_bytes=48 << 20),
        name="scan_forward",
    )(first_pre, first_pre, taps, mix_pre, mix_pre, bc_taps, step_cols, sum_cols, sum_rows)


def scan_gated(intra, state_in, bc_low, sum_cols, second_pre, gate_at):
    length, inner = intra.shape
    pairs = sum_cols.shape[0]
    wide = inner // pairs
    size = wide // 2
    state_dim = bc_low.shape[1] // 2

    def body(intra_ref, state_ref, c_ref, col_ref, gate_ref, out_ref, act_ref):
        carried = low_dot(c_ref[...], state_ref[...], 1, 0)
        gate = gate_ref[...]
        silu = gate * jax.nn.sigmoid(gate)
        for head in range(2):
            lanes = slice(head * size, (head + 1) * size)
            growth = jnp.exp(col_ref[0][:, head : head + 1])
            whole = intra_ref[:, lanes] + carried[:, lanes] * growth
            out_ref[:, lanes] = whole
            act_ref[:, lanes] = (whole * silu[:, lanes]).astype(jnp.bfloat16)

    block = pl.BlockSpec((length, wide), lambda i: (0, i))
    return pl.pallas_call(
        body,
        grid=(pairs,),
        out_shape=(
            jax.ShapeDtypeStruct((length, inner), jnp.float32),
            jax.ShapeDtypeStruct((length, inner), jnp.bfloat16),
        ),
        in_specs=[
            block,
            pl.BlockSpec((state_dim, wide), lambda i: (0, i)),
            pl.BlockSpec((length, state_dim), lambda i: (0, 1)),
            pl.BlockSpec((1, length, 2), lambda i: (i, 0, 0)),
            pl.BlockSpec((length, wide), lambda i: (0, gate_at // wide + i)),
        ],
        out_specs=(block, block),
        compiler_params=pltpu.CompilerParams(vmem_limit_bytes=48 << 20),
        name="scan_gated",
    )(intra, state_in, bc_low, sum_cols, second_pre)


def scan_gated_back(out_grads, whole, bc_low, sum_cols, second_pre, gate_at):
    length, inner = whole.shape
    pairs = sum_cols.shape[0]
    wide = inner // pairs
    size = wide // 2
    state_dim = bc_low.shape[1] // 2

    def body(grad_ref, whole_ref, c_ref, col_ref, gate_ref, gate_grad_ref, state_ref):
        gate = gate_ref[...]
        sigmoid = jax.nn.sigmoid(gate)
        grad = grad_ref[...]
        gate_grad = grad * whole_ref[...] * silu_slope(gate, sigmoid)
        gate_grad_ref[:length] = gate_grad.astype(jnp.bfloat16)
        gate_grad_ref[length:] = jnp.zeros((EXTRA, wide), jnp.bfloat16)
        inside = grad * (gate * sigmoid)
        grown = [
            inside[:, head * size : (head + 1) * size] * jnp.exp(col_ref[0][:, head : head + 1])
            for head in range(2)
        ]
        state_ref[...] = low_dot(c_ref[...], jnp.concatenate(grown, axis=1), 0, 0).astype(
            jnp.bfloat16
        )

    block = pl.BlockSpec((length, wide), lambda i: (0, i))
    return pl.pallas_call(
        body,
        grid=(pairs,),
        out_shape=(
            jax.ShapeDtypeStruct((length + EXTRA, inner), jnp.bfloat16),
            jax.ShapeDtypeStruct((state_dim, inner), jnp.bfloat16),
        ),
        in_specs=[
            block,
            block,
            pl.BlockSpec((length, state_dim), lambda i: (0, 1)),
            pl.BlockSpec((1, length, 2), lambda i: (i, 0, 0)),
            pl.BlockSpec((length, wide), lambda i: (0, gate_at // wide + i)),
        ],
        out_specs=(
            pl.BlockSpec((length + EXTRA, wide), lambda i: (0, i)),
            pl.BlockSpec((state_dim, wide), lambda i: (0, i)),
        ),
        compiler_params=pltpu.CompilerParams(vmem_limit_bytes=48 << 20),
        name="scan_gated_back",
    )(out_grads, whole, bc_low, sum_cols, second_pre)


def scan_back(
    first_pre, mix_pre, taps, bc_taps, step_cols, sum_cols, sum_rows,
    out_grads, second_pre, gate_at, state_in, end_grad, bc_low,
):
    length = first_pre.shape[0] - EXTRA
    pairs = step_cols.shape[0]
    state_dim, inner = state_in.shape
    shared = bc_low.shape[1]
    wide = inner // pairs
    size = wide // 2
    part = min(SCAN_ROWS, length)

    def body(
        in_ref, rim_ref, tap_ref, bc_ref, bc_rim_ref, bc_tap_ref, step_ref, col_ref, row_ref,
        grad_ref, gate_ref, state_ref, end_ref, bc_low_ref,
        in_grad_ref, tap_grad_ref, step_grad_ref, sum_grad_ref, bc_grad_ref, bc_tap_grad_ref,
        gram_ref, gram_grad_ref, acts_grad_ref, back_ref,
    ):
        b_low = bc_low_ref[:, :state_dim]
        c_low = bc_low_ref[:, state_dim:]

        @pl.when(pl.program_id(0) == 0)
        def _():
            gram_ref[...] = lower_gram(c_low, b_low)
            gram_grad_ref[...] = jnp.zeros_like(gram_grad_ref)
            acts_grad_ref[...] = jnp.zeros_like(acts_grad_ref)

        taps_here = tap_ref[...]
        extended, pre = convolved(rim_ref[...], in_ref[...], taps_here)
        sigmoid = jax.nn.sigmoid(pre)
        acts = pre * sigmoid
        gate = gate_ref[...]
        out_grad = grad_ref[...] * (gate * jax.nn.sigmoid(gate))
        state = state_ref[...]
        end = end_ref[...]
        from_end = low_dot(b_low, end, 1, 0)
        from_start = low_dot(c_low, state, 1, 0)
        state_dot = jnp.sum(
            state.astype(jnp.float32) * end.astype(jnp.float32), axis=0, keepdims=True
        )
        last_row = lax.broadcasted_iota(jnp.int32, (length, 1), 0) == length - 1
        acts_grads, tails, grown_grads = ([], [], [])
        for head in range(2):
            lanes = slice(head * size, (head + 1) * size)
            step = step_ref[0][:, head : head + 1]
            col = col_ref[0][:, head : head + 1]
            row = row_ref[0][head : head + 1, :]
            here = acts[:, lanes]
            stepped = here * step
            stepped_low = stepped.astype(jnp.bfloat16)
            grad = out_grad[:, lanes]
            grad_low = grad.astype(jnp.bfloat16)
            grad_wide = grad_low.astype(jnp.float32)
            back_ref[...] = jnp.zeros_like(back_ref)
            row_terms = []
            for at in range(0, length, part):
                to = at + part
                decay = jnp.exp(jnp.minimum(col[at:to] - row[:, :to], 0.0))
                weights = (decay * gram_ref[at:to, :to]).astype(jnp.bfloat16)
                again = low_dot(weights, stepped_low[:to], 1, 0)
                row_terms.append(jnp.sum(again * grad_wide[at:to], axis=1, keepdims=True))
                back_ref[:to] += low_dot(weights, grad_low[at:to], 0, 0)
                gram_grad_ref[at:to, :to] += decay * low_dot(
                    grad_low[at:to], stepped_low[:to], 1, 1
                )
            back = back_ref[...]
            tail = jnp.exp(col[length - 1 : length] - col)
            growth = jnp.exp(col)
            ended = from_end[:, lanes] * tail
            end_terms = jnp.sum(ended * stepped, axis=1, keepdims=True)
            col_terms = jnp.sum(back * stepped_low.astype(jnp.float32), axis=1, keepdims=True)
            start_terms = growth * jnp.sum(from_start[:, lanes] * grad, axis=1, keepdims=True)
            whole = jnp.sum(end_terms, axis=0, keepdims=True) + growth[
                length - 1 : length
            ] * jnp.sum(state_dot[:, lanes], axis=1, keepdims=True)
            sum_grad_ref[0, :, head : head + 1] = (
                jnp.concatenate(row_terms, axis=0)
                + start_terms
                - col_terms
                - end_terms
                + jnp.where(last_row, whole, 0.0)
            )
            back = back + ended
            step_grad_ref[0, :, head : head + 1] = jnp.sum(back * here, axis=1, keepdims=True)
            acts_grads.append(taps_here[KW + 1 : KW + 2, lanes] * grad + back * step)
            tails.append((stepped * tail).astype(jnp.bfloat16))
            grown_grads.append((grad * growth).astype(jnp.bfloat16))
        acts_grad_ref[:, :state_dim] += low_dot(jnp.concatenate(tails, axis=1), end, 1, 1)
        acts_grad_ref[:, state_dim:] += low_dot(jnp.concatenate(grown_grads, axis=1), state, 1, 1)
        pre_grad = jnp.concatenate(acts_grads, axis=1) * silu_slope(pre, sigmoid)
        total, rows = convolved_back(extended, pre_grad, taps_here)
        gap = jnp.zeros((EXTRA - 8, wide), jnp.float32)
        in_grad_ref[...] = jnp.concatenate([total[8:], gap, total[:8]], axis=0).astype(jnp.bfloat16)
        rows.append(jnp.sum(out_grad * acts, axis=0, keepdims=True))
        rows.append(jnp.zeros((8 - len(rows), wide), jnp.float32))
        tap_grad_ref[...] = jnp.concatenate(rows, axis=0)

        @pl.when(pl.program_id(0) == pairs - 1)
        def _():
            gram_grad = gram_grad_ref[...]
            rows_of = lax.broadcasted_iota(jnp.int32, (length, length), 0)
            cols_of = lax.broadcasted_iota(jnp.int32, (length, length), 1)
            gram_grad = jnp.where(rows_of >= cols_of, gram_grad, 0.0).astype(jnp.bfloat16)
            acts_grad_ref[:, :state_dim] += low_dot(gram_grad, c_low, 0, 0)
            acts_grad_ref[:, state_dim:] += low_dot(gram_grad, b_low, 1, 0)
            bc_taps_here = bc_tap_ref[...]
            bc_extended, bc_pre = convolved(bc_rim_ref[...], bc_ref[...], bc_taps_here)
            bc_pre_grad = acts_grad_ref[...] * silu_slope(bc_pre, jax.nn.sigmoid(bc_pre))
            bc_total, bc_rows = convolved_back(bc_extended, bc_pre_grad, bc_taps_here)
            bc_grad_ref[:length] = bc_total[8:]
            bc_grad_ref[length : length + EXTRA - 8] = jnp.zeros((EXTRA - 8, shared), jnp.float32)
            bc_grad_ref[length + EXTRA - 8 :] = bc_total[:8]
            bc_rows.append(jnp.zeros((8 - len(bc_rows), shared), jnp.float32))
            bc_tap_grad_ref[...] = jnp.concatenate(bc_rows, axis=0)

    block = pl.BlockSpec((length, wide), lambda i: (0, i))
    eight = pl.BlockSpec((8, wide), lambda i: (0, i))
    table = pl.BlockSpec((1, length, 2), lambda i: (i, 0, 0))
    state_block = pl.BlockSpec((state_dim, wide), lambda i: (0, i))
    bc_block = pl.BlockSpec((length, shared), lambda i: (0, 0))
    bc_eight = pl.BlockSpec((8, shared), lambda i: (0, 0))
    wide_low = jax.ShapeDtypeStruct((length + EXTRA, inner), jnp.bfloat16)
    eight_f32 = jax.ShapeDtypeStruct((8, inner), jnp.float32)
    table_f32 = jax.ShapeDtypeStruct(step_cols.shape, jnp.float32)
    bc_f32 = jax.ShapeDtypeStruct((length + EXTRA, shared), jnp.float32)
    bc_eight_f32 = jax.ShapeDtypeStruct((8, shared), jnp.float32)
    return pl.pallas_call(
        body,
        grid=(pairs,),
        out_shape=(
            wide_low, eight_f32, table_f32, table_f32, bc_f32, bc_eight_f32
        ),
        in_specs=scan_blocks(shared, length, wide)
        + [
            block,
            pl.BlockSpec((length, wide), lambda i: (0, gate_at // wide + i)),
            state_block,
            state_block,
            bc_block,
        ],
        out_specs=(
            pl.BlockSpec((length + EXTRA, wide), lambda i: (0, i)),
            eight,
            table,
            table,
            pl.BlockSpec((length + EXTRA, shared), lambda i: (0, 0)),
            bc_eight,
        ),
        scratch_shapes=[
            pltpu.VMEM((length, length), jnp.float32),
            pltpu.VMEM((length, length), jnp.float32),
            pltpu.VMEM((length, shared), jnp.float32),
            pltpu.VMEM((length, size), jnp.float32),
        ],
        compiler_params=pltpu.CompilerParams(vmem_limit_bytes=56 << 20),
        name="scan_back",
    )(
        first_pre, first_pre, taps, mix_pre, mix_pre, bc_taps, step_cols, sum_cols, sum_rows,
        out_grads, second_pre, state_in, end_grad, bc_low,
    )


def turned(values, cos_wide, sin_wide):
    return values * cos_wide + pltpu.roll(values, values.shape[1] // 2, 1) * sin_wide


def own_mask(at, rows, keys, limit):
    query_row = lax.broadcasted_iota(jnp.int32, (rows, keys), 0) + at
    key_row = lax.broadcasted_iota(jnp.int32, (rows, keys), 1)
    return (key_row <= query_row) & (key_row < limit)


def attention_forward(layout, second_pre, query_at, window, cos_wide, sin_wide, heads):
    length = second_pre.shape[0] - EXTRA
    part = min(ATTN_ROWS, length)
    own_at = window.shape[0] - length
    scale = HD ** (-0.5)

    def body(layout_ref, query_ref, window_ref, cos_ref, sin_ref, out_ref, turned_ref, total_ref):
        query = turned(query_ref[...], cos_ref[...], sin_ref[...]).astype(jnp.bfloat16)
        turned_ref[...] = query
        for at in range(0, length, part):
            to = at + part
            here = query[at:to]

            def scores_of(keys):
                return scale * low_dot(here, keys, 1, 1)

            keys = window_ref[own_at : own_at + to, :HD]
            values = window_ref[own_at : own_at + to, HD:]
            scores = jnp.where(
                own_mask(at, part, to, layout_ref[1]), scores_of(keys), masked_score
            )
            top = jnp.max(scores, axis=1, keepdims=True)
            shares = jnp.exp(scores - top)
            total = jnp.sum(shares, axis=1, keepdims=True)
            acc = low_dot(shares, values, 1, 0)

            def earlier(distance, carry):
                top, total, acc = carry
                start = pl.multiple_of(own_at - distance * length, length)
                scores = scores_of(window_ref[pl.ds(start, length), :HD])
                new_top = jnp.maximum(top, jnp.max(scores, axis=1, keepdims=True))
                fade = jnp.exp(top - new_top)
                shares = jnp.exp(scores - new_top)
                total = fade * total + jnp.sum(shares, axis=1, keepdims=True)
                acc = fade * acc + low_dot(shares, window_ref[pl.ds(start, length), HD:], 1, 0)
                return (new_top, total, acc)

            top, total, acc = lax.fori_loop(1, layout_ref[0] + 1, earlier, (top, total, acc))
            out_ref[at:to] = (acc / total).astype(jnp.bfloat16)
            total_ref[0, at:to] = top + jnp.log(total)

    head = pl.BlockSpec((length, HD), lambda i, layout_ref: (0, i))
    whole = pl.BlockSpec((length, HD), lambda i, layout_ref: (0, 0))
    return pl.pallas_call(
        body,
        out_shape=(
            jax.ShapeDtypeStruct((length, heads * HD), jnp.bfloat16),
            jax.ShapeDtypeStruct((length, heads * HD), jnp.bfloat16),
            jax.ShapeDtypeStruct((heads, length, 1), jnp.float32),
        ),
        grid_spec=pltpu.PrefetchScalarGridSpec(
            num_scalar_prefetch=1,
            grid=(heads,),
            in_specs=[
                pl.BlockSpec((length, HD), lambda i, layout_ref: (0, query_at // HD + i)),
                pl.BlockSpec(window.shape, lambda i, layout_ref: (0, 0)),
                whole,
                whole,
            ],
            out_specs=(
                head,
                head,
                pl.BlockSpec((1, length, 1), lambda i, layout_ref: (i, 0, 0)),
            ),
        ),
        compiler_params=pltpu.CompilerParams(vmem_limit_bytes=48 << 20),
        name="attention_forward",
    )(layout, second_pre, window, cos_wide, sin_wide)


def attention_back(layout, query, window, out, totals, mixed_grad, grad_at, cos_wide, sin_wide):
    length = query.shape[0]
    heads = query.shape[1] // HD
    part = min(ATTN_ROWS, length)
    own_at = window.shape[0] - length
    scale = HD ** (-0.5)

    def body(
        layout_ref, query_ref, window_ref, out_in_ref, total_ref, grad_ref, cos_ref, sin_ref,
        query_grad_ref, window_grad_ref, own_grad_ref, sum_ref, acc_ref,
    ):
        @pl.when(pl.program_id(0) == 0)
        def _():
            sum_ref[...] = jnp.zeros_like(sum_ref)

        for at in range(0, length, part):
            to = at + part
            here = query_ref[at:to]
            grad = grad_ref[at:to].astype(jnp.bfloat16)
            dots = jnp.sum(
                grad.astype(jnp.float32) * out_in_ref[at:to].astype(jnp.float32),
                axis=1,
                keepdims=True,
            )
            total = total_ref[0, at:to]

            def step(start, count, mask):
                keys = window_ref[pl.ds(start, count), :HD]
                values = window_ref[pl.ds(start, count), HD:]
                probs = jnp.exp(scale * low_dot(here, keys, 1, 1) - total)
                if mask is not None:
                    probs = jnp.where(mask, probs, 0.0)
                score_grad = (probs * (low_dot(grad, values, 1, 1) - dots)).astype(jnp.bfloat16)
                sum_ref[pl.ds(start, count), :HD] += low_dot(score_grad, here, 0, 0)
                sum_ref[pl.ds(start, count), HD:] += low_dot(probs, grad, 0, 0)
                return low_dot(score_grad, keys, 1, 0)

            acc_ref[...] = step(own_at, to, own_mask(at, part, to, layout_ref[1]))

            def earlier(distance, carry):
                start = pl.multiple_of(own_at - distance * length, length)
                acc_ref[...] += step(start, length, None)
                return carry

            lax.fori_loop(1, layout_ref[0] + 1, earlier, 0)
            query_grad_ref[at:to] = turned(
                acc_ref[...] * scale, cos_ref[at:to], -sin_ref[at:to]
            ).astype(jnp.bfloat16)

        @pl.when(pl.program_id(0) == heads - 1)
        def _():
            own_grad_ref[:, :HD] = sum_ref[own_at:, :HD] * scale
            own_grad_ref[:, HD:] = sum_ref[own_at:, HD:]
            window_grad_ref[:, :HD] = (sum_ref[:own_at, :HD] * scale).astype(jnp.bfloat16)
            window_grad_ref[:, HD:] = sum_ref[:own_at, HD:].astype(jnp.bfloat16)

    head = pl.BlockSpec((length, HD), lambda i, layout_ref: (0, i))
    whole = pl.BlockSpec((length, HD), lambda i, layout_ref: (0, 0))
    return pl.pallas_call(
        body,
        out_shape=(
            jax.ShapeDtypeStruct(query.shape, jnp.bfloat16),
            jax.ShapeDtypeStruct((own_at, 2 * HD), jnp.bfloat16),
            jax.ShapeDtypeStruct((length, 2 * HD), jnp.float32),
        ),
        grid_spec=pltpu.PrefetchScalarGridSpec(
            num_scalar_prefetch=1,
            grid=(heads,),
            in_specs=[
                head,
                pl.BlockSpec(window.shape, lambda i, layout_ref: (0, 0)),
                head,
                pl.BlockSpec((1, length, 1), lambda i, layout_ref: (i, 0, 0)),
                pl.BlockSpec((length, HD), lambda i, layout_ref: (0, grad_at // HD + i)),
                whole,
                whole,
            ],
            out_specs=(
                head,
                pl.BlockSpec((own_at, 2 * HD), lambda i, layout_ref: (0, 0)),
                pl.BlockSpec((length, 2 * HD), lambda i, layout_ref: (0, 0)),
            ),
            scratch_shapes=[
                pltpu.VMEM(window.shape, jnp.float32),
                pltpu.VMEM((part, HD), jnp.float32),
            ],
        ),
        compiler_params=pltpu.CompilerParams(vmem_limit_bytes=56 << 20),
        name="attention_back",
    )(layout, query, window, out, totals, mixed_grad, cos_wide, sin_wide)


def per_device(
    tokens,
    cotangent,
    mix_norm_gain,
    ssm_gate_proj,
    ssm_input_proj,
    ssm_bc_proj,
    ssm_step_proj,
    conv_in_weight,
    conv_in_bias,
    conv_bc_weight,
    conv_bc_bias,
    step_bias,
    decay_log,
    skip_gain,
    ssm_out_proj,
    query_proj,
    key_proj,
    value_proj,
    attn_out_proj,
    ffn_norm_gain,
    ffn_gate_proj,
    ffn_up_proj,
    ffn_down_proj,
    extra_blocks,
    seq_order,
    pad_rows,
):
    block_rows = tokens.shape[0]
    block_index = lax.axis_index("ctx")
    seq_count = seq_order.shape[0]
    slot_ids = jnp.arange(seq_count, dtype=jnp.int32)
    chosen = (seq_order[:, None] == slot_ids[None, :]).astype(jnp.int32)
    counts = jnp.sum(chosen * extra_blocks[None, :], axis=1) + 1
    slot_pads = jnp.sum(chosen * pad_rows[None, :], axis=1)
    slot_ends = jnp.cumsum(counts)
    starts = slot_ends - counts
    inside = (starts <= block_index) & (block_index < slot_ends)
    within = jnp.sum(jnp.where(inside, block_index - starts, 0))
    pad_here = jnp.sum(jnp.where(inside & (slot_ends - 1 == block_index), slot_pads, 0))
    row_ids = jnp.arange(block_rows, dtype=jnp.int32)
    valid_rows = (row_ids < block_rows - pad_here).astype(jnp.float32)
    positions = within * block_rows + row_ids
    keep_state = (within > 0).astype(jnp.float32)
    devices = lax.axis_size("ctx")
    codes = jnp.asarray(slot_devices(devices), jnp.int32)
    from_whole = jnp.bitwise_xor(codes, block_index)
    to_whole = jnp.argsort(from_whole).astype(jnp.int32)
    rows_here = mix_norm_gain.shape[0]
    misc_here = jnp.concatenate(
        [
            ssm_step_proj,
            mix_norm_gain[:, None],
            ffn_norm_gain[:, None],
            conv_bc_weight.reshape(rows_here, 1),
            jnp.pad(conv_bc_bias, (0, rows_here - conv_bc_bias.shape[0]))[:, None],
        ],
        axis=1,
    )
    steps = ssm_step_proj.shape[1]
    misc_here = jnp.pad(misc_here, ((0, 0), (0, 128 - misc_here.shape[1])))
    inner, shared = (ssm_input_proj.shape[1], ssm_bc_proj.shape[1])
    heads_wide, pair_wide = (query_proj.shape[1], key_proj.shape[1])
    across = [4 * k for k in range(1, devices // 4)]
    mix_here = jnp.concatenate([ssm_bc_proj, misc_here, query_proj, key_proj, value_proj], axis=1)
    out_here = jnp.concatenate([ssm_out_proj, attn_out_proj], axis=0)
    first_here = jnp.concatenate([ssm_input_proj, mix_here, ssm_gate_proj], axis=1)
    first_held = spread([([0], first_here)], 0, across)
    gate_from = inner + mix_here.shape[1]
    input_held = spread([(here, piece[:, :inner]) for here, piece in first_held], 0, [1], merge=True)
    mix_held = [(here, piece[:, inner:gate_from]) for here, piece in first_held]
    mix_held = spread(mix_held, 0, [2], merge=True)
    gate_held = [(here, piece[:, gate_from:]) for here, piece in first_held]
    near = (input_held[-1][1], mix_held[-1][1])
    input_held = spread(input_held, 0, [2])
    mix_held = spread(mix_held, 0, [1])
    ffn_here = lax.optimization_barrier((ffn_gate_proj, ffn_up_proj, ffn_down_proj, *near))[:3]
    ffn_gate_weight = lax.all_gather(ffn_here[0], "ctx", axis=0, tiled=True)
    ffn_up_weight = lax.all_gather(ffn_here[1], "ctx", axis=0, tiled=True)
    ffn_down_weight = lax.all_gather(ffn_here[2], "ctx", axis=1, tiled=True)
    out_held = spread([([0], out_here)], 1, across, near)
    input_weight = joined(input_held, 0)
    mix_weights = joined(mix_held, 0)
    misc = mix_weights[:, shared : shared + 128]
    mix_gain = misc[:, steps].astype(jnp.float32)

    def whole_order(column):
        return jnp.take(column.reshape(devices, rows_here), to_whole, axis=0)

    conv_bc_full = whole_order(misc[:, steps + 2]).reshape(shared, KW)
    conv_bc_offset = whole_order(misc[:, steps + 3])[:, : conv_bc_bias.shape[0]].reshape(shared)
    gain_two = whole_order(misc[:, steps + 1]).reshape(-1)
    inputs = tokens.astype(jnp.float32)
    rim_rows = KW - 1
    edge = shifted(tokens[block_rows - EXTRA :], "ctx", 1)
    edge_rows = jnp.arange(EXTRA, dtype=jnp.int32)[:, None] >= EXTRA - rim_rows
    edge = jnp.where(edge_rows & (within > 0), edge, jnp.zeros_like(edge))
    tokens_longer = jnp.concatenate([tokens, edge], axis=0)
    normed_low = rms_scale(
        reordered(tokens_longer, from_whole).astype(jnp.float32), mix_gain
    ).astype(jnp.bfloat16)
    first_pre = plain_product(normed_low, input_weight)
    mix_pre = plain_product(normed_low, mix_weights)
    step_raw = mix_pre[:block_rows, shared : shared + steps]
    query_at = shared + 128
    key_at = query_at + heads_wide
    key_pre = mix_pre[:block_rows, key_at : key_at + pair_wide]
    value_pre = mix_pre[:block_rows, key_at + pair_wide :]
    gate_held = spread(gate_held, 0, [2], (first_pre,), merge=True)
    out_held = spread(out_held, 1, [1], (first_pre,), merge=True)
    head_dim = inner // steps
    skips = jnp.repeat(skip_gain.astype(jnp.float32), head_dim)[None, :]
    taps = jnp.concatenate(
        [conv_in_weight.astype(jnp.float32).T, conv_in_bias.astype(jnp.float32)[None, :], skips]
    )
    taps = jnp.pad(taps, ((0, 8 - taps.shape[0]), (0, 0)))
    bc_taps = jnp.concatenate(
        [conv_bc_full.astype(jnp.float32).T, conv_bc_offset.astype(jnp.float32)[None, :]]
    )
    bc_taps = jnp.pad(bc_taps, ((0, 8 - bc_taps.shape[0]), (0, 0)))
    step_in = step_raw + step_bias.astype(jnp.float32)[None, :]
    step_size = jax.nn.softplus(step_in)
    rate = -jnp.exp(decay_log.astype(jnp.float32))[None, :]
    lower = (row_ids[:, None] >= row_ids[None, :]).astype(jnp.float32)
    log_decay = jnp.dot(lower, rate * step_size, precision=highest)

    def by_pairs(table):
        return table.reshape(block_rows, steps // 2, 2).transpose(1, 0, 2)

    def from_pairs(table):
        return table.transpose(1, 0, 2).reshape(block_rows, steps)

    step_cols = by_pairs(step_size)
    sum_cols = by_pairs(log_decay)
    sum_rows = log_decay.T.reshape(steps // 2, 2, block_rows)
    intra_out, local_states, bc_low = scan_forward(
        first_pre, mix_pre, taps, bc_taps, step_cols, sum_cols, sum_rows, inner, shared
    )
    decay_row = keep_state * jnp.repeat(jnp.exp(log_decay[block_rows - 1]), head_dim)[None, :]
    keep_low = keep_state.astype(jnp.bfloat16)
    reached, returned = carried_states(local_states, decay_row, False)
    state_in = keep_low * reached
    gate_held = spread(gate_held, 0, [1], (returned,))
    out_held = spread(out_held, 1, [2], (returned,))
    cos_table, sin_table = rotary_tables(positions)
    cos_wide = jnp.concatenate([cos_table, cos_table], axis=1)
    sin_wide = jnp.concatenate([-sin_table, sin_table], axis=1)
    key_rot = rotate(key_pre.reshape(block_rows, -1, HD), cos_table, sin_table)
    own_pair = jnp.concatenate(
        [key_rot.reshape(block_rows, HD).astype(jnp.bfloat16), value_pre.astype(jnp.bfloat16)],
        axis=1,
    )
    earlier_pairs = [shifted(own_pair, "ctx", distance) for distance in range(MAXB - 1, 0, -1)]
    window = jnp.concatenate(earlier_pairs + [own_pair], axis=0)
    layout = jnp.stack([within, block_rows - pad_here]).astype(jnp.int32)
    attn_low, query_rot, log_totals = attention_forward(
        layout, mix_pre, query_at, window, cos_wide, sin_wide, heads_wide // HD
    )
    gate_weight = joined(gate_held, 0)
    gate_pre = plain_product(normed_low, gate_weight)
    scan_out, ssm_low = scan_gated(intra_out, state_in, bc_low, sum_cols, gate_pre, 0)
    out_weights = joined(out_held, 1)
    mixed_low = jnp.concatenate([ssm_low, attn_low], axis=1)
    mixed_part = plain_product(mixed_low, out_weights)
    hidden = inputs + reordered(pair_sum(mixed_part), to_whole)
    normed_two, norm_two_back = jax.vjp(rms_scale, hidden, gain_two.astype(jnp.float32))
    normed_two_low = normed_two.astype(jnp.bfloat16)
    ffn_gate = plain_product(normed_two_low, ffn_gate_weight)
    ffn_up = plain_product(normed_two_low, ffn_up_weight)
    ffn_act = (jax.nn.silu(ffn_gate) * ffn_up).astype(jnp.bfloat16)
    ffn_part = plain_product(ffn_act, ffn_down_weight)
    ffn_sum = pair_sum(ffn_part)
    layer_out = ((hidden + ffn_sum) * valid_rows[:, None]).astype(jnp.bfloat16)
    cot_low = (cotangent.astype(jnp.float32) * valid_rows[:, None]).astype(jnp.bfloat16)
    grad_out = cot_low.astype(jnp.float32)

    def in_quarters(value):
        return jnp.split(value, 4, axis=1)

    def rows_grad(left_side, right_side, first, gates=()):
        parts = [product_of_cols(part, right_side) for part in in_quarters(left_side)]
        return Reduction(parts, 0, first, gates)

    def cols_grad(left_side, right_side, first, gates=()):
        parts = [product_of_cols(left_side, part) for part in in_quarters(right_side)]
        return Reduction(parts, 1, first, gates)

    ffn_down_grad = lax.psum_scatter(
        product_of_cols(ffn_act, cot_low).astype(jnp.bfloat16), "ctx", scatter_dimension=1, tiled=True
    )
    act_grad = product_by_rows(cot_low, ffn_down_weight)
    gate_sigmoid = jax.nn.sigmoid(ffn_gate)
    ffn_gate_low = (
        act_grad * ffn_up * gate_sigmoid * (1.0 + ffn_gate * (1.0 - gate_sigmoid))
    ).astype(jnp.bfloat16)
    ffn_up_low = (act_grad * jax.nn.silu(ffn_gate)).astype(jnp.bfloat16)
    norm_two_part = product_by_rows(ffn_gate_low, ffn_gate_weight) + product_by_rows(
        ffn_up_low, ffn_up_weight
    )
    norm_two_grad = pair_sum(norm_two_part)
    hidden_norm_grad, gain_two_grad = norm_two_back(norm_two_grad)
    hidden_grad = grad_out + hidden_norm_grad
    hidden_low = reordered(hidden_grad.astype(jnp.bfloat16), from_whole)
    mixed_grad = product_by_rows(hidden_low, out_weights)
    ssm_gate_low, state_in_grad = scan_gated_back(
        mixed_grad, scan_out, bc_low, sum_cols, gate_pre, 0
    )
    end_grad, returned = carried_states(keep_low * state_in_grad, decay_row, True)
    gate_late, up_late = lax.optimization_barrier((ffn_gate_low, ffn_up_low, ssm_gate_low))[:2]
    ffn_gate_grad = lax.psum_scatter(
        product_of_cols(normed_two_low, gate_late).astype(jnp.bfloat16),
        "ctx",
        scatter_dimension=0,
        tiled=True,
    )
    layout = after(layout, returned)
    query_grad_low, window_grad, own_pair_grad = attention_back(
        layout, query_rot, window, attn_low, log_totals, mixed_grad, inner, cos_wide, sin_wide
    )
    for distance in range(1, MAXB):
        at = (MAXB - 1 - distance) * block_rows
        own_pair_grad = own_pair_grad + shifted(
            window_grad[at : at + block_rows], "ctx", -distance
        ).astype(jnp.float32)
    up_sum = rows_grad(
        reordered(normed_two_low, from_whole), up_late, 1, (end_grad, query_grad_low)
    )
    out_sum = cols_grad(mixed_low, hidden_low, 1, (end_grad, query_grad_low))
    gate_sum = rows_grad(normed_low, ssm_gate_low, 2, (end_grad, query_grad_low))
    key_grad_low = (
        rotate(own_pair_grad[:, :HD].reshape(block_rows, 1, HD), cos_table, -sin_table)
        .reshape(block_rows, HD)
        .astype(jnp.bfloat16)
    )
    value_grad_low = own_pair_grad[:, HD:].astype(jnp.bfloat16)
    input_grad_low, tap_grad, step_part, sum_part, bc_pre_part, bc_tap_grad = scan_back(
        first_pre, mix_pre, taps, bc_taps, step_cols, sum_cols, sum_rows,
        mixed_grad, gate_pre, 0, state_in, end_grad, bc_low,
    )
    up_sum.onward(input_grad_low)
    out_sum.onward(input_grad_low)
    gate_sum.onward(input_grad_low)
    rate_grad = lax.dot_general(
        lower, from_pairs(sum_part), (((0,), (0,)), ((), ())), precision=highest
    )
    step_grad = (from_pairs(step_part) + rate * rate_grad) * jax.nn.sigmoid(step_in)
    step_grad_low = step_grad.astype(jnp.bfloat16)
    tap_sums = [
        tap_grad[:KW].T,
        tap_grad[KW],
        jnp.sum(step_grad, axis=0),
        jnp.sum(rate_grad * rate * step_size, axis=0),
        jnp.sum(tap_grad[KW + 1].reshape(steps, head_dim), axis=1),
    ]
    no_misc = jnp.zeros((block_rows, 128 - steps), jnp.bfloat16)
    mix_grads = jnp.concatenate(
        [step_grad_low, no_misc, query_grad_low, key_grad_low, value_grad_low], axis=1
    )
    mix_grads = jnp.pad(mix_grads, ((0, EXTRA), (0, 0)))
    bc_grad_low = pair_sum(bc_pre_part).astype(jnp.bfloat16)
    input_sum = rows_grad(normed_low, input_grad_low, 1)
    mix_sum = rows_grad(normed_low, jnp.concatenate([bc_grad_low, mix_grads], axis=1), 2)
    mix_grads = jnp.concatenate([bc_pre_part.astype(jnp.bfloat16), mix_grads], axis=1)
    norm_one_part = (
        product_by_rows(input_grad_low, input_weight)
        + product_by_rows(mix_grads, mix_weights)
        + product_by_rows(ssm_gate_low, gate_weight)
    )
    up_sum.last(norm_one_part)
    out_sum.last(norm_one_part)
    gate_sum.last(norm_one_part)
    input_sum.onward(norm_one_part)
    mix_sum.onward(norm_one_part)
    norm_one_grad = reordered(pair_sum(norm_one_part), to_whole)
    conv_bc_grads = jnp.concatenate([bc_tap_grad[:KW].T.reshape(-1), bc_tap_grad[KW]])
    conv_bc_grads = conv_bc_grads + swap(conv_bc_grads)
    longer = tokens_longer.astype(jnp.float32)
    scale_one = lax.rsqrt(jnp.mean(longer * longer, axis=1, keepdims=True) + epsilon)
    gain_one_grad = jnp.sum(norm_one_grad * longer * scale_one, axis=0)
    edge_back = shifted(keep_state * norm_one_grad[block_rows + EXTRA - 8 :], "ctx", -1)
    norm_one_grad = norm_one_grad[:block_rows] + jnp.pad(edge_back, ((block_rows - 8, 0), (0, 0)))
    _, norm_one_back = jax.vjp(lambda v: rms_scale(v, whole_order(mix_gain).reshape(-1)), inputs)
    tokens_grad = hidden_grad + norm_one_back(norm_one_grad)[0]
    small = [
        tap_sums[0].reshape(-1),
        *tap_sums[1:],
        conv_bc_grads,
        gain_one_grad,
        gain_two_grad,
    ]
    packed = jnp.concatenate(small)
    filled = -packed.shape[0] % 1024
    packed = summed(jnp.pad(packed, (0, filled)).reshape(-1, 128)).reshape(-1)
    sums, at = ([], 0)
    for part in small:
        sums.append(packed[at : at + part.shape[0]])
        at += part.shape[0]

    def own(vector, count):
        return lax.dynamic_slice_in_dim(vector, block_index * count, count, 0)

    input_sum.last()
    mix_sum.last()
    mix_grad = mix_sum.total()
    out_grad = out_sum.total()
    conv_bc_sums = sums[5]
    conv_rows = conv_bc_weight.shape[0]
    return (
        layer_out,
        tokens_grad.astype(jnp.bfloat16),
        own(sums[6], rows_here),
        gate_sum.total(),
        input_sum.total(),
        mix_grad[:, :shared],
        mix_grad[:, shared : shared + steps],
        sums[0].reshape(inner, KW),
        sums[1],
        own(conv_bc_sums[: shared * KW], conv_rows * KW).reshape(conv_rows, KW),
        own(conv_bc_sums[shared * KW :], conv_rows),
        sums[2],
        sums[3],
        sums[4],
        out_grad[:inner],
        mix_grad[:, query_at:key_at],
        mix_grad[:, key_at : key_at + pair_wide],
        mix_grad[:, key_at + pair_wide :],
        out_grad[inner:],
        own(sums[7], rows_here),
        ffn_gate_grad.astype(jnp.float32),
        up_sum.total(),
        ffn_down_grad.astype(jnp.float32),
    )


def solution(mesh):
    return jax.shard_map(
        per_device,
        mesh=mesh,
        in_specs=(
            P("ctx", None),
            P("ctx", None),
            P("ctx"),
            P("ctx", "wt"),
            P("ctx", "wt"),
            P("ctx", None),
            P("ctx", "wt"),
            P("wt", None),
            P("wt"),
            P("ctx", None),
            P("ctx"),
            P("wt"),
            P("wt"),
            P("wt"),
            P("wt", "ctx"),
            P("ctx", "wt"),
            P("ctx", "wt"),
            P("ctx", "wt"),
            P("wt", "ctx"),
            P("ctx"),
            P("ctx", "wt"),
            P("ctx", "wt"),
            P("wt", "ctx"),
            P(),
            P(),
            P(),
        ),
        out_specs=(
            P("ctx", None),
            P("ctx", None),
            P("ctx"),
            P("ctx", "wt"),
            P("ctx", "wt"),
            P("ctx", None),
            P("ctx", "wt"),
            P("wt", None),
            P("wt"),
            P("ctx", None),
            P("ctx"),
            P("wt"),
            P("wt"),
            P("wt"),
            P("wt", "ctx"),
            P("ctx", "wt"),
            P("ctx", "wt"),
            P("ctx", "wt"),
            P("wt", "ctx"),
            P("ctx"),
            P("ctx", "wt"),
            P("ctx", "wt"),
            P("wt", "ctx"),
        ),
        check_vma=False,
    )
```

```python
import jax
import jax.numpy as jnp
from jax import lax
from jax.experimental import pallas as pl
from jax.experimental.pallas import tpu as pltpu
from jax.sharding import PartitionSpec as P


HD = 128
KW = 4
MAXB = 8
EXTRA = 16
SCAN_ROWS = 128
ATTN_ROWS = 256


epsilon = 1e-05
rope_base = 100000000000.0
highest = lax.Precision.HIGHEST
masked_score = -1e30


def shifted(value, axis, steps):
    count = lax.axis_size(axis)
    leading, last = (max(0, -steps), min(count, count - steps))
    return lax.ppermute(value, axis, [(source, source + steps) for source in range(leading, last)])


def hop(value, code):
    if code == 0:
        return value
    count = lax.axis_size("ctx")
    return lax.ppermute(value, "ctx", [(source, source ^ code) for source in range(count)])


def swap(value):
    return lax.ppermute(value, "wt", [(0, 1), (1, 0)])


def pair_sum(value):
    rounded = lax.reduce_precision(value, 8, 7)
    return rounded + swap(rounded.astype(jnp.bfloat16)).astype(jnp.float32)


def slot_devices(count):
    high = count // 4
    return [4 * (slot % high) + slot // high for slot in range(count)]


def after(value, *gates):
    return lax.optimization_barrier((value, *gates))[0]


def spread(held, axis, codes, gates=(), merge=False):
    if merge:
        every = [code for here, _ in held for code in here]
        held = [(every, jnp.concatenate([array for _, array in held], axis=axis))]
    taken = list(held)
    for here, array in held:
        operand = after(array, *gates) if gates else array
        for code in codes:
            taken.append(([one ^ code for one in here], hop(operand, code)))
    return taken


def joined(held, axis):
    size = sum(array.shape[axis] for _, array in held) // sum(len(here) for here, _ in held)
    found = {code: (i, at) for i, (here, _) in enumerate(held) for at, code in enumerate(here)}
    runs = []
    for code in slot_devices(len(found)):
        i, at = found[code]
        if runs and runs[-1][0] == i and runs[-1][2] == at:
            runs[-1][2] = at + 1
        else:
            runs.append([i, at, at + 1])
    return jnp.concatenate(
        [lax.slice_in_dim(held[i][1], at * size, to * size, axis=axis) for i, at, to in runs],
        axis=axis,
    )


class Reduction:
    def __init__(self, parts, axis, first, gates=()):
        self.axis, self.second = (axis, 3 - first)
        self.near, self.far = (parts[0], parts[3 - first])
        low = [parts[k].astype(jnp.bfloat16) for k in (first, 3)]
        if gates:
            low = lax.optimization_barrier((*low, *gates))[:2]
        self.got = [hop(part, first) for part in low]

    def onward(self, *gates):
        got = lax.optimization_barrier((*self.got, *gates))[:2] if gates else self.got
        self.far_low = (self.far + got[1].astype(jnp.float32)).astype(jnp.bfloat16)
        self.near = self.near + got[0].astype(jnp.float32)
        self.got = [hop(self.far_low, self.second)]

    def last(self, *gates):
        high = lax.axis_size("ctx") // 4
        got = after(self.got[0], *gates) if gates else self.got[0]
        quarter = self.near + got.astype(jnp.float32)
        blocks = jnp.split(quarter, high, axis=self.axis)
        self.block = blocks[0]
        self.blocks_low = [block.astype(jnp.bfloat16) for block in blocks[1:]]
        self.got = [hop(block, 4 * (k + 1)) for k, block in enumerate(self.blocks_low)]

    def total(self):
        total = self.block
        for got in self.got:
            total = total + got.astype(jnp.float32)
        return total


def summed(value):
    bit = 1
    while bit < lax.axis_size("ctx"):
        value = value + hop(value, bit)
        bit *= 2
    return value


def reordered(value, order):
    blocks = order.shape[0]
    rows, width = value.shape[0], value.shape[1] // blocks
    if width % 128:
        return jnp.take(value.reshape(rows, blocks, width), order, axis=1).reshape(rows, -1)

    steps = 4 if rows % 64 == 0 else 3
    part = rows // steps

    def body(order_ref, in_ref, out_ref):
        for slot in range(blocks):
            start = pl.multiple_of(order_ref[slot] * width, width)
            out_ref[:, slot * width : (slot + 1) * width] = in_ref[:, pl.ds(start, width)]

    block = pl.BlockSpec((part, value.shape[1]), lambda i, order_ref: (i, 0))
    return pl.pallas_call(
        body,
        out_shape=jax.ShapeDtypeStruct(value.shape, value.dtype),
        grid_spec=pltpu.PrefetchScalarGridSpec(
            num_scalar_prefetch=1, grid=(steps,), in_specs=[block], out_specs=block
        ),
        name="reordered",
    )(order, value)


def carried_states(states, decays, reverse):
    me = lax.axis_index("ctx")
    place = me % 4
    width = states.shape[1] // 4
    low = states.astype(jnp.bfloat16)

    def quarter(value, index):
        return lax.dynamic_slice_in_dim(value, index * width, width, 1)

    got = [hop(quarter(low, place ^ k), k) for k in range(4)]
    got_decay = [hop(quarter(decays, place ^ k), k) for k in range(4)]

    def in_order(pieces):
        odd = place % 2 == 1
        pieces = [jnp.where(odd, pieces[k ^ 1], pieces[k]) for k in range(4)]
        upper = place >= 2
        return [jnp.where(upper, pieces[k ^ 2], pieces[k]) for k in range(4)]

    blocks = [piece.astype(jnp.float32) for piece in in_order(got)]
    rates = in_order(got_decay)
    if reverse:
        blocks, rates = (blocks[::-1], rates[::-1])
    total, rate = (blocks[0], rates[0])
    for block, block_rate in zip(blocks[1:], rates[1:]):
        total, rate = (block + block_rate * total, block_rate * rate)
    step = -4 if reverse else 4
    total_low = total.astype(jnp.bfloat16)
    near, near_rate = (shifted(total_low, "ctx", step), shifted(rate, "ctx", step))
    far = shifted(total_low, "ctx", 2 * step)
    state = near.astype(jnp.float32) + near_rate * far.astype(jnp.float32)
    reached = []
    for block, block_rate in zip(blocks, rates):
        reached.append(state.astype(jnp.bfloat16))
        state = block + block_rate * state
    if reverse:
        reached = reached[::-1]
    mine = in_order(reached)
    back = in_order([hop(mine[k], k) for k in range(4)])
    return (jnp.concatenate(back, axis=1), mine[1])


def plain_product(left_side, right_side):
    return jnp.dot(left_side, right_side, preferred_element_type=jnp.float32)


def product_by_rows(left_side, right_side):
    return lax.dot_general(
        left_side, right_side, (((1,), (1,)), ((), ())), preferred_element_type=jnp.float32
    )


def product_of_cols(left_side, right_side):
    return lax.dot_general(
        left_side, right_side, (((0,), (0,)), ((), ())), preferred_element_type=jnp.float32
    )


def rms_scale(values, gain_vec):
    return (
        values * lax.rsqrt(jnp.mean(values * values, axis=-1, keepdims=True) + epsilon) * gain_vec
    )


def rotary_tables(positions):
    exponents = jnp.arange(HD // 2, dtype=jnp.float32) * (2.0 / HD)
    frequency = jnp.power(jnp.float32(rope_base), -exponents)
    angles = positions.astype(jnp.float32)[:, None] * frequency[None, :]
    return (jnp.cos(angles), jnp.sin(angles))


def rotate(values, cos_table, sin_table):
    half_dim = values.shape[-1] // 2
    first_half = values[..., :half_dim]
    second_half = values[..., half_dim:]
    cos_table = cos_table[:, None, :]
    sin_table = sin_table[:, None, :]
    return jnp.concatenate(
        [
            first_half * cos_table - second_half * sin_table,
            second_half * cos_table + first_half * sin_table,
        ],
        axis=-1,
    )


def convolved(rim, block, taps):
    length = block.shape[0]
    extended = jnp.concatenate([rim, block], axis=0)
    first = rim.shape[0] - (KW - 1)
    summed = taps[KW : KW + 1]
    for j in range(KW):
        summed = summed + extended[first + j : first + j + length] * taps[j : j + 1]
    return (extended, summed)


def convolved_back(extended, pre_grad, taps):
    length = pre_grad.shape[0]
    rim_rows = extended.shape[0] - length
    first = rim_rows - (KW - 1)
    zeros = jnp.zeros((8, pre_grad.shape[1]), jnp.float32)
    padded = jnp.concatenate([zeros, pre_grad, zeros], axis=0)
    total = jnp.zeros_like(extended)
    rows = []
    for j in range(KW):
        start = 8 - rim_rows + KW - 1 - j
        total = total + padded[start : start + rim_rows + length] * taps[j : j + 1]
        rows.append(
            jnp.sum(pre_grad * extended[first + j : first + j + length], axis=0, keepdims=True)
        )
    rows.append(jnp.sum(pre_grad, axis=0, keepdims=True))
    return (total, rows)


def silu_slope(value, sigmoid):
    return sigmoid * (1.0 + value * (1.0 - sigmoid))


def low_dot(left_side, right_side, left_axis, right_axis):
    return lax.dot_general(
        left_side.astype(jnp.bfloat16),
        right_side.astype(jnp.bfloat16),
        (((left_axis,), (right_axis,)), ((), ())),
        preferred_element_type=jnp.float32,
    )


def lower_gram(c_low, b_low):
    length = c_low.shape[0]
    gram = low_dot(c_low, b_low, 1, 1)
    rows = lax.broadcasted_iota(jnp.int32, (length, length), 0)
    cols = lax.broadcasted_iota(jnp.int32, (length, length), 1)
    return jnp.where(rows >= cols, gram, 0.0)


def scan_blocks(shared, length, wide):
    return [
        pl.BlockSpec((length, wide), lambda i: (0, i)),
        pl.BlockSpec((8, wide), lambda i: ((length + EXTRA) // 8 - 1, i)),
        pl.BlockSpec((8, wide), lambda i: (0, i)),
        pl.BlockSpec((length, shared), lambda i: (0, 0)),
        pl.BlockSpec((8, shared), lambda i: ((length + EXTRA) // 8 - 1, 0)),
        pl.BlockSpec((8, shared), lambda i: (0, 0)),
        pl.BlockSpec((1, length, 2), lambda i: (i, 0, 0)),
        pl.BlockSpec((1, length, 2), lambda i: (i, 0, 0)),
        pl.BlockSpec((1, 2, length), lambda i: (i, 0, 0)),
    ]


def scan_forward(first_pre, mix_pre, taps, bc_taps, step_cols, sum_cols, sum_rows, inner, shared):
    length = first_pre.shape[0] - EXTRA
    pairs = step_cols.shape[0]
    wide = inner // pairs
    size = wide // 2
    state_dim = shared // 2
    part = min(SCAN_ROWS, length)

    def body(
        in_ref, rim_ref, tap_ref, bc_ref, bc_rim_ref, bc_tap_ref, step_ref, col_ref, row_ref,
        out_ref, state_ref, bc_low_ref, gram_ref,
    ):
        @pl.when(pl.program_id(0) == 0)
        def _():
            _, pre = convolved(bc_rim_ref[...], bc_ref[...], bc_tap_ref[...])
            acts = (pre * jax.nn.sigmoid(pre)).astype(jnp.bfloat16)
            bc_low_ref[...] = acts
            gram_ref[...] = lower_gram(acts[:, state_dim:], acts[:, :state_dim])

        taps_here = tap_ref[...]
        _, pre = convolved(rim_ref[...], in_ref[...], taps_here)
        acts = pre * jax.nn.sigmoid(pre)
        tails = []
        for head in range(2):
            lanes = slice(head * size, (head + 1) * size)
            step = step_ref[0][:, head : head + 1]
            col = col_ref[0][:, head : head + 1]
            row = row_ref[0][head : head + 1, :]
            stepped = acts[:, lanes] * step
            stepped_low = stepped.astype(jnp.bfloat16)
            for at in range(0, length, part):
                end = at + part
                decay = jnp.exp(jnp.minimum(col[at:end] - row[:, :end], 0.0))
                weights = (decay * gram_ref[at:end, :end]).astype(jnp.bfloat16)
                out_ref[at:end, lanes] = low_dot(weights, stepped_low[:end], 1, 0) + (
                    taps_here[KW + 1 : KW + 2, lanes] * acts[at:end, lanes]
                )
            tails.append(stepped * jnp.exp(col[length - 1 : length] - col))
        tail = jnp.concatenate(tails, axis=1)
        state_ref[...] = low_dot(bc_low_ref[:, :state_dim], tail, 0, 0).astype(jnp.bfloat16)

    return pl.pallas_call(
        body,
        grid=(pairs,),
        out_shape=(
            jax.ShapeDtypeStruct((length, inner), jnp.float32),
            jax.ShapeDtypeStruct((state_dim, inner), jnp.bfloat16),
            jax.ShapeDtypeStruct((length, shared), jnp.bfloat16),
        ),
        in_specs=scan_blocks(shared, length, wide),
        out_specs=(
            pl.BlockSpec((length, wide), lambda i: (0, i)),
            pl.BlockSpec((state_dim, wide), lambda i: (0, i)),
            pl.BlockSpec((length, shared), lambda i: (0, 0)),
        ),
        scratch_shapes=[pltpu.VMEM((length, length), jnp.float32)],
        compiler_params=pltpu.CompilerParams(vmem_limit_bytes=48 << 20),
        name="scan_forward",
    )(first_pre, first_pre, taps, mix_pre, mix_pre, bc_taps, step_cols, sum_cols, sum_rows)


def scan_gated(intra, state_in, bc_low, sum_cols, second_pre, gate_at):
    length, inner = intra.shape
    pairs = sum_cols.shape[0]
    wide = inner // pairs
    size = wide // 2
    state_dim = bc_low.shape[1] // 2

    def body(intra_ref, state_ref, c_ref, col_ref, gate_ref, out_ref, act_ref):
        carried = low_dot(c_ref[...], state_ref[...], 1, 0)
        gate = gate_ref[...]
        silu = gate * jax.nn.sigmoid(gate)
        for head in range(2):
            lanes = slice(head * size, (head + 1) * size)
            growth = jnp.exp(col_ref[0][:, head : head + 1])
            whole = intra_ref[:, lanes] + carried[:, lanes] * growth
            out_ref[:, lanes] = whole
            act_ref[:, lanes] = (whole * silu[:, lanes]).astype(jnp.bfloat16)

    block = pl.BlockSpec((length, wide), lambda i: (0, i))
    return pl.pallas_call(
        body,
        grid=(pairs,),
        out_shape=(
            jax.ShapeDtypeStruct((length, inner), jnp.float32),
            jax.ShapeDtypeStruct((length, inner), jnp.bfloat16),
        ),
        in_specs=[
            block,
            pl.BlockSpec((state_dim, wide), lambda i: (0, i)),
            pl.BlockSpec((length, state_dim), lambda i: (0, 1)),
            pl.BlockSpec((1, length, 2), lambda i: (i, 0, 0)),
            pl.BlockSpec((length, wide), lambda i: (0, gate_at // wide + i)),
        ],
        out_specs=(block, block),
        compiler_params=pltpu.CompilerParams(vmem_limit_bytes=48 << 20),
        name="scan_gated",
    )(intra, state_in, bc_low, sum_cols, second_pre)


def scan_gated_back(out_grads, whole, bc_low, sum_cols, second_pre, gate_at):
    length, inner = whole.shape
    pairs = sum_cols.shape[0]
    wide = inner // pairs
    size = wide // 2
    state_dim = bc_low.shape[1] // 2

    def body(grad_ref, whole_ref, c_ref, col_ref, gate_ref, gate_grad_ref, state_ref):
        gate = gate_ref[...]
        sigmoid = jax.nn.sigmoid(gate)
        grad = grad_ref[...]
        gate_grad = grad * whole_ref[...] * silu_slope(gate, sigmoid)
        gate_grad_ref[:length] = gate_grad.astype(jnp.bfloat16)
        gate_grad_ref[length:] = jnp.zeros((EXTRA, wide), jnp.bfloat16)
        inside = grad * (gate * sigmoid)
        grown = [
            inside[:, head * size : (head + 1) * size] * jnp.exp(col_ref[0][:, head : head + 1])
            for head in range(2)
        ]
        state_ref[...] = low_dot(c_ref[...], jnp.concatenate(grown, axis=1), 0, 0).astype(
            jnp.bfloat16
        )

    block = pl.BlockSpec((length, wide), lambda i: (0, i))
    return pl.pallas_call(
        body,
        grid=(pairs,),
        out_shape=(
            jax.ShapeDtypeStruct((length + EXTRA, inner), jnp.bfloat16),
            jax.ShapeDtypeStruct((state_dim, inner), jnp.bfloat16),
        ),
        in_specs=[
            block,
            block,
            pl.BlockSpec((length, state_dim), lambda i: (0, 1)),
            pl.BlockSpec((1, length, 2), lambda i: (i, 0, 0)),
            pl.BlockSpec((length, wide), lambda i: (0, gate_at // wide + i)),
        ],
        out_specs=(
            pl.BlockSpec((length + EXTRA, wide), lambda i: (0, i)),
            pl.BlockSpec((state_dim, wide), lambda i: (0, i)),
        ),
        compiler_params=pltpu.CompilerParams(vmem_limit_bytes=48 << 20),
        name="scan_gated_back",
    )(out_grads, whole, bc_low, sum_cols, second_pre)


def scan_back(
    first_pre, mix_pre, taps, bc_taps, step_cols, sum_cols, sum_rows,
    out_grads, second_pre, gate_at, state_in, end_grad, bc_low,
):
    length = first_pre.shape[0] - EXTRA
    pairs = step_cols.shape[0]
    state_dim, inner = state_in.shape
    shared = bc_low.shape[1]
    wide = inner // pairs
    size = wide // 2
    part = min(SCAN_ROWS, length)

    def body(
        in_ref, rim_ref, tap_ref, bc_ref, bc_rim_ref, bc_tap_ref, step_ref, col_ref, row_ref,
        grad_ref, gate_ref, state_ref, end_ref, bc_low_ref,
        in_grad_ref, tap_grad_ref, step_grad_ref, sum_grad_ref, bc_grad_ref, bc_tap_grad_ref,
        gram_ref, gram_grad_ref, acts_grad_ref, back_ref,
    ):
        b_low = bc_low_ref[:, :state_dim]
        c_low = bc_low_ref[:, state_dim:]

        @pl.when(pl.program_id(0) == 0)
        def _():
            gram_ref[...] = lower_gram(c_low, b_low)
            gram_grad_ref[...] = jnp.zeros_like(gram_grad_ref)
            acts_grad_ref[...] = jnp.zeros_like(acts_grad_ref)

        taps_here = tap_ref[...]
        extended, pre = convolved(rim_ref[...], in_ref[...], taps_here)
        sigmoid = jax.nn.sigmoid(pre)
        acts = pre * sigmoid
        gate = gate_ref[...]
        out_grad = grad_ref[...] * (gate * jax.nn.sigmoid(gate))
        state = state_ref[...]
        end = end_ref[...]
        from_end = low_dot(b_low, end, 1, 0)
        from_start = low_dot(c_low, state, 1, 0)
        state_dot = jnp.sum(
            state.astype(jnp.float32) * end.astype(jnp.float32), axis=0, keepdims=True
        )
        last_row = lax.broadcasted_iota(jnp.int32, (length, 1), 0) == length - 1
        acts_grads, tails, grown_grads = ([], [], [])
        for head in range(2):
            lanes = slice(head * size, (head + 1) * size)
            step = step_ref[0][:, head : head + 1]
            col = col_ref[0][:, head : head + 1]
            row = row_ref[0][head : head + 1, :]
            here = acts[:, lanes]
            stepped = here * step
            stepped_low = stepped.astype(jnp.bfloat16)
            grad = out_grad[:, lanes]
            grad_low = grad.astype(jnp.bfloat16)
            grad_wide = grad_low.astype(jnp.float32)
            back_ref[...] = jnp.zeros_like(back_ref)
            row_terms = []
            for at in range(0, length, part):
                to = at + part
                decay = jnp.exp(jnp.minimum(col[at:to] - row[:, :to], 0.0))
                weights = (decay * gram_ref[at:to, :to]).astype(jnp.bfloat16)
                again = low_dot(weights, stepped_low[:to], 1, 0)
                row_terms.append(jnp.sum(again * grad_wide[at:to], axis=1, keepdims=True))
                back_ref[:to] += low_dot(weights, grad_low[at:to], 0, 0)
                gram_grad_ref[at:to, :to] += decay * low_dot(
                    grad_low[at:to], stepped_low[:to], 1, 1
                )
            back = back_ref[...]
            tail = jnp.exp(col[length - 1 : length] - col)
            growth = jnp.exp(col)
            ended = from_end[:, lanes] * tail
            end_terms = jnp.sum(ended * stepped, axis=1, keepdims=True)
            col_terms = jnp.sum(back * stepped_low.astype(jnp.float32), axis=1, keepdims=True)
            start_terms = growth * jnp.sum(from_start[:, lanes] * grad, axis=1, keepdims=True)
            whole = jnp.sum(end_terms, axis=0, keepdims=True) + growth[
                length - 1 : length
            ] * jnp.sum(state_dot[:, lanes], axis=1, keepdims=True)
            sum_grad_ref[0, :, head : head + 1] = (
                jnp.concatenate(row_terms, axis=0)
                + start_terms
                - col_terms
                - end_terms
                + jnp.where(last_row, whole, 0.0)
            )
            back = back + ended
            step_grad_ref[0, :, head : head + 1] = jnp.sum(back * here, axis=1, keepdims=True)
            acts_grads.append(taps_here[KW + 1 : KW + 2, lanes] * grad + back * step)
            tails.append((stepped * tail).astype(jnp.bfloat16))
            grown_grads.append((grad * growth).astype(jnp.bfloat16))
        acts_grad_ref[:, :state_dim] += low_dot(jnp.concatenate(tails, axis=1), end, 1, 1)
        acts_grad_ref[:, state_dim:] += low_dot(jnp.concatenate(grown_grads, axis=1), state, 1, 1)
        pre_grad = jnp.concatenate(acts_grads, axis=1) * silu_slope(pre, sigmoid)
        total, rows = convolved_back(extended, pre_grad, taps_here)
        gap = jnp.zeros((EXTRA - 8, wide), jnp.float32)
        in_grad_ref[...] = jnp.concatenate([total[8:], gap, total[:8]], axis=0).astype(jnp.bfloat16)
        rows.append(jnp.sum(out_grad * acts, axis=0, keepdims=True))
        rows.append(jnp.zeros((8 - len(rows), wide), jnp.float32))
        tap_grad_ref[...] = jnp.concatenate(rows, axis=0)

        @pl.when(pl.program_id(0) == pairs - 1)
        def _():
            gram_grad = gram_grad_ref[...]
            rows_of = lax.broadcasted_iota(jnp.int32, (length, length), 0)
            cols_of = lax.broadcasted_iota(jnp.int32, (length, length), 1)
            gram_grad = jnp.where(rows_of >= cols_of, gram_grad, 0.0).astype(jnp.bfloat16)
            acts_grad_ref[:, :state_dim] += low_dot(gram_grad, c_low, 0, 0)
            acts_grad_ref[:, state_dim:] += low_dot(gram_grad, b_low, 1, 0)
            bc_taps_here = bc_tap_ref[...]
            bc_extended, bc_pre = convolved(bc_rim_ref[...], bc_ref[...], bc_taps_here)
            bc_pre_grad = acts_grad_ref[...] * silu_slope(bc_pre, jax.nn.sigmoid(bc_pre))
            bc_total, bc_rows = convolved_back(bc_extended, bc_pre_grad, bc_taps_here)
            bc_grad_ref[:length] = bc_total[8:]
            bc_grad_ref[length : length + EXTRA - 8] = jnp.zeros((EXTRA - 8, shared), jnp.float32)
            bc_grad_ref[length + EXTRA - 8 :] = bc_total[:8]
            bc_rows.append(jnp.zeros((8 - len(bc_rows), shared), jnp.float32))
            bc_tap_grad_ref[...] = jnp.concatenate(bc_rows, axis=0)

    block = pl.BlockSpec((length, wide), lambda i: (0, i))
    eight = pl.BlockSpec((8, wide), lambda i: (0, i))
    table = pl.BlockSpec((1, length, 2), lambda i: (i, 0, 0))
    state_block = pl.BlockSpec((state_dim, wide), lambda i: (0, i))
    bc_block = pl.BlockSpec((length, shared), lambda i: (0, 0))
    bc_eight = pl.BlockSpec((8, shared), lambda i: (0, 0))
    wide_low = jax.ShapeDtypeStruct((length + EXTRA, inner), jnp.bfloat16)
    eight_f32 = jax.ShapeDtypeStruct((8, inner), jnp.float32)
    table_f32 = jax.ShapeDtypeStruct(step_cols.shape, jnp.float32)
    bc_f32 = jax.ShapeDtypeStruct((length + EXTRA, shared), jnp.float32)
    bc_eight_f32 = jax.ShapeDtypeStruct((8, shared), jnp.float32)
    return pl.pallas_call(
        body,
        grid=(pairs,),
        out_shape=(
            wide_low, eight_f32, table_f32, table_f32, bc_f32, bc_eight_f32
        ),
        in_specs=scan_blocks(shared, length, wide)
        + [
            block,
            pl.BlockSpec((length, wide), lambda i: (0, gate_at // wide + i)),
            state_block,
            state_block,
            bc_block,
        ],
        out_specs=(
            pl.BlockSpec((length + EXTRA, wide), lambda i: (0, i)),
            eight,
            table,
            table,
            pl.BlockSpec((length + EXTRA, shared), lambda i: (0, 0)),
            bc_eight,
        ),
        scratch_shapes=[
            pltpu.VMEM((length, length), jnp.float32),
            pltpu.VMEM((length, length), jnp.float32),
            pltpu.VMEM((length, shared), jnp.float32),
            pltpu.VMEM((length, size), jnp.float32),
        ],
        compiler_params=pltpu.CompilerParams(vmem_limit_bytes=56 << 20),
        name="scan_back",
    )(
        first_pre, first_pre, taps, mix_pre, mix_pre, bc_taps, step_cols, sum_cols, sum_rows,
        out_grads, second_pre, state_in, end_grad, bc_low,
    )


def turned(values, cos_wide, sin_wide):
    return values * cos_wide + pltpu.roll(values, values.shape[1] // 2, 1) * sin_wide


def own_mask(at, rows, keys, limit):
    query_row = lax.broadcasted_iota(jnp.int32, (rows, keys), 0) + at
    key_row = lax.broadcasted_iota(jnp.int32, (rows, keys), 1)
    return (key_row <= query_row) & (key_row < limit)


def attention_forward(layout, second_pre, query_at, window, cos_wide, sin_wide, heads):
    length = second_pre.shape[0] - EXTRA
    part = min(ATTN_ROWS, length)
    own_at = window.shape[0] - length
    scale = HD ** (-0.5)

    def body(layout_ref, query_ref, window_ref, cos_ref, sin_ref, out_ref, turned_ref, total_ref):
        query = turned(query_ref[...], cos_ref[...], sin_ref[...]).astype(jnp.bfloat16)
        turned_ref[...] = query
        for at in range(0, length, part):
            to = at + part
            here = query[at:to]

            def scores_of(keys):
                return scale * low_dot(here, keys, 1, 1)

            keys = window_ref[own_at : own_at + to, :HD]
            values = window_ref[own_at : own_at + to, HD:]
            scores = jnp.where(
                own_mask(at, part, to, layout_ref[1]), scores_of(keys), masked_score
            )
            top = jnp.max(scores, axis=1, keepdims=True)
            shares = jnp.exp(scores - top)
            total = jnp.sum(shares, axis=1, keepdims=True)
            acc = low_dot(shares, values, 1, 0)

            def earlier(distance, carry):
                top, total, acc = carry
                start = pl.multiple_of(own_at - distance * length, length)
                scores = scores_of(window_ref[pl.ds(start, length), :HD])
                new_top = jnp.maximum(top, jnp.max(scores, axis=1, keepdims=True))
                fade = jnp.exp(top - new_top)
                shares = jnp.exp(scores - new_top)
                total = fade * total + jnp.sum(shares, axis=1, keepdims=True)
                acc = fade * acc + low_dot(shares, window_ref[pl.ds(start, length), HD:], 1, 0)
                return (new_top, total, acc)

            top, total, acc = lax.fori_loop(1, layout_ref[0] + 1, earlier, (top, total, acc))
            out_ref[at:to] = (acc / total).astype(jnp.bfloat16)
            total_ref[0, at:to] = top + jnp.log(total)

    head = pl.BlockSpec((length, HD), lambda i, layout_ref: (0, i))
    whole = pl.BlockSpec((length, HD), lambda i, layout_ref: (0, 0))
    return pl.pallas_call(
        body,
        out_shape=(
            jax.ShapeDtypeStruct((length, heads * HD), jnp.bfloat16),
            jax.ShapeDtypeStruct((length, heads * HD), jnp.bfloat16),
            jax.ShapeDtypeStruct((heads, length, 1), jnp.float32),
        ),
        grid_spec=pltpu.PrefetchScalarGridSpec(
            num_scalar_prefetch=1,
            grid=(heads,),
            in_specs=[
                pl.BlockSpec((length, HD), lambda i, layout_ref: (0, query_at // HD + i)),
                pl.BlockSpec(window.shape, lambda i, layout_ref: (0, 0)),
                whole,
                whole,
            ],
            out_specs=(
                head,
                head,
                pl.BlockSpec((1, length, 1), lambda i, layout_ref: (i, 0, 0)),
            ),
        ),
        compiler_params=pltpu.CompilerParams(vmem_limit_bytes=48 << 20),
        name="attention_forward",
    )(layout, second_pre, window, cos_wide, sin_wide)


def attention_back(layout, query, window, out, totals, mixed_grad, grad_at, cos_wide, sin_wide):
    length = query.shape[0]
    heads = query.shape[1] // HD
    part = min(ATTN_ROWS, length)
    own_at = window.shape[0] - length
    scale = HD ** (-0.5)

    def body(
        layout_ref, query_ref, window_ref, out_in_ref, total_ref, grad_ref, cos_ref, sin_ref,
        query_grad_ref, window_grad_ref, own_grad_ref, sum_ref, acc_ref,
    ):
        @pl.when(pl.program_id(0) == 0)
        def _():
            sum_ref[...] = jnp.zeros_like(sum_ref)

        for at in range(0, length, part):
            to = at + part
            here = query_ref[at:to]
            grad = grad_ref[at:to].astype(jnp.bfloat16)
            dots = jnp.sum(
                grad.astype(jnp.float32) * out_in_ref[at:to].astype(jnp.float32),
                axis=1,
                keepdims=True,
            )
            total = total_ref[0, at:to]

            def step(start, count, mask):
                keys = window_ref[pl.ds(start, count), :HD]
                values = window_ref[pl.ds(start, count), HD:]
                probs = jnp.exp(scale * low_dot(here, keys, 1, 1) - total)
                if mask is not None:
                    probs = jnp.where(mask, probs, 0.0)
                score_grad = (probs * (low_dot(grad, values, 1, 1) - dots)).astype(jnp.bfloat16)
                sum_ref[pl.ds(start, count), :HD] += low_dot(score_grad, here, 0, 0)
                sum_ref[pl.ds(start, count), HD:] += low_dot(probs, grad, 0, 0)
                return low_dot(score_grad, keys, 1, 0)

            acc_ref[...] = step(own_at, to, own_mask(at, part, to, layout_ref[1]))

            def earlier(distance, carry):
                start = pl.multiple_of(own_at - distance * length, length)
                acc_ref[...] += step(start, length, None)
                return carry

            lax.fori_loop(1, layout_ref[0] + 1, earlier, 0)
            query_grad_ref[at:to] = turned(
                acc_ref[...] * scale, cos_ref[at:to], -sin_ref[at:to]
            ).astype(jnp.bfloat16)

        @pl.when(pl.program_id(0) == heads - 1)
        def _():
            own_grad_ref[:, :HD] = sum_ref[own_at:, :HD] * scale
            own_grad_ref[:, HD:] = sum_ref[own_at:, HD:]
            window_grad_ref[:, :HD] = (sum_ref[:own_at, :HD] * scale).astype(jnp.bfloat16)
            window_grad_ref[:, HD:] = sum_ref[:own_at, HD:].astype(jnp.bfloat16)

    head = pl.BlockSpec((length, HD), lambda i, layout_ref: (0, i))
    whole = pl.BlockSpec((length, HD), lambda i, layout_ref: (0, 0))
    return pl.pallas_call(
        body,
        out_shape=(
            jax.ShapeDtypeStruct(query.shape, jnp.bfloat16),
            jax.ShapeDtypeStruct((own_at, 2 * HD), jnp.bfloat16),
            jax.ShapeDtypeStruct((length, 2 * HD), jnp.float32),
        ),
        grid_spec=pltpu.PrefetchScalarGridSpec(
            num_scalar_prefetch=1,
            grid=(heads,),
            in_specs=[
                head,
                pl.BlockSpec(window.shape, lambda i, layout_ref: (0, 0)),
                head,
                pl.BlockSpec((1, length, 1), lambda i, layout_ref: (i, 0, 0)),
                pl.BlockSpec((length, HD), lambda i, layout_ref: (0, grad_at // HD + i)),
                whole,
                whole,
            ],
            out_specs=(
                head,
                pl.BlockSpec((own_at, 2 * HD), lambda i, layout_ref: (0, 0)),
                pl.BlockSpec((length, 2 * HD), lambda i, layout_ref: (0, 0)),
            ),
            scratch_shapes=[
                pltpu.VMEM(window.shape, jnp.float32),
                pltpu.VMEM((part, HD), jnp.float32),
            ],
        ),
        compiler_params=pltpu.CompilerParams(vmem_limit_bytes=56 << 20),
        name="attention_back",
    )(layout, query, window, out, totals, mixed_grad, cos_wide, sin_wide)


def per_device(
    tokens,
    cotangent,
    mix_norm_gain,
    ssm_gate_proj,
    ssm_input_proj,
    ssm_bc_proj,
    ssm_step_proj,
    conv_in_weight,
    conv_in_bias,
    conv_bc_weight,
    conv_bc_bias,
    step_bias,
    decay_log,
    skip_gain,
    ssm_out_proj,
    query_proj,
    key_proj,
    value_proj,
    attn_out_proj,
    ffn_norm_gain,
    ffn_gate_proj,
    ffn_up_proj,
    ffn_down_proj,
    extra_blocks,
    seq_order,
    pad_rows,
):
    block_rows = tokens.shape[0]
    block_index = lax.axis_index("ctx")
    seq_count = seq_order.shape[0]
    slot_ids = jnp.arange(seq_count, dtype=jnp.int32)
    chosen = (seq_order[:, None] == slot_ids[None, :]).astype(jnp.int32)
    counts = jnp.sum(chosen * extra_blocks[None, :], axis=1) + 1
    slot_pads = jnp.sum(chosen * pad_rows[None, :], axis=1)
    slot_ends = jnp.cumsum(counts)
    starts = slot_ends - counts
    inside = (starts <= block_index) & (block_index < slot_ends)
    within = jnp.sum(jnp.where(inside, block_index - starts, 0))
    pad_here = jnp.sum(jnp.where(inside & (slot_ends - 1 == block_index), slot_pads, 0))
    row_ids = jnp.arange(block_rows, dtype=jnp.int32)
    valid_rows = (row_ids < block_rows - pad_here).astype(jnp.float32)
    positions = within * block_rows + row_ids
    keep_state = (within > 0).astype(jnp.float32)
    devices = lax.axis_size("ctx")
    codes = jnp.asarray(slot_devices(devices), jnp.int32)
    from_whole = jnp.bitwise_xor(codes, block_index)
    to_whole = jnp.argsort(from_whole).astype(jnp.int32)
    rows_here = mix_norm_gain.shape[0]
    misc_here = jnp.concatenate(
        [
            ssm_step_proj,
            mix_norm_gain[:, None],
            ffn_norm_gain[:, None],
            conv_bc_weight.reshape(rows_here, 1),
            jnp.pad(conv_bc_bias, (0, rows_here - conv_bc_bias.shape[0]))[:, None],
        ],
        axis=1,
    )
    steps = ssm_step_proj.shape[1]
    misc_here = jnp.pad(misc_here, ((0, 0), (0, 128 - misc_here.shape[1])))
    inner, shared = (ssm_input_proj.shape[1], ssm_bc_proj.shape[1])
    heads_wide, pair_wide = (query_proj.shape[1], key_proj.shape[1])
    across = [4 * k for k in range(1, devices // 4)]
    mix_here = jnp.concatenate([ssm_bc_proj, misc_here, query_proj, key_proj, value_proj], axis=1)
    out_here = jnp.concatenate([ssm_out_proj, attn_out_proj], axis=0)
    first_here = jnp.concatenate([ssm_input_proj, mix_here, ssm_gate_proj], axis=1)
    first_held = spread([([0], first_here)], 0, across)
    gate_from = inner + mix_here.shape[1]
    input_held = spread([(here, piece[:, :inner]) for here, piece in first_held], 0, [1], merge=True)
    mix_held = [(here, piece[:, inner:gate_from]) for here, piece in first_held]
    mix_held = spread(mix_held, 0, [2], merge=True)
    gate_held = [(here, piece[:, gate_from:]) for here, piece in first_held]
    near = (input_held[-1][1], mix_held[-1][1])
    input_held = spread(input_held, 0, [2])
    mix_held = spread(mix_held, 0, [1])
    ffn_gate_weight = lax.all_gather(ffn_gate_proj, "ctx", axis=0, tiled=True)
    ffn_up_weight = lax.all_gather(after(ffn_up_proj, *near), "ctx", axis=0, tiled=True)
    out_held = spread([([0], out_here)], 1, across, near)
    input_weight = joined(input_held, 0)
    mix_weights = joined(mix_held, 0)
    misc = mix_weights[:, shared : shared + 128]
    mix_gain = misc[:, steps].astype(jnp.float32)

    def whole_order(column):
        return jnp.take(column.reshape(devices, rows_here), to_whole, axis=0)

    conv_bc_full = whole_order(misc[:, steps + 2]).reshape(shared, KW)
    conv_bc_offset = whole_order(misc[:, steps + 3])[:, : conv_bc_bias.shape[0]].reshape(shared)
    gain_two = whole_order(misc[:, steps + 1]).reshape(-1)
    inputs = tokens.astype(jnp.float32)
    rim_rows = KW - 1
    edge = shifted(tokens[block_rows - EXTRA :], "ctx", 1)
    edge_rows = jnp.arange(EXTRA, dtype=jnp.int32)[:, None] >= EXTRA - rim_rows
    edge = jnp.where(edge_rows & (within > 0), edge, jnp.zeros_like(edge))
    tokens_longer = jnp.concatenate([tokens, edge], axis=0)
    normed_low = rms_scale(
        reordered(tokens_longer, from_whole).astype(jnp.float32), mix_gain
    ).astype(jnp.bfloat16)
    first_pre = plain_product(normed_low, input_weight)
    mix_pre = plain_product(normed_low, mix_weights)
    ffn_down_weight = lax.all_gather(after(ffn_down_proj, mix_pre), "ctx", axis=1, tiled=True)
    step_raw = mix_pre[:block_rows, shared : shared + steps]
    query_at = shared + 128
    key_at = query_at + heads_wide
    key_pre = mix_pre[:block_rows, key_at : key_at + pair_wide]
    value_pre = mix_pre[:block_rows, key_at + pair_wide :]
    gate_held = spread(gate_held, 0, [2], (first_pre,), merge=True)
    out_held = spread(out_held, 1, [1], (first_pre,), merge=True)
    head_dim = inner // steps
    skips = jnp.repeat(skip_gain.astype(jnp.float32), head_dim)[None, :]
    taps = jnp.concatenate(
        [conv_in_weight.astype(jnp.float32).T, conv_in_bias.astype(jnp.float32)[None, :], skips]
    )
    taps = jnp.pad(taps, ((0, 8 - taps.shape[0]), (0, 0)))
    bc_taps = jnp.concatenate(
        [conv_bc_full.astype(jnp.float32).T, conv_bc_offset.astype(jnp.float32)[None, :]]
    )
    bc_taps = jnp.pad(bc_taps, ((0, 8 - bc_taps.shape[0]), (0, 0)))
    step_in = step_raw + step_bias.astype(jnp.float32)[None, :]
    step_size = jax.nn.softplus(step_in)
    rate = -jnp.exp(decay_log.astype(jnp.float32))[None, :]
    lower = (row_ids[:, None] >= row_ids[None, :]).astype(jnp.float32)
    log_decay = jnp.dot(lower, rate * step_size, precision=highest)

    def by_pairs(table):
        return table.reshape(block_rows, steps // 2, 2).transpose(1, 0, 2)

    def from_pairs(table):
        return table.transpose(1, 0, 2).reshape(block_rows, steps)

    step_cols = by_pairs(step_size)
    sum_cols = by_pairs(log_decay)
    sum_rows = log_decay.T.reshape(steps // 2, 2, block_rows)
    intra_out, local_states, bc_low = scan_forward(
        first_pre, mix_pre, taps, bc_taps, step_cols, sum_cols, sum_rows, inner, shared
    )
    decay_row = keep_state * jnp.repeat(jnp.exp(log_decay[block_rows - 1]), head_dim)[None, :]
    keep_low = keep_state.astype(jnp.bfloat16)
    reached, returned = carried_states(local_states, decay_row, False)
    state_in = keep_low * reached
    gate_held = spread(gate_held, 0, [1], (returned,))
    out_held = spread(out_held, 1, [2], (returned,))
    cos_table, sin_table = rotary_tables(positions)
    cos_wide = jnp.concatenate([cos_table, cos_table], axis=1)
    sin_wide = jnp.concatenate([-sin_table, sin_table], axis=1)
    key_rot = rotate(key_pre.reshape(block_rows, -1, HD), cos_table, sin_table)
    own_pair = jnp.concatenate(
        [key_rot.reshape(block_rows, HD).astype(jnp.bfloat16), value_pre.astype(jnp.bfloat16)],
        axis=1,
    )
    earlier_pairs = [shifted(own_pair, "ctx", distance) for distance in range(MAXB - 1, 0, -1)]
    window = jnp.concatenate(earlier_pairs + [own_pair], axis=0)
    layout = jnp.stack([within, block_rows - pad_here]).astype(jnp.int32)
    attn_low, query_rot, log_totals = attention_forward(
        layout, mix_pre, query_at, window, cos_wide, sin_wide, heads_wide // HD
    )
    gate_weight = joined(gate_held, 0)
    gate_pre = plain_product(normed_low, gate_weight)
    scan_out, ssm_low = scan_gated(intra_out, state_in, bc_low, sum_cols, gate_pre, 0)
    out_weights = joined(out_held, 1)
    mixed_low = jnp.concatenate([ssm_low, attn_low], axis=1)
    mixed_part = plain_product(mixed_low, out_weights)
    hidden = inputs + reordered(pair_sum(mixed_part), to_whole)
    normed_two, norm_two_back = jax.vjp(rms_scale, hidden, gain_two.astype(jnp.float32))
    normed_two_low = normed_two.astype(jnp.bfloat16)
    ffn_gate = plain_product(normed_two_low, ffn_gate_weight)
    ffn_up = plain_product(normed_two_low, ffn_up_weight)
    ffn_act = (jax.nn.silu(ffn_gate) * ffn_up).astype(jnp.bfloat16)
    ffn_part = plain_product(ffn_act, ffn_down_weight)
    ffn_sum = pair_sum(ffn_part)
    layer_out = ((hidden + ffn_sum) * valid_rows[:, None]).astype(jnp.bfloat16)
    cot_low = (cotangent.astype(jnp.float32) * valid_rows[:, None]).astype(jnp.bfloat16)
    grad_out = cot_low.astype(jnp.float32)

    def in_quarters(value):
        return jnp.split(value, 4, axis=1)

    def rows_grad(left_side, right_side, first, gates=()):
        parts = [product_of_cols(part, right_side) for part in in_quarters(left_side)]
        return Reduction(parts, 0, first, gates)

    def cols_grad(left_side, right_side, first, gates=()):
        parts = [product_of_cols(left_side, part) for part in in_quarters(right_side)]
        return Reduction(parts, 1, first, gates)

    down_sum = cols_grad(ffn_act, reordered(cot_low, from_whole), 1)
    act_grad = product_by_rows(cot_low, ffn_down_weight)
    gate_sigmoid = jax.nn.sigmoid(ffn_gate)
    ffn_gate_low = (
        act_grad * ffn_up * gate_sigmoid * (1.0 + ffn_gate * (1.0 - gate_sigmoid))
    ).astype(jnp.bfloat16)
    ffn_up_low = (act_grad * jax.nn.silu(ffn_gate)).astype(jnp.bfloat16)
    norm_two_part = product_by_rows(ffn_gate_low, ffn_gate_weight) + product_by_rows(
        ffn_up_low, ffn_up_weight
    )
    ffn_up_grad = lax.psum_scatter(
        product_of_cols(normed_two_low, ffn_up_low).astype(jnp.bfloat16),
        "ctx",
        scatter_dimension=0,
        tiled=True,
    )
    norm_two_grad = pair_sum(norm_two_part)
    hidden_norm_grad, gain_two_grad = norm_two_back(norm_two_grad)
    hidden_grad = grad_out + hidden_norm_grad
    hidden_low = reordered(hidden_grad.astype(jnp.bfloat16), from_whole)
    mixed_grad = product_by_rows(hidden_low, out_weights)
    ssm_gate_low, state_in_grad = scan_gated_back(
        mixed_grad, scan_out, bc_low, sum_cols, gate_pre, 0
    )
    end_grad, returned = carried_states(keep_low * state_in_grad, decay_row, True)
    gate_late = after(ffn_gate_low, ssm_gate_low)
    ffn_gate_grad = lax.psum_scatter(
        product_of_cols(normed_two_low, gate_late).astype(jnp.bfloat16),
        "ctx",
        scatter_dimension=0,
        tiled=True,
    )
    layout = after(layout, returned)
    query_grad_low, window_grad, own_pair_grad = attention_back(
        layout, query_rot, window, attn_low, log_totals, mixed_grad, inner, cos_wide, sin_wide
    )
    for distance in range(1, MAXB):
        at = (MAXB - 1 - distance) * block_rows
        own_pair_grad = own_pair_grad + shifted(
            window_grad[at : at + block_rows], "ctx", -distance
        ).astype(jnp.float32)
    down_sum.onward(end_grad, query_grad_low)
    out_sum = cols_grad(mixed_low, hidden_low, 1, (end_grad, query_grad_low))
    gate_sum = rows_grad(normed_low, ssm_gate_low, 2, (end_grad, query_grad_low))
    key_grad_low = (
        rotate(own_pair_grad[:, :HD].reshape(block_rows, 1, HD), cos_table, -sin_table)
        .reshape(block_rows, HD)
        .astype(jnp.bfloat16)
    )
    value_grad_low = own_pair_grad[:, HD:].astype(jnp.bfloat16)
    input_grad_low, tap_grad, step_part, sum_part, bc_pre_part, bc_tap_grad = scan_back(
        first_pre, mix_pre, taps, bc_taps, step_cols, sum_cols, sum_rows,
        mixed_grad, gate_pre, 0, state_in, end_grad, bc_low,
    )
    rate_grad = lax.dot_general(
        lower, from_pairs(sum_part), (((0,), (0,)), ((), ())), precision=highest
    )
    step_grad = (from_pairs(step_part) + rate * rate_grad) * jax.nn.sigmoid(step_in)
    step_grad_low = step_grad.astype(jnp.bfloat16)
    tap_sums = [
        tap_grad[:KW].T,
        tap_grad[KW],
        jnp.sum(step_grad, axis=0),
        jnp.sum(rate_grad * rate * step_size, axis=0),
        jnp.sum(tap_grad[KW + 1].reshape(steps, head_dim), axis=1),
    ]
    no_misc = jnp.zeros((block_rows, 128 - steps), jnp.bfloat16)
    mix_grads = jnp.concatenate(
        [step_grad_low, no_misc, query_grad_low, key_grad_low, value_grad_low], axis=1
    )
    mix_grads = jnp.pad(mix_grads, ((0, EXTRA), (0, 0)))
    bc_grad_low = pair_sum(bc_pre_part).astype(jnp.bfloat16)
    input_sum = rows_grad(normed_low, input_grad_low, 1)
    mix_sum = rows_grad(normed_low, jnp.concatenate([bc_grad_low, mix_grads], axis=1), 2)
    mix_grads = jnp.concatenate([bc_pre_part.astype(jnp.bfloat16), mix_grads], axis=1)
    norm_one_part = (
        product_by_rows(input_grad_low, input_weight)
        + product_by_rows(mix_grads, mix_weights)
        + product_by_rows(ssm_gate_low, gate_weight)
    )
    gate_sum.onward(norm_one_part)
    out_sum.onward(gate_sum.far_low)
    down_sum.last(out_sum.far_low)
    mix_sum.onward(*down_sum.blocks_low)
    input_sum.onward(mix_sum.far_low)
    gate_sum.last(input_sum.far_low)
    out_sum.last(*gate_sum.blocks_low)
    mix_sum.last(*out_sum.blocks_low)
    input_sum.last(*mix_sum.blocks_low)
    norm_one_grad = reordered(pair_sum(norm_one_part), to_whole)
    conv_bc_grads = jnp.concatenate([bc_tap_grad[:KW].T.reshape(-1), bc_tap_grad[KW]])
    conv_bc_grads = conv_bc_grads + swap(conv_bc_grads)
    longer = tokens_longer.astype(jnp.float32)
    scale_one = lax.rsqrt(jnp.mean(longer * longer, axis=1, keepdims=True) + epsilon)
    gain_one_grad = jnp.sum(norm_one_grad * longer * scale_one, axis=0)
    edge_back = shifted(keep_state * norm_one_grad[block_rows + EXTRA - 8 :], "ctx", -1)
    norm_one_grad = norm_one_grad[:block_rows] + jnp.pad(edge_back, ((block_rows - 8, 0), (0, 0)))
    _, norm_one_back = jax.vjp(lambda v: rms_scale(v, whole_order(mix_gain).reshape(-1)), inputs)
    tokens_grad = hidden_grad + norm_one_back(norm_one_grad)[0]
    small = [
        tap_sums[0].reshape(-1),
        *tap_sums[1:],
        conv_bc_grads,
        gain_one_grad,
        gain_two_grad,
    ]
    packed = jnp.concatenate(small)
    filled = -packed.shape[0] % 1024
    packed = summed(jnp.pad(packed, (0, filled)).reshape(-1, 128)).reshape(-1)
    sums, at = ([], 0)
    for part in small:
        sums.append(packed[at : at + part.shape[0]])
        at += part.shape[0]

    def own(vector, count):
        return lax.dynamic_slice_in_dim(vector, block_index * count, count, 0)

    mix_grad = mix_sum.total()
    out_grad = out_sum.total()
    conv_bc_sums = sums[5]
    conv_rows = conv_bc_weight.shape[0]
    return (
        layer_out,
        tokens_grad.astype(jnp.bfloat16),
        own(sums[6], rows_here),
        gate_sum.total(),
        input_sum.total(),
        mix_grad[:, :shared],
        mix_grad[:, shared : shared + steps],
        sums[0].reshape(inner, KW),
        sums[1],
        own(conv_bc_sums[: shared * KW], conv_rows * KW).reshape(conv_rows, KW),
        own(conv_bc_sums[shared * KW :], conv_rows),
        sums[2],
        sums[3],
        sums[4],
        out_grad[:inner],
        mix_grad[:, query_at:key_at],
        mix_grad[:, key_at : key_at + pair_wide],
        mix_grad[:, key_at + pair_wide :],
        out_grad[inner:],
        own(sums[7], rows_here),
        ffn_gate_grad.astype(jnp.float32),
        ffn_up_grad.astype(jnp.float32),
        down_sum.total(),
    )


def solution(mesh):
    return jax.shard_map(
        per_device,
        mesh=mesh,
        in_specs=(
            P("ctx", None),
            P("ctx", None),
            P("ctx"),
            P("ctx", "wt"),
            P("ctx", "wt"),
            P("ctx", None),
            P("ctx", "wt"),
            P("wt", None),
            P("wt"),
            P("ctx", None),
            P("ctx"),
            P("wt"),
            P("wt"),
            P("wt"),
            P("wt", "ctx"),
            P("ctx", "wt"),
            P("ctx", "wt"),
            P("ctx", "wt"),
            P("wt", "ctx"),
            P("ctx"),
            P("ctx", "wt"),
            P("ctx", "wt"),
            P("wt", "ctx"),
            P(),
            P(),
            P(),
        ),
        out_specs=(
            P("ctx", None),
            P("ctx", None),
            P("ctx"),
            P("ctx", "wt"),
            P("ctx", "wt"),
            P("ctx", None),
            P("ctx", "wt"),
            P("wt", None),
            P("wt"),
            P("ctx", None),
            P("ctx"),
            P("wt"),
            P("wt"),
            P("wt"),
            P("wt", "ctx"),
            P("ctx", "wt"),
            P("ctx", "wt"),
            P("ctx", "wt"),
            P("wt", "ctx"),
            P("ctx"),
            P("ctx", "wt"),
            P("ctx", "wt"),
            P("wt", "ctx"),
        ),
        check_vma=False,
    )
```

```python
import jax
import jax.numpy as jnp
from jax import lax
from jax.experimental import pallas as pl
from jax.experimental.pallas import tpu as pltpu
from jax.sharding import PartitionSpec as P


HD = 128
KW = 4
MAXB = 8
EXTRA = 16
SCAN_ROWS = 128
ATTN_ROWS = 256


epsilon = 1e-05
rope_base = 100000000000.0
highest = lax.Precision.HIGHEST
masked_score = -1e30


def shifted(value, axis, steps):
    count = lax.axis_size(axis)
    leading, last = (max(0, -steps), min(count, count - steps))
    return lax.ppermute(value, axis, [(source, source + steps) for source in range(leading, last)])


def hop(value, code):
    if code == 0:
        return value
    count = lax.axis_size("ctx")
    return lax.ppermute(value, "ctx", [(source, source ^ code) for source in range(count)])


def swap(value):
    return lax.ppermute(value, "wt", [(0, 1), (1, 0)])


def pair_sum(value):
    rounded = lax.reduce_precision(value, 8, 7)
    return rounded + swap(rounded.astype(jnp.bfloat16)).astype(jnp.float32)


def slot_devices(count):
    high = count // 4
    return [4 * (slot % high) + slot // high for slot in range(count)]


def after(value, *gates):
    return lax.optimization_barrier((value, *gates))[0]


def spread(held, axis, codes, gates=(), merge=False):
    if merge:
        every = [code for here, _ in held for code in here]
        held = [(every, jnp.concatenate([array for _, array in held], axis=axis))]
    taken = list(held)
    for here, array in held:
        operand = after(array, *gates) if gates else array
        for code in codes:
            taken.append(([one ^ code for one in here], hop(operand, code)))
    return taken


def joined(held, axis):
    size = sum(array.shape[axis] for _, array in held) // sum(len(here) for here, _ in held)
    found = {code: (i, at) for i, (here, _) in enumerate(held) for at, code in enumerate(here)}
    runs = []
    for code in slot_devices(len(found)):
        i, at = found[code]
        if runs and runs[-1][0] == i and runs[-1][2] == at:
            runs[-1][2] = at + 1
        else:
            runs.append([i, at, at + 1])
    return jnp.concatenate(
        [lax.slice_in_dim(held[i][1], at * size, to * size, axis=axis) for i, at, to in runs],
        axis=axis,
    )


class Reduction:
    def __init__(self, parts, axis, first, gates=(), later=()):
        self.axis, self.second = (axis, 3 - first)
        self.near, self.far = (parts[0], parts[3 - first])
        low = [parts[k].astype(jnp.bfloat16) for k in (first, 3)]
        if gates:
            low = list(lax.optimization_barrier((*low, *gates))[:2])
        if later:
            low[1] = after(low[1], *later)
        one = hop(low[0], first)
        self.got = [one, hop(low[1], first)]

    def onward(self, *gates):
        got = lax.optimization_barrier((*self.got, *gates))[:2] if gates else self.got
        self.far_low = (self.far + got[1].astype(jnp.float32)).astype(jnp.bfloat16)
        self.near = self.near + got[0].astype(jnp.float32)
        self.got = [hop(self.far_low, self.second)]

    def last(self, *gates):
        high = lax.axis_size("ctx") // 4
        got = after(self.got[0], *gates) if gates else self.got[0]
        quarter = self.near + got.astype(jnp.float32)
        blocks = jnp.split(quarter, high, axis=self.axis)
        self.block = blocks[0]
        self.blocks_low = [block.astype(jnp.bfloat16) for block in blocks[1:]]
        self.got = [hop(block, 4 * (k + 1)) for k, block in enumerate(self.blocks_low)]

    def total(self):
        total = self.block
        for got in self.got:
            total = total + got.astype(jnp.float32)
        return total


def summed(value):
    bit = 1
    while bit < lax.axis_size("ctx"):
        value = value + hop(value, bit)
        bit *= 2
    return value


def reordered(value, order):
    blocks = order.shape[0]
    rows, width = value.shape[0], value.shape[1] // blocks
    if width % 128:
        return jnp.take(value.reshape(rows, blocks, width), order, axis=1).reshape(rows, -1)

    steps = 4 if rows % 64 == 0 else 3
    part = rows // steps

    def body(order_ref, in_ref, out_ref):
        for slot in range(blocks):
            start = pl.multiple_of(order_ref[slot] * width, width)
            out_ref[:, slot * width : (slot + 1) * width] = in_ref[:, pl.ds(start, width)]

    block = pl.BlockSpec((part, value.shape[1]), lambda i, order_ref: (i, 0))
    return pl.pallas_call(
        body,
        out_shape=jax.ShapeDtypeStruct(value.shape, value.dtype),
        grid_spec=pltpu.PrefetchScalarGridSpec(
            num_scalar_prefetch=1, grid=(steps,), in_specs=[block], out_specs=block
        ),
        name="reordered",
    )(order, value)


def carried_states(states, decays, reverse):
    me = lax.axis_index("ctx")
    place = me % 4
    width = states.shape[1] // 4
    low = states.astype(jnp.bfloat16)

    def quarter(value, index):
        return lax.dynamic_slice_in_dim(value, index * width, width, 1)

    got = [hop(quarter(low, place ^ k), k) for k in range(4)]
    got_decay = [hop(quarter(decays, place ^ k), k) for k in range(4)]

    def in_order(pieces):
        odd = place % 2 == 1
        pieces = [jnp.where(odd, pieces[k ^ 1], pieces[k]) for k in range(4)]
        upper = place >= 2
        return [jnp.where(upper, pieces[k ^ 2], pieces[k]) for k in range(4)]

    blocks = [piece.astype(jnp.float32) for piece in in_order(got)]
    rates = in_order(got_decay)
    if reverse:
        blocks, rates = (blocks[::-1], rates[::-1])
    total, rate = (blocks[0], rates[0])
    for block, block_rate in zip(blocks[1:], rates[1:]):
        total, rate = (block + block_rate * total, block_rate * rate)
    step = -4 if reverse else 4
    total_low = total.astype(jnp.bfloat16)
    near, near_rate = (shifted(total_low, "ctx", step), shifted(rate, "ctx", step))
    far = shifted(total_low, "ctx", 2 * step)
    state = near.astype(jnp.float32) + near_rate * far.astype(jnp.float32)
    reached = []
    for block, block_rate in zip(blocks, rates):
        reached.append(state.astype(jnp.bfloat16))
        state = block + block_rate * state
    if reverse:
        reached = reached[::-1]
    mine = in_order(reached)
    back = in_order([hop(mine[k], k) for k in range(4)])
    return (jnp.concatenate(back, axis=1), mine[1])


def plain_product(left_side, right_side):
    return jnp.dot(left_side, right_side, preferred_element_type=jnp.float32)


def product_by_rows(left_side, right_side):
    return lax.dot_general(
        left_side, right_side, (((1,), (1,)), ((), ())), preferred_element_type=jnp.float32
    )


def product_of_cols(left_side, right_side):
    return lax.dot_general(
        left_side, right_side, (((0,), (0,)), ((), ())), preferred_element_type=jnp.float32
    )


def rms_scale(values, gain_vec):
    return (
        values * lax.rsqrt(jnp.mean(values * values, axis=-1, keepdims=True) + epsilon) * gain_vec
    )


def rotary_tables(positions):
    exponents = jnp.arange(HD // 2, dtype=jnp.float32) * (2.0 / HD)
    frequency = jnp.power(jnp.float32(rope_base), -exponents)
    angles = positions.astype(jnp.float32)[:, None] * frequency[None, :]
    return (jnp.cos(angles), jnp.sin(angles))


def rotate(values, cos_table, sin_table):
    half_dim = values.shape[-1] // 2
    first_half = values[..., :half_dim]
    second_half = values[..., half_dim:]
    cos_table = cos_table[:, None, :]
    sin_table = sin_table[:, None, :]
    return jnp.concatenate(
        [
            first_half * cos_table - second_half * sin_table,
            second_half * cos_table + first_half * sin_table,
        ],
        axis=-1,
    )


def convolved(rim, block, taps):
    length = block.shape[0]
    extended = jnp.concatenate([rim, block], axis=0)
    first = rim.shape[0] - (KW - 1)
    summed = taps[KW : KW + 1]
    for j in range(KW):
        summed = summed + extended[first + j : first + j + length] * taps[j : j + 1]
    return (extended, summed)


def convolved_back(extended, pre_grad, taps):
    length = pre_grad.shape[0]
    rim_rows = extended.shape[0] - length
    first = rim_rows - (KW - 1)
    zeros = jnp.zeros((8, pre_grad.shape[1]), jnp.float32)
    padded = jnp.concatenate([zeros, pre_grad, zeros], axis=0)
    total = jnp.zeros_like(extended)
    rows = []
    for j in range(KW):
        start = 8 - rim_rows + KW - 1 - j
        total = total + padded[start : start + rim_rows + length] * taps[j : j + 1]
        rows.append(
            jnp.sum(pre_grad * extended[first + j : first + j + length], axis=0, keepdims=True)
        )
    rows.append(jnp.sum(pre_grad, axis=0, keepdims=True))
    return (total, rows)


def silu_slope(value, sigmoid):
    return sigmoid * (1.0 + value * (1.0 - sigmoid))


def low_dot(left_side, right_side, left_axis, right_axis):
    return lax.dot_general(
        left_side.astype(jnp.bfloat16),
        right_side.astype(jnp.bfloat16),
        (((left_axis,), (right_axis,)), ((), ())),
        preferred_element_type=jnp.float32,
    )


def lower_gram(c_low, b_low):
    length = c_low.shape[0]
    gram = low_dot(c_low, b_low, 1, 1)
    rows = lax.broadcasted_iota(jnp.int32, (length, length), 0)
    cols = lax.broadcasted_iota(jnp.int32, (length, length), 1)
    return jnp.where(rows >= cols, gram, 0.0)


def scan_blocks(shared, length, wide):
    return [
        pl.BlockSpec((length, wide), lambda i: (0, i)),
        pl.BlockSpec((8, wide), lambda i: ((length + EXTRA) // 8 - 1, i)),
        pl.BlockSpec((8, wide), lambda i: (0, i)),
        pl.BlockSpec((length, shared), lambda i: (0, 0)),
        pl.BlockSpec((8, shared), lambda i: ((length + EXTRA) // 8 - 1, 0)),
        pl.BlockSpec((8, shared), lambda i: (0, 0)),
        pl.BlockSpec((1, length, 2), lambda i: (i, 0, 0)),
        pl.BlockSpec((1, length, 2), lambda i: (i, 0, 0)),
        pl.BlockSpec((1, 2, length), lambda i: (i, 0, 0)),
    ]


def scan_forward(first_pre, mix_pre, taps, bc_taps, step_cols, sum_cols, sum_rows, inner, shared):
    length = first_pre.shape[0] - EXTRA
    pairs = step_cols.shape[0]
    wide = inner // pairs
    size = wide // 2
    state_dim = shared // 2
    part = min(SCAN_ROWS, length)

    def body(
        in_ref, rim_ref, tap_ref, bc_ref, bc_rim_ref, bc_tap_ref, step_ref, col_ref, row_ref,
        out_ref, state_ref, bc_low_ref, gram_ref,
    ):
        @pl.when(pl.program_id(0) == 0)
        def _():
            _, pre = convolved(bc_rim_ref[...], bc_ref[...], bc_tap_ref[...])
            acts = (pre * jax.nn.sigmoid(pre)).astype(jnp.bfloat16)
            bc_low_ref[...] = acts
            gram_ref[...] = lower_gram(acts[:, state_dim:], acts[:, :state_dim])

        taps_here = tap_ref[...]
        _, pre = convolved(rim_ref[...], in_ref[...], taps_here)
        acts = pre * jax.nn.sigmoid(pre)
        tails = []
        for head in range(2):
            lanes = slice(head * size, (head + 1) * size)
            step = step_ref[0][:, head : head + 1]
            col = col_ref[0][:, head : head + 1]
            row = row_ref[0][head : head + 1, :]
            stepped = acts[:, lanes] * step
            stepped_low = stepped.astype(jnp.bfloat16)
            for at in range(0, length, part):
                end = at + part
                decay = jnp.exp(jnp.minimum(col[at:end] - row[:, :end], 0.0))
                weights = (decay * gram_ref[at:end, :end]).astype(jnp.bfloat16)
                out_ref[at:end, lanes] = low_dot(weights, stepped_low[:end], 1, 0) + (
                    taps_here[KW + 1 : KW + 2, lanes] * acts[at:end, lanes]
                )
            tails.append(stepped * jnp.exp(col[length - 1 : length] - col))
        tail = jnp.concatenate(tails, axis=1)
        state_ref[...] = low_dot(bc_low_ref[:, :state_dim], tail, 0, 0).astype(jnp.bfloat16)

    return pl.pallas_call(
        body,
        grid=(pairs,),
        out_shape=(
            jax.ShapeDtypeStruct((length, inner), jnp.float32),
            jax.ShapeDtypeStruct((state_dim, inner), jnp.bfloat16),
            jax.ShapeDtypeStruct((length, shared), jnp.bfloat16),
        ),
        in_specs=scan_blocks(shared, length, wide),
        out_specs=(
            pl.BlockSpec((length, wide), lambda i: (0, i)),
            pl.BlockSpec((state_dim, wide), lambda i: (0, i)),
            pl.BlockSpec((length, shared), lambda i: (0, 0)),
        ),
        scratch_shapes=[pltpu.VMEM((length, length), jnp.float32)],
        compiler_params=pltpu.CompilerParams(vmem_limit_bytes=48 << 20),
        name="scan_forward",
    )(first_pre, first_pre, taps, mix_pre, mix_pre, bc_taps, step_cols, sum_cols, sum_rows)


def scan_gated(intra, state_in, bc_low, sum_cols, second_pre, gate_at):
    length, inner = intra.shape
    pairs = sum_cols.shape[0]
    wide = inner // pairs
    size = wide // 2
    state_dim = bc_low.shape[1] // 2

    def body(intra_ref, state_ref, c_ref, col_ref, gate_ref, out_ref, act_ref):
        carried = low_dot(c_ref[...], state_ref[...], 1, 0)
        gate = gate_ref[...]
        silu = gate * jax.nn.sigmoid(gate)
        for head in range(2):
            lanes = slice(head * size, (head + 1) * size)
            growth = jnp.exp(col_ref[0][:, head : head + 1])
            whole = intra_ref[:, lanes] + carried[:, lanes] * growth
            out_ref[:, lanes] = whole
            act_ref[:, lanes] = (whole * silu[:, lanes]).astype(jnp.bfloat16)

    block = pl.BlockSpec((length, wide), lambda i: (0, i))
    return pl.pallas_call(
        body,
        grid=(pairs,),
        out_shape=(
            jax.ShapeDtypeStruct((length, inner), jnp.float32),
            jax.ShapeDtypeStruct((length, inner), jnp.bfloat16),
        ),
        in_specs=[
            block,
            pl.BlockSpec((state_dim, wide), lambda i: (0, i)),
            pl.BlockSpec((length, state_dim), lambda i: (0, 1)),
            pl.BlockSpec((1, length, 2), lambda i: (i, 0, 0)),
            pl.BlockSpec((length, wide), lambda i: (0, gate_at // wide + i)),
        ],
        out_specs=(block, block),
        compiler_params=pltpu.CompilerParams(vmem_limit_bytes=48 << 20),
        name="scan_gated",
    )(intra, state_in, bc_low, sum_cols, second_pre)


def scan_gated_back(out_grads, whole, bc_low, sum_cols, second_pre, gate_at):
    length, inner = whole.shape
    pairs = sum_cols.shape[0]
    wide = inner // pairs
    size = wide // 2
    state_dim = bc_low.shape[1] // 2

    def body(grad_ref, whole_ref, c_ref, col_ref, gate_ref, gate_grad_ref, state_ref):
        gate = gate_ref[...]
        sigmoid = jax.nn.sigmoid(gate)
        grad = grad_ref[...]
        gate_grad = grad * whole_ref[...] * silu_slope(gate, sigmoid)
        gate_grad_ref[:length] = gate_grad.astype(jnp.bfloat16)
        gate_grad_ref[length:] = jnp.zeros((EXTRA, wide), jnp.bfloat16)
        inside = grad * (gate * sigmoid)
        grown = [
            inside[:, head * size : (head + 1) * size] * jnp.exp(col_ref[0][:, head : head + 1])
            for head in range(2)
        ]
        state_ref[...] = low_dot(c_ref[...], jnp.concatenate(grown, axis=1), 0, 0).astype(
            jnp.bfloat16
        )

    block = pl.BlockSpec((length, wide), lambda i: (0, i))
    return pl.pallas_call(
        body,
        grid=(pairs,),
        out_shape=(
            jax.ShapeDtypeStruct((length + EXTRA, inner), jnp.bfloat16),
            jax.ShapeDtypeStruct((state_dim, inner), jnp.bfloat16),
        ),
        in_specs=[
            block,
            block,
            pl.BlockSpec((length, state_dim), lambda i: (0, 1)),
            pl.BlockSpec((1, length, 2), lambda i: (i, 0, 0)),
            pl.BlockSpec((length, wide), lambda i: (0, gate_at // wide + i)),
        ],
        out_specs=(
            pl.BlockSpec((length + EXTRA, wide), lambda i: (0, i)),
            pl.BlockSpec((state_dim, wide), lambda i: (0, i)),
        ),
        compiler_params=pltpu.CompilerParams(vmem_limit_bytes=48 << 20),
        name="scan_gated_back",
    )(out_grads, whole, bc_low, sum_cols, second_pre)


def scan_back(
    first_pre, mix_pre, taps, bc_taps, step_cols, sum_cols, sum_rows,
    out_grads, second_pre, gate_at, state_in, end_grad, bc_low,
):
    length = first_pre.shape[0] - EXTRA
    pairs = step_cols.shape[0]
    state_dim, inner = state_in.shape
    shared = bc_low.shape[1]
    wide = inner // pairs
    size = wide // 2
    part = min(SCAN_ROWS, length)

    def body(
        in_ref, rim_ref, tap_ref, bc_ref, bc_rim_ref, bc_tap_ref, step_ref, col_ref, row_ref,
        grad_ref, gate_ref, state_ref, end_ref, bc_low_ref,
        in_grad_ref, tap_grad_ref, step_grad_ref, sum_grad_ref, bc_grad_ref, bc_tap_grad_ref,
        gram_ref, gram_grad_ref, acts_grad_ref, back_ref,
    ):
        b_low = bc_low_ref[:, :state_dim]
        c_low = bc_low_ref[:, state_dim:]

        @pl.when(pl.program_id(0) == 0)
        def _():
            gram_ref[...] = lower_gram(c_low, b_low)
            gram_grad_ref[...] = jnp.zeros_like(gram_grad_ref)
            acts_grad_ref[...] = jnp.zeros_like(acts_grad_ref)

        taps_here = tap_ref[...]
        extended, pre = convolved(rim_ref[...], in_ref[...], taps_here)
        sigmoid = jax.nn.sigmoid(pre)
        acts = pre * sigmoid
        gate = gate_ref[...]
        out_grad = grad_ref[...] * (gate * jax.nn.sigmoid(gate))
        state = state_ref[...]
        end = end_ref[...]
        from_end = low_dot(b_low, end, 1, 0)
        from_start = low_dot(c_low, state, 1, 0)
        state_dot = jnp.sum(
            state.astype(jnp.float32) * end.astype(jnp.float32), axis=0, keepdims=True
        )
        last_row = lax.broadcasted_iota(jnp.int32, (length, 1), 0) == length - 1
        acts_grads, tails, grown_grads = ([], [], [])
        for head in range(2):
            lanes = slice(head * size, (head + 1) * size)
            step = step_ref[0][:, head : head + 1]
            col = col_ref[0][:, head : head + 1]
            row = row_ref[0][head : head + 1, :]
            here = acts[:, lanes]
            stepped = here * step
            stepped_low = stepped.astype(jnp.bfloat16)
            grad = out_grad[:, lanes]
            grad_low = grad.astype(jnp.bfloat16)
            grad_wide = grad_low.astype(jnp.float32)
            back_ref[...] = jnp.zeros_like(back_ref)
            row_terms = []
            for at in range(0, length, part):
                to = at + part
                decay = jnp.exp(jnp.minimum(col[at:to] - row[:, :to], 0.0))
                weights = (decay * gram_ref[at:to, :to]).astype(jnp.bfloat16)
                again = low_dot(weights, stepped_low[:to], 1, 0)
                row_terms.append(jnp.sum(again * grad_wide[at:to], axis=1, keepdims=True))
                back_ref[:to] += low_dot(weights, grad_low[at:to], 0, 0)
                gram_grad_ref[at:to, :to] += decay * low_dot(
                    grad_low[at:to], stepped_low[:to], 1, 1
                )
            back = back_ref[...]
            tail = jnp.exp(col[length - 1 : length] - col)
            growth = jnp.exp(col)
            ended = from_end[:, lanes] * tail
            end_terms = jnp.sum(ended * stepped, axis=1, keepdims=True)
            col_terms = jnp.sum(back * stepped_low.astype(jnp.float32), axis=1, keepdims=True)
            start_terms = growth * jnp.sum(from_start[:, lanes] * grad, axis=1, keepdims=True)
            whole = jnp.sum(end_terms, axis=0, keepdims=True) + growth[
                length - 1 : length
            ] * jnp.sum(state_dot[:, lanes], axis=1, keepdims=True)
            sum_grad_ref[0, :, head : head + 1] = (
                jnp.concatenate(row_terms, axis=0)
                + start_terms
                - col_terms
                - end_terms
                + jnp.where(last_row, whole, 0.0)
            )
            back = back + ended
            step_grad_ref[0, :, head : head + 1] = jnp.sum(back * here, axis=1, keepdims=True)
            acts_grads.append(taps_here[KW + 1 : KW + 2, lanes] * grad + back * step)
            tails.append((stepped * tail).astype(jnp.bfloat16))
            grown_grads.append((grad * growth).astype(jnp.bfloat16))
        acts_grad_ref[:, :state_dim] += low_dot(jnp.concatenate(tails, axis=1), end, 1, 1)
        acts_grad_ref[:, state_dim:] += low_dot(jnp.concatenate(grown_grads, axis=1), state, 1, 1)
        pre_grad = jnp.concatenate(acts_grads, axis=1) * silu_slope(pre, sigmoid)
        total, rows = convolved_back(extended, pre_grad, taps_here)
        gap = jnp.zeros((EXTRA - 8, wide), jnp.float32)
        in_grad_ref[...] = jnp.concatenate([total[8:], gap, total[:8]], axis=0).astype(jnp.bfloat16)
        rows.append(jnp.sum(out_grad * acts, axis=0, keepdims=True))
        rows.append(jnp.zeros((8 - len(rows), wide), jnp.float32))
        tap_grad_ref[...] = jnp.concatenate(rows, axis=0)

        @pl.when(pl.program_id(0) == pairs - 1)
        def _():
            gram_grad = gram_grad_ref[...]
            rows_of = lax.broadcasted_iota(jnp.int32, (length, length), 0)
            cols_of = lax.broadcasted_iota(jnp.int32, (length, length), 1)
            gram_grad = jnp.where(rows_of >= cols_of, gram_grad, 0.0).astype(jnp.bfloat16)
            acts_grad_ref[:, :state_dim] += low_dot(gram_grad, c_low, 0, 0)
            acts_grad_ref[:, state_dim:] += low_dot(gram_grad, b_low, 1, 0)
            bc_taps_here = bc_tap_ref[...]
            bc_extended, bc_pre = convolved(bc_rim_ref[...], bc_ref[...], bc_taps_here)
            bc_pre_grad = acts_grad_ref[...] * silu_slope(bc_pre, jax.nn.sigmoid(bc_pre))
            bc_total, bc_rows = convolved_back(bc_extended, bc_pre_grad, bc_taps_here)
            bc_grad_ref[:length] = bc_total[8:]
            bc_grad_ref[length : length + EXTRA - 8] = jnp.zeros((EXTRA - 8, shared), jnp.float32)
            bc_grad_ref[length + EXTRA - 8 :] = bc_total[:8]
            bc_rows.append(jnp.zeros((8 - len(bc_rows), shared), jnp.float32))
            bc_tap_grad_ref[...] = jnp.concatenate(bc_rows, axis=0)

    block = pl.BlockSpec((length, wide), lambda i: (0, i))
    eight = pl.BlockSpec((8, wide), lambda i: (0, i))
    table = pl.BlockSpec((1, length, 2), lambda i: (i, 0, 0))
    state_block = pl.BlockSpec((state_dim, wide), lambda i: (0, i))
    bc_block = pl.BlockSpec((length, shared), lambda i: (0, 0))
    bc_eight = pl.BlockSpec((8, shared), lambda i: (0, 0))
    wide_low = jax.ShapeDtypeStruct((length + EXTRA, inner), jnp.bfloat16)
    eight_f32 = jax.ShapeDtypeStruct((8, inner), jnp.float32)
    table_f32 = jax.ShapeDtypeStruct(step_cols.shape, jnp.float32)
    bc_f32 = jax.ShapeDtypeStruct((length + EXTRA, shared), jnp.float32)
    bc_eight_f32 = jax.ShapeDtypeStruct((8, shared), jnp.float32)
    return pl.pallas_call(
        body,
        grid=(pairs,),
        out_shape=(
            wide_low, eight_f32, table_f32, table_f32, bc_f32, bc_eight_f32
        ),
        in_specs=scan_blocks(shared, length, wide)
        + [
            block,
            pl.BlockSpec((length, wide), lambda i: (0, gate_at // wide + i)),
            state_block,
            state_block,
            bc_block,
        ],
        out_specs=(
            pl.BlockSpec((length + EXTRA, wide), lambda i: (0, i)),
            eight,
            table,
            table,
            pl.BlockSpec((length + EXTRA, shared), lambda i: (0, 0)),
            bc_eight,
        ),
        scratch_shapes=[
            pltpu.VMEM((length, length), jnp.float32),
            pltpu.VMEM((length, length), jnp.float32),
            pltpu.VMEM((length, shared), jnp.float32),
            pltpu.VMEM((length, size), jnp.float32),
        ],
        compiler_params=pltpu.CompilerParams(vmem_limit_bytes=56 << 20),
        name="scan_back",
    )(
        first_pre, first_pre, taps, mix_pre, mix_pre, bc_taps, step_cols, sum_cols, sum_rows,
        out_grads, second_pre, state_in, end_grad, bc_low,
    )


def turned(values, cos_wide, sin_wide):
    return values * cos_wide + pltpu.roll(values, values.shape[1] // 2, 1) * sin_wide


def own_mask(at, rows, keys, limit):
    query_row = lax.broadcasted_iota(jnp.int32, (rows, keys), 0) + at
    key_row = lax.broadcasted_iota(jnp.int32, (rows, keys), 1)
    return (key_row <= query_row) & (key_row < limit)


def attention_forward(layout, second_pre, query_at, window, cos_wide, sin_wide, heads):
    length = second_pre.shape[0] - EXTRA
    part = min(ATTN_ROWS, length)
    own_at = window.shape[0] - length
    scale = HD ** (-0.5)

    def body(layout_ref, query_ref, window_ref, cos_ref, sin_ref, out_ref, turned_ref, total_ref):
        query = turned(query_ref[...], cos_ref[...], sin_ref[...]).astype(jnp.bfloat16)
        turned_ref[...] = query
        for at in range(0, length, part):
            to = at + part
            here = query[at:to]

            def scores_of(keys):
                return scale * low_dot(here, keys, 1, 1)

            keys = window_ref[own_at : own_at + to, :HD]
            values = window_ref[own_at : own_at + to, HD:]
            scores = jnp.where(
                own_mask(at, part, to, layout_ref[1]), scores_of(keys), masked_score
            )
            top = jnp.max(scores, axis=1, keepdims=True)
            shares = jnp.exp(scores - top)
            total = jnp.sum(shares, axis=1, keepdims=True)
            acc = low_dot(shares, values, 1, 0)

            def earlier(distance, carry):
                top, total, acc = carry
                start = pl.multiple_of(own_at - distance * length, length)
                scores = scores_of(window_ref[pl.ds(start, length), :HD])
                new_top = jnp.maximum(top, jnp.max(scores, axis=1, keepdims=True))
                fade = jnp.exp(top - new_top)
                shares = jnp.exp(scores - new_top)
                total = fade * total + jnp.sum(shares, axis=1, keepdims=True)
                acc = fade * acc + low_dot(shares, window_ref[pl.ds(start, length), HD:], 1, 0)
                return (new_top, total, acc)

            top, total, acc = lax.fori_loop(1, layout_ref[0] + 1, earlier, (top, total, acc))
            out_ref[at:to] = (acc / total).astype(jnp.bfloat16)
            total_ref[0, at:to] = top + jnp.log(total)

    head = pl.BlockSpec((length, HD), lambda i, layout_ref: (0, i))
    whole = pl.BlockSpec((length, HD), lambda i, layout_ref: (0, 0))
    return pl.pallas_call(
        body,
        out_shape=(
            jax.ShapeDtypeStruct((length, heads * HD), jnp.bfloat16),
            jax.ShapeDtypeStruct((length, heads * HD), jnp.bfloat16),
            jax.ShapeDtypeStruct((heads, length, 1), jnp.float32),
        ),
        grid_spec=pltpu.PrefetchScalarGridSpec(
            num_scalar_prefetch=1,
            grid=(heads,),
            in_specs=[
                pl.BlockSpec((length, HD), lambda i, layout_ref: (0, query_at // HD + i)),
                pl.BlockSpec(window.shape, lambda i, layout_ref: (0, 0)),
                whole,
                whole,
            ],
            out_specs=(
                head,
                head,
                pl.BlockSpec((1, length, 1), lambda i, layout_ref: (i, 0, 0)),
            ),
        ),
        compiler_params=pltpu.CompilerParams(vmem_limit_bytes=48 << 20),
        name="attention_forward",
    )(layout, second_pre, window, cos_wide, sin_wide)


def attention_back(layout, query, window, out, totals, mixed_grad, grad_at, cos_wide, sin_wide):
    length = query.shape[0]
    heads = query.shape[1] // HD
    part = min(ATTN_ROWS, length)
    own_at = window.shape[0] - length
    scale = HD ** (-0.5)

    def body(
        layout_ref, query_ref, window_ref, out_in_ref, total_ref, grad_ref, cos_ref, sin_ref,
        query_grad_ref, window_grad_ref, own_grad_ref, sum_ref, acc_ref,
    ):
        @pl.when(pl.program_id(0) == 0)
        def _():
            sum_ref[...] = jnp.zeros_like(sum_ref)

        for at in range(0, length, part):
            to = at + part
            here = query_ref[at:to]
            grad = grad_ref[at:to].astype(jnp.bfloat16)
            dots = jnp.sum(
                grad.astype(jnp.float32) * out_in_ref[at:to].astype(jnp.float32),
                axis=1,
                keepdims=True,
            )
            total = total_ref[0, at:to]

            def step(start, count, mask):
                keys = window_ref[pl.ds(start, count), :HD]
                values = window_ref[pl.ds(start, count), HD:]
                probs = jnp.exp(scale * low_dot(here, keys, 1, 1) - total)
                if mask is not None:
                    probs = jnp.where(mask, probs, 0.0)
                score_grad = (probs * (low_dot(grad, values, 1, 1) - dots)).astype(jnp.bfloat16)
                sum_ref[pl.ds(start, count), :HD] += low_dot(score_grad, here, 0, 0)
                sum_ref[pl.ds(start, count), HD:] += low_dot(probs, grad, 0, 0)
                return low_dot(score_grad, keys, 1, 0)

            acc_ref[...] = step(own_at, to, own_mask(at, part, to, layout_ref[1]))

            def earlier(distance, carry):
                start = pl.multiple_of(own_at - distance * length, length)
                acc_ref[...] += step(start, length, None)
                return carry

            lax.fori_loop(1, layout_ref[0] + 1, earlier, 0)
            query_grad_ref[at:to] = turned(
                acc_ref[...] * scale, cos_ref[at:to], -sin_ref[at:to]
            ).astype(jnp.bfloat16)

        @pl.when(pl.program_id(0) == heads - 1)
        def _():
            own_grad_ref[:, :HD] = sum_ref[own_at:, :HD] * scale
            own_grad_ref[:, HD:] = sum_ref[own_at:, HD:]
            window_grad_ref[:, :HD] = (sum_ref[:own_at, :HD] * scale).astype(jnp.bfloat16)
            window_grad_ref[:, HD:] = sum_ref[:own_at, HD:].astype(jnp.bfloat16)

    head = pl.BlockSpec((length, HD), lambda i, layout_ref: (0, i))
    whole = pl.BlockSpec((length, HD), lambda i, layout_ref: (0, 0))
    return pl.pallas_call(
        body,
        out_shape=(
            jax.ShapeDtypeStruct(query.shape, jnp.bfloat16),
            jax.ShapeDtypeStruct((own_at, 2 * HD), jnp.bfloat16),
            jax.ShapeDtypeStruct((length, 2 * HD), jnp.float32),
        ),
        grid_spec=pltpu.PrefetchScalarGridSpec(
            num_scalar_prefetch=1,
            grid=(heads,),
            in_specs=[
                head,
                pl.BlockSpec(window.shape, lambda i, layout_ref: (0, 0)),
                head,
                pl.BlockSpec((1, length, 1), lambda i, layout_ref: (i, 0, 0)),
                pl.BlockSpec((length, HD), lambda i, layout_ref: (0, grad_at // HD + i)),
                whole,
                whole,
            ],
            out_specs=(
                head,
                pl.BlockSpec((own_at, 2 * HD), lambda i, layout_ref: (0, 0)),
                pl.BlockSpec((length, 2 * HD), lambda i, layout_ref: (0, 0)),
            ),
            scratch_shapes=[
                pltpu.VMEM(window.shape, jnp.float32),
                pltpu.VMEM((part, HD), jnp.float32),
            ],
        ),
        compiler_params=pltpu.CompilerParams(vmem_limit_bytes=56 << 20),
        name="attention_back",
    )(layout, query, window, out, totals, mixed_grad, cos_wide, sin_wide)


def per_device(
    tokens,
    cotangent,
    mix_norm_gain,
    ssm_gate_proj,
    ssm_input_proj,
    ssm_bc_proj,
    ssm_step_proj,
    conv_in_weight,
    conv_in_bias,
    conv_bc_weight,
    conv_bc_bias,
    step_bias,
    decay_log,
    skip_gain,
    ssm_out_proj,
    query_proj,
    key_proj,
    value_proj,
    attn_out_proj,
    ffn_norm_gain,
    ffn_gate_proj,
    ffn_up_proj,
    ffn_down_proj,
    extra_blocks,
    seq_order,
    pad_rows,
):
    block_rows = tokens.shape[0]
    block_index = lax.axis_index("ctx")
    seq_count = seq_order.shape[0]
    slot_ids = jnp.arange(seq_count, dtype=jnp.int32)
    chosen = (seq_order[:, None] == slot_ids[None, :]).astype(jnp.int32)
    counts = jnp.sum(chosen * extra_blocks[None, :], axis=1) + 1
    slot_pads = jnp.sum(chosen * pad_rows[None, :], axis=1)
    slot_ends = jnp.cumsum(counts)
    starts = slot_ends - counts
    inside = (starts <= block_index) & (block_index < slot_ends)
    within = jnp.sum(jnp.where(inside, block_index - starts, 0))
    pad_here = jnp.sum(jnp.where(inside & (slot_ends - 1 == block_index), slot_pads, 0))
    row_ids = jnp.arange(block_rows, dtype=jnp.int32)
    valid_rows = (row_ids < block_rows - pad_here).astype(jnp.float32)
    positions = within * block_rows + row_ids
    keep_state = (within > 0).astype(jnp.float32)
    devices = lax.axis_size("ctx")
    codes = jnp.asarray(slot_devices(devices), jnp.int32)
    from_whole = jnp.bitwise_xor(codes, block_index)
    to_whole = jnp.argsort(from_whole).astype(jnp.int32)
    rows_here = mix_norm_gain.shape[0]
    misc_here = jnp.concatenate(
        [
            ssm_step_proj,
            mix_norm_gain[:, None],
            ffn_norm_gain[:, None],
            conv_bc_weight.reshape(rows_here, 1),
            jnp.pad(conv_bc_bias, (0, rows_here - conv_bc_bias.shape[0]))[:, None],
        ],
        axis=1,
    )
    steps = ssm_step_proj.shape[1]
    misc_here = jnp.pad(misc_here, ((0, 0), (0, 128 - misc_here.shape[1])))
    inner, shared = (ssm_input_proj.shape[1], ssm_bc_proj.shape[1])
    heads_wide, pair_wide = (query_proj.shape[1], key_proj.shape[1])
    across = [4 * k for k in range(1, devices // 4)]
    mix_here = jnp.concatenate([ssm_bc_proj, misc_here, query_proj, key_proj, value_proj], axis=1)
    out_here = jnp.concatenate([ssm_out_proj, attn_out_proj], axis=0)
    first_here = jnp.concatenate([ssm_input_proj, mix_here, ssm_gate_proj], axis=1)
    first_held = spread([([0], first_here)], 0, across)
    gate_from = inner + mix_here.shape[1]
    input_held = spread([(here, piece[:, :inner]) for here, piece in first_held], 0, [1], merge=True)
    mix_held = [(here, piece[:, inner:gate_from]) for here, piece in first_held]
    mix_held = spread(mix_held, 0, [2], merge=True)
    gate_held = [(here, piece[:, gate_from:]) for here, piece in first_held]
    near = (input_held[-1][1], mix_held[-1][1])
    input_held = spread(input_held, 0, [2])
    mix_held = spread(mix_held, 0, [1])
    ffn_gate_weight = lax.all_gather(after(ffn_gate_proj, *near), "ctx", axis=0, tiled=True)
    out_held = spread([([0], out_here)], 1, across, near)
    input_weight = joined(input_held, 0)
    mix_weights = joined(mix_held, 0)
    misc = mix_weights[:, shared : shared + 128]
    mix_gain = misc[:, steps].astype(jnp.float32)

    def whole_order(column):
        return jnp.take(column.reshape(devices, rows_here), to_whole, axis=0)

    conv_bc_full = whole_order(misc[:, steps + 2]).reshape(shared, KW)
    conv_bc_offset = whole_order(misc[:, steps + 3])[:, : conv_bc_bias.shape[0]].reshape(shared)
    gain_two = whole_order(misc[:, steps + 1]).reshape(-1)
    inputs = tokens.astype(jnp.float32)
    rim_rows = KW - 1
    edge = shifted(tokens[block_rows - EXTRA :], "ctx", 1)
    edge_rows = jnp.arange(EXTRA, dtype=jnp.int32)[:, None] >= EXTRA - rim_rows
    edge = jnp.where(edge_rows & (within > 0), edge, jnp.zeros_like(edge))
    tokens_longer = jnp.concatenate([tokens, edge], axis=0)
    normed_low = rms_scale(
        reordered(tokens_longer, from_whole).astype(jnp.float32), mix_gain
    ).astype(jnp.bfloat16)
    first_pre = plain_product(normed_low, input_weight)
    mix_pre = plain_product(normed_low, mix_weights)
    ffn_up_weight = lax.all_gather(after(ffn_up_proj, mix_pre), "ctx", axis=0, tiled=True)
    step_raw = mix_pre[:block_rows, shared : shared + steps]
    query_at = shared + 128
    key_at = query_at + heads_wide
    key_pre = mix_pre[:block_rows, key_at : key_at + pair_wide]
    value_pre = mix_pre[:block_rows, key_at + pair_wide :]
    gate_held = spread(gate_held, 0, [2], (first_pre,), merge=True)
    out_held = spread(out_held, 1, [1], (first_pre,), merge=True)
    head_dim = inner // steps
    skips = jnp.repeat(skip_gain.astype(jnp.float32), head_dim)[None, :]
    taps = jnp.concatenate(
        [conv_in_weight.astype(jnp.float32).T, conv_in_bias.astype(jnp.float32)[None, :], skips]
    )
    taps = jnp.pad(taps, ((0, 8 - taps.shape[0]), (0, 0)))
    bc_taps = jnp.concatenate(
        [conv_bc_full.astype(jnp.float32).T, conv_bc_offset.astype(jnp.float32)[None, :]]
    )
    bc_taps = jnp.pad(bc_taps, ((0, 8 - bc_taps.shape[0]), (0, 0)))
    step_in = step_raw + step_bias.astype(jnp.float32)[None, :]
    step_size = jax.nn.softplus(step_in)
    rate = -jnp.exp(decay_log.astype(jnp.float32))[None, :]
    lower = (row_ids[:, None] >= row_ids[None, :]).astype(jnp.float32)
    log_decay = jnp.dot(lower, rate * step_size, precision=highest)

    def by_pairs(table):
        return table.reshape(block_rows, steps // 2, 2).transpose(1, 0, 2)

    def from_pairs(table):
        return table.transpose(1, 0, 2).reshape(block_rows, steps)

    step_cols = by_pairs(step_size)
    sum_cols = by_pairs(log_decay)
    sum_rows = log_decay.T.reshape(steps // 2, 2, block_rows)
    intra_out, local_states, bc_low = scan_forward(
        first_pre, mix_pre, taps, bc_taps, step_cols, sum_cols, sum_rows, inner, shared
    )
    ffn_down_weight = lax.all_gather(after(ffn_down_proj, local_states), "ctx", axis=1, tiled=True)
    decay_row = keep_state * jnp.repeat(jnp.exp(log_decay[block_rows - 1]), head_dim)[None, :]
    keep_low = keep_state.astype(jnp.bfloat16)
    reached, returned = carried_states(local_states, decay_row, False)
    state_in = keep_low * reached
    gate_held = spread(gate_held, 0, [1], (returned,))
    out_held = spread(out_held, 1, [2], (returned,))
    cos_table, sin_table = rotary_tables(positions)
    cos_wide = jnp.concatenate([cos_table, cos_table], axis=1)
    sin_wide = jnp.concatenate([-sin_table, sin_table], axis=1)
    key_rot = rotate(key_pre.reshape(block_rows, -1, HD), cos_table, sin_table)
    own_pair = jnp.concatenate(
        [key_rot.reshape(block_rows, HD).astype(jnp.bfloat16), value_pre.astype(jnp.bfloat16)],
        axis=1,
    )
    earlier_pairs = [shifted(own_pair, "ctx", distance) for distance in range(MAXB - 1, 0, -1)]
    window = jnp.concatenate(earlier_pairs + [own_pair], axis=0)
    layout = jnp.stack([within, block_rows - pad_here]).astype(jnp.int32)
    attn_low, query_rot, log_totals = attention_forward(
        layout, mix_pre, query_at, window, cos_wide, sin_wide, heads_wide // HD
    )
    gate_weight = joined(gate_held, 0)
    gate_pre = plain_product(normed_low, gate_weight)
    scan_out, ssm_low = scan_gated(intra_out, state_in, bc_low, sum_cols, gate_pre, 0)
    out_weights = joined(out_held, 1)
    mixed_low = jnp.concatenate([ssm_low, attn_low], axis=1)
    mixed_part = plain_product(mixed_low, out_weights)
    hidden = inputs + reordered(pair_sum(mixed_part), to_whole)
    normed_two, norm_two_back = jax.vjp(rms_scale, hidden, gain_two.astype(jnp.float32))
    normed_two_low = normed_two.astype(jnp.bfloat16)
    ffn_gate = plain_product(normed_two_low, ffn_gate_weight)
    ffn_up = plain_product(normed_two_low, ffn_up_weight)
    ffn_act = (jax.nn.silu(ffn_gate) * ffn_up).astype(jnp.bfloat16)
    ffn_part = plain_product(ffn_act, ffn_down_weight)
    ffn_sum = pair_sum(ffn_part)
    layer_out = ((hidden + ffn_sum) * valid_rows[:, None]).astype(jnp.bfloat16)
    cot_low = (cotangent.astype(jnp.float32) * valid_rows[:, None]).astype(jnp.bfloat16)
    grad_out = cot_low.astype(jnp.float32)

    def in_quarters(value):
        return jnp.split(value, 4, axis=1)

    def rows_grad(left_side, right_side, first, gates=(), later=()):
        parts = [product_of_cols(part, right_side) for part in in_quarters(left_side)]
        return Reduction(parts, 0, first, gates, later)

    def cols_grad(left_side, right_side, first, gates=()):
        parts = [product_of_cols(left_side, part) for part in in_quarters(right_side)]
        return Reduction(parts, 1, first, gates)

    down_sum = cols_grad(ffn_act, reordered(cot_low, from_whole), 1)
    act_grad = product_by_rows(cot_low, ffn_down_weight)
    gate_sigmoid = jax.nn.sigmoid(ffn_gate)
    ffn_gate_low = (
        act_grad * ffn_up * gate_sigmoid * (1.0 + ffn_gate * (1.0 - gate_sigmoid))
    ).astype(jnp.bfloat16)
    ffn_up_low = (act_grad * jax.nn.silu(ffn_gate)).astype(jnp.bfloat16)
    norm_two_part = product_by_rows(ffn_gate_low, ffn_gate_weight) + product_by_rows(
        ffn_up_low, ffn_up_weight
    )
    norm_two_grad = pair_sum(norm_two_part)
    hidden_norm_grad, gain_two_grad = norm_two_back(norm_two_grad)
    hidden_grad = grad_out + hidden_norm_grad
    hidden_low = reordered(hidden_grad.astype(jnp.bfloat16), from_whole)
    mixed_grad = product_by_rows(hidden_low, out_weights)
    ssm_gate_low, state_in_grad = scan_gated_back(
        mixed_grad, scan_out, bc_low, sum_cols, gate_pre, 0
    )
    end_grad, returned = carried_states(keep_low * state_in_grad, decay_row, True)
    layout = after(layout, returned)
    query_grad_low, window_grad, own_pair_grad = attention_back(
        layout, query_rot, window, attn_low, log_totals, mixed_grad, inner, cos_wide, sin_wide
    )
    for distance in range(1, MAXB):
        at = (MAXB - 1 - distance) * block_rows
        own_pair_grad = own_pair_grad + shifted(
            window_grad[at : at + block_rows], "ctx", -distance
        ).astype(jnp.float32)
    down_sum.onward(end_grad, query_grad_low)
    free = (end_grad, query_grad_low)
    normed_two_slots = reordered(normed_two_low, from_whole)
    swish_sum = rows_grad(normed_two_slots, ffn_gate_low, 2, (ssm_gate_low,), free)
    up_sum = rows_grad(normed_two_slots, ffn_up_low, 1, (ssm_gate_low,), free)
    out_sum = cols_grad(mixed_low, hidden_low, 1, free)
    gate_sum = rows_grad(normed_low, ssm_gate_low, 2, free)
    key_grad_low = (
        rotate(own_pair_grad[:, :HD].reshape(block_rows, 1, HD), cos_table, -sin_table)
        .reshape(block_rows, HD)
        .astype(jnp.bfloat16)
    )
    value_grad_low = own_pair_grad[:, HD:].astype(jnp.bfloat16)
    input_grad_low, tap_grad, step_part, sum_part, bc_pre_part, bc_tap_grad = scan_back(
        first_pre, mix_pre, taps, bc_taps, step_cols, sum_cols, sum_rows,
        mixed_grad, gate_pre, 0, state_in, end_grad, bc_low,
    )
    rate_grad = lax.dot_general(
        lower, from_pairs(sum_part), (((0,), (0,)), ((), ())), precision=highest
    )
    step_grad = (from_pairs(step_part) + rate * rate_grad) * jax.nn.sigmoid(step_in)
    step_grad_low = step_grad.astype(jnp.bfloat16)
    tap_sums = [
        tap_grad[:KW].T,
        tap_grad[KW],
        jnp.sum(step_grad, axis=0),
        jnp.sum(rate_grad * rate * step_size, axis=0),
        jnp.sum(tap_grad[KW + 1].reshape(steps, head_dim), axis=1),
    ]
    no_misc = jnp.zeros((block_rows, 128 - steps), jnp.bfloat16)
    mix_grads = jnp.concatenate(
        [step_grad_low, no_misc, query_grad_low, key_grad_low, value_grad_low], axis=1
    )
    mix_grads = jnp.pad(mix_grads, ((0, EXTRA), (0, 0)))
    bc_grad_low = pair_sum(bc_pre_part).astype(jnp.bfloat16)
    input_sum = rows_grad(normed_low, input_grad_low, 1)
    mix_sum = rows_grad(normed_low, jnp.concatenate([bc_grad_low, mix_grads], axis=1), 2)
    mix_grads = jnp.concatenate([bc_pre_part.astype(jnp.bfloat16), mix_grads], axis=1)
    norm_one_part = (
        product_by_rows(input_grad_low, input_weight)
        + product_by_rows(mix_grads, mix_weights)
        + product_by_rows(ssm_gate_low, gate_weight)
    )
    up_sum.onward(norm_one_part)
    swish_sum.onward(up_sum.far_low)
    down_sum.last(swish_sum.far_low)
    out_sum.onward(*down_sum.blocks_low)
    gate_sum.onward(out_sum.far_low)
    up_sum.last(gate_sum.far_low)
    swish_sum.last(*up_sum.blocks_low)
    mix_sum.onward(*swish_sum.blocks_low)
    input_sum.onward(mix_sum.far_low)
    gate_sum.last(input_sum.far_low)
    out_sum.last(*gate_sum.blocks_low)
    mix_sum.last(*out_sum.blocks_low)
    input_sum.last(*mix_sum.blocks_low)
    norm_one_grad = reordered(pair_sum(norm_one_part), to_whole)
    conv_bc_grads = jnp.concatenate([bc_tap_grad[:KW].T.reshape(-1), bc_tap_grad[KW]])
    conv_bc_grads = conv_bc_grads + swap(conv_bc_grads)
    longer = tokens_longer.astype(jnp.float32)
    scale_one = lax.rsqrt(jnp.mean(longer * longer, axis=1, keepdims=True) + epsilon)
    gain_one_grad = jnp.sum(norm_one_grad * longer * scale_one, axis=0)
    edge_back = shifted(keep_state * norm_one_grad[block_rows + EXTRA - 8 :], "ctx", -1)
    norm_one_grad = norm_one_grad[:block_rows] + jnp.pad(edge_back, ((block_rows - 8, 0), (0, 0)))
    _, norm_one_back = jax.vjp(lambda v: rms_scale(v, whole_order(mix_gain).reshape(-1)), inputs)
    tokens_grad = hidden_grad + norm_one_back(norm_one_grad)[0]
    small = [
        tap_sums[0].reshape(-1),
        *tap_sums[1:],
        conv_bc_grads,
        gain_one_grad,
        gain_two_grad,
    ]
    packed = jnp.concatenate(small)
    filled = -packed.shape[0] % 1024
    packed = summed(jnp.pad(packed, (0, filled)).reshape(-1, 128)).reshape(-1)
    sums, at = ([], 0)
    for part in small:
        sums.append(packed[at : at + part.shape[0]])
        at += part.shape[0]

    def own(vector, count):
        return lax.dynamic_slice_in_dim(vector, block_index * count, count, 0)

    mix_grad = mix_sum.total()
    out_grad = out_sum.total()
    conv_bc_sums = sums[5]
    conv_rows = conv_bc_weight.shape[0]
    return (
        layer_out,
        tokens_grad.astype(jnp.bfloat16),
        own(sums[6], rows_here),
        gate_sum.total(),
        input_sum.total(),
        mix_grad[:, :shared],
        mix_grad[:, shared : shared + steps],
        sums[0].reshape(inner, KW),
        sums[1],
        own(conv_bc_sums[: shared * KW], conv_rows * KW).reshape(conv_rows, KW),
        own(conv_bc_sums[shared * KW :], conv_rows),
        sums[2],
        sums[3],
        sums[4],
        out_grad[:inner],
        mix_grad[:, query_at:key_at],
        mix_grad[:, key_at : key_at + pair_wide],
        mix_grad[:, key_at + pair_wide :],
        out_grad[inner:],
        own(sums[7], rows_here),
        swish_sum.total(),
        up_sum.total(),
        down_sum.total(),
    )


def solution(mesh):
    return jax.shard_map(
        per_device,
        mesh=mesh,
        in_specs=(
            P("ctx", None),
            P("ctx", None),
            P("ctx"),
            P("ctx", "wt"),
            P("ctx", "wt"),
            P("ctx", None),
            P("ctx", "wt"),
            P("wt", None),
            P("wt"),
            P("ctx", None),
            P("ctx"),
            P("wt"),
            P("wt"),
            P("wt"),
            P("wt", "ctx"),
            P("ctx", "wt"),
            P("ctx", "wt"),
            P("ctx", "wt"),
            P("wt", "ctx"),
            P("ctx"),
            P("ctx", "wt"),
            P("ctx", "wt"),
            P("wt", "ctx"),
            P(),
            P(),
            P(),
        ),
        out_specs=(
            P("ctx", None),
            P("ctx", None),
            P("ctx"),
            P("ctx", "wt"),
            P("ctx", "wt"),
            P("ctx", None),
            P("ctx", "wt"),
            P("wt", None),
            P("wt"),
            P("ctx", None),
            P("ctx"),
            P("wt"),
            P("wt"),
            P("wt"),
            P("wt", "ctx"),
            P("ctx", "wt"),
            P("ctx", "wt"),
            P("ctx", "wt"),
            P("wt", "ctx"),
            P("ctx"),
            P("ctx", "wt"),
            P("ctx", "wt"),
            P("wt", "ctx"),
        ),
        check_vma=False,
    )
```

```python
import jax
import jax.numpy as jnp
from jax import lax
from jax.experimental import pallas as pl
from jax.experimental.pallas import tpu as pltpu
from jax.sharding import PartitionSpec as P


HD = 128
KW = 4
MAXB = 8
EXTRA = 16
SCAN_ROWS = 128
ATTN_ROWS = 256


epsilon = 1e-05
rope_base = 100000000000.0
highest = lax.Precision.HIGHEST
masked_score = -1e30


def shifted(value, axis, steps):
    count = lax.axis_size(axis)
    leading, last = (max(0, -steps), min(count, count - steps))
    return lax.ppermute(value, axis, [(source, source + steps) for source in range(leading, last)])


def hop(value, code):
    if code == 0:
        return value
    count = lax.axis_size("ctx")
    return lax.ppermute(value, "ctx", [(source, source ^ code) for source in range(count)])


def swap(value):
    return lax.ppermute(value, "wt", [(0, 1), (1, 0)])


def pair_sum(value):
    rounded = lax.reduce_precision(value, 8, 7)
    return rounded + swap(rounded.astype(jnp.bfloat16)).astype(jnp.float32)


def slot_devices(count):
    high = count // 4
    return [4 * (slot % high) + slot // high for slot in range(count)]


def after(value, *gates):
    return lax.optimization_barrier((value, *gates))[0]


def spread(held, axis, codes, gates=(), merge=False):
    if merge:
        every = [code for here, _ in held for code in here]
        held = [(every, jnp.concatenate([array for _, array in held], axis=axis))]
    taken = list(held)
    for here, array in held:
        operand = after(array, *gates) if gates else array
        for code in codes:
            taken.append(([one ^ code for one in here], hop(operand, code)))
    return taken


def joined(held, axis):
    size = sum(array.shape[axis] for _, array in held) // sum(len(here) for here, _ in held)
    found = {code: (i, at) for i, (here, _) in enumerate(held) for at, code in enumerate(here)}
    runs = []
    for code in slot_devices(len(found)):
        i, at = found[code]
        if runs and runs[-1][0] == i and runs[-1][2] == at:
            runs[-1][2] = at + 1
        else:
            runs.append([i, at, at + 1])
    return jnp.concatenate(
        [lax.slice_in_dim(held[i][1], at * size, to * size, axis=axis) for i, at, to in runs],
        axis=axis,
    )


class Reduction:
    def __init__(self, parts, axis, first, gates=(), later=()):
        self.axis, self.second = (axis, 3 - first)
        self.near, self.far = (parts[0], parts[3 - first])
        low = [parts[k].astype(jnp.bfloat16) for k in (first, 3)]
        if gates:
            low = list(lax.optimization_barrier((*low, *gates))[:2])
        if later:
            low[1] = after(low[1], *later)
        one = hop(low[0], first)
        self.got = [one, hop(low[1], first)]

    def onward(self, *gates):
        got = lax.optimization_barrier((*self.got, *gates))[:2] if gates else self.got
        self.far_low = (self.far + got[1].astype(jnp.float32)).astype(jnp.bfloat16)
        self.near = self.near + got[0].astype(jnp.float32)
        self.got = [hop(self.far_low, self.second)]

    def last(self, *gates):
        high = lax.axis_size("ctx") // 4
        got = after(self.got[0], *gates) if gates else self.got[0]
        quarter = self.near + got.astype(jnp.float32)
        blocks = jnp.split(quarter, high, axis=self.axis)
        self.block = blocks[0]
        self.blocks_low = [block.astype(jnp.bfloat16) for block in blocks[1:]]
        self.got = [hop(block, 4 * (k + 1)) for k, block in enumerate(self.blocks_low)]

    def total(self):
        total = self.block
        for got in self.got:
            total = total + got.astype(jnp.float32)
        return total


def summed(value, bits):
    for bit in bits:
        value = value + hop(value, bit)
    return value


def reordered(value, order):
    blocks = order.shape[0]
    rows, width = value.shape[0], value.shape[1] // blocks
    if width % 128:
        return jnp.take(value.reshape(rows, blocks, width), order, axis=1).reshape(rows, -1)

    steps = 4 if rows % 64 == 0 else 3
    part = rows // steps

    def body(order_ref, in_ref, out_ref):
        for slot in range(blocks):
            start = pl.multiple_of(order_ref[slot] * width, width)
            out_ref[:, slot * width : (slot + 1) * width] = in_ref[:, pl.ds(start, width)]

    block = pl.BlockSpec((part, value.shape[1]), lambda i, order_ref: (i, 0))
    return pl.pallas_call(
        body,
        out_shape=jax.ShapeDtypeStruct(value.shape, value.dtype),
        grid_spec=pltpu.PrefetchScalarGridSpec(
            num_scalar_prefetch=1, grid=(steps,), in_specs=[block], out_specs=block
        ),
        name="reordered",
    )(order, value)


def carried_states(states, decays, reverse):
    me = lax.axis_index("ctx")
    place = me % 4
    width = states.shape[1] // 4
    low = states.astype(jnp.bfloat16)

    def quarter(value, index):
        return lax.dynamic_slice_in_dim(value, index * width, width, 1)

    got = [hop(quarter(low, place ^ k), k) for k in range(4)]
    got_decay = [hop(quarter(decays, place ^ k), k) for k in range(4)]

    def in_order(pieces):
        odd = place % 2 == 1
        pieces = [jnp.where(odd, pieces[k ^ 1], pieces[k]) for k in range(4)]
        upper = place >= 2
        return [jnp.where(upper, pieces[k ^ 2], pieces[k]) for k in range(4)]

    blocks = [piece.astype(jnp.float32) for piece in in_order(got)]
    rates = in_order(got_decay)
    if reverse:
        blocks, rates = (blocks[::-1], rates[::-1])
    total, rate = (blocks[0], rates[0])
    for block, block_rate in zip(blocks[1:], rates[1:]):
        total, rate = (block + block_rate * total, block_rate * rate)
    step = -4 if reverse else 4
    total_low = total.astype(jnp.bfloat16)
    near, near_rate = (shifted(total_low, "ctx", step), shifted(rate, "ctx", step))
    far = shifted(total_low, "ctx", 2 * step)
    state = near.astype(jnp.float32) + near_rate * far.astype(jnp.float32)
    reached = []
    for block, block_rate in zip(blocks, rates):
        reached.append(state.astype(jnp.bfloat16))
        state = block + block_rate * state
    if reverse:
        reached = reached[::-1]
    mine = in_order(reached)
    back = in_order([hop(mine[k], k) for k in range(4)])
    return (jnp.concatenate(back, axis=1), mine[1])


def plain_product(left_side, right_side):
    return jnp.dot(left_side, right_side, preferred_element_type=jnp.float32)


def product_by_rows(left_side, right_side):
    return lax.dot_general(
        left_side, right_side, (((1,), (1,)), ((), ())), preferred_element_type=jnp.float32
    )


def product_of_cols(left_side, right_side):
    return lax.dot_general(
        left_side, right_side, (((0,), (0,)), ((), ())), preferred_element_type=jnp.float32
    )


def rms_scale(values, gain_vec):
    return (
        values * lax.rsqrt(jnp.mean(values * values, axis=-1, keepdims=True) + epsilon) * gain_vec
    )


def rotary_tables(positions):
    exponents = jnp.arange(HD // 2, dtype=jnp.float32) * (2.0 / HD)
    frequency = jnp.power(jnp.float32(rope_base), -exponents)
    angles = positions.astype(jnp.float32)[:, None] * frequency[None, :]
    return (jnp.cos(angles), jnp.sin(angles))


def rotate(values, cos_table, sin_table):
    half_dim = values.shape[-1] // 2
    first_half = values[..., :half_dim]
    second_half = values[..., half_dim:]
    cos_table = cos_table[:, None, :]
    sin_table = sin_table[:, None, :]
    return jnp.concatenate(
        [
            first_half * cos_table - second_half * sin_table,
            second_half * cos_table + first_half * sin_table,
        ],
        axis=-1,
    )


def convolved(rim, block, taps):
    length = block.shape[0]
    extended = jnp.concatenate([rim, block], axis=0)
    first = rim.shape[0] - (KW - 1)
    summed = taps[KW : KW + 1]
    for j in range(KW):
        summed = summed + extended[first + j : first + j + length] * taps[j : j + 1]
    return (extended, summed)


def convolved_back(extended, pre_grad, taps):
    length = pre_grad.shape[0]
    rim_rows = extended.shape[0] - length
    first = rim_rows - (KW - 1)
    zeros = jnp.zeros((8, pre_grad.shape[1]), jnp.float32)
    padded = jnp.concatenate([zeros, pre_grad, zeros], axis=0)
    total = jnp.zeros_like(extended)
    rows = []
    for j in range(KW):
        start = 8 - rim_rows + KW - 1 - j
        total = total + padded[start : start + rim_rows + length] * taps[j : j + 1]
        rows.append(
            jnp.sum(pre_grad * extended[first + j : first + j + length], axis=0, keepdims=True)
        )
    rows.append(jnp.sum(pre_grad, axis=0, keepdims=True))
    return (total, rows)


def silu_slope(value, sigmoid):
    return sigmoid * (1.0 + value * (1.0 - sigmoid))


def low_dot(left_side, right_side, left_axis, right_axis):
    return lax.dot_general(
        left_side.astype(jnp.bfloat16),
        right_side.astype(jnp.bfloat16),
        (((left_axis,), (right_axis,)), ((), ())),
        preferred_element_type=jnp.float32,
    )


def lower_gram(c_low, b_low):
    length = c_low.shape[0]
    gram = low_dot(c_low, b_low, 1, 1)
    rows = lax.broadcasted_iota(jnp.int32, (length, length), 0)
    cols = lax.broadcasted_iota(jnp.int32, (length, length), 1)
    return jnp.where(rows >= cols, gram, 0.0)


def scan_blocks(shared, length, wide):
    return [
        pl.BlockSpec((length, wide), lambda i: (0, i)),
        pl.BlockSpec((8, wide), lambda i: ((length + EXTRA) // 8 - 1, i)),
        pl.BlockSpec((8, wide), lambda i: (0, i)),
        pl.BlockSpec((length, shared), lambda i: (0, 0)),
        pl.BlockSpec((8, shared), lambda i: ((length + EXTRA) // 8 - 1, 0)),
        pl.BlockSpec((8, shared), lambda i: (0, 0)),
        pl.BlockSpec((1, length, 2), lambda i: (i, 0, 0)),
        pl.BlockSpec((1, length, 2), lambda i: (i, 0, 0)),
        pl.BlockSpec((1, 2, length), lambda i: (i, 0, 0)),
    ]


def scan_forward(first_pre, mix_pre, taps, bc_taps, step_cols, sum_cols, sum_rows, inner, shared):
    length = first_pre.shape[0] - EXTRA
    pairs = step_cols.shape[0]
    wide = inner // pairs
    size = wide // 2
    state_dim = shared // 2
    part = min(SCAN_ROWS, length)

    def body(
        in_ref, rim_ref, tap_ref, bc_ref, bc_rim_ref, bc_tap_ref, step_ref, col_ref, row_ref,
        out_ref, state_ref, bc_low_ref, gram_ref,
    ):
        @pl.when(pl.program_id(0) == 0)
        def _():
            _, pre = convolved(bc_rim_ref[...], bc_ref[...], bc_tap_ref[...])
            acts = (pre * jax.nn.sigmoid(pre)).astype(jnp.bfloat16)
            bc_low_ref[...] = acts
            gram_ref[...] = lower_gram(acts[:, state_dim:], acts[:, :state_dim])

        taps_here = tap_ref[...]
        _, pre = convolved(rim_ref[...], in_ref[...], taps_here)
        acts = pre * jax.nn.sigmoid(pre)
        tails = []
        for head in range(2):
            lanes = slice(head * size, (head + 1) * size)
            step = step_ref[0][:, head : head + 1]
            col = col_ref[0][:, head : head + 1]
            row = row_ref[0][head : head + 1, :]
            stepped = acts[:, lanes] * step
            stepped_low = stepped.astype(jnp.bfloat16)
            for at in range(0, length, part):
                end = at + part
                decay = jnp.exp(jnp.minimum(col[at:end] - row[:, :end], 0.0))
                weights = (decay * gram_ref[at:end, :end]).astype(jnp.bfloat16)
                out_ref[at:end, lanes] = low_dot(weights, stepped_low[:end], 1, 0) + (
                    taps_here[KW + 1 : KW + 2, lanes] * acts[at:end, lanes]
                )
            tails.append(stepped * jnp.exp(col[length - 1 : length] - col))
        tail = jnp.concatenate(tails, axis=1)
        state_ref[...] = low_dot(bc_low_ref[:, :state_dim], tail, 0, 0).astype(jnp.bfloat16)

    return pl.pallas_call(
        body,
        grid=(pairs,),
        out_shape=(
            jax.ShapeDtypeStruct((length, inner), jnp.float32),
            jax.ShapeDtypeStruct((state_dim, inner), jnp.bfloat16),
            jax.ShapeDtypeStruct((length, shared), jnp.bfloat16),
        ),
        in_specs=scan_blocks(shared, length, wide),
        out_specs=(
            pl.BlockSpec((length, wide), lambda i: (0, i)),
            pl.BlockSpec((state_dim, wide), lambda i: (0, i)),
            pl.BlockSpec((length, shared), lambda i: (0, 0)),
        ),
        scratch_shapes=[pltpu.VMEM((length, length), jnp.float32)],
        compiler_params=pltpu.CompilerParams(vmem_limit_bytes=48 << 20),
        name="scan_forward",
    )(first_pre, first_pre, taps, mix_pre, mix_pre, bc_taps, step_cols, sum_cols, sum_rows)


def scan_gated(intra, state_in, bc_low, sum_cols, second_pre, gate_at):
    length, inner = intra.shape
    pairs = sum_cols.shape[0]
    wide = inner // pairs
    size = wide // 2
    state_dim = bc_low.shape[1] // 2

    def body(intra_ref, state_ref, c_ref, col_ref, gate_ref, out_ref, act_ref):
        carried = low_dot(c_ref[...], state_ref[...], 1, 0)
        gate = gate_ref[...]
        silu = gate * jax.nn.sigmoid(gate)
        for head in range(2):
            lanes = slice(head * size, (head + 1) * size)
            growth = jnp.exp(col_ref[0][:, head : head + 1])
            whole = intra_ref[:, lanes] + carried[:, lanes] * growth
            out_ref[:, lanes] = whole
            act_ref[:, lanes] = (whole * silu[:, lanes]).astype(jnp.bfloat16)

    block = pl.BlockSpec((length, wide), lambda i: (0, i))
    return pl.pallas_call(
        body,
        grid=(pairs,),
        out_shape=(
            jax.ShapeDtypeStruct((length, inner), jnp.float32),
            jax.ShapeDtypeStruct((length, inner), jnp.bfloat16),
        ),
        in_specs=[
            block,
            pl.BlockSpec((state_dim, wide), lambda i: (0, i)),
            pl.BlockSpec((length, state_dim), lambda i: (0, 1)),
            pl.BlockSpec((1, length, 2), lambda i: (i, 0, 0)),
            pl.BlockSpec((length, wide), lambda i: (0, gate_at // wide + i)),
        ],
        out_specs=(block, block),
        compiler_params=pltpu.CompilerParams(vmem_limit_bytes=48 << 20),
        name="scan_gated",
    )(intra, state_in, bc_low, sum_cols, second_pre)


def scan_gated_back(out_grads, whole, bc_low, sum_cols, second_pre, gate_at):
    length, inner = whole.shape
    pairs = sum_cols.shape[0]
    wide = inner // pairs
    size = wide // 2
    state_dim = bc_low.shape[1] // 2

    def body(grad_ref, whole_ref, c_ref, col_ref, gate_ref, gate_grad_ref, state_ref):
        gate = gate_ref[...]
        sigmoid = jax.nn.sigmoid(gate)
        grad = grad_ref[...]
        gate_grad = grad * whole_ref[...] * silu_slope(gate, sigmoid)
        gate_grad_ref[:length] = gate_grad.astype(jnp.bfloat16)
        gate_grad_ref[length:] = jnp.zeros((EXTRA, wide), jnp.bfloat16)
        inside = grad * (gate * sigmoid)
        grown = [
            inside[:, head * size : (head + 1) * size] * jnp.exp(col_ref[0][:, head : head + 1])
            for head in range(2)
        ]
        state_ref[...] = low_dot(c_ref[...], jnp.concatenate(grown, axis=1), 0, 0).astype(
            jnp.bfloat16
        )

    block = pl.BlockSpec((length, wide), lambda i: (0, i))
    return pl.pallas_call(
        body,
        grid=(pairs,),
        out_shape=(
            jax.ShapeDtypeStruct((length + EXTRA, inner), jnp.bfloat16),
            jax.ShapeDtypeStruct((state_dim, inner), jnp.bfloat16),
        ),
        in_specs=[
            block,
            block,
            pl.BlockSpec((length, state_dim), lambda i: (0, 1)),
            pl.BlockSpec((1, length, 2), lambda i: (i, 0, 0)),
            pl.BlockSpec((length, wide), lambda i: (0, gate_at // wide + i)),
        ],
        out_specs=(
            pl.BlockSpec((length + EXTRA, wide), lambda i: (0, i)),
            pl.BlockSpec((state_dim, wide), lambda i: (0, i)),
        ),
        compiler_params=pltpu.CompilerParams(vmem_limit_bytes=48 << 20),
        name="scan_gated_back",
    )(out_grads, whole, bc_low, sum_cols, second_pre)


def scan_back(
    first_pre, mix_pre, taps, bc_taps, step_cols, sum_cols, sum_rows,
    out_grads, second_pre, gate_at, state_in, end_grad, bc_low,
):
    length = first_pre.shape[0] - EXTRA
    pairs = step_cols.shape[0]
    state_dim, inner = state_in.shape
    shared = bc_low.shape[1]
    wide = inner // pairs
    size = wide // 2
    part = min(SCAN_ROWS, length)

    def body(
        in_ref, rim_ref, tap_ref, bc_ref, bc_rim_ref, bc_tap_ref, step_ref, col_ref, row_ref,
        grad_ref, gate_ref, state_ref, end_ref, bc_low_ref,
        in_grad_ref, tap_grad_ref, step_grad_ref, sum_grad_ref, bc_grad_ref, bc_tap_grad_ref,
        gram_ref, gram_grad_ref, acts_grad_ref, back_ref,
    ):
        b_low = bc_low_ref[:, :state_dim]
        c_low = bc_low_ref[:, state_dim:]

        @pl.when(pl.program_id(0) == 0)
        def _():
            gram_ref[...] = lower_gram(c_low, b_low)
            gram_grad_ref[...] = jnp.zeros_like(gram_grad_ref)
            acts_grad_ref[...] = jnp.zeros_like(acts_grad_ref)

        taps_here = tap_ref[...]
        extended, pre = convolved(rim_ref[...], in_ref[...], taps_here)
        sigmoid = jax.nn.sigmoid(pre)
        acts = pre * sigmoid
        gate = gate_ref[...]
        out_grad = grad_ref[...] * (gate * jax.nn.sigmoid(gate))
        state = state_ref[...]
        end = end_ref[...]
        from_end = low_dot(b_low, end, 1, 0)
        from_start = low_dot(c_low, state, 1, 0)
        state_dot = jnp.sum(
            state.astype(jnp.float32) * end.astype(jnp.float32), axis=0, keepdims=True
        )
        last_row = lax.broadcasted_iota(jnp.int32, (length, 1), 0) == length - 1
        acts_grads, tails, grown_grads = ([], [], [])
        for head in range(2):
            lanes = slice(head * size, (head + 1) * size)
            step = step_ref[0][:, head : head + 1]
            col = col_ref[0][:, head : head + 1]
            row = row_ref[0][head : head + 1, :]
            here = acts[:, lanes]
            stepped = here * step
            stepped_low = stepped.astype(jnp.bfloat16)
            grad = out_grad[:, lanes]
            grad_low = grad.astype(jnp.bfloat16)
            grad_wide = grad_low.astype(jnp.float32)
            back_ref[...] = jnp.zeros_like(back_ref)
            row_terms = []
            for at in range(0, length, part):
                to = at + part
                decay = jnp.exp(jnp.minimum(col[at:to] - row[:, :to], 0.0))
                weights = (decay * gram_ref[at:to, :to]).astype(jnp.bfloat16)
                again = low_dot(weights, stepped_low[:to], 1, 0)
                row_terms.append(jnp.sum(again * grad_wide[at:to], axis=1, keepdims=True))
                back_ref[:to] += low_dot(weights, grad_low[at:to], 0, 0)
                gram_grad_ref[at:to, :to] += decay * low_dot(
                    grad_low[at:to], stepped_low[:to], 1, 1
                )
            back = back_ref[...]
            tail = jnp.exp(col[length - 1 : length] - col)
            growth = jnp.exp(col)
            ended = from_end[:, lanes] * tail
            end_terms = jnp.sum(ended * stepped, axis=1, keepdims=True)
            col_terms = jnp.sum(back * stepped_low.astype(jnp.float32), axis=1, keepdims=True)
            start_terms = growth * jnp.sum(from_start[:, lanes] * grad, axis=1, keepdims=True)
            whole = jnp.sum(end_terms, axis=0, keepdims=True) + growth[
                length - 1 : length
            ] * jnp.sum(state_dot[:, lanes], axis=1, keepdims=True)
            sum_grad_ref[0, :, head : head + 1] = (
                jnp.concatenate(row_terms, axis=0)
                + start_terms
                - col_terms
                - end_terms
                + jnp.where(last_row, whole, 0.0)
            )
            back = back + ended
            step_grad_ref[0, :, head : head + 1] = jnp.sum(back * here, axis=1, keepdims=True)
            acts_grads.append(taps_here[KW + 1 : KW + 2, lanes] * grad + back * step)
            tails.append((stepped * tail).astype(jnp.bfloat16))
            grown_grads.append((grad * growth).astype(jnp.bfloat16))
        acts_grad_ref[:, :state_dim] += low_dot(jnp.concatenate(tails, axis=1), end, 1, 1)
        acts_grad_ref[:, state_dim:] += low_dot(jnp.concatenate(grown_grads, axis=1), state, 1, 1)
        pre_grad = jnp.concatenate(acts_grads, axis=1) * silu_slope(pre, sigmoid)
        total, rows = convolved_back(extended, pre_grad, taps_here)
        gap = jnp.zeros((EXTRA - 8, wide), jnp.float32)
        in_grad_ref[...] = jnp.concatenate([total[8:], gap, total[:8]], axis=0).astype(jnp.bfloat16)
        rows.append(jnp.sum(out_grad * acts, axis=0, keepdims=True))
        rows.append(jnp.zeros((8 - len(rows), wide), jnp.float32))
        tap_grad_ref[...] = jnp.concatenate(rows, axis=0)

        @pl.when(pl.program_id(0) == pairs - 1)
        def _():
            gram_grad = gram_grad_ref[...]
            rows_of = lax.broadcasted_iota(jnp.int32, (length, length), 0)
            cols_of = lax.broadcasted_iota(jnp.int32, (length, length), 1)
            gram_grad = jnp.where(rows_of >= cols_of, gram_grad, 0.0).astype(jnp.bfloat16)
            acts_grad_ref[:, :state_dim] += low_dot(gram_grad, c_low, 0, 0)
            acts_grad_ref[:, state_dim:] += low_dot(gram_grad, b_low, 1, 0)
            bc_taps_here = bc_tap_ref[...]
            bc_extended, bc_pre = convolved(bc_rim_ref[...], bc_ref[...], bc_taps_here)
            bc_pre_grad = acts_grad_ref[...] * silu_slope(bc_pre, jax.nn.sigmoid(bc_pre))
            bc_total, bc_rows = convolved_back(bc_extended, bc_pre_grad, bc_taps_here)
            bc_grad_ref[:length] = bc_total[8:]
            bc_grad_ref[length : length + EXTRA - 8] = jnp.zeros((EXTRA - 8, shared), jnp.float32)
            bc_grad_ref[length + EXTRA - 8 :] = bc_total[:8]
            bc_rows.append(jnp.zeros((8 - len(bc_rows), shared), jnp.float32))
            bc_tap_grad_ref[...] = jnp.concatenate(bc_rows, axis=0)

    block = pl.BlockSpec((length, wide), lambda i: (0, i))
    eight = pl.BlockSpec((8, wide), lambda i: (0, i))
    table = pl.BlockSpec((1, length, 2), lambda i: (i, 0, 0))
    state_block = pl.BlockSpec((state_dim, wide), lambda i: (0, i))
    bc_block = pl.BlockSpec((length, shared), lambda i: (0, 0))
    bc_eight = pl.BlockSpec((8, shared), lambda i: (0, 0))
    wide_low = jax.ShapeDtypeStruct((length + EXTRA, inner), jnp.bfloat16)
    eight_f32 = jax.ShapeDtypeStruct((8, inner), jnp.float32)
    table_f32 = jax.ShapeDtypeStruct(step_cols.shape, jnp.float32)
    bc_f32 = jax.ShapeDtypeStruct((length + EXTRA, shared), jnp.float32)
    bc_eight_f32 = jax.ShapeDtypeStruct((8, shared), jnp.float32)
    return pl.pallas_call(
        body,
        grid=(pairs,),
        out_shape=(
            wide_low, eight_f32, table_f32, table_f32, bc_f32, bc_eight_f32
        ),
        in_specs=scan_blocks(shared, length, wide)
        + [
            block,
            pl.BlockSpec((length, wide), lambda i: (0, gate_at // wide + i)),
            state_block,
            state_block,
            bc_block,
        ],
        out_specs=(
            pl.BlockSpec((length + EXTRA, wide), lambda i: (0, i)),
            eight,
            table,
            table,
            pl.BlockSpec((length + EXTRA, shared), lambda i: (0, 0)),
            bc_eight,
        ),
        scratch_shapes=[
            pltpu.VMEM((length, length), jnp.float32),
            pltpu.VMEM((length, length), jnp.float32),
            pltpu.VMEM((length, shared), jnp.float32),
            pltpu.VMEM((length, size), jnp.float32),
        ],
        compiler_params=pltpu.CompilerParams(vmem_limit_bytes=56 << 20),
        name="scan_back",
    )(
        first_pre, first_pre, taps, mix_pre, mix_pre, bc_taps, step_cols, sum_cols, sum_rows,
        out_grads, second_pre, state_in, end_grad, bc_low,
    )


def turned(values, cos_wide, sin_wide):
    return values * cos_wide + pltpu.roll(values, values.shape[1] // 2, 1) * sin_wide


def own_mask(at, rows, keys, limit):
    query_row = lax.broadcasted_iota(jnp.int32, (rows, keys), 0) + at
    key_row = lax.broadcasted_iota(jnp.int32, (rows, keys), 1)
    return (key_row <= query_row) & (key_row < limit)


def attention_forward(layout, second_pre, query_at, window, cos_wide, sin_wide, heads):
    length = second_pre.shape[0] - EXTRA
    part = min(ATTN_ROWS, length)
    own_at = window.shape[0] - length
    scale = HD ** (-0.5)

    def body(layout_ref, query_ref, window_ref, cos_ref, sin_ref, out_ref, turned_ref, total_ref):
        query = turned(query_ref[...], cos_ref[...], sin_ref[...]).astype(jnp.bfloat16)
        turned_ref[...] = query
        for at in range(0, length, part):
            to = at + part
            here = query[at:to]

            def scores_of(keys):
                return scale * low_dot(here, keys, 1, 1)

            keys = window_ref[own_at : own_at + to, :HD]
            values = window_ref[own_at : own_at + to, HD:]
            scores = jnp.where(
                own_mask(at, part, to, layout_ref[1]), scores_of(keys), masked_score
            )
            top = jnp.max(scores, axis=1, keepdims=True)
            shares = jnp.exp(scores - top)
            total = jnp.sum(shares, axis=1, keepdims=True)
            acc = low_dot(shares, values, 1, 0)

            def earlier(distance, carry):
                top, total, acc = carry
                start = pl.multiple_of(own_at - distance * length, length)
                scores = scores_of(window_ref[pl.ds(start, length), :HD])
                new_top = jnp.maximum(top, jnp.max(scores, axis=1, keepdims=True))
                fade = jnp.exp(top - new_top)
                shares = jnp.exp(scores - new_top)
                total = fade * total + jnp.sum(shares, axis=1, keepdims=True)
                acc = fade * acc + low_dot(shares, window_ref[pl.ds(start, length), HD:], 1, 0)
                return (new_top, total, acc)

            top, total, acc = lax.fori_loop(1, layout_ref[0] + 1, earlier, (top, total, acc))
            out_ref[at:to] = (acc / total).astype(jnp.bfloat16)
            total_ref[0, at:to] = top + jnp.log(total)

    head = pl.BlockSpec((length, HD), lambda i, layout_ref: (0, i))
    whole = pl.BlockSpec((length, HD), lambda i, layout_ref: (0, 0))
    return pl.pallas_call(
        body,
        out_shape=(
            jax.ShapeDtypeStruct((length, heads * HD), jnp.bfloat16),
            jax.ShapeDtypeStruct((length, heads * HD), jnp.bfloat16),
            jax.ShapeDtypeStruct((heads, length, 1), jnp.float32),
        ),
        grid_spec=pltpu.PrefetchScalarGridSpec(
            num_scalar_prefetch=1,
            grid=(heads,),
            in_specs=[
                pl.BlockSpec((length, HD), lambda i, layout_ref: (0, query_at // HD + i)),
                pl.BlockSpec(window.shape, lambda i, layout_ref: (0, 0)),
                whole,
                whole,
            ],
            out_specs=(
                head,
                head,
                pl.BlockSpec((1, length, 1), lambda i, layout_ref: (i, 0, 0)),
            ),
        ),
        compiler_params=pltpu.CompilerParams(vmem_limit_bytes=48 << 20),
        name="attention_forward",
    )(layout, second_pre, window, cos_wide, sin_wide)


def attention_back(layout, query, window, out, totals, mixed_grad, grad_at, cos_wide, sin_wide):
    length = query.shape[0]
    heads = query.shape[1] // HD
    part = min(ATTN_ROWS, length)
    own_at = window.shape[0] - length
    scale = HD ** (-0.5)

    def body(
        layout_ref, query_ref, window_ref, out_in_ref, total_ref, grad_ref, cos_ref, sin_ref,
        query_grad_ref, window_grad_ref, own_grad_ref, sum_ref, acc_ref,
    ):
        @pl.when(pl.program_id(0) == 0)
        def _():
            sum_ref[...] = jnp.zeros_like(sum_ref)

        for at in range(0, length, part):
            to = at + part
            here = query_ref[at:to]
            grad = grad_ref[at:to].astype(jnp.bfloat16)
            dots = jnp.sum(
                grad.astype(jnp.float32) * out_in_ref[at:to].astype(jnp.float32),
                axis=1,
                keepdims=True,
            )
            total = total_ref[0, at:to]

            def step(start, count, mask):
                keys = window_ref[pl.ds(start, count), :HD]
                values = window_ref[pl.ds(start, count), HD:]
                probs = jnp.exp(scale * low_dot(here, keys, 1, 1) - total)
                if mask is not None:
                    probs = jnp.where(mask, probs, 0.0)
                score_grad = (probs * (low_dot(grad, values, 1, 1) - dots)).astype(jnp.bfloat16)
                sum_ref[pl.ds(start, count), :HD] += low_dot(score_grad, here, 0, 0)
                sum_ref[pl.ds(start, count), HD:] += low_dot(probs, grad, 0, 0)
                return low_dot(score_grad, keys, 1, 0)

            acc_ref[...] = step(own_at, to, own_mask(at, part, to, layout_ref[1]))

            def earlier(distance, carry):
                start = pl.multiple_of(own_at - distance * length, length)
                acc_ref[...] += step(start, length, None)
                return carry

            lax.fori_loop(1, layout_ref[0] + 1, earlier, 0)
            query_grad_ref[at:to] = turned(
                acc_ref[...] * scale, cos_ref[at:to], -sin_ref[at:to]
            ).astype(jnp.bfloat16)

        @pl.when(pl.program_id(0) == heads - 1)
        def _():
            own_grad_ref[:, :HD] = sum_ref[own_at:, :HD] * scale
            own_grad_ref[:, HD:] = sum_ref[own_at:, HD:]
            window_grad_ref[:, :HD] = (sum_ref[:own_at, :HD] * scale).astype(jnp.bfloat16)
            window_grad_ref[:, HD:] = sum_ref[:own_at, HD:].astype(jnp.bfloat16)

    head = pl.BlockSpec((length, HD), lambda i, layout_ref: (0, i))
    whole = pl.BlockSpec((length, HD), lambda i, layout_ref: (0, 0))
    return pl.pallas_call(
        body,
        out_shape=(
            jax.ShapeDtypeStruct(query.shape, jnp.bfloat16),
            jax.ShapeDtypeStruct((own_at, 2 * HD), jnp.bfloat16),
            jax.ShapeDtypeStruct((length, 2 * HD), jnp.float32),
        ),
        grid_spec=pltpu.PrefetchScalarGridSpec(
            num_scalar_prefetch=1,
            grid=(heads,),
            in_specs=[
                head,
                pl.BlockSpec(window.shape, lambda i, layout_ref: (0, 0)),
                head,
                pl.BlockSpec((1, length, 1), lambda i, layout_ref: (i, 0, 0)),
                pl.BlockSpec((length, HD), lambda i, layout_ref: (0, grad_at // HD + i)),
                whole,
                whole,
            ],
            out_specs=(
                head,
                pl.BlockSpec((own_at, 2 * HD), lambda i, layout_ref: (0, 0)),
                pl.BlockSpec((length, 2 * HD), lambda i, layout_ref: (0, 0)),
            ),
            scratch_shapes=[
                pltpu.VMEM(window.shape, jnp.float32),
                pltpu.VMEM((part, HD), jnp.float32),
            ],
        ),
        compiler_params=pltpu.CompilerParams(vmem_limit_bytes=56 << 20),
        name="attention_back",
    )(layout, query, window, out, totals, mixed_grad, cos_wide, sin_wide)


def per_device(
    tokens,
    cotangent,
    mix_norm_gain,
    ssm_gate_proj,
    ssm_input_proj,
    ssm_bc_proj,
    ssm_step_proj,
    conv_in_weight,
    conv_in_bias,
    conv_bc_weight,
    conv_bc_bias,
    step_bias,
    decay_log,
    skip_gain,
    ssm_out_proj,
    query_proj,
    key_proj,
    value_proj,
    attn_out_proj,
    ffn_norm_gain,
    ffn_gate_proj,
    ffn_up_proj,
    ffn_down_proj,
    extra_blocks,
    seq_order,
    pad_rows,
):
    block_rows = tokens.shape[0]
    block_index = lax.axis_index("ctx")
    seq_count = seq_order.shape[0]
    slot_ids = jnp.arange(seq_count, dtype=jnp.int32)
    chosen = (seq_order[:, None] == slot_ids[None, :]).astype(jnp.int32)
    counts = jnp.sum(chosen * extra_blocks[None, :], axis=1) + 1
    slot_pads = jnp.sum(chosen * pad_rows[None, :], axis=1)
    slot_ends = jnp.cumsum(counts)
    starts = slot_ends - counts
    inside = (starts <= block_index) & (block_index < slot_ends)
    within = jnp.sum(jnp.where(inside, block_index - starts, 0))
    pad_here = jnp.sum(jnp.where(inside & (slot_ends - 1 == block_index), slot_pads, 0))
    row_ids = jnp.arange(block_rows, dtype=jnp.int32)
    valid_rows = (row_ids < block_rows - pad_here).astype(jnp.float32)
    positions = within * block_rows + row_ids
    keep_state = (within > 0).astype(jnp.float32)
    devices = lax.axis_size("ctx")
    codes = jnp.asarray(slot_devices(devices), jnp.int32)
    from_whole = jnp.bitwise_xor(codes, block_index)
    to_whole = jnp.argsort(from_whole).astype(jnp.int32)
    rows_here = mix_norm_gain.shape[0]
    misc_here = jnp.concatenate(
        [
            ssm_step_proj,
            mix_norm_gain[:, None],
            ffn_norm_gain[:, None],
            conv_bc_weight.reshape(rows_here, 1),
            jnp.pad(conv_bc_bias, (0, rows_here - conv_bc_bias.shape[0]))[:, None],
        ],
        axis=1,
    )
    steps = ssm_step_proj.shape[1]
    misc_here = jnp.pad(misc_here, ((0, 0), (0, 128 - misc_here.shape[1])))
    inner, shared = (ssm_input_proj.shape[1], ssm_bc_proj.shape[1])
    heads_wide, pair_wide = (query_proj.shape[1], key_proj.shape[1])
    across = [4 * k for k in range(1, devices // 4)]
    mix_here = jnp.concatenate([ssm_bc_proj, misc_here, query_proj, key_proj, value_proj], axis=1)
    out_here = jnp.concatenate([ssm_out_proj, attn_out_proj], axis=0)
    first_here = jnp.concatenate([ssm_input_proj, mix_here, ssm_gate_proj], axis=1)
    first_held = spread([([0], first_here)], 0, across)
    gate_from = inner + mix_here.shape[1]
    input_held = spread([(here, piece[:, :inner]) for here, piece in first_held], 0, [1], merge=True)
    mix_held = [(here, piece[:, inner:gate_from]) for here, piece in first_held]
    mix_held = spread(mix_held, 0, [2], merge=True)
    gate_held = [(here, piece[:, gate_from:]) for here, piece in first_held]
    near = (input_held[-1][1], mix_held[-1][1])
    input_held = spread(input_held, 0, [2])
    mix_held = spread(mix_held, 0, [1])
    ffn_gate_weight = lax.all_gather(after(ffn_gate_proj, first_held[-1][1]), "ctx", axis=0, tiled=True)
    out_held = spread([([0], out_here)], 1, across, near)
    input_weight = joined(input_held, 0)
    mix_weights = joined(mix_held, 0)
    misc = mix_weights[:, shared : shared + 128]
    mix_gain = misc[:, steps].astype(jnp.float32)

    def whole_order(column):
        return jnp.take(column.reshape(devices, rows_here), to_whole, axis=0)

    conv_bc_full = whole_order(misc[:, steps + 2]).reshape(shared, KW)
    conv_bc_offset = whole_order(misc[:, steps + 3])[:, : conv_bc_bias.shape[0]].reshape(shared)
    gain_two = whole_order(misc[:, steps + 1]).reshape(-1)
    inputs = tokens.astype(jnp.float32)
    rim_rows = KW - 1
    edge = shifted(tokens[block_rows - EXTRA :], "ctx", 1)
    edge_rows = jnp.arange(EXTRA, dtype=jnp.int32)[:, None] >= EXTRA - rim_rows
    edge = jnp.where(edge_rows & (within > 0), edge, jnp.zeros_like(edge))
    tokens_longer = jnp.concatenate([tokens, edge], axis=0)
    normed_low = rms_scale(
        reordered(tokens_longer, from_whole).astype(jnp.float32), mix_gain
    ).astype(jnp.bfloat16)
    first_pre = plain_product(normed_low, input_weight)
    mix_pre = plain_product(normed_low, mix_weights)
    ffn_up_weight = lax.all_gather(after(ffn_up_proj, mix_pre), "ctx", axis=0, tiled=True)
    step_raw = mix_pre[:block_rows, shared : shared + steps]
    query_at = shared + 128
    key_at = query_at + heads_wide
    key_pre = mix_pre[:block_rows, key_at : key_at + pair_wide]
    value_pre = mix_pre[:block_rows, key_at + pair_wide :]
    gate_held = spread(gate_held, 0, [2], (first_pre,), merge=True)
    out_held = spread(out_held, 1, [1], (first_pre,), merge=True)
    head_dim = inner // steps
    skips = jnp.repeat(skip_gain.astype(jnp.float32), head_dim)[None, :]
    taps = jnp.concatenate(
        [conv_in_weight.astype(jnp.float32).T, conv_in_bias.astype(jnp.float32)[None, :], skips]
    )
    taps = jnp.pad(taps, ((0, 8 - taps.shape[0]), (0, 0)))
    bc_taps = jnp.concatenate(
        [conv_bc_full.astype(jnp.float32).T, conv_bc_offset.astype(jnp.float32)[None, :]]
    )
    bc_taps = jnp.pad(bc_taps, ((0, 8 - bc_taps.shape[0]), (0, 0)))
    step_in = step_raw + step_bias.astype(jnp.float32)[None, :]
    step_size = jax.nn.softplus(step_in)
    rate = -jnp.exp(decay_log.astype(jnp.float32))[None, :]
    lower = (row_ids[:, None] >= row_ids[None, :]).astype(jnp.float32)
    log_decay = jnp.dot(lower, rate * step_size, precision=highest)

    def by_pairs(table):
        return table.reshape(block_rows, steps // 2, 2).transpose(1, 0, 2)

    def from_pairs(table):
        return table.transpose(1, 0, 2).reshape(block_rows, steps)

    step_cols = by_pairs(step_size)
    sum_cols = by_pairs(log_decay)
    sum_rows = log_decay.T.reshape(steps // 2, 2, block_rows)
    intra_out, local_states, bc_low = scan_forward(
        first_pre, mix_pre, taps, bc_taps, step_cols, sum_cols, sum_rows, inner, shared
    )
    ffn_down_weight = lax.all_gather(after(ffn_down_proj, local_states), "ctx", axis=1, tiled=True)
    decay_row = keep_state * jnp.repeat(jnp.exp(log_decay[block_rows - 1]), head_dim)[None, :]
    keep_low = keep_state.astype(jnp.bfloat16)
    reached, returned = carried_states(local_states, decay_row, False)
    state_in = keep_low * reached
    gate_held = spread(gate_held, 0, [1], (returned,))
    out_held = spread(out_held, 1, [2], (returned,))
    cos_table, sin_table = rotary_tables(positions)
    cos_wide = jnp.concatenate([cos_table, cos_table], axis=1)
    sin_wide = jnp.concatenate([-sin_table, sin_table], axis=1)
    key_rot = rotate(key_pre.reshape(block_rows, -1, HD), cos_table, sin_table)
    own_pair = jnp.concatenate(
        [key_rot.reshape(block_rows, HD).astype(jnp.bfloat16), value_pre.astype(jnp.bfloat16)],
        axis=1,
    )
    earlier_pairs = [shifted(own_pair, "ctx", distance) for distance in range(MAXB - 1, 0, -1)]
    window = jnp.concatenate(earlier_pairs + [own_pair], axis=0)
    layout = jnp.stack([within, block_rows - pad_here]).astype(jnp.int32)
    attn_low, query_rot, log_totals = attention_forward(
        layout, mix_pre, query_at, window, cos_wide, sin_wide, heads_wide // HD
    )
    gate_weight = joined(gate_held, 0)
    gate_pre = plain_product(normed_low, gate_weight)
    scan_out, ssm_low = scan_gated(intra_out, state_in, bc_low, sum_cols, gate_pre, 0)
    out_weights = joined(out_held, 1)
    mixed_low = jnp.concatenate([ssm_low, attn_low], axis=1)
    mixed_part = plain_product(mixed_low, out_weights)
    hidden = inputs + reordered(pair_sum(mixed_part), to_whole)
    normed_two, norm_two_back = jax.vjp(rms_scale, hidden, gain_two.astype(jnp.float32))
    normed_two_low = normed_two.astype(jnp.bfloat16)
    ffn_gate = plain_product(normed_two_low, ffn_gate_weight)
    ffn_up = plain_product(normed_two_low, ffn_up_weight)
    ffn_act = (jax.nn.silu(ffn_gate) * ffn_up).astype(jnp.bfloat16)
    ffn_part = plain_product(ffn_act, ffn_down_weight)
    ffn_sum = pair_sum(ffn_part)
    layer_out = ((hidden + ffn_sum) * valid_rows[:, None]).astype(jnp.bfloat16)
    cot_low = (cotangent.astype(jnp.float32) * valid_rows[:, None]).astype(jnp.bfloat16)
    grad_out = cot_low.astype(jnp.float32)

    def in_quarters(value):
        return jnp.split(value, 4, axis=1)

    def rows_grad(left_side, right_side, first, gates=(), later=()):
        parts = [product_of_cols(part, right_side) for part in in_quarters(left_side)]
        return Reduction(parts, 0, first, gates, later)

    def cols_grad(left_side, right_side, first, gates=()):
        parts = [product_of_cols(left_side, part) for part in in_quarters(right_side)]
        return Reduction(parts, 1, first, gates)

    down_sum = cols_grad(ffn_act, reordered(cot_low, from_whole), 1)
    act_grad = product_by_rows(cot_low, ffn_down_weight)
    gate_sigmoid = jax.nn.sigmoid(ffn_gate)
    ffn_gate_low = (
        act_grad * ffn_up * gate_sigmoid * (1.0 + ffn_gate * (1.0 - gate_sigmoid))
    ).astype(jnp.bfloat16)
    ffn_up_low = (act_grad * jax.nn.silu(ffn_gate)).astype(jnp.bfloat16)
    norm_two_part = product_by_rows(ffn_gate_low, ffn_gate_weight) + product_by_rows(
        ffn_up_low, ffn_up_weight
    )
    norm_two_grad = pair_sum(norm_two_part)
    hidden_norm_grad, gain_two_grad = norm_two_back(norm_two_grad)
    hidden_grad = grad_out + hidden_norm_grad
    hidden_low = reordered(hidden_grad.astype(jnp.bfloat16), from_whole)
    mixed_grad = product_by_rows(hidden_low, out_weights)
    ssm_gate_low, state_in_grad = scan_gated_back(
        mixed_grad, scan_out, bc_low, sum_cols, gate_pre, 0
    )
    end_grad, returned = carried_states(keep_low * state_in_grad, decay_row, True)
    layout = after(layout, returned)
    query_grad_low, window_grad, own_pair_grad = attention_back(
        layout, query_rot, window, attn_low, log_totals, mixed_grad, inner, cos_wide, sin_wide
    )
    for distance in range(1, MAXB):
        at = (MAXB - 1 - distance) * block_rows
        own_pair_grad = own_pair_grad + shifted(
            window_grad[at : at + block_rows], "ctx", -distance
        ).astype(jnp.float32)
    down_sum.onward(end_grad, query_grad_low)
    free = (end_grad, query_grad_low)
    normed_two_slots = reordered(normed_two_low, from_whole)
    swish_sum = rows_grad(normed_two_slots, ffn_gate_low, 2, (ssm_gate_low,), free)
    up_sum = rows_grad(normed_two_slots, ffn_up_low, 1, (ssm_gate_low,), free)
    out_sum = cols_grad(mixed_low, hidden_low, 1, free)
    gate_sum = rows_grad(normed_low, ssm_gate_low, 2, free)
    key_grad_low = (
        rotate(own_pair_grad[:, :HD].reshape(block_rows, 1, HD), cos_table, -sin_table)
        .reshape(block_rows, HD)
        .astype(jnp.bfloat16)
    )
    value_grad_low = own_pair_grad[:, HD:].astype(jnp.bfloat16)
    input_grad_low, tap_grad, step_part, sum_part, bc_pre_part, bc_tap_grad = scan_back(
        first_pre, mix_pre, taps, bc_taps, step_cols, sum_cols, sum_rows,
        mixed_grad, gate_pre, 0, state_in, end_grad, bc_low,
    )
    rate_grad = lax.dot_general(
        lower, from_pairs(sum_part), (((0,), (0,)), ((), ())), precision=highest
    )
    step_grad = (from_pairs(step_part) + rate * rate_grad) * jax.nn.sigmoid(step_in)
    step_grad_low = step_grad.astype(jnp.bfloat16)
    tap_sums = [
        tap_grad[:KW].T,
        tap_grad[KW],
        jnp.sum(step_grad, axis=0),
        jnp.sum(rate_grad * rate * step_size, axis=0),
        jnp.sum(tap_grad[KW + 1].reshape(steps, head_dim), axis=1),
    ]
    no_misc = jnp.zeros((block_rows, 128 - steps), jnp.bfloat16)
    mix_grads = jnp.concatenate(
        [step_grad_low, no_misc, query_grad_low, key_grad_low, value_grad_low], axis=1
    )
    mix_grads = jnp.pad(mix_grads, ((0, EXTRA), (0, 0)))
    bc_grad_low = pair_sum(bc_pre_part).astype(jnp.bfloat16)
    input_sum = rows_grad(normed_low, input_grad_low, 1)
    mix_sum = rows_grad(normed_low, jnp.concatenate([bc_grad_low, mix_grads], axis=1), 2)
    mix_grads = jnp.concatenate([bc_pre_part.astype(jnp.bfloat16), mix_grads], axis=1)
    norm_one_part = (
        product_by_rows(input_grad_low, input_weight)
        + product_by_rows(mix_grads, mix_weights)
        + product_by_rows(ssm_gate_low, gate_weight)
    )
    up_sum.onward(norm_one_part)
    swish_sum.onward(up_sum.far_low)
    norm_one_grad = reordered(pair_sum(norm_one_part), to_whole)
    conv_bc_grads = jnp.concatenate([bc_tap_grad[:KW].T.reshape(-1), bc_tap_grad[KW]])
    conv_bc_grads = conv_bc_grads + swap(conv_bc_grads)
    longer = tokens_longer.astype(jnp.float32)
    scale_one = lax.rsqrt(jnp.mean(longer * longer, axis=1, keepdims=True) + epsilon)
    gain_one_grad = jnp.sum(norm_one_grad * longer * scale_one, axis=0)
    small = [
        tap_sums[0].reshape(-1),
        *tap_sums[1:],
        conv_bc_grads,
        gain_one_grad,
        gain_two_grad,
    ]
    packed = jnp.concatenate(small)
    filled = -packed.shape[0] % 1024
    high_bits = [bit for bit in (32, 16, 8, 4) if bit < devices]
    packed = summed(jnp.pad(packed, (0, filled)).reshape(-1, 128), high_bits)
    down_sum.last(packed)
    out_sum.onward(*down_sum.blocks_low)
    gate_sum.onward(out_sum.far_low)
    up_sum.last(gate_sum.far_low)
    swish_sum.last(*up_sum.blocks_low)
    mix_sum.onward(*swish_sum.blocks_low)
    input_sum.onward(mix_sum.far_low)
    gate_sum.last(input_sum.far_low)
    out_sum.last(*gate_sum.blocks_low)
    mix_sum.last(*out_sum.blocks_low)
    input_sum.last(*mix_sum.blocks_low)
    edge_grad = after(norm_one_grad[block_rows + EXTRA - 8 :], *input_sum.blocks_low)
    edge_back = shifted(keep_state * edge_grad, "ctx", -1)
    norm_one_grad = norm_one_grad[:block_rows] + jnp.pad(edge_back, ((block_rows - 8, 0), (0, 0)))
    _, norm_one_back = jax.vjp(lambda v: rms_scale(v, whole_order(mix_gain).reshape(-1)), inputs)
    tokens_grad = hidden_grad + norm_one_back(norm_one_grad)[0]
    packed = summed(after(packed, *input_sum.blocks_low), (2, 1)).reshape(-1)
    sums, at = ([], 0)
    for part in small:
        sums.append(packed[at : at + part.shape[0]])
        at += part.shape[0]

    def own(vector, count):
        return lax.dynamic_slice_in_dim(vector, block_index * count, count, 0)

    mix_grad = mix_sum.total()
    out_grad = out_sum.total()
    conv_bc_sums = sums[5]
    conv_rows = conv_bc_weight.shape[0]
    return (
        layer_out,
        tokens_grad.astype(jnp.bfloat16),
        own(sums[6], rows_here),
        gate_sum.total(),
        input_sum.total(),
        mix_grad[:, :shared],
        mix_grad[:, shared : shared + steps],
        sums[0].reshape(inner, KW),
        sums[1],
        own(conv_bc_sums[: shared * KW], conv_rows * KW).reshape(conv_rows, KW),
        own(conv_bc_sums[shared * KW :], conv_rows),
        sums[2],
        sums[3],
        sums[4],
        out_grad[:inner],
        mix_grad[:, query_at:key_at],
        mix_grad[:, key_at : key_at + pair_wide],
        mix_grad[:, key_at + pair_wide :],
        out_grad[inner:],
        own(sums[7], rows_here),
        swish_sum.total(),
        up_sum.total(),
        down_sum.total(),
    )


def solution(mesh):
    return jax.shard_map(
        per_device,
        mesh=mesh,
        in_specs=(
            P("ctx", None),
            P("ctx", None),
            P("ctx"),
            P("ctx", "wt"),
            P("ctx", "wt"),
            P("ctx", None),
            P("ctx", "wt"),
            P("wt", None),
            P("wt"),
            P("ctx", None),
            P("ctx"),
            P("wt"),
            P("wt"),
            P("wt"),
            P("wt", "ctx"),
            P("ctx", "wt"),
            P("ctx", "wt"),
            P("ctx", "wt"),
            P("wt", "ctx"),
            P("ctx"),
            P("ctx", "wt"),
            P("ctx", "wt"),
            P("wt", "ctx"),
            P(),
            P(),
            P(),
        ),
        out_specs=(
            P("ctx", None),
            P("ctx", None),
            P("ctx"),
            P("ctx", "wt"),
            P("ctx", "wt"),
            P("ctx", None),
            P("ctx", "wt"),
            P("wt", None),
            P("wt"),
            P("ctx", None),
            P("ctx"),
            P("wt"),
            P("wt"),
            P("wt"),
            P("wt", "ctx"),
            P("ctx", "wt"),
            P("ctx", "wt"),
            P("ctx", "wt"),
            P("wt", "ctx"),
            P("ctx"),
            P("ctx", "wt"),
            P("ctx", "wt"),
            P("wt", "ctx"),
        ),
        check_vma=False,
    )
```
